32 devices in a mesh: groups: 2 (over y), leaf: 4 (over z), sub: 2 (over x), vec: 2 (over core).
Axes of the slice: x: 2, y: 2, z: 4, core: 2. Of those that a mesh axis runs over, the one named last changes fastest.
Arguments:
- points: float32 [6, 262144], P('groups', ('leaf', 'sub')), parts along dimension 0, may hold values from 0 to 1
- inv_scale: float32 [6], P('groups'), parts along dimension 0, may hold values from 2 to 6
- noise: float32 [524288], P(('groups', 'leaf', 'sub')), parts along dimension 0, may hold values from 0.05 to 0.5
- vectors: bfloat16 [32, 262144], P(('groups', 'vec'), ('leaf', 'sub')), parts along dimension 0, may hold values from -6 to 6
- leaf_basis: bfloat16 [2048, 64, 256], P(('groups', 'leaf', 'sub')), parts along dimension 0, may hold values from -0.375 to 0.375
- local_transfer: bfloat16 [2032, 2, 64, 64], P(('groups', 'leaf', 'sub')), parts along dimension 0, may hold values from -0.5 to 0.5
- top_transfer: bfloat16 [8, 2, 64, 64], P('groups'), parts along dimension 0, may hold values from -0.5 to 0.5
- local_coupling: bfloat16 [4080, 3, 64, 64], P(('groups', 'leaf', 'sub')), parts along dimension 0, may hold values from -0.4375 to 0.4375
- top_coupling: bfloat16 [8, 3, 64, 64], P('groups'), parts along dimension 0, may hold values from -0.4375 to 0.4375
- local_partners: int32 [4080, 3], P(('groups', 'leaf', 'sub')), parts along dimension 0, may hold values from 0 to 1023, as said below
- top_partners: int32 [8, 3], P('groups'), parts along dimension 0, may hold values from 0 to 3, as said below
- near_offsets: int32 [2048], P(('groups', 'leaf', 'sub')), parts along dimension 0, may hold values from 0 to 511, as said below
- near_cols: int32 [8192], P(('groups', 'leaf', 'sub')), parts along dimension 0, may hold values from 0 to 1023, as said below
Outputs:
- product: float32 [32, 262144], P(('groups', 'vec'), ('leaf', 'sub')), parts along dimension 0
The draws below stay inside these ranges and needn't reach their ends.
There are 2 independent parts, one for each index of `groups`. The reference program is written for one: setup_inputs(seed, part) draws one part's arguments, and reference() takes and returns one part's arrays. A program takes and returns all parts, laid end to end along the dimension named above; each array names one. Nothing has to cross between parts.
Inputs may be any that keep to these rules, and one draw needn't show every extreme that they name: `local_partners`: row e * 255 + 2 ** k - 1 + h lists the far-field partners of node e * 2 ** k + h of level t + k (see the steps): 3 distinct nodes of that level, never the node itself, all in the node's aligned group of 2 ** 3 nodes. `top_partners`: row 2 ** m - 4 + i lists the far-field partners of node i of level m: 3 distinct nodes of that level, never the node itself, all in the node's aligned group of 2 ** 3 nodes (at level 2, the other three nodes). `near_offsets`: within each device's 128 leaves the offsets rise from 0; each leaf owns 1 to 7 consecutive blocks, some leaf of every device exactly 7, and a device's leaves own exactly 512 blocks. `near_cols`: A leaf's first block is the leaf itself; its column leaves are distinct and each lies within 128 leaves of the row leaf in tree order.
All inputs are finite; a program needn't handle non-finite values.
Results may differ from the reference program's by a relative error of at most 0.0028.
Values may be sent and summed in bfloat16 or wider, within the bound.
No kernel may reach another device: no remote copies, remote signals or barrier semaphores. Data moves between devices by JAX's collectives and lax.ppermute only.
A program may use at most 128 MiB of HBM per device.

```python
import math
import jax
import jax.numpy as jnp
from jax import lax

LEAF = 256
BASIS_RANK = 64
VECTOR_COUNT = 16
LD = 128
NEAR_AVG = 4
FAR = 3
SPAN = 3
NDEV = 8
NLEAVES = 1024
NPTS = 262144
NLOC = 255
NTOP = 4
NBD = 512
MOST = 7


def floor_log(values, limit):
    running = jnp.zeros_like(values)
    for power in range(1, limit + 1):
        running = running + (values >= 2 ** power).astype(jnp.int32)
    return running


def power_two(exponent):
    return jnp.left_shift(jnp.ones_like(exponent), exponent)


def pick_partners(key, node_index, group_width, row_count):
    member_count = 2 ** SPAN
    scores = jax.random.randint(key, (row_count, member_count), 0, 1 << 20)
    member = jnp.arange(member_count, dtype=jnp.int32)[None, :]
    scores = scores * member_count + member
    own_slot = (node_index % group_width)[:, None]
    banned = (member == own_slot) | (member >= group_width[:, None])
    scores = jnp.where(banned, scores + (1 << 27), scores)
    order = jnp.argsort(scores, axis=1)
    chosen = order[:, :FAR].astype(jnp.int32)
    base_node = node_index - node_index % group_width
    return (base_node[:, None] + chosen).astype(jnp.int32)


def draw_local_partners(key, part):
    heap_ids = jnp.tile(jnp.arange(1, NLOC + 1, dtype=jnp.int32), NDEV)
    device_ids = jnp.repeat(jnp.arange(NDEV, dtype=jnp.int32), NLOC)
    depth_local = floor_log(heap_ids, LD.bit_length())
    node_index = device_ids * power_two(depth_local) + heap_ids - power_two(depth_local)
    group_width = jnp.full_like(node_index, 2 ** SPAN)
    return pick_partners(jax.random.fold_in(key, 21), node_index, group_width, NDEV * NLOC)


def draw_top_partners(key, part):
    heap_ids = jnp.arange(NTOP, dtype=jnp.int32) + 4
    depth_top = floor_log(heap_ids, NDEV.bit_length())
    node_index = heap_ids - power_two(depth_top)
    group_width = jnp.minimum(power_two(depth_top), 2 ** SPAN)
    return pick_partners(jax.random.fold_in(key, 22), node_index, group_width, NTOP)


def near_layout(key):
    base_key = jax.random.fold_in(key, 31)
    pair_count = LD // 2
    shifts = jax.random.randint(jax.random.fold_in(base_key, 1), (NDEV, pair_count), 1 - NEAR_AVG, NEAR_AVG)
    forced = jax.random.randint(jax.random.fold_in(base_key, 2), (NDEV, 1), 0, pair_count)
    shifts = jnp.where(jnp.arange(pair_count, dtype=jnp.int32)[None, :] == forced, NEAR_AVG - 1, shifts)
    counts = jnp.stack([NEAR_AVG + shifts, NEAR_AVG - shifts], axis=2).reshape(NDEV, LD)
    starts = (jnp.cumsum(counts, axis=1) - counts).astype(jnp.int32)
    span_width = 2 * LD
    offsets = jnp.concatenate([jnp.arange(-LD, 0, dtype=jnp.int32), jnp.arange(1, LD + 1, dtype=jnp.int32)])
    leaf_ids = jnp.arange(NLEAVES, dtype=jnp.int32)[:, None]
    target = leaf_ids + offsets[None, :]
    scores = jax.random.randint(jax.random.fold_in(base_key, 3), (NLEAVES, span_width), 0, 2 * LD) + 2 * jnp.abs(offsets)[None, :]
    scores = scores * span_width + jnp.arange(span_width, dtype=jnp.int32)[None, :]
    outside = (target < 0) | (target >= NLEAVES)
    scores = jnp.where(outside, scores + (1 << 26), scores)
    order = jnp.argsort(scores, axis=1)[:, :MOST - 1]
    chosen = jnp.take_along_axis(target, order, axis=1)
    columns = jnp.concatenate([leaf_ids, chosen], axis=1)
    slot_ids = jnp.arange(NBD, dtype=jnp.int32)
    owner = jnp.sum((starts[:, None, :] <= slot_ids[None, :, None]).astype(jnp.int32), axis=2) - 1
    within = slot_ids[None, :] - jnp.take_along_axis(starts, owner, axis=1)
    leaf_global = owner + jnp.arange(NDEV, dtype=jnp.int32)[:, None] * LD
    cols = columns[leaf_global.reshape(-1), within.reshape(-1)]
    return (starts.reshape(-1).astype(jnp.int32), cols.astype(jnp.int32))


def draw_near_offsets(key, part):
    return near_layout(key)[0]


def draw_near_cols(key, part):
    return near_layout(key)[1]


def level_of(rng, extent, pieces, least, top_value):
    def one(position, shards_of):
        heights = jax.random.uniform(jax.random.fold_in(jax.random.fold_in(rng, 6), position), (shards_of,), jnp.float32, least / len(pieces), top_value / len(pieces))
        return jnp.repeat(jnp.exp(heights), extent[position] // shards_of).reshape((-1,) + (1,) * (len(extent) - position - 1))

    factor_of = one(*pieces[0])
    for cut in pieces[1:]:
        factor_of = factor_of * one(*cut)
    return factor_of


def gaussian(own_key, shape, width, most, cuts=(), kind=jnp.bfloat16):
    factor_of = level_of(own_key, shape, cuts, -0.22, 0.18) if cuts else 1.0
    drawn = jax.random.normal(own_key, shape, jnp.float32) * width * factor_of
    return jnp.minimum(jnp.maximum(drawn, -most), most).astype(kind)


def setup_inputs(seed: int = 0, part: int = 0) -> dict:
    streams_of = jax.random.split(jax.random.key(seed), 14)
    part_keys = jax.random.split(jax.random.fold_in(streams_of[13], part), 14)
    return {
        "points": jnp.clip(1.0 * jax.random.uniform(part_keys[0], (3, NPTS), jnp.float32) ** level_of(part_keys[0], (3, NPTS), ((1, 8),), -0.2, 0.2), 0.0, 1.0),
        "inv_scale": jnp.clip(jnp.exp(jax.random.uniform(part_keys[1], (3,), jnp.float32, math.log(2.0), math.log(6.0))), 2.0, 6.0),
        "noise": jnp.clip(jnp.exp(math.log(0.5) - 2.3025851 * jax.random.uniform(part_keys[2], (NPTS,), jnp.float32) ** level_of(part_keys[2], (NPTS,), ((0, 8),), -0.2, 0.2)), 0.05, 0.5),
        "vectors": gaussian(part_keys[3], (VECTOR_COUNT, NPTS), 1.0, 6.0, ((0, 2), (1, 8))),
        "leaf_basis": gaussian(part_keys[4], (NLEAVES, BASIS_RANK, LEAF), LEAF ** -0.5, 0.375, ((0, 8),)),
        "local_transfer": gaussian(part_keys[5], (NDEV * (LD - 1), 2, BASIS_RANK, BASIS_RANK), (2 * BASIS_RANK) ** -0.5, 0.5, ((0, 8),)),
        "top_transfer": gaussian(part_keys[6], (NTOP, 2, BASIS_RANK, BASIS_RANK), (2 * BASIS_RANK) ** -0.5, 0.5),
        "local_coupling": gaussian(part_keys[7], (NDEV * NLOC, FAR, BASIS_RANK, BASIS_RANK), (FAR * BASIS_RANK) ** -0.5, 0.4375, ((0, 8),)),
        "top_coupling": gaussian(part_keys[8], (NTOP, FAR, BASIS_RANK, BASIS_RANK), (FAR * BASIS_RANK) ** -0.5, 0.4375),
        "local_partners": draw_local_partners(jax.random.fold_in(jax.random.fold_in(streams_of[13], part), 71), part),
        "top_partners": draw_top_partners(jax.random.fold_in(jax.random.fold_in(streams_of[13], part), 71), part),
        "near_offsets": draw_near_offsets(jax.random.fold_in(jax.random.fold_in(streams_of[13], part), 71), part),
        "near_cols": draw_near_cols(jax.random.fold_in(jax.random.fold_in(streams_of[13], part), 71), part),
    }


TOP_DEPTH = lax.Precision.HIGHEST

def matern_block(row_coords, col_coords, inv_scale):
    running = jnp.zeros(row_coords.shape[1:] + (col_coords.shape[2],), jnp.float32)
    for axis_index in range(3):
        spread = (row_coords[axis_index][:, :, None] - col_coords[axis_index][:, None, :]) * inv_scale[axis_index]
        running = running + spread * spread
    scaled = jnp.sqrt(3.0 * running)
    return (1.0 + scaled) * jnp.exp(-scaled)

def round_low(values):
    return lax.optimization_barrier(values.astype(jnp.bfloat16)).astype(jnp.float32)

def level_slice(local_array, top_array, hierarchy_level, dev_levels):
    if hierarchy_level < dev_levels:
        return top_array[2 ** hierarchy_level - 4:2 ** (hierarchy_level + 1) - 4]
    current_depth = hierarchy_level - dev_levels
    per_device = local_array.shape[0] // NDEV
    grouped = local_array.reshape((NDEV, per_device) + local_array.shape[1:])
    picked = grouped[:, 2 ** current_depth - 1:2 ** (current_depth + 1) - 1]
    return picked.reshape((-1,) + local_array.shape[1:])

def reference(points, inv_scale, noise, vectors, leaf_basis, local_transfer, top_transfer, local_coupling, top_coupling, local_partners, top_partners, near_offsets, near_cols):
    dev_levels = NDEV.bit_length() - 1
    leaf_levels = LD.bit_length() - 1
    last_level = dev_levels + leaf_levels
    vec_float = vectors.astype(jnp.float32)
    leaf_vec = vec_float.reshape(VECTOR_COUNT, NLEAVES, LEAF)
    coords = points.reshape(3, NLEAVES, LEAF)
    slot_ids = jnp.arange(NBD, dtype=jnp.int32)
    starts = near_offsets.reshape(NDEV, LD)
    row_local = lax.optimization_barrier(jnp.sum((starts[:, None, :] <= slot_ids[None, :, None]).astype(jnp.int32), axis=2)) - 1
    rows_all = (row_local + (jnp.arange(NDEV, dtype=jnp.int32) * LD)[:, None]).astype(jnp.int32)
    cols_all = near_cols.reshape(NDEV, NBD).astype(jnp.int32)

    def near_device(running, block_ids):
        rows_now, cols_now = block_ids
        kernel = round_low(matern_block(coords[:, rows_now], coords[:, cols_now], inv_scale))
        product = jnp.einsum('bij,vbj->vbi', kernel, leaf_vec[:, cols_now], precision=TOP_DEPTH)
        return (running.at[:, rows_now].add(product), None)
    start_sum = jnp.zeros((VECTOR_COUNT, NLEAVES, LEAF), jnp.float32)
    near_sum = lax.scan(near_device, start_sum, (rows_all, cols_all))[0].reshape(VECTOR_COUNT, NPTS)
    basis_float = leaf_basis.astype(jnp.float32)
    upward_pass = {}
    upward_pass[last_level] = jnp.einsum('nrl,vnl->nvr', basis_float, leaf_vec, precision=TOP_DEPTH)
    for hierarchy_level in range(last_level - 1, 1, -1):
        current_pairs = level_slice(local_transfer, top_transfer, hierarchy_level, dev_levels).astype(jnp.float32)
        child_node = upward_pass[hierarchy_level + 1].reshape(-1, 2, VECTOR_COUNT, BASIS_RANK)
        upward_pass[hierarchy_level] = jnp.einsum('fwza,fwka->fkz', current_pairs, child_node, precision=TOP_DEPTH)
    coupled = {}
    for hierarchy_level in range(2, last_level + 1):
        mats = level_slice(local_coupling, top_coupling, hierarchy_level, dev_levels).astype(jnp.float32)
        partner_ids = level_slice(local_partners, top_partners, hierarchy_level, dev_levels).astype(jnp.int32)
        coupled[hierarchy_level] = jnp.einsum('nfrs,nfvs->nvr', mats, upward_pass[hierarchy_level][partner_ids], precision=TOP_DEPTH)
    current_downward = coupled[2]
    for hierarchy_level in range(2, last_level):
        current_pairs = level_slice(local_transfer, top_transfer, hierarchy_level, dev_levels).astype(jnp.float32)
        pushed_down = jnp.einsum('tkhb,tuh->tkub', current_pairs, current_downward, precision=TOP_DEPTH).reshape(-1, VECTOR_COUNT, BASIS_RANK)
        current_downward = coupled[hierarchy_level + 1] + pushed_down
    down_low = round_low(current_downward)
    far_part = jnp.einsum('nrl,nvr->vnl', basis_float, down_low, precision=TOP_DEPTH).reshape(VECTOR_COUNT, NPTS)
    return near_sum + noise[None, :] * vec_float + far_part
```

```python
import functools
import math

import jax
import jax.numpy as jnp
from jax import lax
from jax.experimental import pallas as pl
from jax.experimental.pallas import tpu as pltpu
from jax.sharding import PartitionSpec as P

BF = jnp.bfloat16
F32 = jnp.float32
LEAF = 256
RANK = 64
SPAN = 3
PART = 8
EXPORT = 2**SPAN - 1
NEG_LOG2E = -1.0 / math.log(2.0)
ROOT3 = math.sqrt(3.0)
TINY = 1e-12
PAIR = 2
PAD = 16
CODE = 1024
VMEM = pltpu.VMEM
SMEM = pltpu.SMEM
NT = (((1,), (1,)), ((), ()))


def vspec():
    return pl.BlockSpec(memory_space=pltpu.VMEM)


def sspec():
    return pl.BlockSpec(memory_space=pltpu.SMEM)


def aspec():
    return pl.BlockSpec(memory_space=pl.ANY)


def params(mib):
    return pltpu.CompilerParams(vmem_limit_bytes=mib << 20)


def lanes(index):
    return pl.ds(pl.multiple_of(index * LEAF, LEAF), LEAF)


def coordinate_rows(raw, scale_ref):
    width = raw.shape[1]
    row = lax.broadcasted_iota(jnp.int32, (8, width), 0)
    scale = jnp.where(
        row == 0, scale_ref[0], jnp.where(row == 1, scale_ref[1], scale_ref[2])
    )
    full = jnp.concatenate([raw, jnp.zeros((5, width), F32)], axis=0)
    scaled = (full - 0.5) * (scale * ROOT3)
    scaled = jnp.where(row < 3, scaled, 0.0)
    high = scaled.astype(BF).astype(F32)
    rest = (scaled - high).astype(BF).astype(F32)
    return high + pltpu.roll(rest, 4, 0)


def norm_parts(rows):
    swapped = pltpu.roll(rows, 4, 0)
    norm = jnp.sum(rows * (rows + swapped), axis=0, keepdims=True)
    high = norm.astype(BF).astype(F32)
    rest = norm - high
    mid = rest.astype(BF).astype(F32)
    return swapped, high, mid, rest - mid


def row_features(rows):
    swapped, high, mid, low = norm_parts(rows)
    row = lax.broadcasted_iota(jnp.int32, rows.shape, 0)
    tail = jnp.where(
        row < 3,
        1.0,
        jnp.where(row == 3, high, jnp.where(row == 4, mid, jnp.where(row == 5, low, 0.0))),
    )
    return jnp.concatenate([rows, swapped, tail, jnp.zeros_like(rows)], axis=0).astype(BF)


def col_features(rows):
    _, high, mid, low = norm_parts(rows)
    row = lax.broadcasted_iota(jnp.int32, rows.shape, 0)
    tail = jnp.where(
        row == 0,
        high,
        jnp.where(row == 1, mid, jnp.where(row == 2, low, jnp.where(row < 6, 1.0, 0.0))),
    )
    both = -2.0 * rows
    return jnp.concatenate([both, both, tail, jnp.zeros_like(rows)], axis=0).T.astype(BF)


def matern(squared):
    squared = jnp.maximum(squared, TINY)
    dist = squared * lax.rsqrt(squared)
    return ((1.0 + dist) * jnp.exp2(dist * NEG_LOG2E)).astype(BF)


def pack_kernel(where_ref, scale_ref, points_ref, vec_ref, got_ref, out_ref):
    half = got_ref.shape[1]
    base = where_ref[1] * half

    def step(i, _):
        here = pl.ds(pl.multiple_of(i * 2048, 2048), 2048)
        there = pl.ds(pl.multiple_of(base + i * 2048, 2048), 2048)
        rows = coordinate_rows(points_ref[:, there], scale_ref)
        out_ref[:, here] = jnp.concatenate(
            [vec_ref[:, there].astype(F32), got_ref[:, here].astype(F32), rows], axis=0
        ).astype(BF)
        return 0

    lax.fori_loop(0, half // 2048, step, 0)


def block_loop(count, list_ref, row_ref, col_ref, val_ref, acc_ref, s0, s1, k0, k1):
    def accumulate(first, kern):
        for q in range(PAIR):
            code = list_ref[first + q]
            here = lanes(code // CODE)
            acc_ref[:, here] += jnp.dot(
                val_ref[code % CODE], kern[q], preferred_element_type=F32
            )

    def distance(first, out):
        for q in range(PAIR):
            code = list_ref[first + q]
            out[q] = jnp.dot(
                col_ref[code % CODE], row_ref[code // CODE], preferred_element_type=F32
            )

    def evaluate(squared, kern):
        for q in range(PAIR):
            kern[q] = matern(squared[q])

    k1[...] = jnp.zeros_like(k1)
    distance(0, s0)

    def step(it, _):
        first = it * 2 * PAIR
        accumulate(jnp.maximum(first - PAIR, 0), k1)
        distance(first + PAIR, s1)
        evaluate(s0, k0)
        accumulate(first, k0)
        distance(first + 2 * PAIR, s0)
        evaluate(s1, k1)
        return 0

    turns = (count + 2 * PAIR - 1) // (2 * PAIR)
    lax.fori_loop(0, turns, step, 0)
    accumulate(jnp.maximum(turns * 2 * PAIR - PAIR, 0), k1)


def load_columns(pack_ref, base, count, col_ref, val_ref):
    def step(i, _):
        for q in range(4):
            leaf = i * 4 + q
            val_ref[base + leaf] = pack_ref[0:16, lanes(leaf)]
            col_ref[base + leaf] = col_features(pack_ref[16:24, lanes(leaf)].astype(F32))
        return 0

    lax.fori_loop(0, count // 4, step, 0)


def near_local_kernel(
    where_ref, scale_ref, offs_ref, cols_ref, points_ref, pack_ref,
    acc_ref, row_ref, far_list, far_count,
    col_ref, val_ref, s0, s1, k0, k1, own_list,
):
    device, half_id = where_ref[0], where_ref[1]
    leaves = offs_ref.shape[0]
    half = leaves // 2
    slots = cols_ref.shape[0]
    each = slots // leaves

    def rows_step(i, carry):
        row, own, far = carry
        for q in range(2):
            leaf = i * 2 + q
            row_ref[leaf] = row_features(coordinate_rows(points_ref[:, lanes(leaf)], scale_ref))
            acc_ref[:, lanes(leaf)] = jnp.zeros((16, LEAF), F32)
            for w in range(each):
                slot = leaf * each + w
                nxt = jnp.minimum(row + 1, leaves - 1)
                row = jnp.where((nxt > row) & (offs_ref[nxt] <= slot), nxt, row)
                col = cols_ref[slot] - device * leaves + leaves
                seg = col // leaves
                inner = col % leaves
                mine = inner // half == half_id
                local = mine & (seg == 1)
                apart = mine & (seg != 1)
                own_list[own] = row * CODE + inner % half
                far_list[far] = row * CODE + (seg // 2) * half + inner % half
                own = own + local.astype(jnp.int32)
                far = far + apart.astype(jnp.int32)
        return row, own, far

    zero = jnp.int32(0)
    _, own, far = lax.fori_loop(0, leaves // 2, rows_step, (zero, zero, zero))
    for q in range(PAD):
        own_list[own + q] = half
        far_list[far + q] = leaves
    far_count[0] = far
    load_columns(pack_ref, 0, half, col_ref, val_ref)
    val_ref[half] = jnp.zeros((16, LEAF), BF)
    col_ref[half] = jnp.zeros(col_ref.shape[1:], BF)
    block_loop(own, own_list, row_ref, col_ref, val_ref, acc_ref, s0, s1, k0, k1)


def near_halo_kernel(
    far_list, far_count, row_ref, left_ref, right_ref, start_ref,
    mine_ref, other_ref,
    acc_ref, col_ref, val_ref, s0, s1, k0, k1,
):
    half = left_ref.shape[1] // LEAF
    acc_ref[...] = start_ref[...]
    load_columns(left_ref, 0, half, col_ref, val_ref)
    load_columns(right_ref, half, half, col_ref, val_ref)
    val_ref[2 * half] = jnp.zeros((16, LEAF), BF)
    col_ref[2 * half] = jnp.zeros(col_ref.shape[1:], BF)
    block_loop(far_count[0], far_list, row_ref, col_ref, val_ref, acc_ref, s0, s1, k0, k1)
    mine_ref[...] = acc_ref[0:8]
    other_ref[...] = acc_ref[8:16]


def split_parts(value):
    high = value.astype(BF).astype(F32)
    return jnp.concatenate([high, value - high], axis=0).astype(BF)


def join_parts(value):
    return value[0:8] + value[8:16]


def mul_nt(left, right):
    return lax.dot_general(left, right, NT, preferred_element_type=F32)


def over_nodes(count, unroll, work):
    group = min(unroll, count)
    if count == group:
        work([jnp.int32(i) for i in range(count)])
        return

    def step(i, _):
        work([i * group + q for q in range(group)])
        return 0

    lax.fori_loop(0, count // group, step, 0)


def up_kernel(vec_ref, basis_hbm, transfer_hbm, coef_ref, export_ref, basis, transfer, sems):
    leaves = basis.shape[0]
    levels = leaves.bit_length() - 1
    chunks = 4
    per = leaves // chunks
    copies = [
        pltpu.make_async_copy(
            basis_hbm.at[pl.ds(c * per, per)], basis.at[pl.ds(c * per, per)], sems.at[c]
        )
        for c in range(chunks)
    ]
    last = pltpu.make_async_copy(transfer_hbm, transfer, sems.at[chunks])
    for copy in copies:
        copy.start()
    last.start()
    for c in range(chunks):
        copies[c].wait()

        def work(nodes, c=c):
            outs = [
                mul_nt(vec_ref[:, lanes(c * per + n)], basis[c * per + n]) for n in nodes
            ]
            for n, out in zip(nodes, outs):
                coef_ref[leaves - 1 + c * per + n] = split_parts(out)

        over_nodes(per, 8, work)
    last.wait()
    for depth in range(levels - 1, -1, -1):
        first = 2**depth - 1

        def work(nodes, first=first):
            outs = []
            for i in nodes:
                node = first + i
                outs.append(
                    mul_nt(coef_ref[2 * node + 1], transfer[node, 0])
                    + mul_nt(coef_ref[2 * node + 2], transfer[node, 1])
                )
            for i, out in zip(nodes, outs):
                coef_ref[first + i] = split_parts(join_parts(out))

        over_nodes(2**depth, 8, work)
    export_ref[...] = coef_ref[0:EXPORT]


def down_kernel(
    dev_levels, where_ref, partners_ref, top_partners_ref, coef_ref, gather_ref, top_e, top_b,
    coupling_hbm, transfer_hbm, out_ref, coupling, transfer, local, down, tree, sems,
):
    device = where_ref[0]
    total = coupling.shape[0]
    leaves = (total + 1) // 2
    levels = leaves.bit_length() - 1
    copy_b0 = pltpu.make_async_copy(
        coupling_hbm.at[pl.ds(0, leaves - 1)], coupling.at[pl.ds(0, leaves - 1)], sems.at[0]
    )
    copy_b1 = pltpu.make_async_copy(
        coupling_hbm.at[pl.ds(leaves - 1, leaves)],
        coupling.at[pl.ds(leaves - 1, leaves)],
        sems.at[1],
    )
    copy_e = pltpu.make_async_copy(transfer_hbm, transfer, sems.at[2])
    copy_b0.start()
    copy_b1.start()
    copy_e.start()

    for level in range(dev_levels - 1, 1, -1):

        def work(nodes, level=level):
            outs = []
            for i in nodes:
                row = 2**level - 4 + i
                if level == dev_levels - 1:
                    kids = [gather_ref[2 * i, 0], gather_ref[2 * i + 1, 0]]
                else:
                    kids = [tree[2 ** (level + 1) + 2 * i + c] for c in range(2)]
                outs.append(mul_nt(kids[0], top_e[row, 0]) + mul_nt(kids[1], top_e[row, 1]))
            for i, out in zip(nodes, outs):
                tree[2**level + i] = split_parts(join_parts(out))

        over_nodes(2**level, 8, work)
    pushed = jnp.zeros((PART, RANK), F32)
    for level in range(2, dev_levels):
        node = device >> (dev_levels - level)
        row = 2**level - 4 + node
        side = device >> (dev_levels - level - 1) & 1
        parts = sum(
            mul_nt(tree[2**level + top_partners_ref[row, f]], top_b[row, f]) for f in range(3)
        )
        here = split_parts(join_parts(parts) + pushed)
        pushed = join_parts(jnp.dot(here, top_e[row, side], preferred_element_type=F32))

    copy_b0.wait()
    for depth in range(levels + 1):
        first = 2**depth - 1
        if depth == levels:
            copy_b1.wait()

        def work(nodes, depth=depth, first=first):
            outs = []
            for i in nodes:
                node = first + i
                part = None
                for f in range(3):
                    mate = partners_ref[node, f]
                    if depth < SPAN:
                        picked = gather_ref[mate >> depth, first + (mate & first)]
                    else:
                        picked = coef_ref[mate - device * 2**depth + first]
                    term = mul_nt(picked, coupling[node, f])
                    part = term if part is None else part + term
                outs.append(part)
            for i, part in zip(nodes, outs):
                local[first + i] = join_parts(part)

        over_nodes(2**depth, 8, work)
    copy_e.wait()
    down[0] = split_parts(local[0] + pushed)
    for depth in range(levels):
        first = 2**depth - 1

        def work(nodes, depth=depth, first=first):
            outs = []
            for i in nodes:
                for c in range(2):
                    outs.append(
                        jnp.dot(down[first + i], transfer[first + i, c], preferred_element_type=F32)
                    )
            for j, i in enumerate(nodes):
                for c in range(2):
                    kid = 2 * (first + i) + 1 + c
                    value = local[kid] + join_parts(outs[2 * j + c])
                    if depth == levels - 1:
                        out_ref[2 * i + c] = value.astype(BF)
                    else:
                        down[kid] = split_parts(value)

        over_nodes(2**depth, 8, work)


def final_kernel(low_ref, basis_ref, noise_ref, vec_ref, mine_ref, got_ref, out_ref):
    for leaf in range(low_ref.shape[0]):
        here = slice(leaf * LEAF, (leaf + 1) * LEAF)
        far = jnp.dot(low_ref[leaf], basis_ref[leaf], preferred_element_type=F32)
        out_ref[:, here] = (
            mine_ref[:, here]
            + got_ref[:, here]
            + noise_ref[:, here] * vec_ref[:, here].astype(F32)
            + far
        )


def body(
    points, inv_scale, noise, vectors, leaf_basis, local_transfer, top_transfer,
    local_coupling, top_coupling, local_partners, top_partners, near_offsets, near_cols,
):
    subs = lax.axis_size("sub")
    count = lax.axis_size("leaf") * subs
    dev_levels = count.bit_length() - 1
    device = lax.axis_index("leaf") * subs + lax.axis_index("sub")
    core = lax.axis_index("vec")
    where = jnp.stack([device, core]).astype(jnp.int32)
    size = vectors.shape[1]
    leaves = near_offsets.shape[0]
    slots = near_cols.shape[0]
    half = size // 2
    sds = jax.ShapeDtypeStruct
    scratch_blocks = [
        VMEM((PAIR, LEAF, LEAF), F32), VMEM((PAIR, LEAF, LEAF), F32),
        VMEM((PAIR, LEAF, LEAF), BF), VMEM((PAIR, LEAF, LEAF), BF),
    ]

    send = lax.dynamic_slice(vectors, (0, (1 - core) * half), (PART, half))
    got = lax.ppermute(send, "vec", [(0, 1), (1, 0)])

    coef, export = pl.pallas_call(
        up_kernel,
        name="up",
        out_shape=(sds((2 * leaves - 1, 16, RANK), BF), sds((EXPORT, 16, RANK), BF)),
        in_specs=[vspec(), aspec(), aspec()],
        out_specs=(vspec(), vspec()),
        scratch_shapes=[
            VMEM(leaf_basis.shape, BF), VMEM(local_transfer.shape, BF),
            pltpu.SemaphoreType.DMA((5,)),
        ],
        compiler_params=params(28),
    )(vectors, leaf_basis, local_transfer)
    gathered = lax.all_gather(export, ("leaf", "sub"))

    pack = pl.pallas_call(
        pack_kernel,
        name="pack",
        out_shape=sds((24, half), BF),
        in_specs=[sspec(), sspec(), vspec(), vspec(), vspec()],
        out_specs=vspec(),
        compiler_params=params(16),
    )(where, inv_scale, points, vectors, got)
    axes = ("leaf", "sub")
    left = lax.ppermute(pack, axes, [(i, i + 1) for i in range(count - 1)])
    right = lax.ppermute(pack, axes, [(i + 1, i) for i in range(count - 1)])

    start, row_feat, far_list, far_count = pl.pallas_call(
        near_local_kernel,
        name="near_local",
        out_shape=(
            sds((16, size), F32), sds((leaves, 32, LEAF), BF),
            sds((slots + PAD,), jnp.int32), sds((1,), jnp.int32),
        ),
        in_specs=[sspec()] * 4 + [vspec()] * 2,
        out_specs=(vspec(), vspec(), sspec(), sspec()),
        scratch_shapes=[
            VMEM((leaves // 2 + 1, LEAF, 32), BF), VMEM((leaves // 2 + 1, 16, LEAF), BF),
            *scratch_blocks, SMEM((slots + PAD,), jnp.int32),
        ],
        compiler_params=params(28),
        cost_estimate=pl.CostEstimate(
            flops=190 * 2 * 256 * 256 * 48, bytes_accessed=8 << 20, transcendentals=190 * 2**17
        ),
    )(where, inv_scale, near_offsets, near_cols, points, pack)

    mine, other = pl.pallas_call(
        near_halo_kernel,
        name="near_halo",
        out_shape=(sds((PART, size), F32), sds((PART, size), F32)),
        in_specs=[sspec(), sspec()] + [vspec()] * 4,
        out_specs=(vspec(), vspec()),
        scratch_shapes=[
            VMEM((16, size), F32),
            VMEM((leaves + 1, LEAF, 32), BF), VMEM((leaves + 1, 16, LEAF), BF),
            *scratch_blocks,
        ],
        compiler_params=params(36),
        cost_estimate=pl.CostEstimate(
            flops=60 * 2 * 256 * 256 * 48, bytes_accessed=8 << 20, transcendentals=60 * 2**17
        ),
    )(far_list, far_count, row_feat, left, right, start)
    swapped = lax.ppermute(other, "vec", [(0, 1), (1, 0)])

    low = pl.pallas_call(
        functools.partial(down_kernel, dev_levels),
        name="down",
        out_shape=sds((leaves, PART, RANK), BF),
        in_specs=[sspec()] * 3 + [vspec()] * 4 + [aspec(), aspec()],
        out_specs=vspec(),
        scratch_shapes=[
            VMEM(local_coupling.shape, BF), VMEM(local_transfer.shape, BF),
            VMEM((2 * leaves - 1, PART, RANK), F32), VMEM((leaves - 1, 16, RANK), BF),
            VMEM((count, 16, RANK), BF), pltpu.SemaphoreType.DMA((3,)),
        ],
        compiler_params=params(36),
        cost_estimate=pl.CostEstimate(
            flops=1300 * 2 * 16 * 64 * 64, bytes_accessed=17 << 20, transcendentals=0
        ),
    )(
        where, local_partners, top_partners, coef, gathered, top_transfer, top_coupling,
        local_coupling, local_transfer,
    )

    per = 16
    wide = per * LEAF
    return pl.pallas_call(
        final_kernel,
        name="final",
        out_shape=sds((PART, size), F32),
        grid=(leaves // per,),
        in_specs=[
            pl.BlockSpec((per, PART, RANK), lambda i: (i, 0, 0)),
            pl.BlockSpec((per, RANK, LEAF), lambda i: (i, 0, 0)),
            pl.BlockSpec((1, wide), lambda i: (0, i)),
            pl.BlockSpec((PART, wide), lambda i: (0, i)),
            pl.BlockSpec((PART, wide), lambda i: (0, i)),
            pl.BlockSpec((PART, wide), lambda i: (0, i)),
        ],
        out_specs=pl.BlockSpec((PART, wide), lambda i: (0, i)),
        compiler_params=params(24),
    )(low, leaf_basis, noise.reshape(1, size), vectors, mine, swapped)


def solution(mesh):
    return jax.shard_map(
        body,
        mesh=mesh,
        in_specs=(
            P("groups", ("leaf", "sub")),
            P("groups"),
            P(("groups", "leaf", "sub")),
            P(("groups", "vec"), ("leaf", "sub")),
            P(("groups", "leaf", "sub"), None, None),
            P(("groups", "leaf", "sub"), None, None, None),
            P("groups", None, None, None),
            P(("groups", "leaf", "sub"), None, None, None),
            P("groups", None, None, None),
            P(("groups", "leaf", "sub"), None),
            P("groups", None),
            P(("groups", "leaf", "sub")),
            P(("groups", "leaf", "sub")),
        ),
        out_specs=P(("groups", "vec"), ("leaf", "sub")),
        check_vma=False,
    )
```

```python
import functools
import math

import jax
import jax.numpy as jnp
from jax import lax
from jax.experimental import pallas as pl
from jax.experimental.pallas import tpu as pltpu
from jax.sharding import PartitionSpec as P

BF = jnp.bfloat16
F32 = jnp.float32
LEAF = 256
RANK = 64
SPAN = 3
PART = 8
EXPORT = 2**SPAN - 1
NEG_LOG2E = -1.0 / math.log(2.0)
ROOT3 = math.sqrt(3.0)
TINY = 1e-12
PAIR = 2
PAD = 16
CODE_BITS = 10
CODE = 2**CODE_BITS
VMEM = pltpu.VMEM
SMEM = pltpu.SMEM
NT = (((1,), (1,)), ((), ()))


def vspec():
    return pl.BlockSpec(memory_space=pltpu.VMEM)


def sspec():
    return pl.BlockSpec(memory_space=pltpu.SMEM)


def aspec():
    return pl.BlockSpec(memory_space=pl.ANY)


def params(mib):
    return pltpu.CompilerParams(vmem_limit_bytes=mib << 20)


def lanes(index):
    return pl.ds(pl.multiple_of(index * LEAF, LEAF), LEAF)


def coordinate_rows(raw, scale_ref):
    width = raw.shape[1]
    row = lax.broadcasted_iota(jnp.int32, (8, width), 0)
    scale = jnp.where(
        row == 0, scale_ref[0], jnp.where(row == 1, scale_ref[1], scale_ref[2])
    )
    full = jnp.concatenate([raw, jnp.zeros((5, width), F32)], axis=0)
    scaled = (full - 0.5) * (scale * ROOT3)
    scaled = jnp.where(row < 3, scaled, 0.0)
    high = scaled.astype(BF).astype(F32)
    rest = (scaled - high).astype(BF).astype(F32)
    return high + pltpu.roll(rest, 4, 0)


def norm_parts(rows):
    swapped = pltpu.roll(rows, 4, 0)
    norm = jnp.sum(rows * (rows + swapped), axis=0, keepdims=True)
    high = norm.astype(BF).astype(F32)
    rest = norm - high
    mid = rest.astype(BF).astype(F32)
    return swapped, high, mid, rest - mid


def row_features(rows):
    swapped, high, mid, low = norm_parts(rows)
    row = lax.broadcasted_iota(jnp.int32, rows.shape, 0)
    tail = jnp.where(
        row < 3,
        1.0,
        jnp.where(row == 3, high, jnp.where(row == 4, mid, jnp.where(row == 5, low, 0.0))),
    )
    return jnp.concatenate([rows, swapped, tail, jnp.zeros_like(rows)], axis=0).astype(BF)


def col_features(rows):
    _, high, mid, low = norm_parts(rows)
    row = lax.broadcasted_iota(jnp.int32, rows.shape, 0)
    tail = jnp.where(
        row == 0,
        high,
        jnp.where(row == 1, mid, jnp.where(row == 2, low, jnp.where(row < 6, 1.0, 0.0))),
    )
    both = -2.0 * rows
    return jnp.concatenate([both, both, tail, jnp.zeros_like(rows)], axis=0).T.astype(BF)


def matern(squared):
    squared = jnp.maximum(squared, TINY)
    dist = squared * lax.rsqrt(squared)
    return ((1.0 + dist) * jnp.exp2(dist * NEG_LOG2E)).astype(BF)


def pack_kernel(where_ref, scale_ref, points_ref, vec_ref, got_ref, out_ref):
    half = got_ref.shape[1]
    base = where_ref[1] * half

    def step(i, _):
        here = pl.ds(pl.multiple_of(i * 2048, 2048), 2048)
        there = pl.ds(pl.multiple_of(base + i * 2048, 2048), 2048)
        rows = coordinate_rows(points_ref[:, there], scale_ref)
        out_ref[:, here] = jnp.concatenate(
            [vec_ref[:, there].astype(F32), got_ref[:, here].astype(F32), rows], axis=0
        ).astype(BF)
        return 0

    lax.fori_loop(0, half // 2048, step, 0)


def block_loop(count, place, list_ref, row_ref, col_ref, val_ref, acc_ref, s0, s1, k0, k1):
    def accumulate(first, kern):
        for q in range(PAIR):
            code = list_ref[first + q]
            here = lanes(code >> CODE_BITS)
            acc_ref[:, here] += jnp.dot(
                val_ref[place(code & (CODE - 1))], kern[q], preferred_element_type=F32
            )

    def distance(first, out):
        for q in range(PAIR):
            code = list_ref[first + q]
            out[q] = jnp.dot(
                col_ref[place(code & (CODE - 1))],
                row_ref[code >> CODE_BITS],
                preferred_element_type=F32,
            )

    def evaluate(squared, kern):
        for q in range(PAIR):
            kern[q] = matern(squared[q])

    k1[...] = jnp.zeros_like(k1)
    distance(0, s0)

    def step(it, _):
        first = it * 2 * PAIR
        accumulate(jnp.maximum(first - PAIR, 0), k1)
        distance(first + PAIR, s1)
        evaluate(s0, k0)
        accumulate(first, k0)
        distance(first + 2 * PAIR, s0)
        evaluate(s1, k1)
        return 0

    turns = (count + 2 * PAIR - 1) // (2 * PAIR)
    lax.fori_loop(0, turns, step, 0)
    accumulate(jnp.maximum(turns * 2 * PAIR - PAIR, 0), k1)


def load_columns(pack_ref, base, count, col_ref, val_ref):
    def step(i, _):
        for q in range(4):
            leaf = i * 4 + q
            val_ref[base + leaf] = pack_ref[0:16, lanes(leaf)]
            col_ref[base + leaf] = col_features(pack_ref[16:24, lanes(leaf)].astype(F32))
        return 0

    lax.fori_loop(0, count // 4, step, 0)


def near_local_kernel(
    where_ref, scale_ref, offs_ref, cols_ref, points_ref, pack_ref,
    acc_ref, row_ref, far_list, far_count,
    col_ref, val_ref, s0, s1, k0, k1, own_list,
):
    device, half_id = where_ref[0], where_ref[1]
    leaves = offs_ref.shape[0]
    half = leaves // 2
    slots = cols_ref.shape[0]
    each = slots // leaves

    far_base = device * leaves - leaves + half_id * half
    half_bits = half.bit_length() - 1

    def rows_step(i, carry):
        row, code, own, far = carry
        for q in range(2):
            leaf = i * 2 + q
            row_ref[leaf] = row_features(coordinate_rows(points_ref[:, lanes(leaf)], scale_ref))
            acc_ref[:, lanes(leaf)] = jnp.zeros((16, LEAF), F32)
            for w in range(each):
                slot = leaf * each + w
                begins = offs_ref[jnp.minimum(row + 1, leaves - 1)] == slot
                row = jnp.where(begins, row + 1, row)
                code = jnp.where(begins, code + CODE, code)
                place = cols_ref[slot] - far_base
                own_list[own] = code + (place - leaves)
                far_list[far] = code + place
                block = place >> half_bits
                own = jnp.where(block == 2, own + 1, own)
                far = jnp.where((block & 3) == 0, far + 1, far)
        return row, code, own, far

    zero = jnp.int32(0)
    _, _, own, far = lax.fori_loop(0, leaves // 2, rows_step, (zero, zero, zero, zero))
    for q in range(PAD):
        own_list[own + q] = half
        far_list[far + q] = 8 * half
    far_count[0] = far
    load_columns(pack_ref, 0, half, col_ref, val_ref)
    val_ref[half] = jnp.zeros((16, LEAF), BF)
    col_ref[half] = jnp.zeros(col_ref.shape[1:], BF)
    block_loop(own, lambda c: c, own_list, row_ref, col_ref, val_ref, acc_ref, s0, s1, k0, k1)


def near_halo_kernel(
    far_list, far_count, row_ref, left_ref, right_ref, start_ref,
    mine_ref, other_ref,
    acc_ref, col_ref, val_ref, s0, s1, k0, k1,
):
    half = left_ref.shape[1] // LEAF
    acc_ref[...] = start_ref[...]
    load_columns(left_ref, 0, half, col_ref, val_ref)
    load_columns(right_ref, half, half, col_ref, val_ref)
    val_ref[2 * half] = jnp.zeros((16, LEAF), BF)
    col_ref[2 * half] = jnp.zeros(col_ref.shape[1:], BF)
    bits = half.bit_length() - 1

    def place(code):
        return (code & (half - 1)) | ((code >> (bits + 2)) << bits)

    block_loop(far_count[0], place, far_list, row_ref, col_ref, val_ref, acc_ref, s0, s1, k0, k1)
    mine_ref[...] = acc_ref[0:8]
    other_ref[...] = acc_ref[8:16]


def split_parts(value):
    high = value.astype(BF).astype(F32)
    return jnp.concatenate([high, value - high], axis=0).astype(BF)


def join_parts(value):
    return value[0:8] + value[8:16]


def mul_nt(left, right):
    return lax.dot_general(left, right, NT, preferred_element_type=F32)


def over_nodes(count, unroll, work):
    group = min(unroll, count)
    if count == group:
        work([jnp.int32(i) for i in range(count)])
        return

    def step(i, _):
        work([i * group + q for q in range(group)])
        return 0

    lax.fori_loop(0, count // group, step, 0)


def side_by_side(first, second):
    return jnp.concatenate([first, second], axis=1)


def doubled(pair):
    low = lax.broadcasted_iota(jnp.int32, pair.shape, 1) < RANK
    turned = pltpu.roll(pair, RANK, 1)
    return jnp.where(low, pair, turned), jnp.where(low, turned, pair)


def up_kernel(vec_ref, basis_ref, raw_ref, coef_ref, export_ref, move_ref, flat, pairs):
    leaves = basis_ref.shape[0]
    levels = leaves.bit_length() - 1
    inner = raw_ref.shape[3]

    def keep(parent, first, second):
        pair = side_by_side(first, second)
        pairs[parent] = split_parts(pair)
        one, two = doubled(pair)
        coef_ref[2 * parent + 1] = split_parts(one)
        coef_ref[2 * parent + 2] = split_parts(two)

    def leaf_step(it, _):
        outs = []
        for q in range(8):
            leaf = it * 8 + q
            outs.append(mul_nt(vec_ref[:, lanes(leaf)], basis_ref[leaf]))
        for q in range(4):
            r = it * 4 + q
            block = jnp.concatenate([raw_ref[0, r], raw_ref[1, r]], axis=0).astype(F32)
            flat[pl.ds(r * leaves, inner)] = block.T
        for q in range(4):
            keep(leaves // 2 - 1 + it * 4 + q, outs[2 * q], outs[2 * q + 1])
        return 0

    lax.fori_loop(0, leaves // 8, leaf_step, 0)
    for depth in range(levels - 1, 0, -1):
        first = 2**depth - 1
        above = 2 ** (depth - 1) - 1

        def work(nodes, first=first, above=above):
            outs = []
            for j in nodes:
                for c in range(2):
                    node = first + 2 * j + c
                    move = flat[pl.ds(node, RANK, stride=leaves)].astype(BF)
                    move_ref[node] = move
                    outs.append(mul_nt(pairs[node], move))
            for j, i in enumerate(nodes):
                keep(above + i, join_parts(outs[2 * j]), join_parts(outs[2 * j + 1]))

        over_nodes(2 ** (depth - 1), 8, work)
    move = flat[pl.ds(0, RANK, stride=leaves)].astype(BF)
    move_ref[0] = move
    root = join_parts(mul_nt(pairs[0], move))
    coef_ref[0] = split_parts(side_by_side(root, root))
    export_ref[0] = coef_ref[0:EXPORT]


def couple_kernel(
    where_ref, partners_ref, coef_ref, raw_ref, local_ref, wide_ref, thin_ref, wide, thin
):
    device = where_ref[0]
    total = raw_ref.shape[3]
    span = total + 1
    levels = span.bit_length() - 2
    low = lax.broadcasted_iota(jnp.int32, (16, 2 * RANK), 1) < RANK

    def turn(i, _):
        for q in range(2):
            r = i * 2 + q
            block = jnp.concatenate([raw_ref[0, r], raw_ref[1, r]], axis=0).astype(F32)
            wide[pl.ds(r * span, total)] = block.T
            thin[pl.ds(r * span, total)] = raw_ref[2, r].astype(F32).T
        return 0

    lax.fori_loop(0, RANK // 2, turn, 0)
    for node in range(EXPORT):
        wide_ref[node] = wide[pl.ds(node, RANK, stride=span)].astype(BF)
        thin_ref[node] = thin[pl.ds(node, RANK, stride=span)].astype(BF)
    for depth in range(SPAN, levels + 1):
        first = 2**depth - 1
        above = 2 ** (depth - 1) - 1
        shift = first - device * 2**depth

        def work(nodes, first=first, above=above, shift=shift):
            outs = []
            for j in nodes:
                for c in range(2):
                    node = first + 2 * j + c
                    mates = [coef_ref[partners_ref[node, f] + shift] for f in range(3)]
                    left = jnp.where(low, mates[0], mates[1])
                    outs.append(
                        mul_nt(left, wide[pl.ds(node, RANK, stride=span)].astype(BF))
                        + mul_nt(
                            mates[2][:, :RANK],
                            thin[pl.ds(node, RANK, stride=span)].astype(BF),
                        )
                    )
            for j, i in enumerate(nodes):
                local_ref[above + i] = side_by_side(
                    join_parts(outs[2 * j]), join_parts(outs[2 * j + 1])
                )

        over_nodes(2 ** (depth - 1), 4, work)


def down_kernel(
    dev_levels, where_ref, partners_ref, top_partners_ref, gather_ref, tops_ref, top_e, top_b,
    wide_ref, thin_ref, local_ref, move_ref, out_ref, down, tree,
):
    device = where_ref[0]
    leaves = out_ref.shape[0]
    levels = leaves.bit_length() - 1
    low = lax.broadcasted_iota(jnp.int32, (16, 2 * RANK), 1) < RANK

    for level in range(dev_levels - 1, 1, -1):

        def work(nodes, level=level):
            outs = []
            for i in nodes:
                row = 2**level - 4 + i
                if level == dev_levels - 1:
                    kids = [tops_ref[(2 * i + c) ^ device, 0][:, :RANK] for c in range(2)]
                else:
                    kids = [tree[2 ** (level + 1) + 2 * i + c] for c in range(2)]
                outs.append(mul_nt(kids[0], top_e[row, 0]) + mul_nt(kids[1], top_e[row, 1]))
            for i, out in zip(nodes, outs):
                tree[2**level + i] = split_parts(join_parts(out))

        over_nodes(2**level, 4, work)

    def near_root(node, depth):
        mates = []
        for f in range(3):
            mate = partners_ref[node, f]
            at = ((mate >> depth) ^ device) & (2**SPAN - 1)
            mates.append(gather_ref[at, 2**depth - 1 + (mate & (2**depth - 1))])
        left = jnp.where(low, mates[0], mates[1])
        return join_parts(
            mul_nt(left, wide_ref[node]) + mul_nt(mates[2][:, :RANK], thin_ref[node])
        )

    shallow = [near_root(node, (node + 1).bit_length() - 1) for node in range(EXPORT)]
    pushed = jnp.zeros((PART, RANK), F32)
    for level in range(2, dev_levels):
        node = device >> (dev_levels - level)
        row = 2**level - 4 + node
        side = device >> (dev_levels - level - 1) & 1
        parts = sum(
            mul_nt(tree[2**level + top_partners_ref[row, f]], top_b[row, f]) for f in range(3)
        )
        here = split_parts(join_parts(parts) + pushed)
        pushed = join_parts(jnp.dot(here, top_e[row, side], preferred_element_type=F32))

    down[0] = split_parts(shallow[0] + pushed)
    for depth in range(levels):
        first = 2**depth - 1

        def work(nodes, depth=depth, first=first):
            outs = [
                jnp.dot(down[first + i], move_ref[first + i], preferred_element_type=F32)
                for i in nodes
            ]
            for i, out in zip(nodes, outs):
                node = first + i
                if depth < SPAN - 1:
                    base = side_by_side(shallow[2 * node + 1], shallow[2 * node + 2])
                else:
                    base = local_ref[node]
                pair = base + join_parts(out)
                if depth == levels - 1:
                    out_ref[2 * i] = pair[:, :RANK].astype(BF)
                    out_ref[2 * i + 1] = pair[:, RANK:].astype(BF)
                else:
                    down[2 * node + 1] = split_parts(pair[:, :RANK])
                    down[2 * node + 2] = split_parts(pair[:, RANK:])

        if depth < SPAN:
            first_nodes = list(range(2**depth))
            work(first_nodes)
        else:
            over_nodes(2**depth, 8, work)


def final_kernel(low_ref, basis_ref, noise_ref, vec_ref, mine_ref, got_ref, out_ref):
    for leaf in range(low_ref.shape[0]):
        here = slice(leaf * LEAF, (leaf + 1) * LEAF)
        far = jnp.dot(low_ref[leaf], basis_ref[leaf], preferred_element_type=F32)
        out_ref[:, here] = (
            mine_ref[:, here]
            + got_ref[:, here]
            + noise_ref[:, here] * vec_ref[:, here].astype(F32)
            + far
        )


def swap_bit(value, bit):
    sub_bits = lax.axis_size("sub").bit_length() - 1
    axis, apart = ("sub", 2**bit) if bit < sub_bits else ("leaf", 2 ** (bit - sub_bits))
    pairs = [(i, i ^ apart) for i in range(lax.axis_size(axis))]
    return lax.ppermute(value, axis, pairs)


def body(
    points, inv_scale, noise, vectors, leaf_basis, local_transfer, top_transfer,
    local_coupling, top_coupling, local_partners, top_partners, near_offsets, near_cols,
):
    subs = lax.axis_size("sub")
    count = lax.axis_size("leaf") * subs
    dev_levels = count.bit_length() - 1
    device = lax.axis_index("leaf") * subs + lax.axis_index("sub")
    core = lax.axis_index("vec")
    where = jnp.stack([device, core]).astype(jnp.int32)
    size = vectors.shape[1]
    leaves = near_offsets.shape[0]
    slots = near_cols.shape[0]
    half = size // 2
    sds = jax.ShapeDtypeStruct
    scratch_blocks = [
        VMEM((PAIR, LEAF, LEAF), F32), VMEM((PAIR, LEAF, LEAF), F32),
        VMEM((PAIR, LEAF, LEAF), BF), VMEM((PAIR, LEAF, LEAF), BF),
    ]

    send = lax.dynamic_slice(vectors, (0, (1 - core) * half), (PART, half))
    got = lax.ppermute(send, "vec", [(0, 1), (1, 0)])

    coef, export, moves = pl.pallas_call(
        up_kernel,
        name="up",
        out_shape=(
            sds((2 * leaves - 1, 16, 2 * RANK), BF), sds((1, EXPORT, 16, 2 * RANK), BF),
            sds((leaves - 1, RANK, 2 * RANK), BF),
        ),
        in_specs=[vspec()] * 3,
        out_specs=(vspec(),) * 3,
        scratch_shapes=[
            VMEM((RANK * leaves, 2 * RANK), F32), VMEM((leaves - 1, 16, 2 * RANK), BF),
        ],
        compiler_params=params(28),
        cost_estimate=pl.CostEstimate(
            flops=300 * 2 * 256 * 256 * 48, bytes_accessed=8 << 20, transcendentals=0
        ),
    )(vectors, leaf_basis, jnp.transpose(local_transfer, (1, 2, 3, 0)))
    gathered = export
    for bit in range(SPAN):
        gathered = jnp.concatenate([gathered, swap_bit(gathered, bit)], axis=0)
    tops = gathered
    for bit in range(SPAN, dev_levels):
        tops = tops[:, 0:1]
        tops = jnp.concatenate([tops, swap_bit(tops, bit)], axis=0)

    pack = pl.pallas_call(
        pack_kernel,
        name="pack",
        out_shape=sds((24, half), BF),
        in_specs=[sspec(), sspec(), vspec(), vspec(), vspec()],
        out_specs=vspec(),
        compiler_params=params(16),
    )(where, inv_scale, points, vectors, got)
    axes = ("leaf", "sub")
    left = lax.ppermute(pack, axes, [(i, i + 1) for i in range(count - 1)])
    right = lax.ppermute(pack, axes, [(i + 1, i) for i in range(count - 1)])

    pack, _ = lax.optimization_barrier((pack, export))
    start, row_feat, far_list, far_count = pl.pallas_call(
        near_local_kernel,
        name="near_local",
        out_shape=(
            sds((16, size), F32), sds((leaves, 32, LEAF), BF),
            sds((slots + PAD,), jnp.int32), sds((1,), jnp.int32),
        ),
        in_specs=[sspec()] * 4 + [vspec()] * 2,
        out_specs=(vspec(), vspec(), sspec(), sspec()),
        scratch_shapes=[
            VMEM((leaves // 2 + 1, LEAF, 32), BF), VMEM((leaves // 2 + 1, 16, LEAF), BF),
            *scratch_blocks, SMEM((slots + PAD,), jnp.int32),
        ],
        compiler_params=params(28),
        cost_estimate=pl.CostEstimate(
            flops=190 * 2 * 256 * 256 * 48, bytes_accessed=8 << 20, transcendentals=190 * 2**17
        ),
    )(where, inv_scale, near_offsets, near_cols, points, pack)

    mine, other = pl.pallas_call(
        near_halo_kernel,
        name="near_halo",
        out_shape=(sds((PART, size), F32), sds((PART, size), F32)),
        in_specs=[sspec(), sspec()] + [vspec()] * 4,
        out_specs=(vspec(), vspec()),
        scratch_shapes=[
            VMEM((16, size), F32),
            VMEM((leaves + 1, LEAF, 32), BF), VMEM((leaves + 1, 16, LEAF), BF),
            *scratch_blocks,
        ],
        compiler_params=params(36),
        cost_estimate=pl.CostEstimate(
            flops=60 * 2 * 256 * 256 * 48, bytes_accessed=8 << 20, transcendentals=60 * 2**17
        ),
    )(far_list, far_count, row_feat, left, right, start)
    swapped = lax.ppermute(other, "vec", [(0, 1), (1, 0)])

    _, coef_late = lax.optimization_barrier((mine, coef))
    local, wide, thin = pl.pallas_call(
        couple_kernel,
        name="couple",
        out_shape=(
            sds((leaves - 1, PART, 2 * RANK), F32), sds((EXPORT, RANK, 2 * RANK), BF),
            sds((EXPORT, RANK, RANK), BF),
        ),
        in_specs=[sspec()] * 2 + [vspec()] * 2,
        out_specs=(vspec(),) * 3,
        scratch_shapes=[
            VMEM((2 * leaves * RANK, 2 * RANK), F32), VMEM((2 * leaves * RANK, RANK), F32),
        ],
        compiler_params=params(36),
        cost_estimate=pl.CostEstimate(
            flops=300 * 2 * 256 * 256 * 48, bytes_accessed=8 << 20, transcendentals=0
        ),
    )(where, local_partners, coef_late, jnp.transpose(local_coupling, (1, 2, 3, 0)))

    low = pl.pallas_call(
        functools.partial(down_kernel, dev_levels),
        name="down",
        out_shape=sds((leaves, PART, RANK), BF),
        in_specs=[sspec()] * 3 + [vspec()] * 8,
        out_specs=vspec(),
        scratch_shapes=[VMEM((leaves - 1, 16, RANK), BF), VMEM((count, 16, RANK), BF)],
        compiler_params=params(24),
        cost_estimate=pl.CostEstimate(
            flops=100 * 2 * 256 * 256 * 48, bytes_accessed=8 << 20, transcendentals=0
        ),
    )(
        where, local_partners, top_partners, gathered, tops, top_transfer, top_coupling,
        wide, thin, local, moves,
    )

    per = 16
    wide = per * LEAF
    return pl.pallas_call(
        final_kernel,
        name="final",
        out_shape=sds((PART, size), F32),
        grid=(leaves // per,),
        in_specs=[
            pl.BlockSpec((per, PART, RANK), lambda i: (i, 0, 0)),
            pl.BlockSpec((per, RANK, LEAF), lambda i: (i, 0, 0)),
            pl.BlockSpec((1, wide), lambda i: (0, i)),
            pl.BlockSpec((PART, wide), lambda i: (0, i)),
            pl.BlockSpec((PART, wide), lambda i: (0, i)),
            pl.BlockSpec((PART, wide), lambda i: (0, i)),
        ],
        out_specs=pl.BlockSpec((PART, wide), lambda i: (0, i)),
        compiler_params=params(24),
    )(low, leaf_basis, noise.reshape(1, size), vectors, mine, swapped)


def solution(mesh):
    return jax.shard_map(
        body,
        mesh=mesh,
        in_specs=(
            P("groups", ("leaf", "sub")),
            P("groups"),
            P(("groups", "leaf", "sub")),
            P(("groups", "vec"), ("leaf", "sub")),
            P(("groups", "leaf", "sub"), None, None),
            P(("groups", "leaf", "sub"), None, None, None),
            P("groups", None, None, None),
            P(("groups", "leaf", "sub"), None, None, None),
            P("groups", None, None, None),
            P(("groups", "leaf", "sub"), None),
            P("groups", None),
            P(("groups", "leaf", "sub")),
            P(("groups", "leaf", "sub")),
        ),
        out_specs=P(("groups", "vec"), ("leaf", "sub")),
        check_vma=False,
    )
```

```python
import functools
import math

import jax
import jax.numpy as jnp
from jax import lax
from jax.experimental import pallas as pl
from jax.experimental.pallas import tpu as pltpu
from jax.sharding import PartitionSpec as P

BF = jnp.bfloat16
F32 = jnp.float32
LEAF = 256
RANK = 64
SPAN = 3
PART = 8
EXPORT = 2**SPAN - 1
NEG_LOG2E = -1.0 / math.log(2.0)
ROOT3 = math.sqrt(3.0)
TINY = 1e-12
PAIR = 2
PAD = 16
CODE_BITS = 10
CODE = 2**CODE_BITS
VMEM = pltpu.VMEM
SMEM = pltpu.SMEM
NT = (((1,), (1,)), ((), ()))


def vspec():
    return pl.BlockSpec(memory_space=pltpu.VMEM)


def sspec():
    return pl.BlockSpec(memory_space=pltpu.SMEM)


def aspec():
    return pl.BlockSpec(memory_space=pl.ANY)


def params(mib):
    return pltpu.CompilerParams(vmem_limit_bytes=mib << 20)


def lanes(index):
    return pl.ds(pl.multiple_of(index * LEAF, LEAF), LEAF)


def coordinate_rows(raw, scale_ref):
    width = raw.shape[1]
    row = lax.broadcasted_iota(jnp.int32, (8, width), 0)
    scale = jnp.where(
        row == 0, scale_ref[0], jnp.where(row == 1, scale_ref[1], scale_ref[2])
    )
    full = jnp.concatenate([raw, jnp.zeros((5, width), F32)], axis=0)
    scaled = (full - 0.5) * (scale * ROOT3)
    scaled = jnp.where(row < 3, scaled, 0.0)
    high = scaled.astype(BF).astype(F32)
    rest = (scaled - high).astype(BF).astype(F32)
    return high + pltpu.roll(rest, 4, 0)


def norm_parts(rows):
    swapped = pltpu.roll(rows, 4, 0)
    norm = jnp.sum(rows * (rows + swapped), axis=0, keepdims=True)
    high = norm.astype(BF).astype(F32)
    rest = norm - high
    mid = rest.astype(BF).astype(F32)
    return swapped, high, mid, rest - mid


def row_features(rows):
    swapped, high, mid, low = norm_parts(rows)
    row = lax.broadcasted_iota(jnp.int32, rows.shape, 0)
    tail = jnp.where(
        row < 3,
        1.0,
        jnp.where(row == 3, high, jnp.where(row == 4, mid, jnp.where(row == 5, low, 0.0))),
    )
    return jnp.concatenate([rows, swapped, tail, jnp.zeros_like(rows)], axis=0).astype(BF)


def col_features(rows):
    _, high, mid, low = norm_parts(rows)
    row = lax.broadcasted_iota(jnp.int32, rows.shape, 0)
    tail = jnp.where(
        row == 0,
        high,
        jnp.where(row == 1, mid, jnp.where(row == 2, low, jnp.where(row < 6, 1.0, 0.0))),
    )
    both = -2.0 * rows
    return jnp.concatenate([both, both, tail, jnp.zeros_like(rows)], axis=0).T.astype(BF)


def matern(squared):
    squared = jnp.maximum(squared, TINY)
    dist = squared * lax.rsqrt(squared)
    return ((1.0 + dist) * jnp.exp2(dist * NEG_LOG2E)).astype(BF)


def pack_kernel(where_ref, scale_ref, points_ref, vec_ref, got_ref, out_ref):
    half = got_ref.shape[1]
    base = where_ref[1] * half

    def step(i, _):
        here = pl.ds(pl.multiple_of(i * 2048, 2048), 2048)
        there = pl.ds(pl.multiple_of(base + i * 2048, 2048), 2048)
        rows = coordinate_rows(points_ref[:, there], scale_ref)
        out_ref[:, here] = jnp.concatenate(
            [vec_ref[:, there].astype(F32), got_ref[:, here].astype(F32), rows], axis=0
        ).astype(BF)
        return 0

    lax.fori_loop(0, half // 2048, step, 0)


def block_loop(count, place, list_ref, row_ref, col_ref, val_ref, sums, s0, s1, k0, k1):
    def accumulate(first, kern):
        for q in range(PAIR):
            code = list_ref[first + q]
            here = lanes(code >> CODE_BITS)
            part = jnp.dot(
                val_ref[place(code & (CODE - 1))], kern[q], preferred_element_type=F32
            )
            sums[0][:, here] += part[:PART]
            sums[1][:, here] += part[PART:]

    def distance(first, out):
        for q in range(PAIR):
            code = list_ref[first + q]
            out[q] = jnp.dot(
                col_ref[place(code & (CODE - 1))],
                row_ref[code >> CODE_BITS],
                preferred_element_type=F32,
            )

    def evaluate(squared, kern):
        for q in range(PAIR):
            kern[q] = matern(squared[q])

    k1[...] = jnp.zeros_like(k1)
    distance(0, s0)

    def step(it, _):
        first = it * 2 * PAIR
        accumulate(jnp.maximum(first - PAIR, 0), k1)
        distance(first + PAIR, s1)
        evaluate(s0, k0)
        accumulate(first, k0)
        distance(first + 2 * PAIR, s0)
        evaluate(s1, k1)
        return 0

    turns = (count + 2 * PAIR - 1) // (2 * PAIR)
    lax.fori_loop(0, turns, step, 0)
    accumulate(jnp.maximum(turns * 2 * PAIR - PAIR, 0), k1)


def load_columns(pack_ref, base, count, col_ref, val_ref):
    def step(i, _):
        for q in range(4):
            leaf = i * 4 + q
            val_ref[base + leaf] = pack_ref[0:16, lanes(leaf)]
            col_ref[base + leaf] = col_features(pack_ref[16:24, lanes(leaf)].astype(F32))
        return 0

    lax.fori_loop(0, count // 4, step, 0)


def near_local_kernel(
    where_ref, scale_ref, offs_ref, cols_ref, points_ref, pack_ref,
    mine_ref, other_ref, row_ref, far_list, far_count,
    col_ref, val_ref, s0, s1, k0, k1, own_list,
):
    device, half_id = where_ref[0], where_ref[1]
    leaves = offs_ref.shape[0]
    half = leaves // 2
    slots = cols_ref.shape[0]
    each = slots // leaves

    far_base = device * leaves - leaves + half_id * half
    half_bits = half.bit_length() - 1

    def rows_step(i, carry):
        row, code, own, far = carry
        for q in range(2):
            leaf = i * 2 + q
            row_ref[leaf] = row_features(coordinate_rows(points_ref[:, lanes(leaf)], scale_ref))
            mine_ref[:, lanes(leaf)] = jnp.zeros((PART, LEAF), F32)
            other_ref[:, lanes(leaf)] = jnp.zeros((PART, LEAF), F32)
            for w in range(each):
                slot = leaf * each + w
                begins = offs_ref[jnp.minimum(row + 1, leaves - 1)] == slot
                row = jnp.where(begins, row + 1, row)
                code = jnp.where(begins, code + CODE, code)
                place = cols_ref[slot] - far_base
                own_list[own] = code + (place - leaves)
                far_list[far] = code + place
                block = place >> half_bits
                own = jnp.where(block == 2, own + 1, own)
                far = jnp.where((block & 3) == 0, far + 1, far)
        return row, code, own, far

    zero = jnp.int32(0)
    _, _, own, far = lax.fori_loop(0, leaves // 2, rows_step, (zero, zero, zero, zero))
    for q in range(PAD):
        own_list[own + q] = half
        far_list[far + q] = 8 * half
    far_count[0] = far
    load_columns(pack_ref, 0, half, col_ref, val_ref)
    val_ref[half] = jnp.zeros((16, LEAF), BF)
    col_ref[half] = jnp.zeros(col_ref.shape[1:], BF)
    sums = (mine_ref, other_ref)
    block_loop(own, lambda c: c, own_list, row_ref, col_ref, val_ref, sums, s0, s1, k0, k1)


def near_halo_kernel(
    far_list, far_count, row_ref, left_ref, right_ref, mine_in, other_in,
    mine_ref, other_ref,
    col_ref, val_ref, s0, s1, k0, k1,
):
    half = left_ref.shape[1] // LEAF
    bits = half.bit_length() - 1
    count = far_count[0]

    def place(code):
        return (code & (half - 1)) | ((code >> (bits + 2)) << bits)

    def load(i, _):
        for q in range(4):
            code = far_list[i * 4 + q] & (CODE - 1)
            here = lanes(code & (half - 1))
            after = code >= 4 * half
            values = jnp.where(after, right_ref[0:16, here], left_ref[0:16, here])
            rows = jnp.where(after, right_ref[16:24, here], left_ref[16:24, here])
            val_ref[place(code)] = values
            col_ref[place(code)] = col_features(rows.astype(F32))
        return 0

    mine_ref[...] = mine_in[...]
    other_ref[...] = other_in[...]
    lax.fori_loop(0, (count + 3) // 4, load, 0)
    val_ref[2 * half] = jnp.zeros((16, LEAF), BF)
    col_ref[2 * half] = jnp.zeros(col_ref.shape[1:], BF)
    sums = (mine_ref, other_ref)
    block_loop(count, place, far_list, row_ref, col_ref, val_ref, sums, s0, s1, k0, k1)


def split_parts(value):
    high = value.astype(BF).astype(F32)
    return jnp.concatenate([high, value - high], axis=0).astype(BF)


def join_parts(value):
    return value[0:8] + value[8:16]


def mul_nt(left, right):
    return lax.dot_general(left, right, NT, preferred_element_type=F32)


def over_nodes(count, unroll, work):
    group = min(unroll, count)
    if count == group:
        work([jnp.int32(i) for i in range(count)])
        return

    def step(i, _):
        work([i * group + q for q in range(group)])
        return 0

    lax.fori_loop(0, count // group, step, 0)


def store_turned(flat, r, block):
    turned = block.T
    count = turned.shape[0] // 8
    width = turned.shape[1]
    rows = pl.ds(pl.multiple_of(r * 8, 8), 8)
    flat[0:count, rows] = turned[: count * 8].reshape(count, 8, width)
    rest = turned.shape[0] - count * 8
    flat[count, pl.ds(pl.multiple_of(r * 8, 8), rest)] = turned[count * 8 :]


def load_node(flat, node):
    return flat[node >> 3, pl.ds(node & 7, RANK, stride=8)].astype(BF)


def side_by_side(first, second):
    return jnp.concatenate([first, second], axis=1)


def doubled(pair):
    low = lax.broadcasted_iota(jnp.int32, pair.shape, 1) < RANK
    turned = pltpu.roll(pair, RANK, 1)
    return jnp.where(low, pair, turned), jnp.where(low, turned, pair)


def up_kernel(vec_ref, basis_ref, raw_ref, coef_ref, export_ref, move_ref, flat, pairs):
    leaves = basis_ref.shape[0]
    levels = leaves.bit_length() - 1

    def keep(parent, first, second):
        pair = side_by_side(first, second)
        pairs[parent] = split_parts(pair)
        one, two = doubled(pair)
        coef_ref[2 * parent + 1] = split_parts(one)
        coef_ref[2 * parent + 2] = split_parts(two)

    def leaf_step(it, _):
        outs = []
        for q in range(8):
            leaf = it * 8 + q
            outs.append(mul_nt(vec_ref[:, lanes(leaf)], basis_ref[leaf]))
        for q in range(4):
            r = it * 4 + q
            block = jnp.concatenate([raw_ref[0, r], raw_ref[1, r]], axis=0).astype(F32)
            store_turned(flat, r, block)
        for q in range(4):
            keep(leaves // 2 - 1 + it * 4 + q, outs[2 * q], outs[2 * q + 1])
        return 0

    lax.fori_loop(0, leaves // 8, leaf_step, 0)
    for depth in range(levels - 1, 0, -1):
        first = 2**depth - 1
        above = 2 ** (depth - 1) - 1

        def work(nodes, first=first, above=above):
            outs = []
            for j in nodes:
                for c in range(2):
                    node = first + 2 * j + c
                    move = load_node(flat, node)
                    move_ref[node] = move
                    outs.append(mul_nt(pairs[node], move))
            for j, i in enumerate(nodes):
                keep(above + i, join_parts(outs[2 * j]), join_parts(outs[2 * j + 1]))

        over_nodes(2 ** (depth - 1), 8, work)
    move = load_node(flat, 0)
    move_ref[0] = move
    root = join_parts(mul_nt(pairs[0], move))
    coef_ref[0] = split_parts(side_by_side(root, root))
    export_ref[0] = coef_ref[0:EXPORT]


def couple_kernel(
    where_ref, partners_ref, coef_ref, raw_ref, local_ref, wide_ref, thin_ref, wide, thin
):
    device = where_ref[0]
    total = raw_ref.shape[3]
    span = total + 1
    levels = span.bit_length() - 2
    low = lax.broadcasted_iota(jnp.int32, (16, 2 * RANK), 1) < RANK

    def turn(i, _):
        for q in range(2):
            r = i * 2 + q
            block = jnp.concatenate([raw_ref[0, r], raw_ref[1, r]], axis=0).astype(F32)
            store_turned(wide, r, block)
            store_turned(thin, r, raw_ref[2, r].astype(F32))
        return 0

    lax.fori_loop(0, RANK // 2, turn, 0)
    for node in range(EXPORT):
        wide_ref[node] = load_node(wide, node)
        thin_ref[node] = load_node(thin, node)
    for depth in range(SPAN, levels + 1):
        first = 2**depth - 1
        above = 2 ** (depth - 1) - 1
        shift = first - device * 2**depth

        def work(nodes, first=first, above=above, shift=shift):
            outs = []
            for j in nodes:
                for c in range(2):
                    node = first + 2 * j + c
                    mates = [coef_ref[partners_ref[node, f] + shift] for f in range(3)]
                    left = jnp.where(low, mates[0], mates[1])
                    outs.append(
                        mul_nt(left, load_node(wide, node))
                        + mul_nt(
                            mates[2][:, :RANK],
                            load_node(thin, node),
                        )
                    )
            for j, i in enumerate(nodes):
                local_ref[above + i] = side_by_side(
                    join_parts(outs[2 * j]), join_parts(outs[2 * j + 1])
                )

        over_nodes(2 ** (depth - 1), 4, work)


def down_kernel(
    dev_levels, where_ref, partners_ref, top_partners_ref, gather_ref, tops_ref, top_e, top_b,
    wide_ref, thin_ref, local_ref, move_ref, out_ref, down, tree,
):
    device = where_ref[0]
    leaves = out_ref.shape[0]
    levels = leaves.bit_length() - 1
    low = lax.broadcasted_iota(jnp.int32, (16, 2 * RANK), 1) < RANK

    for level in range(dev_levels - 1, 1, -1):

        def work(nodes, level=level):
            outs = []
            for i in nodes:
                row = 2**level - 4 + i
                if level == dev_levels - 1:
                    kids = [tops_ref[(2 * i + c) ^ device, 0][:, :RANK] for c in range(2)]
                else:
                    kids = [tree[2 ** (level + 1) + 2 * i + c] for c in range(2)]
                outs.append(mul_nt(kids[0], top_e[row, 0]) + mul_nt(kids[1], top_e[row, 1]))
            for i, out in zip(nodes, outs):
                tree[2**level + i] = split_parts(join_parts(out))

        over_nodes(2**level, 4, work)

    def near_root(node, depth):
        mates = []
        for f in range(3):
            mate = partners_ref[node, f]
            at = ((mate >> depth) ^ device) & (2**SPAN - 1)
            mates.append(gather_ref[at, 2**depth - 1 + (mate & (2**depth - 1))])
        left = jnp.where(low, mates[0], mates[1])
        return join_parts(
            mul_nt(left, wide_ref[node]) + mul_nt(mates[2][:, :RANK], thin_ref[node])
        )

    shallow = [near_root(node, (node + 1).bit_length() - 1) for node in range(EXPORT)]
    pushed = jnp.zeros((PART, RANK), F32)
    for level in range(2, dev_levels):
        node = device >> (dev_levels - level)
        row = 2**level - 4 + node
        side = device >> (dev_levels - level - 1) & 1
        parts = sum(
            mul_nt(tree[2**level + top_partners_ref[row, f]], top_b[row, f]) for f in range(3)
        )
        here = split_parts(join_parts(parts) + pushed)
        pushed = join_parts(jnp.dot(here, top_e[row, side], preferred_element_type=F32))

    down[0] = split_parts(shallow[0] + pushed)
    for depth in range(levels):
        first = 2**depth - 1

        def work(nodes, depth=depth, first=first):
            outs = [
                jnp.dot(down[first + i], move_ref[first + i], preferred_element_type=F32)
                for i in nodes
            ]
            for i, out in zip(nodes, outs):
                node = first + i
                if depth < SPAN - 1:
                    base = side_by_side(shallow[2 * node + 1], shallow[2 * node + 2])
                else:
                    base = local_ref[node]
                pair = base + join_parts(out)
                if depth == levels - 1:
                    out_ref[2 * i] = pair[:, :RANK].astype(BF)
                    out_ref[2 * i + 1] = pair[:, RANK:].astype(BF)
                else:
                    down[2 * node + 1] = split_parts(pair[:, :RANK])
                    down[2 * node + 2] = split_parts(pair[:, RANK:])

        if depth < SPAN:
            first_nodes = list(range(2**depth))
            work(first_nodes)
        else:
            over_nodes(2**depth, 8, work)


def final_kernel(low_ref, basis_ref, noise_ref, vec_ref, mine_ref, got_ref, out_ref):
    def work(nodes):
        fars = [
            jnp.dot(low_ref[n], basis_ref[n], preferred_element_type=F32) for n in nodes
        ]
        for n, far in zip(nodes, fars):
            here = lanes(n)
            near = mine_ref[:, here] + got_ref[:, here]
            out_ref[:, here] = near + noise_ref[:, here] * vec_ref[:, here].astype(F32) + far

    over_nodes(low_ref.shape[0], 8, work)


def swap_bit(value, bit):
    sub_bits = lax.axis_size("sub").bit_length() - 1
    axis, apart = ("sub", 2**bit) if bit < sub_bits else ("leaf", 2 ** (bit - sub_bits))
    pairs = [(i, i ^ apart) for i in range(lax.axis_size(axis))]
    return lax.ppermute(value, axis, pairs)


def body(
    points, inv_scale, noise, vectors, leaf_basis, local_transfer, top_transfer,
    local_coupling, top_coupling, local_partners, top_partners, near_offsets, near_cols,
):
    subs = lax.axis_size("sub")
    count = lax.axis_size("leaf") * subs
    dev_levels = count.bit_length() - 1
    device = lax.axis_index("leaf") * subs + lax.axis_index("sub")
    core = lax.axis_index("vec")
    where = jnp.stack([device, core]).astype(jnp.int32)
    size = vectors.shape[1]
    leaves = near_offsets.shape[0]
    slots = near_cols.shape[0]
    half = size // 2
    sds = jax.ShapeDtypeStruct
    scratch_blocks = [
        VMEM((PAIR, LEAF, LEAF), F32), VMEM((PAIR, LEAF, LEAF), F32),
        VMEM((PAIR, LEAF, LEAF), BF), VMEM((PAIR, LEAF, LEAF), BF),
    ]

    send = lax.dynamic_slice(vectors, (0, (1 - core) * half), (PART, half))
    got = lax.ppermute(send, "vec", [(0, 1), (1, 0)])

    coef, export, moves = pl.pallas_call(
        up_kernel,
        name="up",
        out_shape=(
            sds((2 * leaves - 1, 16, 2 * RANK), BF), sds((1, EXPORT, 16, 2 * RANK), BF),
            sds((leaves - 1, RANK, 2 * RANK), BF),
        ),
        in_specs=[vspec()] * 3,
        out_specs=(vspec(),) * 3,
        scratch_shapes=[
            VMEM((leaves // 8, RANK * 8, 2 * RANK), F32), VMEM((leaves - 1, 16, 2 * RANK), BF),
        ],
        compiler_params=params(28),
        cost_estimate=pl.CostEstimate(
            flops=300 * 2 * 256 * 256 * 48, bytes_accessed=8 << 20, transcendentals=0
        ),
    )(vectors, leaf_basis, jnp.transpose(local_transfer, (1, 2, 3, 0)))
    gathered = jnp.concatenate([export, swap_bit(export, 0)], axis=0)

    pack = pl.pallas_call(
        pack_kernel,
        name="pack",
        out_shape=sds((24, half), BF),
        in_specs=[sspec(), sspec(), vspec(), vspec(), vspec()],
        out_specs=vspec(),
        compiler_params=params(16),
    )(where, inv_scale, points, vectors, got)
    axes = ("leaf", "sub")
    left = lax.ppermute(pack, axes, [(i, i + 1) for i in range(count - 1)])
    right = lax.ppermute(pack, axes, [(i + 1, i) for i in range(count - 1)])

    pack, _ = lax.optimization_barrier((pack, export))
    mine, other, row_feat, far_list, far_count = pl.pallas_call(
        near_local_kernel,
        name="near_local",
        out_shape=(
            sds((PART, size), F32), sds((PART, size), F32), sds((leaves, 32, LEAF), BF),
            sds((slots + PAD,), jnp.int32), sds((1,), jnp.int32),
        ),
        in_specs=[sspec()] * 4 + [vspec()] * 2,
        out_specs=(vspec(), vspec(), vspec(), sspec(), sspec()),
        scratch_shapes=[
            VMEM((leaves // 2 + 1, LEAF, 32), BF), VMEM((leaves // 2 + 1, 16, LEAF), BF),
            *scratch_blocks, SMEM((slots + PAD,), jnp.int32),
        ],
        compiler_params=params(28),
        cost_estimate=pl.CostEstimate(
            flops=190 * 2 * 256 * 256 * 48, bytes_accessed=8 << 20, transcendentals=190 * 2**17
        ),
    )(where, inv_scale, near_offsets, near_cols, points, pack)

    far_list, gathered = lax.optimization_barrier((far_list, gathered))
    gathered = jnp.concatenate([gathered, swap_bit(gathered, 1)], axis=0)
    mine, other = pl.pallas_call(
        near_halo_kernel,
        name="near_halo",
        out_shape=(sds((PART, size), F32), sds((PART, size), F32)),
        in_specs=[sspec(), sspec()] + [vspec()] * 5,
        out_specs=(vspec(), vspec()),
        scratch_shapes=[
            VMEM((leaves + 1, LEAF, 32), BF), VMEM((leaves + 1, 16, LEAF), BF),
            *scratch_blocks,
        ],
        compiler_params=params(36),
        cost_estimate=pl.CostEstimate(
            flops=60 * 2 * 256 * 256 * 48, bytes_accessed=8 << 20, transcendentals=60 * 2**17
        ),
    )(far_list, far_count, row_feat, left, right, mine, other)
    swapped = lax.ppermute(other, "vec", [(0, 1), (1, 0)])

    _, coef_late, gathered = lax.optimization_barrier((mine, coef, gathered))
    gathered = jnp.concatenate([gathered, swap_bit(gathered, 2)], axis=0)
    tops = gathered
    for bit in range(SPAN, dev_levels):
        tops = tops[:, 0:1]
        tops = jnp.concatenate([tops, swap_bit(tops, bit)], axis=0)
    local, wide, thin = pl.pallas_call(
        couple_kernel,
        name="couple",
        out_shape=(
            sds((leaves - 1, PART, 2 * RANK), F32), sds((EXPORT, RANK, 2 * RANK), BF),
            sds((EXPORT, RANK, RANK), BF),
        ),
        in_specs=[sspec()] * 2 + [vspec()] * 2,
        out_specs=(vspec(),) * 3,
        scratch_shapes=[
            VMEM((leaves // 4, RANK * 8, 2 * RANK), F32),
            VMEM((leaves // 4, RANK * 8, RANK), F32),
        ],
        compiler_params=params(36),
        cost_estimate=pl.CostEstimate(
            flops=300 * 2 * 256 * 256 * 48, bytes_accessed=8 << 20, transcendentals=0
        ),
    )(where, local_partners, coef_late, jnp.transpose(local_coupling, (1, 2, 3, 0)))

    low = pl.pallas_call(
        functools.partial(down_kernel, dev_levels),
        name="down",
        out_shape=sds((leaves, PART, RANK), BF),
        in_specs=[sspec()] * 3 + [vspec()] * 8,
        out_specs=vspec(),
        scratch_shapes=[VMEM((leaves - 1, 16, RANK), BF), VMEM((count, 16, RANK), BF)],
        compiler_params=params(24),
        cost_estimate=pl.CostEstimate(
            flops=100 * 2 * 256 * 256 * 48, bytes_accessed=8 << 20, transcendentals=0
        ),
    )(
        where, local_partners, top_partners, gathered, tops, top_transfer, top_coupling,
        wide, thin, local, moves,
    )

    return pl.pallas_call(
        final_kernel,
        name="final",
        out_shape=sds((PART, size), F32),
        in_specs=[vspec()] * 6,
        out_specs=vspec(),
        compiler_params=params(16),
    )(low, leaf_basis, noise.reshape(1, size), vectors, mine, swapped)


def solution(mesh):
    return jax.shard_map(
        body,
        mesh=mesh,
        in_specs=(
            P("groups", ("leaf", "sub")),
            P("groups"),
            P(("groups", "leaf", "sub")),
            P(("groups", "vec"), ("leaf", "sub")),
            P(("groups", "leaf", "sub"), None, None),
            P(("groups", "leaf", "sub"), None, None, None),
            P("groups", None, None, None),
            P(("groups", "leaf", "sub"), None, None, None),
            P("groups", None, None, None),
            P(("groups", "leaf", "sub"), None),
            P("groups", None),
            P(("groups", "leaf", "sub")),
            P(("groups", "leaf", "sub")),
        ),
        out_specs=P(("groups", "vec"), ("leaf", "sub")),
        check_vma=False,
    )
```

```python
import functools
import math

import jax
import jax.numpy as jnp
from jax import lax
from jax.experimental import pallas as pl
from jax.experimental.pallas import tpu as pltpu
from jax.sharding import PartitionSpec as P

BF = jnp.bfloat16
F32 = jnp.float32
LEAF = 256
RANK = 64
SPAN = 3
PART = 8
EXPORT = 2**SPAN - 1
NEG_LOG2E = -1.0 / math.log(2.0)
ROOT3 = math.sqrt(3.0)
TINY = 1e-12
PAIR = 2
PAD = 16
TURNS = 2
CODE_BITS = 10
CODE = 2**CODE_BITS
VMEM = pltpu.VMEM
SMEM = pltpu.SMEM
NT = (((1,), (1,)), ((), ()))


def vspec():
    return pl.BlockSpec(memory_space=pltpu.VMEM)


def sspec():
    return pl.BlockSpec(memory_space=pltpu.SMEM)


def hspec():
    return pl.BlockSpec(memory_space=pltpu.HBM)


def fetch(pairs, sems):
    copies = [
        pltpu.make_async_copy(source, target, sems.at[i])
        for i, (source, target) in enumerate(pairs)
    ]
    for copy in copies:
        copy.start()
    return copies


def params(mib):
    return pltpu.CompilerParams(vmem_limit_bytes=mib << 20)


def lanes(index):
    return pl.ds(pl.multiple_of(index * LEAF, LEAF), LEAF)


def whole(scalar):
    return scalar.astype(jnp.int32)


def coordinate_rows(raw, scale_ref):
    width = raw.shape[1]
    row = lax.broadcasted_iota(jnp.int32, (8, width), 0)
    scale = jnp.where(
        row == 0, scale_ref[0], jnp.where(row == 1, scale_ref[1], scale_ref[2])
    )
    full = jnp.concatenate([raw, jnp.zeros((5, width), F32)], axis=0)
    scaled = (full - 0.5) * (scale * ROOT3)
    scaled = jnp.where(row < 3, scaled, 0.0)
    high = scaled.astype(BF).astype(F32)
    rest = (scaled - high).astype(BF).astype(F32)
    return high + pltpu.roll(rest, 4, 0)


def norm_parts(rows):
    swapped = pltpu.roll(rows, 4, 0)
    norm = jnp.sum(rows * (rows + swapped), axis=0, keepdims=True)
    high = norm.astype(BF).astype(F32)
    rest = norm - high
    mid = rest.astype(BF).astype(F32)
    return swapped, high, mid, rest - mid


def row_features(rows):
    swapped, high, mid, low = norm_parts(rows)
    row = lax.broadcasted_iota(jnp.int32, rows.shape, 0)
    tail = jnp.where(
        row < 3,
        1.0,
        jnp.where(row == 3, high, jnp.where(row == 4, mid, jnp.where(row == 5, low, 0.0))),
    )
    return jnp.concatenate([rows, swapped, tail, jnp.zeros_like(rows)], axis=0).astype(BF)


def col_features(rows):
    _, high, mid, low = norm_parts(rows)
    row = lax.broadcasted_iota(jnp.int32, rows.shape, 0)
    tail = jnp.where(
        row == 0,
        high,
        jnp.where(row == 1, mid, jnp.where(row == 2, low, jnp.where(row < 6, 1.0, 0.0))),
    )
    both = -2.0 * rows
    return jnp.concatenate([both, both, tail, jnp.zeros_like(rows)], axis=0).T.astype(BF)


def matern(squared):
    squared = jnp.maximum(squared, TINY)
    dist = squared * lax.rsqrt(squared)
    return ((1.0 + dist) * jnp.exp2(dist * NEG_LOG2E)).astype(BF)


def pack_kernel(scale_ref, points_hbm, vec_hbm, got_hbm, out_ref, points, mine, got, sems):
    half = out_ref.shape[1]
    core = whole(scale_ref[4])
    there = pl.ds(pl.multiple_of(core * half, half), half)
    copies = fetch(
        [
            (points_hbm.at[:, there], points), (vec_hbm.at[:, there], mine),
            (got_hbm.at[:, there], got),
        ],
        sems,
    )
    for copy in copies:
        copy.wait()

    def step(i, _):
        here = pl.ds(pl.multiple_of(i * 2048, 2048), 2048)
        rows = coordinate_rows(points[:, here], scale_ref)
        out_ref[:, here] = jnp.concatenate(
            [mine[:, here].astype(F32), got[:, here].astype(F32), rows], axis=0
        ).astype(BF)
        return 0

    lax.fori_loop(0, half // 2048, step, 0)


def block_loop(count, place, list_ref, row_ref, col_ref, val_ref, sums, s0, s1, k0, k1):
    def accumulate(first, kern):
        for q in range(PAIR):
            code = list_ref[first + q]
            here = lanes(code >> CODE_BITS)
            part = jnp.dot(
                val_ref[place(code & (CODE - 1))], kern[q], preferred_element_type=F32
            )
            sums[0][:, here] += part[:PART]
            sums[1][:, here] += part[PART:]

    def distance(first, out):
        for q in range(PAIR):
            code = list_ref[first + q]
            out[q] = jnp.dot(
                col_ref[place(code & (CODE - 1))],
                row_ref[code >> CODE_BITS],
                preferred_element_type=F32,
            )

    def evaluate(squared, kern):
        for q in range(PAIR):
            kern[q] = matern(squared[q])

    k1[...] = jnp.zeros_like(k1)
    distance(0, s0)

    def step(it, _):
        for turn in range(TURNS):
            first = (it * TURNS + turn) * 2 * PAIR
            accumulate(jnp.maximum(first - PAIR, 0), k1)
            distance(first + PAIR, s1)
            evaluate(s0, k0)
            accumulate(first, k0)
            distance(first + 2 * PAIR, s0)
            evaluate(s1, k1)
        return 0

    turns = (count + TURNS * 2 * PAIR - 1) // (TURNS * 2 * PAIR)
    lax.fori_loop(0, turns, step, 0)
    accumulate(jnp.maximum(turns * TURNS * 2 * PAIR - PAIR, 0), k1)


def load_columns(pack_ref, base, count, col_ref, val_ref):
    def step(i, _):
        for q in range(4):
            leaf = i * 4 + q
            val_ref[base + leaf] = pack_ref[0:16, lanes(leaf)]
            col_ref[base + leaf] = col_features(pack_ref[16:24, lanes(leaf)].astype(F32))
        return 0

    lax.fori_loop(0, count // 4, step, 0)


def near_local_kernel(
    scale_ref, offs_ref, cols_ref, points_ref, pack_ref,
    mine_ref, other_ref, row_ref, far_list, far_count,
    col_ref, val_ref, s0, s1, k0, k1, own_list,
):
    device, half_id = whole(scale_ref[3]), whole(scale_ref[4])
    leaves = offs_ref.shape[0]
    half = leaves // 2
    slots = cols_ref.shape[0]
    each = slots // leaves

    far_base = device * leaves - leaves + half_id * half
    half_bits = half.bit_length() - 1

    def rows_step(i, carry):
        row, code, own, far = carry
        for q in range(2):
            leaf = i * 2 + q
            row_ref[leaf] = row_features(coordinate_rows(points_ref[:, lanes(leaf)], scale_ref))
            mine_ref[:, lanes(leaf)] = jnp.zeros((PART, LEAF), F32)
            other_ref[:, lanes(leaf)] = jnp.zeros((PART, LEAF), F32)
            for w in range(each):
                slot = leaf * each + w
                begins = offs_ref[jnp.minimum(row + 1, leaves - 1)] == slot
                row = jnp.where(begins, row + 1, row)
                code = jnp.where(begins, code + CODE, code)
                place = cols_ref[slot] - far_base
                own_list[own] = code + (place - leaves)
                far_list[far] = code + place
                block = place >> half_bits
                own = jnp.where(block == 2, own + 1, own)
                far = jnp.where((block & 3) == 0, far + 1, far)
        return row, code, own, far

    zero = jnp.int32(0)
    _, _, own, far = lax.fori_loop(0, leaves // 2, rows_step, (zero, zero, zero, zero))
    for q in range(PAD):
        own_list[own + q] = half
        far_list[far + q] = 8 * half
    far_count[0] = far
    load_columns(pack_ref, 0, half, col_ref, val_ref)
    val_ref[half] = jnp.zeros((16, LEAF), BF)
    col_ref[half] = jnp.zeros(col_ref.shape[1:], BF)
    sums = (mine_ref, other_ref)
    block_loop(own, lambda c: c, own_list, row_ref, col_ref, val_ref, sums, s0, s1, k0, k1)


def near_halo_kernel(
    far_list, far_count, row_ref, left_ref, right_ref, mine_in, other_in,
    mine_ref, other_ref,
    col_ref, val_ref, s0, s1, k0, k1,
):
    half = left_ref.shape[1] // LEAF
    bits = half.bit_length() - 1
    count = far_count[0]

    def place(code):
        return (code & (half - 1)) | ((code >> (bits + 2)) << bits)

    def load(i, _):
        for q in range(4):
            code = far_list[i * 4 + q] & (CODE - 1)
            here = lanes(code & (half - 1))
            after = code >= 4 * half
            values = jnp.where(after, right_ref[0:16, here], left_ref[0:16, here])
            rows = jnp.where(after, right_ref[16:24, here], left_ref[16:24, here])
            val_ref[place(code)] = values
            col_ref[place(code)] = col_features(rows.astype(F32))
        return 0

    mine_ref[...] = mine_in[...]
    other_ref[...] = other_in[...]
    lax.fori_loop(0, (count + 3) // 4, load, 0)
    val_ref[2 * half] = jnp.zeros((16, LEAF), BF)
    col_ref[2 * half] = jnp.zeros(col_ref.shape[1:], BF)
    sums = (mine_ref, other_ref)
    block_loop(count, place, far_list, row_ref, col_ref, val_ref, sums, s0, s1, k0, k1)


def split_parts(value):
    high = value.astype(BF).astype(F32)
    return jnp.concatenate([high, value - high], axis=0).astype(BF)


def join_parts(value):
    return value[0:8] + value[8:16]


def mul_nt(left, right):
    return lax.dot_general(left, right, NT, preferred_element_type=F32)


def over_nodes(count, unroll, work):
    group = min(unroll, count)
    if count == group:
        work([jnp.int32(i) for i in range(count)])
        return

    def step(i, _):
        work([i * group + q for q in range(group)])
        return 0

    lax.fori_loop(0, count // group, step, 0)


def store_turned(flat, r, block):
    turned = block.T
    count = turned.shape[0] // 8
    width = turned.shape[1]
    rows = pl.ds(pl.multiple_of(r * 8, 8), 8)
    flat[0:count, rows] = turned[: count * 8].reshape(count, 8, width)
    rest = turned.shape[0] - count * 8
    flat[count, pl.ds(pl.multiple_of(r * 8, 8), rest)] = turned[count * 8 :]


def load_node(flat, node):
    return flat[node >> 3, pl.ds(node & 7, RANK, stride=8)].astype(BF)


def side_by_side(first, second):
    return jnp.concatenate([first, second], axis=1)


def doubled(pair):
    low = lax.broadcasted_iota(jnp.int32, pair.shape, 1) < RANK
    turned = pltpu.roll(pair, RANK, 1)
    return jnp.where(low, pair, turned), jnp.where(low, turned, pair)


def up_kernel(
    vec_hbm, basis_hbm, raw_hbm, coef_ref, export_ref, move_ref,
    vec_ref, basis_ref, raw_ref, flat, pairs, sems,
):
    leaves = basis_ref.shape[0]
    chunks = 4
    per = leaves // chunks
    wide = per * LEAF
    deep = RANK // chunks
    copies = fetch(
        [
            pair
            for c in range(chunks)
            for pair in (
                (vec_hbm.at[:, c * wide : (c + 1) * wide], vec_ref.at[:, c * wide : (c + 1) * wide]),
                (basis_hbm.at[c * per : (c + 1) * per], basis_ref.at[c * per : (c + 1) * per]),
                (
                    raw_hbm.at[:, c * deep : (c + 1) * deep],
                    raw_ref.at[:, c * deep : (c + 1) * deep],
                ),
            )
        ],
        sems,
    )
    levels = leaves.bit_length() - 1

    def keep(parent, first, second):
        pair = side_by_side(first, second)
        pairs[parent] = split_parts(pair)
        one, two = doubled(pair)
        coef_ref[2 * parent + 1] = split_parts(one)
        coef_ref[2 * parent + 2] = split_parts(two)

    def leaf_step(it, _):
        outs = []
        for q in range(8):
            leaf = it * 8 + q
            outs.append(mul_nt(vec_ref[:, lanes(leaf)], basis_ref[leaf]))
        for q in range(4):
            r = it * 4 + q
            block = jnp.concatenate([raw_ref[0, r], raw_ref[1, r]], axis=0).astype(F32)
            store_turned(flat, r, block)
        for q in range(4):
            keep(leaves // 2 - 1 + it * 4 + q, outs[2 * q], outs[2 * q + 1])
        return 0

    for c in range(chunks):
        for copy in copies[3 * c : 3 * c + 3]:
            copy.wait()
        lax.fori_loop(c * per // 8, (c + 1) * per // 8, leaf_step, 0)
    for depth in range(levels - 1, 0, -1):
        first = 2**depth - 1
        above = 2 ** (depth - 1) - 1

        def work(nodes, first=first, above=above):
            outs = []
            for j in nodes:
                for c in range(2):
                    node = first + 2 * j + c
                    move = load_node(flat, node)
                    move_ref[node] = move
                    outs.append(mul_nt(pairs[node], move))
            for j, i in enumerate(nodes):
                keep(above + i, join_parts(outs[2 * j]), join_parts(outs[2 * j + 1]))

        over_nodes(2 ** (depth - 1), 8, work)
    move = load_node(flat, 0)
    move_ref[0] = move
    root = join_parts(mul_nt(pairs[0], move))
    coef_ref[0] = split_parts(side_by_side(root, root))
    export_ref[...] = coef_ref[0:EXPORT]


def couple_kernel(
    scale_ref, partners_ref, coef_ref, raw_hbm, local_ref, wide_ref, thin_ref,
    raw_ref, wide, thin, sems,
):
    device = whole(scale_ref[3])
    total = raw_ref.shape[3]
    chunks = 4
    deep = RANK // chunks
    copies = fetch(
        [
            (raw_hbm.at[:, c * deep : (c + 1) * deep], raw_ref.at[:, c * deep : (c + 1) * deep])
            for c in range(chunks)
        ],
        sems,
    )
    span = total + 1
    levels = span.bit_length() - 2
    low = lax.broadcasted_iota(jnp.int32, (16, 2 * RANK), 1) < RANK

    def turn(i, _):
        for q in range(4):
            r = i * 4 + q
            block = jnp.concatenate([raw_ref[0, r], raw_ref[1, r]], axis=0).astype(F32)
            store_turned(wide, r, block)
            store_turned(thin, r, raw_ref[2, r].astype(F32))
        return 0

    for c in range(chunks):
        copies[c].wait()
        lax.fori_loop(c * deep // 4, (c + 1) * deep // 4, turn, 0)
    for node in range(EXPORT):
        wide_ref[node] = load_node(wide, node)
        thin_ref[node] = load_node(thin, node)
    for depth in range(SPAN, levels + 1):
        first = 2**depth - 1
        above = 2 ** (depth - 1) - 1
        shift = first - device * 2**depth

        def work(nodes, first=first, above=above, shift=shift):
            outs = []
            for j in nodes:
                for c in range(2):
                    node = first + 2 * j + c
                    mates = [coef_ref[partners_ref[f, node] + shift] for f in range(3)]
                    left = jnp.where(low, mates[0], mates[1])
                    outs.append(
                        mul_nt(left, load_node(wide, node))
                        + mul_nt(
                            mates[2][:, :RANK],
                            load_node(thin, node),
                        )
                    )
            for j, i in enumerate(nodes):
                local_ref[above + i] = side_by_side(
                    join_parts(outs[2 * j]), join_parts(outs[2 * j + 1])
                )

        over_nodes(2 ** (depth - 1), 8, work)


def down_kernel(
    dev_levels, scale_ref, partners_ref, top_partners_ref, top_e, top_b, wide_ref, thin_ref,
    local_ref, move_ref, *refs,
):
    exports, (basis_hbm, noise_hbm, vec_hbm, near_hbm, swap_hbm, out_hbm) = refs[:9], refs[9:15]
    gather_ref, down, tree, low_ref, basis, noise, vec, near, swap, out, sems = refs[15:]
    device = whole(scale_ref[3])
    leaves = low_ref.shape[0]
    levels = leaves.bit_length() - 1
    copies = fetch(
        [
            (basis_hbm, basis), (noise_hbm, noise), (vec_hbm, vec), (near_hbm, near),
            (swap_hbm, swap),
        ],
        sems,
    )
    for i in range(2**SPAN):
        gather_ref[i] = exports[i][...]
    tops_ref = gather_ref if dev_levels == SPAN else exports[2**SPAN]
    low = lax.broadcasted_iota(jnp.int32, (16, 2 * RANK), 1) < RANK

    for level in range(dev_levels - 1, 1, -1):

        def work(nodes, level=level):
            outs = []
            for i in nodes:
                row = 2**level - 4 + i
                if level == dev_levels - 1:
                    kids = [tops_ref[(2 * i + c) ^ device, 0][:, :RANK] for c in range(2)]
                else:
                    kids = [tree[2 ** (level + 1) + 2 * i + c] for c in range(2)]
                outs.append(mul_nt(kids[0], top_e[row, 0]) + mul_nt(kids[1], top_e[row, 1]))
            for i, out in zip(nodes, outs):
                tree[2**level + i] = split_parts(join_parts(out))

        over_nodes(2**level, 4, work)

    def near_root(node, depth):
        mates = []
        for f in range(3):
            mate = partners_ref[f, node]
            at = ((mate >> depth) ^ device) & (2**SPAN - 1)
            mates.append(gather_ref[at, 2**depth - 1 + (mate & (2**depth - 1))])
        left = jnp.where(low, mates[0], mates[1])
        return join_parts(
            mul_nt(left, wide_ref[node]) + mul_nt(mates[2][:, :RANK], thin_ref[node])
        )

    shallow = [near_root(node, (node + 1).bit_length() - 1) for node in range(EXPORT)]
    pushed = jnp.zeros((PART, RANK), F32)
    for level in range(2, dev_levels):
        node = device >> (dev_levels - level)
        row = 2**level - 4 + node
        side = device >> (dev_levels - level - 1) & 1
        parts = sum(
            mul_nt(tree[2**level + top_partners_ref[row, f]], top_b[row, f]) for f in range(3)
        )
        here = split_parts(join_parts(parts) + pushed)
        pushed = join_parts(jnp.dot(here, top_e[row, side], preferred_element_type=F32))

    down[0] = split_parts(shallow[0] + pushed)
    for depth in range(levels):
        first = 2**depth - 1

        def work(nodes, depth=depth, first=first):
            outs = [
                jnp.dot(down[first + i], move_ref[first + i], preferred_element_type=F32)
                for i in nodes
            ]
            for i, out in zip(nodes, outs):
                node = first + i
                if depth < SPAN - 1:
                    base = side_by_side(shallow[2 * node + 1], shallow[2 * node + 2])
                else:
                    base = local_ref[node]
                pair = base + join_parts(out)
                if depth == levels - 1:
                    low_ref[2 * i] = pair[:, :RANK].astype(BF)
                    low_ref[2 * i + 1] = pair[:, RANK:].astype(BF)
                else:
                    down[2 * node + 1] = split_parts(pair[:, :RANK])
                    down[2 * node + 2] = split_parts(pair[:, RANK:])

        if depth < SPAN:
            first_nodes = list(range(2**depth))
            work(first_nodes)
        else:
            over_nodes(2**depth, 8, work)

    for copy in copies:
        copy.wait()
    chunks = 4
    per = leaves // chunks
    wide = per * LEAF
    sends = []
    for c in range(chunks):

        def last(nodes, c=c):
            rows = [c * per + i for i in nodes]
            fars = [jnp.dot(low_ref[n], basis[n], preferred_element_type=F32) for n in rows]
            for n, far in zip(rows, fars):
                here = lanes(n)
                total = near[:, here] + swap[:, here]
                out[:, here] = total + noise[:, here] * vec[:, here].astype(F32) + far

        over_nodes(per, 8, last)
        piece = slice(c * wide, (c + 1) * wide)
        send = pltpu.make_async_copy(
            out.at[:, piece], out_hbm.at[:, piece], sems.at[len(copies) + c]
        )
        send.start()
        sends.append(send)
    for send in sends:
        send.wait()


def swap_mask(value, mask):
    leaf, sub = lax.axis_size("leaf"), lax.axis_size("sub")
    pairs = [(i, i ^ mask) for i in range(leaf * sub)]
    return lax.ppermute(value, ("leaf", "sub"), pairs)


def body(
    points, inv_scale, noise, vectors, leaf_basis, local_transfer, top_transfer,
    local_coupling, top_coupling, local_partners, top_partners, near_offsets, near_cols,
):
    subs = lax.axis_size("sub")
    count = lax.axis_size("leaf") * subs
    dev_levels = count.bit_length() - 1
    device = lax.axis_index("leaf") * subs + lax.axis_index("sub")
    core = lax.axis_index("vec")
    scale = jnp.concatenate([inv_scale, jnp.stack([device, core]).astype(F32)])
    size = vectors.shape[1]
    leaves = near_offsets.shape[0]
    slots = near_cols.shape[0]
    half = size // 2
    sds = jax.ShapeDtypeStruct
    scratch_blocks = [
        VMEM((PAIR, LEAF, LEAF), F32), VMEM((PAIR, LEAF, LEAF), F32),
        VMEM((PAIR, LEAF, LEAF), BF), VMEM((PAIR, LEAF, LEAF), BF),
    ]

    got = lax.ppermute(vectors, "vec", [(0, 1), (1, 0)])

    moves_raw = jnp.transpose(local_transfer, (1, 2, 3, 0))
    coef, export, moves = pl.pallas_call(
        up_kernel,
        name="up",
        out_shape=(
            sds((2 * leaves - 1, 16, 2 * RANK), BF), sds((EXPORT, 16, 2 * RANK), BF),
            sds((leaves - 1, RANK, 2 * RANK), BF),
        ),
        in_specs=[hspec()] * 3,
        out_specs=(vspec(),) * 3,
        scratch_shapes=[
            VMEM(vectors.shape, BF), VMEM(leaf_basis.shape, BF), VMEM(moves_raw.shape, BF),
            VMEM((leaves // 8, RANK * 8, 2 * RANK), F32), VMEM((leaves - 1, 16, 2 * RANK), BF),
            pltpu.SemaphoreType.DMA((12,)),
        ],
        compiler_params=params(28),
        cost_estimate=pl.CostEstimate(
            flops=300 * 2 * 256 * 256 * 48, bytes_accessed=8 << 20, transcendentals=0
        ),
    )(vectors, leaf_basis, moves_raw)
    pack = pl.pallas_call(
        pack_kernel,
        name="pack",
        out_shape=sds((24, half), BF),
        in_specs=[sspec(), hspec(), hspec(), hspec()],
        out_specs=vspec(),
        scratch_shapes=[
            VMEM((3, half), F32), VMEM((PART, half), BF), VMEM((PART, half), BF),
            pltpu.SemaphoreType.DMA((3,)),
        ],
        compiler_params=params(16),
    )(scale, points, vectors, got)
    axes = ("leaf", "sub")
    left = lax.ppermute(pack, axes, [(i, i + 1) for i in range(count - 1)])
    right = lax.ppermute(pack, axes, [(i + 1, i) for i in range(count - 1)])

    pack, _ = lax.optimization_barrier((pack, export))
    mine, other, row_feat, far_list, far_count = pl.pallas_call(
        near_local_kernel,
        name="near_local",
        out_shape=(
            sds((PART, size), F32), sds((PART, size), F32), sds((leaves, 32, LEAF), BF),
            sds((slots + PAD,), jnp.int32), sds((1,), jnp.int32),
        ),
        in_specs=[sspec()] * 3 + [vspec()] * 2,
        out_specs=(vspec(), vspec(), vspec(), sspec(), sspec()),
        scratch_shapes=[
            VMEM((leaves // 2 + 1, LEAF, 32), BF), VMEM((leaves // 2 + 1, 16, LEAF), BF),
            *scratch_blocks, SMEM((slots + PAD,), jnp.int32),
        ],
        compiler_params=params(28),
        cost_estimate=pl.CostEstimate(
            flops=190 * 2 * 256 * 256 * 48, bytes_accessed=8 << 20, transcendentals=190 * 2**17
        ),
    )(scale, near_offsets, near_cols, points, pack)

    exports = [export] + [swap_mask(export, mask) for mask in range(1, 2**SPAN)]
    tops = export[None]
    for bit in range(SPAN, dev_levels):
        if bit == SPAN:
            tops = jnp.stack([part[0:1] for part in exports])
        tops = jnp.concatenate([tops, swap_mask(tops, 2**bit)], axis=0)
    mine, other = pl.pallas_call(
        near_halo_kernel,
        name="near_halo",
        out_shape=(sds((PART, size), F32), sds((PART, size), F32)),
        in_specs=[sspec(), sspec()] + [vspec()] * 5,
        out_specs=(vspec(), vspec()),
        scratch_shapes=[
            VMEM((leaves + 1, LEAF, 32), BF), VMEM((leaves + 1, 16, LEAF), BF),
            *scratch_blocks,
        ],
        compiler_params=params(36),
        cost_estimate=pl.CostEstimate(
            flops=60 * 2 * 256 * 256 * 48, bytes_accessed=8 << 20, transcendentals=60 * 2**17
        ),
    )(far_list, far_count, row_feat, left, right, mine, other)
    swapped = lax.ppermute(other, "vec", [(0, 1), (1, 0)])

    _, coef_late = lax.optimization_barrier((mine, coef))
    ties_raw = jnp.transpose(local_coupling, (1, 2, 3, 0))
    mates = jnp.transpose(local_partners)
    local, wide, thin = pl.pallas_call(
        couple_kernel,
        name="couple",
        out_shape=(
            sds((leaves - 1, PART, 2 * RANK), F32), sds((EXPORT, RANK, 2 * RANK), BF),
            sds((EXPORT, RANK, RANK), BF),
        ),
        in_specs=[sspec()] * 2 + [vspec(), hspec()],
        out_specs=(vspec(),) * 3,
        scratch_shapes=[
            VMEM(ties_raw.shape, BF),
            VMEM((leaves // 4, RANK * 8, 2 * RANK), F32),
            VMEM((leaves // 4, RANK * 8, RANK), F32), pltpu.SemaphoreType.DMA((4,)),
        ],
        compiler_params=params(36),
        cost_estimate=pl.CostEstimate(
            flops=300 * 2 * 256 * 256 * 48, bytes_accessed=8 << 20, transcendentals=0
        ),
    )(scale, mates, coef_late, ties_raw)

    return pl.pallas_call(
        functools.partial(down_kernel, dev_levels),
        name="down",
        out_shape=sds((PART, size), F32),
        in_specs=[sspec()] * 3 + [vspec()] * 15 + [hspec()] * 5,
        out_specs=hspec(),
        scratch_shapes=[
            VMEM((2**SPAN, EXPORT, 16, 2 * RANK), BF), VMEM((leaves - 1, 16, RANK), BF),
            VMEM((count, 16, RANK), BF), VMEM((leaves, PART, RANK), BF),
            VMEM(leaf_basis.shape, BF), VMEM((1, size), F32), VMEM(vectors.shape, BF),
            VMEM((PART, size), F32), VMEM((PART, size), F32), VMEM((PART, size), F32),
            pltpu.SemaphoreType.DMA((9,)),
        ],
        compiler_params=params(32),
        cost_estimate=pl.CostEstimate(
            flops=100 * 2 * 256 * 256 * 48, bytes_accessed=8 << 20, transcendentals=0
        ),
    )(
        scale, mates, top_partners, top_transfer, top_coupling, wide, thin, local, moves,
        *exports, tops, leaf_basis, noise.reshape(1, size), vectors, mine, swapped,
    )


def solution(mesh):
    return jax.shard_map(
        body,
        mesh=mesh,
        in_specs=(
            P("groups", ("leaf", "sub")),
            P("groups"),
            P(("groups", "leaf", "sub")),
            P(("groups", "vec"), ("leaf", "sub")),
            P(("groups", "leaf", "sub"), None, None),
            P(("groups", "leaf", "sub"), None, None, None),
            P("groups", None, None, None),
            P(("groups", "leaf", "sub"), None, None, None),
            P("groups", None, None, None),
            P(("groups", "leaf", "sub"), None),
            P("groups", None),
            P(("groups", "leaf", "sub")),
            P(("groups", "leaf", "sub")),
        ),
        out_specs=P(("groups", "vec"), ("leaf", "sub")),
        check_vma=False,
    )
```

```python
import functools
import math

import jax
import jax.numpy as jnp
from jax import lax
from jax.experimental import pallas as pl
from jax.experimental.pallas import tpu as pltpu
from jax.sharding import PartitionSpec as P

BF = jnp.bfloat16
F32 = jnp.float32
LEAF = 256
RANK = 64
SPAN = 3
PART = 8
ALL = 2 * PART
EXPORT = 2**SPAN
NEG_LOG2E = -1.0 / math.log(2.0)
ROOT3 = math.sqrt(3.0)
TINY = 1e-12
PAIR = 2
PAD = 16
TURNS = 2
CODE_BITS = 10
CODE = 2**CODE_BITS
VMEM = pltpu.VMEM
SMEM = pltpu.SMEM
NT = (((1,), (1,)), ((), ()))


def vspec():
    return pl.BlockSpec(memory_space=pltpu.VMEM)


def sspec():
    return pl.BlockSpec(memory_space=pltpu.SMEM)


def hspec():
    return pl.BlockSpec(memory_space=pltpu.HBM)


def fetch(pairs, sems):
    copies = [
        pltpu.make_async_copy(source, target, sems.at[i])
        for i, (source, target) in enumerate(pairs)
    ]
    for copy in copies:
        copy.start()
    return copies


def params(mib):
    return pltpu.CompilerParams(vmem_limit_bytes=mib << 20)


def lanes(index):
    return pl.ds(pl.multiple_of(index * LEAF, LEAF), LEAF)


def whole(scalar):
    return scalar.astype(jnp.int32)


def coordinate_rows(raw, scale_ref):
    width = raw.shape[1]
    row = lax.broadcasted_iota(jnp.int32, (8, width), 0)
    scale = jnp.where(
        row == 0, scale_ref[0], jnp.where(row == 1, scale_ref[1], scale_ref[2])
    )
    full = jnp.concatenate([raw, jnp.zeros((5, width), F32)], axis=0)
    scaled = (full - 0.5) * (scale * ROOT3)
    scaled = jnp.where(row < 3, scaled, 0.0)
    high = scaled.astype(BF).astype(F32)
    rest = (scaled - high).astype(BF).astype(F32)
    return high + pltpu.roll(rest, 4, 0)


def norm_parts(rows):
    swapped = pltpu.roll(rows, 4, 0)
    norm = jnp.sum(rows * (rows + swapped), axis=0, keepdims=True)
    high = norm.astype(BF).astype(F32)
    rest = norm - high
    mid = rest.astype(BF).astype(F32)
    return swapped, high, mid, rest - mid


def row_features(rows):
    swapped, high, mid, low = norm_parts(rows)
    row = lax.broadcasted_iota(jnp.int32, rows.shape, 0)
    tail = jnp.where(
        row < 3,
        1.0,
        jnp.where(row == 3, high, jnp.where(row == 4, mid, jnp.where(row == 5, low, 0.0))),
    )
    return jnp.concatenate([rows, swapped, tail, jnp.zeros_like(rows)], axis=0).astype(BF)


def col_features(rows):
    _, high, mid, low = norm_parts(rows)
    row = lax.broadcasted_iota(jnp.int32, rows.shape, 0)
    tail = jnp.where(
        row == 0,
        high,
        jnp.where(row == 1, mid, jnp.where(row == 2, low, jnp.where(row < 6, 1.0, 0.0))),
    )
    both = -2.0 * rows
    return jnp.concatenate([both, both, tail, jnp.zeros_like(rows)], axis=0).T.astype(BF)


def matern(squared):
    squared = jnp.maximum(squared, TINY)
    dist = squared * lax.rsqrt(squared)
    return ((1.0 + dist) * jnp.exp2(dist * NEG_LOG2E)).astype(BF)


def pack_kernel(scale_ref, points_hbm, vec_hbm, got_hbm, out_ref, points, mine, got, sems):
    half = out_ref.shape[1]
    core = whole(scale_ref[4])
    there = pl.ds(pl.multiple_of(core * half, half), half)
    copies = fetch(
        [
            (points_hbm.at[:, there], points), (vec_hbm.at[:, there], mine),
            (got_hbm.at[:, there], got),
        ],
        sems,
    )
    for copy in copies:
        copy.wait()

    def step(i, _):
        here = pl.ds(pl.multiple_of(i * 2048, 2048), 2048)
        rows = coordinate_rows(points[:, here], scale_ref)
        one, two = mine[:, here].astype(F32), got[:, here].astype(F32)
        first, second = jnp.where(core == 0, one, two), jnp.where(core == 0, two, one)
        out_ref[:, here] = jnp.concatenate([first, second, rows], axis=0).astype(BF)
        return 0

    lax.fori_loop(0, half // 2048, step, 0)


def block_loop(count, place, list_ref, row_ref, col_ref, val_ref, sums, s0, s1, k0, k1):
    def accumulate(first, kern):
        for q in range(PAIR):
            code = list_ref[first + q]
            here = lanes(code >> CODE_BITS)
            part = jnp.dot(
                val_ref[place(code & (CODE - 1))], kern[q], preferred_element_type=F32
            )
            sums[0][:, here] += part[:PART]
            sums[1][:, here] += part[PART:]

    def distance(first, out):
        for q in range(PAIR):
            code = list_ref[first + q]
            out[q] = jnp.dot(
                col_ref[place(code & (CODE - 1))],
                row_ref[code >> CODE_BITS],
                preferred_element_type=F32,
            )

    def evaluate(squared, kern):
        for q in range(PAIR):
            kern[q] = matern(squared[q])

    k1[...] = jnp.zeros_like(k1)
    distance(0, s0)

    def step(it, _):
        for turn in range(TURNS):
            first = (it * TURNS + turn) * 2 * PAIR
            accumulate(jnp.maximum(first - PAIR, 0), k1)
            distance(first + PAIR, s1)
            evaluate(s0, k0)
            accumulate(first, k0)
            distance(first + 2 * PAIR, s0)
            evaluate(s1, k1)
        return 0

    turns = (count + TURNS * 2 * PAIR - 1) // (TURNS * 2 * PAIR)
    lax.fori_loop(0, turns, step, 0)
    accumulate(jnp.maximum(turns * TURNS * 2 * PAIR - PAIR, 0), k1)


def load_columns(pack_ref, base, count, col_ref, val_ref):
    def step(i, _):
        for q in range(4):
            leaf = i * 4 + q
            val_ref[base + leaf] = pack_ref[0:16, lanes(leaf)]
            col_ref[base + leaf] = col_features(pack_ref[16:24, lanes(leaf)].astype(F32))
        return 0

    lax.fori_loop(0, count // 4, step, 0)


def near_local_kernel(
    scale_ref, offs_ref, cols_ref, points_ref, pack_ref,
    mine_ref, other_ref, row_ref, far_list, far_count,
    col_ref, val_ref, s0, s1, k0, k1, own_list,
):
    device, half_id = whole(scale_ref[3]), whole(scale_ref[4])
    leaves = offs_ref.shape[0]
    half = leaves // 2
    slots = cols_ref.shape[0]
    each = slots // leaves

    far_base = device * leaves - leaves + half_id * half
    half_bits = half.bit_length() - 1

    def rows_step(i, carry):
        row, code, own, far = carry
        for q in range(2):
            leaf = i * 2 + q
            row_ref[leaf] = row_features(coordinate_rows(points_ref[:, lanes(leaf)], scale_ref))
            mine_ref[:, lanes(leaf)] = jnp.zeros((PART, LEAF), F32)
            other_ref[:, lanes(leaf)] = jnp.zeros((PART, LEAF), F32)
            for w in range(each):
                slot = leaf * each + w
                begins = offs_ref[jnp.minimum(row + 1, leaves - 1)] == slot
                row = jnp.where(begins, row + 1, row)
                code = jnp.where(begins, code + CODE, code)
                place = cols_ref[slot] - far_base
                own_list[own] = code + (place - leaves)
                far_list[far] = code + place
                block = place >> half_bits
                own = jnp.where(block == 2, own + 1, own)
                far = jnp.where((block & 3) == 0, far + 1, far)
        return row, code, own, far

    zero = jnp.int32(0)
    _, _, own, far = lax.fori_loop(0, leaves // 2, rows_step, (zero, zero, zero, zero))
    for q in range(PAD):
        own_list[own + q] = half
        far_list[far + q] = 8 * half
    far_count[0] = far
    load_columns(pack_ref, 0, half, col_ref, val_ref)
    val_ref[half] = jnp.zeros((16, LEAF), BF)
    col_ref[half] = jnp.zeros(col_ref.shape[1:], BF)
    sums = (mine_ref, other_ref)
    block_loop(own, lambda c: c, own_list, row_ref, col_ref, val_ref, sums, s0, s1, k0, k1)


def near_halo_kernel(
    scale_ref, far_list, far_count, row_ref, left_ref, right_ref, first_in, second_in,
    mine_ref, other_ref,
    first, second, col_ref, val_ref, s0, s1, k0, k1,
):
    core = whole(scale_ref[4])
    half = left_ref.shape[1] // LEAF
    bits = half.bit_length() - 1
    count = far_count[0]

    def place(code):
        return (code & (half - 1)) | ((code >> (bits + 2)) << bits)

    def load(i, _):
        for q in range(4):
            code = far_list[i * 4 + q] & (CODE - 1)
            here = lanes(code & (half - 1))
            after = code >= 4 * half
            values = jnp.where(after, right_ref[0:16, here], left_ref[0:16, here])
            rows = jnp.where(after, right_ref[16:24, here], left_ref[16:24, here])
            val_ref[place(code)] = values
            col_ref[place(code)] = col_features(rows.astype(F32))
        return 0

    first[...] = first_in[...]
    second[...] = second_in[...]
    lax.fori_loop(0, (count + 3) // 4, load, 0)
    val_ref[2 * half] = jnp.zeros((16, LEAF), BF)
    col_ref[2 * half] = jnp.zeros(col_ref.shape[1:], BF)
    sums = (first, second)
    block_loop(count, place, far_list, row_ref, col_ref, val_ref, sums, s0, s1, k0, k1)

    @pl.when(core == 0)
    def _():
        mine_ref[...] = first[...]
        other_ref[...] = second[...]

    @pl.when(core == 1)
    def _():
        mine_ref[...] = second[...]
        other_ref[...] = first[...]


def split_parts(value):
    high = value.astype(BF).astype(F32)
    return jnp.concatenate([high, value - high], axis=0).astype(BF)


def join_parts(value):
    return value[0:ALL] + value[ALL : 2 * ALL]


def mul_nt(left, right):
    return lax.dot_general(left, right, NT, preferred_element_type=F32)


def over_nodes(count, unroll, work):
    group = min(unroll, count)
    if count == group:
        work([jnp.int32(i) for i in range(count)])
        return

    def step(i, _):
        work([i * group + q for q in range(group)])
        return 0

    lax.fori_loop(0, count // group, step, 0)


def store_turned(flat, r, block):
    turned = block.T
    count = turned.shape[0] // 8
    width = turned.shape[1]
    rows = pl.ds(pl.multiple_of(r * 8, 8), 8)
    flat[0:count, rows] = turned[: count * 8].reshape(count, 8, width)
    rest = turned.shape[0] - count * 8
    flat[count, pl.ds(pl.multiple_of(r * 8, 8), rest)] = turned[count * 8 :]


def load_node(flat, node):
    return flat[node >> 3, pl.ds(node & 7, RANK, stride=8)].astype(BF)


def side_by_side(first, second):
    return jnp.concatenate([first, second], axis=1)


def doubled(pair):
    low = lax.broadcasted_iota(jnp.int32, pair.shape, 1) < RANK
    turned = pltpu.roll(pair, RANK, 1)
    return jnp.where(low, pair, turned), jnp.where(low, turned, pair)


def up_kernel(
    scale_ref, pack_ref, basis_hbm, raw_hbm, coef_ref, export_ref, move_ref,
    basis_ref, raw_ref, flat, pairs, sems,
):
    core = whole(scale_ref[4])
    leaves = basis_ref.shape[0]
    levels = leaves.bit_length() - 1
    chunks = 4
    per = leaves // chunks
    deep = RANK // chunks
    copies = fetch(
        [
            pair
            for c in range(chunks)
            for pair in (
                (
                    basis_hbm.at[pl.ds(core * leaves + c * per, per)],
                    basis_ref.at[c * per : (c + 1) * per],
                ),
                (
                    raw_hbm.at[:, c * deep : (c + 1) * deep],
                    raw_ref.at[:, c * deep : (c + 1) * deep],
                ),
            )
        ],
        sems,
    )

    def keep(parent, first, second):
        pair = side_by_side(first, second)
        pairs[parent] = split_parts(pair)
        one, two = doubled(pair)
        coef_ref[2 * parent + 1] = split_parts(one)
        coef_ref[2 * parent + 2] = split_parts(two)

    def leaf_step(it, _):
        outs = []
        for q in range(8):
            leaf = it * 8 + q
            outs.append(mul_nt(pack_ref[0:ALL, lanes(leaf)], basis_ref[leaf]))
        for q in range(8):
            r = it * 8 + q
            block = jnp.concatenate([raw_ref[0, r], raw_ref[1, r]], axis=0).astype(F32)
            store_turned(flat, r, block)
        for q in range(4):
            keep(leaves // 2 - 1 + it * 4 + q, outs[2 * q], outs[2 * q + 1])
        return 0

    for c in range(chunks):
        for copy in copies[2 * c : 2 * c + 2]:
            copy.wait()
        lax.fori_loop(c * per // 8, (c + 1) * per // 8, leaf_step, 0)
    root_move = load_node(flat, 0)
    move_ref[leaves - 1] = root_move
    for depth in range(levels - 1, 0, -1):
        first = 2**depth - 1
        above = 2 ** (depth - 1) - 1
        start = 2 ** (depth + 1) - 1 + core * 2**depth

        def work(nodes, first=first, above=above, start=start):
            outs = []
            for j in nodes:
                for c in range(2):
                    move = load_node(flat, start + 2 * j + c)
                    move_ref[first + 2 * j + c] = move
                    outs.append(mul_nt(pairs[first + 2 * j + c], move))
            for j, i in enumerate(nodes):
                keep(above + i, join_parts(outs[2 * j]), join_parts(outs[2 * j + 1]))

        over_nodes(2 ** (depth - 1), 8, work)
    move = load_node(flat, 1 + core)
    move_ref[0] = move
    crown = join_parts(mul_nt(pairs[0], move))
    crown = split_parts(side_by_side(crown, crown))
    coef_ref[0] = crown
    side = lax.broadcasted_iota(jnp.int32, crown.shape, 1) // RANK
    root = join_parts(mul_nt(jnp.where(side == core, crown.astype(F32), 0.0).astype(BF), root_move))
    export_ref[0] = split_parts(side_by_side(root, root))
    export_ref[1:EXPORT] = coef_ref[0 : EXPORT - 1]


def joint(first, second, third):
    return jnp.concatenate([first, second, third], axis=1)


def couple_kernel(
    scale_ref, partners_ref, coef_ref, raw_hbm, local_ref, tie_ref, raw_ref, wide, thin, sems,
):
    device, core = whole(scale_ref[3]), whole(scale_ref[4])
    levels = (raw_ref.shape[3] + 1).bit_length() - 2
    chunks = 4
    deep = RANK // chunks
    copies = fetch(
        [
            (raw_hbm.at[:, c * deep : (c + 1) * deep], raw_ref.at[:, c * deep : (c + 1) * deep])
            for c in range(chunks)
        ],
        sems,
    )
    low = lax.broadcasted_iota(jnp.int32, (2 * ALL, 2 * RANK), 1) < RANK

    def turn(i, _):
        for q in range(8):
            r = i * 8 + q
            block = jnp.concatenate([raw_ref[0, r], raw_ref[1, r]], axis=0).astype(F32)
            store_turned(wide, r, block)
            store_turned(thin, r, raw_ref[2, r].astype(F32))
        return 0

    for c in range(chunks):
        copies[c].wait()
        lax.fori_loop(c * deep // 8, (c + 1) * deep // 8, turn, 0)

    def tie(node):
        return jnp.concatenate([load_node(wide, node), load_node(thin, node)], axis=1)

    tie_ref[0] = tie(0)
    for depth in range(1, SPAN + 1):
        for i in range(2 ** (depth - 1)):
            tie_ref[2 ** (depth - 1) + i] = tie(2**depth - 1 + core * 2 ** (depth - 1) + i)
    for depth in range(SPAN + 1, levels + 1):
        half = 2 ** (depth - 1)
        above = half // 2 - 1
        start = 2**depth - 1 + core * half
        shift = half - 1 - device * 2**depth - core * half

        def work(nodes, above=above, start=start, shift=shift):
            outs = []
            for j in nodes:
                for c in range(2):
                    node = start + 2 * j + c
                    mates = [coef_ref[partners_ref[f, node] + shift] for f in range(3)]
                    left = jnp.concatenate(
                        [jnp.where(low, mates[0], mates[1]), mates[2][:, :RANK]], axis=1
                    )
                    outs.append(mul_nt(left, tie(node)))
            for j, i in enumerate(nodes):
                local_ref[above + i] = side_by_side(
                    join_parts(outs[2 * j]), join_parts(outs[2 * j + 1])
                )

        over_nodes(half // 2, 8, work)


def down_kernel(
    dev_levels, scale_ref, partners_ref, top_partners_ref, top_e, top_b, tie_ref,
    local_ref, move_ref, gather_ref, mine_ref, other_ref, down, tree,
):
    device, core = whole(scale_ref[3]), whole(scale_ref[4])
    leaves = mine_ref.shape[0]
    levels = leaves.bit_length() - 1
    count = 2**dev_levels

    def roots(nodes):
        for i in nodes:
            parts = join_parts(gather_ref[2 * i, 0].astype(F32)) + join_parts(
                gather_ref[2 * i + 1, 0].astype(F32)
            )
            tree[count + i] = split_parts(parts[:, :RANK])

    over_nodes(count, 8, roots)
    for level in range(dev_levels - 1, 1, -1):

        def work(nodes, level=level):
            outs = []
            for i in nodes:
                row = 2**level - 4 + i
                kids = [tree[2 ** (level + 1) + 2 * i + c] for c in range(2)]
                outs.append(mul_nt(kids[0], top_e[row, 0]) + mul_nt(kids[1], top_e[row, 1]))
            for i, out in zip(nodes, outs):
                tree[2**level + i] = split_parts(join_parts(out))

        over_nodes(2**level, 4, work)

    mates = [tree[count + partners_ref[f, 0]] for f in range(3)]
    shallow = [join_parts(mul_nt(joint(*mates), tie_ref[0]))]
    for depth in range(1, SPAN + 1):
        half = 2 ** (depth - 1)
        for i in range(half):
            node = 2**depth - 1 + core * half + i
            picks = []
            for f in range(3):
                mate = partners_ref[f, node]
                picks.append(
                    gather_ref[mate >> (depth - 1), half + (mate & (half - 1))][:, :RANK]
                )
            shallow.append(join_parts(mul_nt(joint(*picks), tie_ref[half + i])))

    pushed = jnp.zeros((ALL, RANK), F32)
    for level in range(2, dev_levels):
        node = device >> (dev_levels - level)
        row = 2**level - 4 + node
        side = device >> (dev_levels - level - 1) & 1
        parts = sum(
            mul_nt(tree[2**level + top_partners_ref[row, f]], top_b[row, f]) for f in range(3)
        )
        here = split_parts(join_parts(parts) + pushed)
        pushed = join_parts(jnp.dot(here, top_e[row, side], preferred_element_type=F32))

    root = split_parts(shallow[0] + pushed)
    both = join_parts(jnp.dot(root, move_ref[leaves - 1], preferred_element_type=F32))
    down[0] = split_parts(shallow[1] + jnp.where(core == 0, both[:, :RANK], both[:, RANK:]))
    for depth in range(levels):
        first = 2**depth - 1

        def work(nodes, depth=depth, first=first):
            outs = [
                jnp.dot(down[first + i], move_ref[first + i], preferred_element_type=F32)
                for i in nodes
            ]
            for i, out in zip(nodes, outs):
                node = first + i
                if depth + 2 <= SPAN:
                    kid = 2 ** (depth + 1) + 2 * i
                    base = side_by_side(shallow[kid], shallow[kid + 1])
                else:
                    base = local_ref[node]
                pair = base + join_parts(out)
                if depth == levels - 1:
                    for c in range(2):
                        value = pair[:, c * RANK : (c + 1) * RANK]
                        one, two = value[:PART], value[PART:]
                        mine_ref[2 * i + c] = jnp.where(core == 0, one, two).astype(BF)
                        other_ref[2 * i + c] = jnp.where(core == 0, two, one).astype(BF)
                else:
                    down[2 * node + 1] = split_parts(pair[:, :RANK])
                    down[2 * node + 2] = split_parts(pair[:, RANK:])

        if depth < SPAN:
            work(list(range(2**depth)))
        else:
            over_nodes(2**depth, 8, work)


def final_kernel(
    scale_ref, mine_ref, got_ref, basis, noise, vec, near, swap, out_hbm, out, sems
):
    core = whole(scale_ref[4])
    leaves = mine_ref.shape[0]
    chunks = 2
    per = leaves // chunks
    wide = per * LEAF
    sends = []
    for part, low_ref in enumerate((mine_ref, got_ref)):
        base = jnp.where(core == part, 0, leaves)
        for c in range(chunks):

            def last(nodes, c=c, low_ref=low_ref, base=base):
                rows = [c * per + i for i in nodes]
                fars = [
                    jnp.dot(low_ref[n], basis[base + n], preferred_element_type=F32)
                    for n in rows
                ]
                for n, far in zip(rows, fars):
                    here = lanes(base + n)
                    total = near[:, here] + swap[:, here]
                    out[:, here] = total + noise[:, here] * vec[:, here].astype(F32) + far

            over_nodes(per, 8, last)
            piece = pl.ds(pl.multiple_of((base + c * per) * LEAF, wide), wide)
            send = pltpu.make_async_copy(
                out.at[:, piece], out_hbm.at[:, piece], sems.at[part * chunks + c]
            )
            send.start()
            sends.append(send)
    for send in sends:
        send.wait()


def body(
    points, inv_scale, noise, vectors, leaf_basis, local_transfer, top_transfer,
    local_coupling, top_coupling, local_partners, top_partners, near_offsets, near_cols,
):
    subs = lax.axis_size("sub")
    count = lax.axis_size("leaf") * subs
    dev_levels = count.bit_length() - 1
    device = lax.axis_index("leaf") * subs + lax.axis_index("sub")
    core = lax.axis_index("vec")
    scale = jnp.concatenate([inv_scale, jnp.stack([device, core]).astype(F32)])
    size = vectors.shape[1]
    leaves = near_offsets.shape[0]
    slots = near_cols.shape[0]
    half = size // 2
    sds = jax.ShapeDtypeStruct
    scratch_blocks = [
        VMEM((PAIR, LEAF, LEAF), F32), VMEM((PAIR, LEAF, LEAF), F32),
        VMEM((PAIR, LEAF, LEAF), BF), VMEM((PAIR, LEAF, LEAF), BF),
    ]

    got = lax.ppermute(vectors, "vec", [(0, 1), (1, 0)])

    pack = pl.pallas_call(
        pack_kernel,
        name="pack",
        out_shape=sds((24, half), BF),
        in_specs=[sspec(), hspec(), hspec(), hspec()],
        out_specs=vspec(),
        scratch_shapes=[
            VMEM((3, half), F32), VMEM((PART, half), BF), VMEM((PART, half), BF),
            pltpu.SemaphoreType.DMA((3,)),
        ],
        compiler_params=params(16),
    )(scale, points, vectors, got)
    axes = ("leaf", "sub")
    left = lax.ppermute(pack, axes, [(i, i + 1) for i in range(count - 1)])
    right = lax.ppermute(pack, axes, [(i + 1, i) for i in range(count - 1)])

    moves_raw = jnp.transpose(local_transfer, (1, 2, 3, 0))
    part = leaves // 2
    coef, export, moves = pl.pallas_call(
        up_kernel,
        name="up",
        out_shape=(
            sds((2 * part - 1, 2 * ALL, 2 * RANK), BF), sds((EXPORT, 2 * ALL, 2 * RANK), BF),
            sds((part, RANK, 2 * RANK), BF),
        ),
        in_specs=[sspec(), vspec(), hspec(), hspec()],
        out_specs=(vspec(),) * 3,
        scratch_shapes=[
            VMEM((part, RANK, LEAF), BF), VMEM(moves_raw.shape, BF),
            VMEM((leaves // 8, RANK * 8, 2 * RANK), F32),
            VMEM((part - 1, 2 * ALL, 2 * RANK), BF), pltpu.SemaphoreType.DMA((8,)),
        ],
        compiler_params=params(28),
        cost_estimate=pl.CostEstimate(flops=8 * 10**9, bytes_accessed=8 << 20, transcendentals=0),
    )(scale, pack, leaf_basis, moves_raw)
    gathered = lax.all_gather(export, ("leaf", "sub", "vec"))
    pack, _ = lax.optimization_barrier((pack, export))
    first, second, row_feat, far_list, far_count = pl.pallas_call(
        near_local_kernel,
        name="near_local",
        out_shape=(
            sds((PART, size), F32), sds((PART, size), F32), sds((leaves, 32, LEAF), BF),
            sds((slots + PAD,), jnp.int32), sds((1,), jnp.int32),
        ),
        in_specs=[sspec()] * 3 + [vspec()] * 2,
        out_specs=(vspec(), vspec(), vspec(), sspec(), sspec()),
        scratch_shapes=[
            VMEM((leaves // 2 + 1, LEAF, 32), BF), VMEM((leaves // 2 + 1, 16, LEAF), BF),
            *scratch_blocks, SMEM((slots + PAD,), jnp.int32),
        ],
        compiler_params=params(28),
        cost_estimate=pl.CostEstimate(
            flops=36 * 10**9, bytes_accessed=8 << 20, transcendentals=190 * 2**17
        ),
    )(scale, near_offsets, near_cols, points, pack)

    mine, other = pl.pallas_call(
        near_halo_kernel,
        name="near_halo",
        out_shape=(sds((PART, size), F32), sds((PART, size), F32)),
        in_specs=[sspec()] * 3 + [vspec()] * 5,
        out_specs=(vspec(), vspec()),
        scratch_shapes=[
            VMEM((PART, size), F32), VMEM((PART, size), F32),
            VMEM((leaves + 1, LEAF, 32), BF), VMEM((leaves + 1, 16, LEAF), BF),
            *scratch_blocks,
        ],
        compiler_params=params(36),
        cost_estimate=pl.CostEstimate(
            flops=4 * 10**9, bytes_accessed=8 << 20, transcendentals=60 * 2**17
        ),
    )(scale, far_list, far_count, row_feat, left, right, first, second)
    swapped = lax.ppermute(other, "vec", [(0, 1), (1, 0)])

    _, coef_late = lax.optimization_barrier((mine, coef))
    ties_raw = jnp.transpose(local_coupling, (1, 2, 3, 0))
    mates = jnp.transpose(local_partners)
    local, ties = pl.pallas_call(
        couple_kernel,
        name="couple",
        out_shape=(
            sds((part - 1, ALL, 2 * RANK), F32), sds((EXPORT, RANK, 3 * RANK), BF),
        ),
        in_specs=[sspec()] * 2 + [vspec(), hspec()],
        out_specs=(vspec(),) * 2,
        scratch_shapes=[
            VMEM(ties_raw.shape, BF),
            VMEM((leaves // 4, RANK * 8, 2 * RANK), F32),
            VMEM((leaves // 4, RANK * 8, RANK), F32), pltpu.SemaphoreType.DMA((4,)),
        ],
        compiler_params=params(36),
        cost_estimate=pl.CostEstimate(flops=9 * 10**9, bytes_accessed=8 << 20, transcendentals=0),
    )(scale, mates, coef_late, ties_raw)

    low_mine, low_other = pl.pallas_call(
        functools.partial(down_kernel, dev_levels),
        name="down",
        out_shape=(sds((part, PART, RANK), BF), sds((part, PART, RANK), BF)),
        in_specs=[sspec()] * 3 + [vspec()] * 6,
        out_specs=(vspec(), vspec()),
        scratch_shapes=[
            VMEM((part - 1, 2 * ALL, RANK), BF), VMEM((2 * count, 2 * ALL, RANK), BF),
        ],
        compiler_params=params(24),
        cost_estimate=pl.CostEstimate(flops=4 * 10**9, bytes_accessed=4 << 20, transcendentals=0),
    )(scale, mates, top_partners, top_transfer, top_coupling, ties, local, moves, gathered)
    low_got = lax.ppermute(low_other, "vec", [(0, 1), (1, 0)])

    return pl.pallas_call(
        final_kernel,
        name="final",
        out_shape=sds((PART, size), F32),
        in_specs=[sspec()] + [vspec()] * 7,
        out_specs=hspec(),
        scratch_shapes=[VMEM((PART, size), F32), pltpu.SemaphoreType.DMA((4,))],
        compiler_params=params(16),
        cost_estimate=pl.CostEstimate(flops=2 * 10**9, bytes_accessed=4 << 20, transcendentals=0),
    )(scale, low_mine, low_got, leaf_basis, noise.reshape(1, size), vectors, mine, swapped)


def solution(mesh):
    return jax.shard_map(
        body,
        mesh=mesh,
        in_specs=(
            P("groups", ("leaf", "sub")),
            P("groups"),
            P(("groups", "leaf", "sub")),
            P(("groups", "vec"), ("leaf", "sub")),
            P(("groups", "leaf", "sub"), None, None),
            P(("groups", "leaf", "sub"), None, None, None),
            P("groups", None, None, None),
            P(("groups", "leaf", "sub"), None, None, None),
            P("groups", None, None, None),
            P(("groups", "leaf", "sub"), None),
            P("groups", None),
            P(("groups", "leaf", "sub")),
            P(("groups", "leaf", "sub")),
        ),
        out_specs=P(("groups", "vec"), ("leaf", "sub")),
        check_vma=False,
    )
```

```python
import functools
import math

import jax
import jax.numpy as jnp
from jax import lax
from jax.experimental import pallas as pl
from jax.experimental.pallas import tpu as pltpu
from jax.sharding import PartitionSpec as P

BF = jnp.bfloat16
F32 = jnp.float32
LEAF = 256
RANK = 64
SPAN = 3
PART = 8
ALL = 2 * PART
EXPORT = 2**SPAN
NEG_LOG2E = -1.0 / math.log(2.0)
ROOT3 = math.sqrt(3.0)
TINY = 1e-12
PAIR = 2
PAD = 16
TURNS = 2
CODE_BITS = 10
CODE = 2**CODE_BITS
VMEM = pltpu.VMEM
SMEM = pltpu.SMEM
NT = (((1,), (1,)), ((), ()))


def vspec():
    return pl.BlockSpec(memory_space=pltpu.VMEM)


def sspec():
    return pl.BlockSpec(memory_space=pltpu.SMEM)


def hspec():
    return pl.BlockSpec(memory_space=pltpu.HBM)


def fetch(pairs, sems):
    copies = [
        pltpu.make_async_copy(source, target, sems.at[i])
        for i, (source, target) in enumerate(pairs)
    ]
    for copy in copies:
        copy.start()
    return copies


def params(mib):
    return pltpu.CompilerParams(vmem_limit_bytes=mib << 20)


def lanes(index):
    return pl.ds(pl.multiple_of(index * LEAF, LEAF), LEAF)


def whole(scalar):
    return scalar.astype(jnp.int32)


def coordinate_rows(raw, scale_ref):
    width = raw.shape[1]
    row = lax.broadcasted_iota(jnp.int32, (8, width), 0)
    scale = jnp.where(
        row == 0, scale_ref[0], jnp.where(row == 1, scale_ref[1], scale_ref[2])
    )
    full = jnp.concatenate([raw, jnp.zeros((5, width), F32)], axis=0)
    scaled = (full - 0.5) * (scale * ROOT3)
    scaled = jnp.where(row < 3, scaled, 0.0)
    high = scaled.astype(BF).astype(F32)
    rest = (scaled - high).astype(BF).astype(F32)
    return high + pltpu.roll(rest, 4, 0)


def norm_parts(rows):
    swapped = pltpu.roll(rows, 4, 0)
    norm = jnp.sum(rows * (rows + swapped), axis=0, keepdims=True)
    high = norm.astype(BF).astype(F32)
    rest = norm - high
    mid = rest.astype(BF).astype(F32)
    return swapped, high, mid, rest - mid


def row_features(rows):
    swapped, high, mid, low = norm_parts(rows)
    row = lax.broadcasted_iota(jnp.int32, rows.shape, 0)
    tail = jnp.where(
        row < 3,
        1.0,
        jnp.where(row == 3, high, jnp.where(row == 4, mid, jnp.where(row == 5, low, 0.0))),
    )
    return jnp.concatenate([rows, swapped, tail, jnp.zeros_like(rows)], axis=0).astype(BF)


def col_features(rows):
    _, high, mid, low = norm_parts(rows)
    row = lax.broadcasted_iota(jnp.int32, rows.shape, 0)
    tail = jnp.where(
        row == 0,
        high,
        jnp.where(row == 1, mid, jnp.where(row == 2, low, jnp.where(row < 6, 1.0, 0.0))),
    )
    both = -2.0 * rows
    return jnp.concatenate([both, both, tail, jnp.zeros_like(rows)], axis=0).T.astype(BF)


def matern(squared):
    squared = jnp.maximum(squared, TINY)
    dist = squared * lax.rsqrt(squared)
    return ((1.0 + dist) * jnp.exp2(dist * NEG_LOG2E)).astype(BF)


def pack_kernel(scale_ref, points_hbm, vec_hbm, got_hbm, out_ref, points, mine, got, sems):
    half = out_ref.shape[1]
    core = whole(scale_ref[4])
    there = pl.ds(pl.multiple_of(core * half, half), half)
    copies = fetch(
        [
            (points_hbm.at[:, there], points), (vec_hbm.at[:, there], mine),
            (got_hbm.at[:, there], got),
        ],
        sems,
    )
    for copy in copies:
        copy.wait()

    def step(i, _):
        here = pl.ds(pl.multiple_of(i * 2048, 2048), 2048)
        rows = coordinate_rows(points[:, here], scale_ref)
        one, two = mine[:, here].astype(F32), got[:, here].astype(F32)
        first, second = jnp.where(core == 0, one, two), jnp.where(core == 0, two, one)
        out_ref[:, here] = jnp.concatenate([first, second, rows], axis=0).astype(BF)
        return 0

    lax.fori_loop(0, half // 2048, step, 0)


def block_loop(count, place, list_ref, row_ref, col_ref, val_ref, sums, s0, s1, k0, k1):
    def accumulate(first, kern):
        for q in range(PAIR):
            code = list_ref[first + q]
            here = lanes(code >> CODE_BITS)
            part = jnp.dot(
                val_ref[place(code & (CODE - 1))], kern[q], preferred_element_type=F32
            )
            sums[0][:, here] += part[:PART]
            sums[1][:, here] += part[PART:]

    def distance(first, out):
        for q in range(PAIR):
            code = list_ref[first + q]
            out[q] = jnp.dot(
                col_ref[place(code & (CODE - 1))],
                row_ref[code >> CODE_BITS],
                preferred_element_type=F32,
            )

    def evaluate(squared, kern):
        for q in range(PAIR):
            kern[q] = matern(squared[q])

    k1[...] = jnp.zeros_like(k1)
    distance(0, s0)

    def step(it, _):
        for turn in range(TURNS):
            first = (it * TURNS + turn) * 2 * PAIR
            accumulate(jnp.maximum(first - PAIR, 0), k1)
            distance(first + PAIR, s1)
            evaluate(s0, k0)
            accumulate(first, k0)
            distance(first + 2 * PAIR, s0)
            evaluate(s1, k1)
        return 0

    turns = (count + TURNS * 2 * PAIR - 1) // (TURNS * 2 * PAIR)
    lax.fori_loop(0, turns, step, 0)
    accumulate(jnp.maximum(turns * TURNS * 2 * PAIR - PAIR, 0), k1)


def load_columns(pack_ref, base, count, col_ref, val_ref):
    def step(i, _):
        for q in range(4):
            leaf = i * 4 + q
            val_ref[base + leaf] = pack_ref[0:16, lanes(leaf)]
            col_ref[base + leaf] = col_features(pack_ref[16:24, lanes(leaf)].astype(F32))
        return 0

    lax.fori_loop(0, count // 4, step, 0)


def near_local_kernel(
    scale_ref, offs_ref, cols_ref, points_ref, pack_ref,
    mine_ref, other_ref, row_ref, far_list, far_count,
    col_ref, val_ref, s0, s1, k0, k1, own_list,
):
    device, half_id = whole(scale_ref[3]), whole(scale_ref[4])
    leaves = offs_ref.shape[0]
    half = leaves // 2
    slots = cols_ref.shape[0]
    each = slots // leaves

    far_base = device * leaves - leaves + half_id * half
    half_bits = half.bit_length() - 1

    def rows_step(i, carry):
        row, code, own, far = carry
        for q in range(2):
            leaf = i * 2 + q
            row_ref[leaf] = row_features(coordinate_rows(points_ref[:, lanes(leaf)], scale_ref))
            mine_ref[:, lanes(leaf)] = jnp.zeros((PART, LEAF), F32)
            other_ref[:, lanes(leaf)] = jnp.zeros((PART, LEAF), F32)
            for w in range(each):
                slot = leaf * each + w
                begins = offs_ref[jnp.minimum(row + 1, leaves - 1)] == slot
                row = jnp.where(begins, row + 1, row)
                code = jnp.where(begins, code + CODE, code)
                place = cols_ref[slot] - far_base
                own_list[own] = code + (place - leaves)
                far_list[far] = code + place
                block = place >> half_bits
                own = jnp.where(block == 2, own + 1, own)
                far = jnp.where((block & 3) == 0, far + 1, far)
        return row, code, own, far

    zero = jnp.int32(0)
    _, _, own, far = lax.fori_loop(0, leaves // 2, rows_step, (zero, zero, zero, zero))
    for q in range(PAD):
        own_list[own + q] = half
        far_list[far + q] = 8 * half
    far_count[0] = far
    load_columns(pack_ref, 0, half, col_ref, val_ref)
    val_ref[half] = jnp.zeros((16, LEAF), BF)
    col_ref[half] = jnp.zeros(col_ref.shape[1:], BF)
    sums = (mine_ref, other_ref)
    block_loop(own, lambda c: c, own_list, row_ref, col_ref, val_ref, sums, s0, s1, k0, k1)


def near_halo_kernel(
    scale_ref, far_list, far_count, row_ref, left_ref, right_ref, first_in, second_in,
    mine_ref, other_ref,
    first, second, col_ref, val_ref, s0, s1, k0, k1,
):
    core = whole(scale_ref[4])
    half = left_ref.shape[1] // LEAF
    bits = half.bit_length() - 1
    count = far_count[0]

    def place(code):
        return (code & (half - 1)) | ((code >> (bits + 2)) << bits)

    def load(i, _):
        for q in range(4):
            code = far_list[i * 4 + q] & (CODE - 1)
            here = lanes(code & (half - 1))
            after = code >= 4 * half
            values = jnp.where(after, right_ref[0:16, here], left_ref[0:16, here])
            rows = jnp.where(after, right_ref[16:24, here], left_ref[16:24, here])
            val_ref[place(code)] = values
            col_ref[place(code)] = col_features(rows.astype(F32))
        return 0

    first[...] = first_in[...]
    second[...] = second_in[...]
    lax.fori_loop(0, (count + 3) // 4, load, 0)
    val_ref[2 * half] = jnp.zeros((16, LEAF), BF)
    col_ref[2 * half] = jnp.zeros(col_ref.shape[1:], BF)
    sums = (first, second)
    block_loop(count, place, far_list, row_ref, col_ref, val_ref, sums, s0, s1, k0, k1)

    @pl.when(core == 0)
    def _():
        mine_ref[...] = first[...]
        other_ref[...] = second[...]

    @pl.when(core == 1)
    def _():
        mine_ref[...] = second[...]
        other_ref[...] = first[...]


def split_parts(value):
    high = value.astype(BF).astype(F32)
    return jnp.concatenate([high, value - high], axis=0).astype(BF)


def join_parts(value):
    return value[0:ALL] + value[ALL : 2 * ALL]


def mul_nt(left, right):
    return lax.dot_general(left, right, NT, preferred_element_type=F32)


def over_nodes(count, unroll, work):
    group = min(unroll, count)
    if count == group:
        work([jnp.int32(i) for i in range(count)])
        return

    def step(i, _):
        work([i * group + q for q in range(group)])
        return 0

    lax.fori_loop(0, count // group, step, 0)


def store_turned(flat, r, block):
    turned = block.T
    count = turned.shape[0] // 8
    width = turned.shape[1]
    rows = pl.ds(pl.multiple_of(r * 8, 8), 8)
    flat[0:count, rows] = turned[: count * 8].reshape(count, 8, width)
    rest = turned.shape[0] - count * 8
    flat[count, pl.ds(pl.multiple_of(r * 8, 8), rest)] = turned[count * 8 :]


def load_node(flat, node):
    return flat[node >> 3, pl.ds(node & 7, RANK, stride=8)].astype(BF)


def side_by_side(first, second):
    return jnp.concatenate([first, second], axis=1)


def doubled(pair):
    low = lax.broadcasted_iota(jnp.int32, pair.shape, 1) < RANK
    turned = pltpu.roll(pair, RANK, 1)
    return jnp.where(low, pair, turned), jnp.where(low, turned, pair)


def up_kernel(
    scale_ref, pack_ref, basis_hbm, raw_hbm, coef_ref, export_ref, move_ref,
    basis_ref, raw_ref, flat, pairs, sems,
):
    core = whole(scale_ref[4])
    leaves = basis_ref.shape[0]
    levels = leaves.bit_length() - 1
    chunks = 4
    per = leaves // chunks
    deep = RANK // chunks
    copies = fetch(
        [
            pair
            for c in range(chunks)
            for pair in (
                (
                    basis_hbm.at[pl.ds(core * leaves + c * per, per)],
                    basis_ref.at[c * per : (c + 1) * per],
                ),
                (
                    raw_hbm.at[:, c * deep : (c + 1) * deep],
                    raw_ref.at[:, c * deep : (c + 1) * deep],
                ),
            )
        ],
        sems,
    )

    def keep(parent, first, second):
        pair = side_by_side(first, second)
        pairs[parent] = split_parts(pair)
        one, two = doubled(pair)
        coef_ref[2 * parent + 1] = split_parts(one)
        coef_ref[2 * parent + 2] = split_parts(two)

    def leaf_step(it, _):
        outs = []
        for q in range(8):
            leaf = it * 8 + q
            outs.append(mul_nt(pack_ref[0:ALL, lanes(leaf)], basis_ref[leaf]))
        for q in range(8):
            r = it * 8 + q
            block = jnp.concatenate([raw_ref[0, r], raw_ref[1, r]], axis=0).astype(F32)
            store_turned(flat, r, block)
        for q in range(4):
            keep(leaves // 2 - 1 + it * 4 + q, outs[2 * q], outs[2 * q + 1])
        return 0

    for c in range(chunks):
        for copy in copies[2 * c : 2 * c + 2]:
            copy.wait()
        lax.fori_loop(c * per // 8, (c + 1) * per // 8, leaf_step, 0)
    root_move = load_node(flat, 0)
    move_ref[leaves - 1] = root_move
    for depth in range(levels - 1, 0, -1):
        first = 2**depth - 1
        above = 2 ** (depth - 1) - 1
        start = 2 ** (depth + 1) - 1 + core * 2**depth

        def work(nodes, first=first, above=above, start=start):
            outs = []
            for j in nodes:
                for c in range(2):
                    move = load_node(flat, start + 2 * j + c)
                    move_ref[first + 2 * j + c] = move
                    outs.append(mul_nt(pairs[first + 2 * j + c], move))
            for j, i in enumerate(nodes):
                keep(above + i, join_parts(outs[2 * j]), join_parts(outs[2 * j + 1]))

        over_nodes(2 ** (depth - 1), 8, work)
    move = load_node(flat, 1 + core)
    move_ref[0] = move
    crown = join_parts(mul_nt(pairs[0], move))
    crown = split_parts(side_by_side(crown, crown))
    coef_ref[0] = crown
    side = lax.broadcasted_iota(jnp.int32, crown.shape, 1) // RANK
    root = join_parts(mul_nt(jnp.where(side == core, crown.astype(F32), 0.0).astype(BF), root_move))
    export_ref[0] = split_parts(side_by_side(root, root))
    export_ref[1:EXPORT] = coef_ref[0 : EXPORT - 1]


def joint(first, second, third):
    return jnp.concatenate([first, second, third], axis=1)


def couple_kernel(
    scale_ref, partners_ref, coef_ref, raw_hbm, local_ref, tie_ref, raw_ref, wide, thin, sems,
):
    device, core = whole(scale_ref[3]), whole(scale_ref[4])
    levels = (raw_ref.shape[3] + 1).bit_length() - 2
    chunks = 4
    deep = RANK // chunks
    copies = fetch(
        [
            (raw_hbm.at[:, c * deep : (c + 1) * deep], raw_ref.at[:, c * deep : (c + 1) * deep])
            for c in range(chunks)
        ],
        sems,
    )
    low = lax.broadcasted_iota(jnp.int32, (2 * ALL, 2 * RANK), 1) < RANK

    def turn(i, _):
        for q in range(8):
            r = i * 8 + q
            block = jnp.concatenate([raw_ref[0, r], raw_ref[1, r]], axis=0).astype(F32)
            store_turned(wide, r, block)
            store_turned(thin, r, raw_ref[2, r].astype(F32))
        return 0

    for c in range(chunks):
        copies[c].wait()
        lax.fori_loop(c * deep // 8, (c + 1) * deep // 8, turn, 0)

    def tie(node):
        return jnp.concatenate([load_node(wide, node), load_node(thin, node)], axis=1)

    tie_ref[0] = tie(0)
    for depth in range(1, SPAN + 1):
        for i in range(2 ** (depth - 1)):
            tie_ref[2 ** (depth - 1) + i] = tie(2**depth - 1 + core * 2 ** (depth - 1) + i)
    for depth in range(SPAN + 1, levels + 1):
        half = 2 ** (depth - 1)
        above = half // 2 - 1
        start = 2**depth - 1 + core * half
        shift = half - 1 - device * 2**depth - core * half

        def work(nodes, above=above, start=start, shift=shift):
            outs = []
            for j in nodes:
                for c in range(2):
                    node = start + 2 * j + c
                    mates = [coef_ref[partners_ref[f, node] + shift] for f in range(3)]
                    left = jnp.concatenate(
                        [jnp.where(low, mates[0], mates[1]), mates[2][:, :RANK]], axis=1
                    )
                    outs.append(mul_nt(left, tie(node)))
            for j, i in enumerate(nodes):
                local_ref[above + i] = side_by_side(
                    join_parts(outs[2 * j]), join_parts(outs[2 * j + 1])
                )

        over_nodes(half // 2, 8, work)


def down_kernel(
    dev_levels, scale_ref, partners_ref, top_partners_ref, top_e, top_b, tie_ref,
    local_ref, move_ref, own_ref, core_ref, next_ref, far_refs, tops_ref, mine_ref, other_ref,
    gather_ref, down, tree,
):
    device, core = whole(scale_ref[3]), whole(scale_ref[4])
    self_id = 2 * device + core
    gather_ref[0] = own_ref[...]
    gather_ref[1] = core_ref[...]
    gather_ref[2:4, 0:4] = next_ref[...]
    for i, far_ref in enumerate(far_refs):
        gather_ref[4 * i + 4 : 4 * i + 8, 0:2] = far_ref[...]
    root_ref = gather_ref if dev_levels == SPAN else tops_ref
    leaves = mine_ref.shape[0]
    levels = leaves.bit_length() - 1
    count = 2**dev_levels

    def roots(nodes):
        for i in nodes:
            parts = join_parts(root_ref[(2 * i) ^ self_id, 0].astype(F32)) + join_parts(
                root_ref[(2 * i + 1) ^ self_id, 0].astype(F32)
            )
            tree[count + i] = split_parts(parts[:, :RANK])

    over_nodes(count, 8, roots)
    for level in range(dev_levels - 1, 1, -1):

        def work(nodes, level=level):
            outs = []
            for i in nodes:
                row = 2**level - 4 + i
                kids = [tree[2 ** (level + 1) + 2 * i + c] for c in range(2)]
                outs.append(mul_nt(kids[0], top_e[row, 0]) + mul_nt(kids[1], top_e[row, 1]))
            for i, out in zip(nodes, outs):
                tree[2**level + i] = split_parts(join_parts(out))

        over_nodes(2**level, 4, work)

    mates = [tree[count + partners_ref[f, 0]] for f in range(3)]
    shallow = [join_parts(mul_nt(joint(*mates), tie_ref[0]))]
    for depth in range(1, SPAN + 1):
        half = 2 ** (depth - 1)
        for i in range(half):
            node = 2**depth - 1 + core * half + i
            picks = []
            for f in range(3):
                mate = partners_ref[f, node]
                at = ((mate >> (depth - 1)) ^ self_id) & (2 * 2**SPAN - 1)
                picks.append(gather_ref[at, half + (mate & (half - 1))][:, :RANK])
            shallow.append(join_parts(mul_nt(joint(*picks), tie_ref[half + i])))

    pushed = jnp.zeros((ALL, RANK), F32)
    for level in range(2, dev_levels):
        node = device >> (dev_levels - level)
        row = 2**level - 4 + node
        side = device >> (dev_levels - level - 1) & 1
        parts = sum(
            mul_nt(tree[2**level + top_partners_ref[row, f]], top_b[row, f]) for f in range(3)
        )
        here = split_parts(join_parts(parts) + pushed)
        pushed = join_parts(jnp.dot(here, top_e[row, side], preferred_element_type=F32))

    root = split_parts(shallow[0] + pushed)
    both = join_parts(jnp.dot(root, move_ref[leaves - 1], preferred_element_type=F32))
    down[0] = split_parts(shallow[1] + jnp.where(core == 0, both[:, :RANK], both[:, RANK:]))
    for depth in range(levels):
        first = 2**depth - 1

        def work(nodes, depth=depth, first=first):
            outs = [
                jnp.dot(down[first + i], move_ref[first + i], preferred_element_type=F32)
                for i in nodes
            ]
            for i, out in zip(nodes, outs):
                node = first + i
                if depth + 2 <= SPAN:
                    kid = 2 ** (depth + 1) + 2 * i
                    base = side_by_side(shallow[kid], shallow[kid + 1])
                else:
                    base = local_ref[node]
                pair = base + join_parts(out)
                if depth == levels - 1:
                    for c in range(2):
                        value = pair[:, c * RANK : (c + 1) * RANK]
                        one, two = value[:PART], value[PART:]
                        mine_ref[2 * i + c] = jnp.where(core == 0, one, two).astype(BF)
                        other_ref[2 * i + c] = jnp.where(core == 0, two, one).astype(BF)
                else:
                    down[2 * node + 1] = split_parts(pair[:, :RANK])
                    down[2 * node + 2] = split_parts(pair[:, RANK:])

        if depth < SPAN:
            work(list(range(2**depth)))
        else:
            over_nodes(2**depth, 8, work)


def final_kernel(
    scale_ref, mine_ref, got_ref, basis, noise, vec, near, swap, out_hbm, out, sems
):
    core = whole(scale_ref[4])
    leaves = mine_ref.shape[0]
    chunks = 2
    per = leaves // chunks
    wide = per * LEAF
    sends = []
    for part, low_ref in enumerate((mine_ref, got_ref)):
        base = jnp.where(core == part, 0, leaves)
        for c in range(chunks):

            def last(nodes, c=c, low_ref=low_ref, base=base):
                rows = [c * per + i for i in nodes]
                fars = [
                    jnp.dot(low_ref[n], basis[base + n], preferred_element_type=F32)
                    for n in rows
                ]
                for n, far in zip(rows, fars):
                    here = lanes(base + n)
                    total = near[:, here] + swap[:, here]
                    out[:, here] = total + noise[:, here] * vec[:, here].astype(F32) + far

            over_nodes(per, 8, last)
            piece = pl.ds(pl.multiple_of((base + c * per) * LEAF, wide), wide)
            send = pltpu.make_async_copy(
                out.at[:, piece], out_hbm.at[:, piece], sems.at[part * chunks + c]
            )
            send.start()
            sends.append(send)
    for send in sends:
        send.wait()


def swap_mask(value, mask):
    total = lax.axis_size("leaf") * lax.axis_size("sub")
    return lax.ppermute(value, ("leaf", "sub"), [(i, i ^ mask) for i in range(total)])


def after(value, anchor):
    return lax.optimization_barrier((value, anchor))[0]


def body(
    points, inv_scale, noise, vectors, leaf_basis, local_transfer, top_transfer,
    local_coupling, top_coupling, local_partners, top_partners, near_offsets, near_cols,
):
    subs = lax.axis_size("sub")
    count = lax.axis_size("leaf") * subs
    dev_levels = count.bit_length() - 1
    device = lax.axis_index("leaf") * subs + lax.axis_index("sub")
    core = lax.axis_index("vec")
    scale = jnp.concatenate([inv_scale, jnp.stack([device, core]).astype(F32)])
    size = vectors.shape[1]
    leaves = near_offsets.shape[0]
    slots = near_cols.shape[0]
    half = size // 2
    sds = jax.ShapeDtypeStruct
    scratch_blocks = [
        VMEM((PAIR, LEAF, LEAF), F32), VMEM((PAIR, LEAF, LEAF), F32),
        VMEM((PAIR, LEAF, LEAF), BF), VMEM((PAIR, LEAF, LEAF), BF),
    ]

    got = lax.ppermute(vectors, "vec", [(0, 1), (1, 0)])

    pack = pl.pallas_call(
        pack_kernel,
        name="pack",
        out_shape=sds((24, half), BF),
        in_specs=[sspec(), hspec(), hspec(), hspec()],
        out_specs=vspec(),
        scratch_shapes=[
            VMEM((3, half), F32), VMEM((PART, half), BF), VMEM((PART, half), BF),
            pltpu.SemaphoreType.DMA((3,)),
        ],
        compiler_params=params(16),
    )(scale, points, vectors, got)
    axes = ("leaf", "sub")
    left = lax.ppermute(pack, axes, [(i, i + 1) for i in range(count - 1)])
    right = lax.ppermute(pack, axes, [(i + 1, i) for i in range(count - 1)])

    moves_raw = jnp.transpose(local_transfer, (1, 2, 3, 0))
    part = leaves // 2
    coef, export, moves = pl.pallas_call(
        up_kernel,
        name="up",
        out_shape=(
            sds((2 * part - 1, 2 * ALL, 2 * RANK), BF), sds((EXPORT, 2 * ALL, 2 * RANK), BF),
            sds((part, RANK, 2 * RANK), BF),
        ),
        in_specs=[sspec(), vspec(), hspec(), hspec()],
        out_specs=(vspec(),) * 3,
        scratch_shapes=[
            VMEM((part, RANK, LEAF), BF), VMEM(moves_raw.shape, BF),
            VMEM((leaves // 8, RANK * 8, 2 * RANK), F32),
            VMEM((part - 1, 2 * ALL, 2 * RANK), BF), pltpu.SemaphoreType.DMA((8,)),
        ],
        compiler_params=params(28),
        cost_estimate=pl.CostEstimate(flops=8 * 10**9, bytes_accessed=8 << 20, transcendentals=0),
    )(scale, pack, leaf_basis, moves_raw)
    from_core = lax.ppermute(export, "vec", [(0, 1), (1, 0)])
    pack, _ = lax.optimization_barrier((pack, export))
    first, second, row_feat, far_list, far_count = pl.pallas_call(
        near_local_kernel,
        name="near_local",
        out_shape=(
            sds((PART, size), F32), sds((PART, size), F32), sds((leaves, 32, LEAF), BF),
            sds((slots + PAD,), jnp.int32), sds((1,), jnp.int32),
        ),
        in_specs=[sspec()] * 3 + [vspec()] * 2,
        out_specs=(vspec(), vspec(), vspec(), sspec(), sspec()),
        scratch_shapes=[
            VMEM((leaves // 2 + 1, LEAF, 32), BF), VMEM((leaves // 2 + 1, 16, LEAF), BF),
            *scratch_blocks, SMEM((slots + PAD,), jnp.int32),
        ],
        compiler_params=params(28),
        cost_estimate=pl.CostEstimate(
            flops=36 * 10**9, bytes_accessed=8 << 20, transcendentals=190 * 2**17
        ),
    )(scale, near_offsets, near_cols, points, pack)

    from_core = after(from_core, far_list)
    near_pair = jnp.stack([export[0:4], from_core[0:4]])
    from_next = swap_mask(near_pair, 1)
    coef_late = after(coef, far_list)
    ties_raw = jnp.transpose(local_coupling, (1, 2, 3, 0))
    mates = jnp.transpose(local_partners)
    local, ties = pl.pallas_call(
        couple_kernel,
        name="couple",
        out_shape=(
            sds((part - 1, ALL, 2 * RANK), F32), sds((EXPORT, RANK, 3 * RANK), BF),
        ),
        in_specs=[sspec()] * 2 + [vspec(), hspec()],
        out_specs=(vspec(),) * 2,
        scratch_shapes=[
            VMEM(ties_raw.shape, BF),
            VMEM((leaves // 4, RANK * 8, 2 * RANK), F32),
            VMEM((leaves // 4, RANK * 8, RANK), F32), pltpu.SemaphoreType.DMA((4,)),
        ],
        compiler_params=params(36),
        cost_estimate=pl.CostEstimate(flops=9 * 10**9, bytes_accessed=8 << 20, transcendentals=0),
    )(scale, mates, coef_late, ties_raw)

    from_next = after(from_next, local)
    quad = jnp.concatenate([near_pair[:, 0:2], from_next[:, 0:2]], axis=0)
    from_far = [swap_mask(quad, mask) for mask in (2, 4, 6)]
    first = after(first, local)
    mine, other = pl.pallas_call(
        near_halo_kernel,
        name="near_halo",
        out_shape=(sds((PART, size), F32), sds((PART, size), F32)),
        in_specs=[sspec()] * 3 + [vspec()] * 5,
        out_specs=(vspec(), vspec()),
        scratch_shapes=[
            VMEM((PART, size), F32), VMEM((PART, size), F32),
            VMEM((leaves + 1, LEAF, 32), BF), VMEM((leaves + 1, 16, LEAF), BF),
            *scratch_blocks,
        ],
        compiler_params=params(36),
        cost_estimate=pl.CostEstimate(
            flops=4 * 10**9, bytes_accessed=8 << 20, transcendentals=60 * 2**17
        ),
    )(scale, far_list, far_count, row_feat, left, right, first, second)
    swapped = lax.ppermute(other, "vec", [(0, 1), (1, 0)])

    tops = export[None, 0:1]
    if dev_levels > SPAN:
        tops = jnp.concatenate(
            [export[None, 0:1], from_core[None, 0:1], from_next[:, 0:1]]
            + [part[:, 0:1] for part in from_far],
            axis=0,
        )
        for bit in range(SPAN, dev_levels):
            tops = jnp.concatenate([tops, swap_mask(tops, 2**bit)], axis=0)
    low_mine, low_other = pl.pallas_call(
        lambda *refs: down_kernel(dev_levels, *refs[:11], refs[11:14], *refs[14:]),
        name="down",
        out_shape=(sds((part, PART, RANK), BF), sds((part, PART, RANK), BF)),
        in_specs=[sspec()] * 3 + [vspec()] * 12,
        out_specs=(vspec(), vspec()),
        scratch_shapes=[
            VMEM((2 * 2**SPAN, EXPORT, 2 * ALL, 2 * RANK), BF),
            VMEM((part - 1, 2 * ALL, RANK), BF), VMEM((2 * count, 2 * ALL, RANK), BF),
        ],
        compiler_params=params(24),
        cost_estimate=pl.CostEstimate(flops=4 * 10**9, bytes_accessed=4 << 20, transcendentals=0),
    )(
        scale, mates, top_partners, top_transfer, top_coupling, ties, local, moves,
        export, from_core, from_next, *from_far, tops,
    )
    low_got = lax.ppermute(low_other, "vec", [(0, 1), (1, 0)])

    return pl.pallas_call(
        final_kernel,
        name="final",
        out_shape=sds((PART, size), F32),
        in_specs=[sspec()] + [vspec()] * 7,
        out_specs=hspec(),
        scratch_shapes=[VMEM((PART, size), F32), pltpu.SemaphoreType.DMA((4,))],
        compiler_params=params(16),
        cost_estimate=pl.CostEstimate(flops=2 * 10**9, bytes_accessed=4 << 20, transcendentals=0),
    )(scale, low_mine, low_got, leaf_basis, noise.reshape(1, size), vectors, mine, swapped)


def solution(mesh):
    return jax.shard_map(
        body,
        mesh=mesh,
        in_specs=(
            P("groups", ("leaf", "sub")),
            P("groups"),
            P(("groups", "leaf", "sub")),
            P(("groups", "vec"), ("leaf", "sub")),
            P(("groups", "leaf", "sub"), None, None),
            P(("groups", "leaf", "sub"), None, None, None),
            P("groups", None, None, None),
            P(("groups", "leaf", "sub"), None, None, None),
            P("groups", None, None, None),
            P(("groups", "leaf", "sub"), None),
            P("groups", None),
            P(("groups", "leaf", "sub")),
            P(("groups", "leaf", "sub")),
        ),
        out_specs=P(("groups", "vec"), ("leaf", "sub")),
        check_vma=False,
    )
```

```python
import functools
import math

import jax
import jax.numpy as jnp
from jax import lax
from jax.experimental import pallas as pl
from jax.experimental.pallas import tpu as pltpu
from jax.sharding import PartitionSpec as P

BF = jnp.bfloat16
F32 = jnp.float32
LEAF = 256
RANK = 64
SPAN = 3
PART = 8
ALL = 2 * PART
EXPORT = 2**SPAN
NEG_LOG2E = -1.0 / math.log(2.0)
ROOT3 = math.sqrt(3.0)
TINY = 1e-12
PAIR = 2
PAD = 16
TURNS = 2
CODE_BITS = 10
CODE = 2**CODE_BITS
VMEM = pltpu.VMEM
SMEM = pltpu.SMEM
NT = (((1,), (1,)), ((), ()))


def vspec():
    return pl.BlockSpec(memory_space=pltpu.VMEM)


def sspec():
    return pl.BlockSpec(memory_space=pltpu.SMEM)


def hspec():
    return pl.BlockSpec(memory_space=pltpu.HBM)


def fetch(pairs, sems):
    copies = [
        pltpu.make_async_copy(source, target, sems.at[i])
        for i, (source, target) in enumerate(pairs)
    ]
    for copy in copies:
        copy.start()
    return copies


def params(mib):
    return pltpu.CompilerParams(vmem_limit_bytes=mib << 20)


def lanes(index):
    return pl.ds(pl.multiple_of(index * LEAF, LEAF), LEAF)


def whole(scalar):
    return scalar.astype(jnp.int32)


def coordinate_rows(raw, scale_ref):
    width = raw.shape[1]
    row = lax.broadcasted_iota(jnp.int32, (8, width), 0)
    scale = jnp.where(
        row == 0, scale_ref[0], jnp.where(row == 1, scale_ref[1], scale_ref[2])
    )
    full = jnp.concatenate([raw, jnp.zeros((5, width), F32)], axis=0)
    scaled = (full - 0.5) * (scale * ROOT3)
    scaled = jnp.where(row < 3, scaled, 0.0)
    high = scaled.astype(BF).astype(F32)
    rest = (scaled - high).astype(BF).astype(F32)
    return high + pltpu.roll(rest, 4, 0)


def norm_parts(rows):
    swapped = pltpu.roll(rows, 4, 0)
    norm = jnp.sum(rows * (rows + swapped), axis=0, keepdims=True)
    high = norm.astype(BF).astype(F32)
    rest = norm - high
    mid = rest.astype(BF).astype(F32)
    return swapped, high, mid, rest - mid


def row_features(rows):
    swapped, high, mid, low = norm_parts(rows)
    row = lax.broadcasted_iota(jnp.int32, rows.shape, 0)
    tail = jnp.where(
        row < 3,
        1.0,
        jnp.where(row == 3, high, jnp.where(row == 4, mid, jnp.where(row == 5, low, 0.0))),
    )
    return jnp.concatenate([rows, swapped, tail, jnp.zeros_like(rows)], axis=0).astype(BF)


def col_features(rows):
    _, high, mid, low = norm_parts(rows)
    row = lax.broadcasted_iota(jnp.int32, rows.shape, 0)
    tail = jnp.where(
        row == 0,
        high,
        jnp.where(row == 1, mid, jnp.where(row == 2, low, jnp.where(row < 6, 1.0, 0.0))),
    )
    both = -2.0 * rows
    return jnp.concatenate([both, both, tail, jnp.zeros_like(rows)], axis=0).T.astype(BF)


def matern(squared):
    squared = jnp.maximum(squared, TINY)
    dist = squared * lax.rsqrt(squared)
    return ((1.0 + dist) * jnp.exp2(dist * NEG_LOG2E)).astype(BF)


def pack_kernel(scale_ref, points_hbm, vec_hbm, got_hbm, out_ref, points, mine, got, sems):
    half = out_ref.shape[1]
    core = whole(scale_ref[4])
    there = pl.ds(pl.multiple_of(core * half, half), half)
    copies = fetch(
        [
            (points_hbm.at[:, there], points), (vec_hbm.at[:, there], mine),
            (got_hbm.at[:, there], got),
        ],
        sems,
    )
    for copy in copies:
        copy.wait()

    def step(i, _):
        here = pl.ds(pl.multiple_of(i * 2048, 2048), 2048)
        rows = coordinate_rows(points[:, here], scale_ref)
        one, two = mine[:, here].astype(F32), got[:, here].astype(F32)
        first, second = jnp.where(core == 0, one, two), jnp.where(core == 0, two, one)
        out_ref[:, here] = jnp.concatenate([first, second, rows], axis=0).astype(BF)
        return 0

    lax.fori_loop(0, half // 2048, step, 0)


def block_loop(count, place, list_ref, row_ref, col_ref, val_ref, sums, s0, s1, k0, k1):
    def accumulate(first, kern):
        for q in range(PAIR):
            code = list_ref[first + q]
            here = lanes(code >> CODE_BITS)
            part = jnp.dot(
                val_ref[place(code & (CODE - 1))], kern[q], preferred_element_type=F32
            )
            sums[0][:, here] += part[:PART]
            sums[1][:, here] += part[PART:]

    def distance(first, out):
        for q in range(PAIR):
            code = list_ref[first + q]
            out[q] = jnp.dot(
                col_ref[place(code & (CODE - 1))],
                row_ref[code >> CODE_BITS],
                preferred_element_type=F32,
            )

    def evaluate(squared, kern):
        for q in range(PAIR):
            kern[q] = matern(squared[q])

    k1[...] = jnp.zeros_like(k1)
    distance(0, s0)

    def step(it, _):
        for turn in range(TURNS):
            first = (it * TURNS + turn) * 2 * PAIR
            accumulate(jnp.maximum(first - PAIR, 0), k1)
            distance(first + PAIR, s1)
            evaluate(s0, k0)
            accumulate(first, k0)
            distance(first + 2 * PAIR, s0)
            evaluate(s1, k1)
        return 0

    turns = (count + TURNS * 2 * PAIR - 1) // (TURNS * 2 * PAIR)
    lax.fori_loop(0, turns, step, 0)
    accumulate(jnp.maximum(turns * TURNS * 2 * PAIR - PAIR, 0), k1)


def load_columns(pack_ref, base, count, col_ref, val_ref):
    def step(i, _):
        for q in range(4):
            leaf = i * 4 + q
            val_ref[base + leaf] = pack_ref[0:16, lanes(leaf)]
            col_ref[base + leaf] = col_features(pack_ref[16:24, lanes(leaf)].astype(F32))
        return 0

    lax.fori_loop(0, count // 4, step, 0)


def near_local_kernel(
    scale_ref, offs_ref, cols_ref, points_ref, pack_ref,
    mine_ref, other_ref, row_ref, far_list, far_count,
    col_ref, val_ref, s0, s1, k0, k1, own_list,
):
    device, half_id = whole(scale_ref[3]), whole(scale_ref[4])
    leaves = offs_ref.shape[0]
    half = leaves // 2
    slots = cols_ref.shape[0]
    each = slots // leaves

    far_base = device * leaves - leaves + half_id * half
    half_bits = half.bit_length() - 1

    def rows_step(i, carry):
        row, code, own, far = carry
        for q in range(2):
            leaf = i * 2 + q
            row_ref[leaf] = row_features(coordinate_rows(points_ref[:, lanes(leaf)], scale_ref))
            mine_ref[:, lanes(leaf)] = jnp.zeros((PART, LEAF), F32)
            other_ref[:, lanes(leaf)] = jnp.zeros((PART, LEAF), F32)
            for w in range(each):
                slot = leaf * each + w
                begins = offs_ref[jnp.minimum(row + 1, leaves - 1)] == slot
                row = jnp.where(begins, row + 1, row)
                code = jnp.where(begins, code + CODE, code)
                place = cols_ref[slot] - far_base
                own_list[own] = code + (place - leaves)
                far_list[far] = code + place
                block = place >> half_bits
                own = jnp.where(block == 2, own + 1, own)
                far = jnp.where((block & 3) == 0, far + 1, far)
        return row, code, own, far

    zero = jnp.int32(0)
    _, _, own, far = lax.fori_loop(0, leaves // 2, rows_step, (zero, zero, zero, zero))
    for q in range(PAD):
        own_list[own + q] = half
        far_list[far + q] = 8 * half
    far_count[0] = far
    load_columns(pack_ref, 0, half, col_ref, val_ref)
    val_ref[half] = jnp.zeros((16, LEAF), BF)
    col_ref[half] = jnp.zeros(col_ref.shape[1:], BF)
    sums = (mine_ref, other_ref)
    block_loop(own, lambda c: c, own_list, row_ref, col_ref, val_ref, sums, s0, s1, k0, k1)


def near_halo_kernel(
    scale_ref, far_list, far_count, row_ref, left_ref, right_ref, first_in, second_in,
    mine_ref, other_ref,
    first, second, col_ref, val_ref, s0, s1, k0, k1,
):
    core = whole(scale_ref[4])
    half = left_ref.shape[1] // LEAF
    bits = half.bit_length() - 1
    count = far_count[0]

    def place(code):
        return (code & (half - 1)) | ((code >> (bits + 2)) << bits)

    def load(i, _):
        for q in range(4):
            code = far_list[i * 4 + q] & (CODE - 1)
            here = lanes(code & (half - 1))
            after = code >= 4 * half
            values = jnp.where(after, right_ref[0:16, here], left_ref[0:16, here])
            rows = jnp.where(after, right_ref[16:24, here], left_ref[16:24, here])
            val_ref[place(code)] = values
            col_ref[place(code)] = col_features(rows.astype(F32))
        return 0

    first[...] = first_in[...]
    second[...] = second_in[...]
    lax.fori_loop(0, (count + 3) // 4, load, 0)
    val_ref[2 * half] = jnp.zeros((16, LEAF), BF)
    col_ref[2 * half] = jnp.zeros(col_ref.shape[1:], BF)
    sums = (first, second)
    block_loop(count, place, far_list, row_ref, col_ref, val_ref, sums, s0, s1, k0, k1)

    @pl.when(core == 0)
    def _():
        mine_ref[...] = first[...]
        other_ref[...] = second[...]

    @pl.when(core == 1)
    def _():
        mine_ref[...] = second[...]
        other_ref[...] = first[...]


def split_parts(value):
    high = value.astype(BF).astype(F32)
    return jnp.concatenate([high, value - high], axis=0).astype(BF)


def join_parts(value):
    return value[0:ALL] + value[ALL : 2 * ALL]


def mul_nt(left, right):
    return lax.dot_general(left, right, NT, preferred_element_type=F32)


def over_nodes(count, unroll, work):
    group = min(unroll, count)
    if count == group:
        work([jnp.int32(i) for i in range(count)])
        return

    def step(i, _):
        work([i * group + q for q in range(group)])
        return 0

    lax.fori_loop(0, count // group, step, 0)


def store_turned(flat, r, block):
    turned = block.T
    count = turned.shape[0] // 8
    width = turned.shape[1]
    rows = pl.ds(pl.multiple_of(r * 8, 8), 8)
    flat[0:count, rows] = turned[: count * 8].reshape(count, 8, width)
    rest = turned.shape[0] - count * 8
    flat[count, pl.ds(pl.multiple_of(r * 8, 8), rest)] = turned[count * 8 :]


def load_node(flat, node):
    return flat[node >> 3, pl.ds(node & 7, RANK, stride=8)].astype(BF)


def side_by_side(first, second):
    return jnp.concatenate([first, second], axis=1)


def doubled(pair):
    low = lax.broadcasted_iota(jnp.int32, pair.shape, 1) < RANK
    turned = pltpu.roll(pair, RANK, 1)
    return jnp.where(low, pair, turned), jnp.where(low, turned, pair)


def up_kernel(
    scale_ref, pack_ref, basis_hbm, raw_hbm, coef_ref, export_ref, move_ref,
    basis_ref, raw_ref, flat, pairs, sems,
):
    core = whole(scale_ref[4])
    leaves = basis_ref.shape[0]
    levels = leaves.bit_length() - 1
    chunks = 4
    per = leaves // chunks
    deep = RANK // chunks
    copies = fetch(
        [
            pair
            for c in range(chunks)
            for pair in (
                (
                    basis_hbm.at[pl.ds(core * leaves + c * per, per)],
                    basis_ref.at[c * per : (c + 1) * per],
                ),
                (
                    raw_hbm.at[:, c * deep : (c + 1) * deep],
                    raw_ref.at[:, c * deep : (c + 1) * deep],
                ),
            )
        ],
        sems,
    )

    def keep(parent, first, second):
        pair = side_by_side(first, second)
        pairs[parent] = split_parts(pair)
        one, two = doubled(pair)
        coef_ref[2 * parent + 1] = split_parts(one)
        coef_ref[2 * parent + 2] = split_parts(two)

    def leaf_step(it, _):
        outs = []
        for q in range(8):
            leaf = it * 8 + q
            outs.append(mul_nt(pack_ref[0:ALL, lanes(leaf)], basis_ref[leaf]))
        for q in range(8):
            r = it * 8 + q
            block = jnp.concatenate([raw_ref[0, r], raw_ref[1, r]], axis=0).astype(F32)
            store_turned(flat, r, block)
        for q in range(4):
            keep(leaves // 2 - 1 + it * 4 + q, outs[2 * q], outs[2 * q + 1])
        return 0

    for c in range(chunks):
        for copy in copies[2 * c : 2 * c + 2]:
            copy.wait()
        lax.fori_loop(c * per // 8, (c + 1) * per // 8, leaf_step, 0)
    root_move = load_node(flat, 0)
    move_ref[leaves - 1] = root_move
    for depth in range(levels - 1, 0, -1):
        first = 2**depth - 1
        above = 2 ** (depth - 1) - 1
        start = 2 ** (depth + 1) - 1 + core * 2**depth

        def work(nodes, first=first, above=above, start=start):
            outs = []
            for j in nodes:
                for c in range(2):
                    move = load_node(flat, start + 2 * j + c)
                    move_ref[first + 2 * j + c] = move
                    outs.append(mul_nt(pairs[first + 2 * j + c], move))
            for j, i in enumerate(nodes):
                keep(above + i, join_parts(outs[2 * j]), join_parts(outs[2 * j + 1]))

        over_nodes(2 ** (depth - 1), 8, work)
    move = load_node(flat, 1 + core)
    move_ref[0] = move
    crown = join_parts(mul_nt(pairs[0], move))
    crown = split_parts(side_by_side(crown, crown))
    coef_ref[0] = crown
    side = lax.broadcasted_iota(jnp.int32, crown.shape, 1) // RANK
    root = join_parts(mul_nt(jnp.where(side == core, crown.astype(F32), 0.0).astype(BF), root_move))
    export_ref[0] = split_parts(side_by_side(root, root))
    export_ref[1:EXPORT] = coef_ref[0 : EXPORT - 1]


def joint(first, second, third):
    return jnp.concatenate([first, second, third], axis=1)


def couple_kernel(
    scale_ref, partners_ref, coef_ref, raw_hbm, local_ref, tie_ref, raw_ref, wide, thin, sems,
):
    device, core = whole(scale_ref[3]), whole(scale_ref[4])
    levels = (raw_ref.shape[3] + 1).bit_length() - 2
    chunks = 4
    deep = RANK // chunks
    copies = fetch(
        [
            (raw_hbm.at[:, c * deep : (c + 1) * deep], raw_ref.at[:, c * deep : (c + 1) * deep])
            for c in range(chunks)
        ],
        sems,
    )
    low = lax.broadcasted_iota(jnp.int32, (2 * ALL, 2 * RANK), 1) < RANK

    def turn(i, _):
        for q in range(8):
            r = i * 8 + q
            block = jnp.concatenate([raw_ref[0, r], raw_ref[1, r]], axis=0).astype(F32)
            store_turned(wide, r, block)
            store_turned(thin, r, raw_ref[2, r].astype(F32))
        return 0

    for c in range(chunks):
        copies[c].wait()
        lax.fori_loop(c * deep // 8, (c + 1) * deep // 8, turn, 0)

    def tie(node):
        return jnp.concatenate([load_node(wide, node), load_node(thin, node)], axis=1)

    tie_ref[0] = tie(0)
    for depth in range(1, SPAN + 1):
        for i in range(2 ** (depth - 1)):
            tie_ref[2 ** (depth - 1) + i] = tie(2**depth - 1 + core * 2 ** (depth - 1) + i)
    for depth in range(SPAN + 1, levels + 1):
        half = 2 ** (depth - 1)
        above = half // 2 - 1
        start = 2**depth - 1 + core * half
        shift = half - 1 - device * 2**depth - core * half

        def work(nodes, above=above, start=start, shift=shift):
            outs = []
            for j in nodes:
                for c in range(2):
                    node = start + 2 * j + c
                    mates = [coef_ref[partners_ref[f, node] + shift] for f in range(3)]
                    left = jnp.concatenate(
                        [jnp.where(low, mates[0], mates[1]), mates[2][:, :RANK]], axis=1
                    )
                    outs.append(mul_nt(left, tie(node)))
            for j, i in enumerate(nodes):
                local_ref[above + i] = side_by_side(
                    join_parts(outs[2 * j]), join_parts(outs[2 * j + 1])
                )

        over_nodes(half // 2, 8, work)


def down_kernel(
    dev_levels, scale_ref, partners_ref, top_partners_ref, top_e, top_b, tie_ref,
    local_ref, move_ref, own_ref, core_ref, next_ref, far_refs, tops_ref, mine_ref, other_ref,
    gather_ref, down, tree,
):
    device, core = whole(scale_ref[3]), whole(scale_ref[4])
    self_id = 2 * device + core
    gather_ref[0] = own_ref[...]
    gather_ref[1] = core_ref[...]
    gather_ref[2:4, 0:4] = next_ref[...]
    for i, far_ref in enumerate(far_refs):
        gather_ref[4 * i + 4 : 4 * i + 8, 0:2] = far_ref[...]
    root_ref = gather_ref if dev_levels == SPAN else tops_ref
    leaves = mine_ref.shape[0]
    levels = leaves.bit_length() - 1
    count = 2**dev_levels

    def roots(nodes):
        for i in nodes:
            parts = join_parts(root_ref[(2 * i) ^ self_id, 0].astype(F32)) + join_parts(
                root_ref[(2 * i + 1) ^ self_id, 0].astype(F32)
            )
            tree[count + i] = split_parts(parts[:, :RANK])

    over_nodes(count, 8, roots)
    for level in range(dev_levels - 1, 1, -1):

        def work(nodes, level=level):
            outs = []
            for i in nodes:
                row = 2**level - 4 + i
                kids = [tree[2 ** (level + 1) + 2 * i + c] for c in range(2)]
                outs.append(mul_nt(kids[0], top_e[row, 0]) + mul_nt(kids[1], top_e[row, 1]))
            for i, out in zip(nodes, outs):
                tree[2**level + i] = split_parts(join_parts(out))

        over_nodes(2**level, 4, work)

    mates = [tree[count + partners_ref[f, 0]] for f in range(3)]
    shallow = [join_parts(mul_nt(joint(*mates), tie_ref[0]))]
    for depth in range(1, SPAN + 1):
        half = 2 ** (depth - 1)
        for i in range(half):
            node = 2**depth - 1 + core * half + i
            picks = []
            for f in range(3):
                mate = partners_ref[f, node]
                at = ((mate >> (depth - 1)) ^ self_id) & (2 * 2**SPAN - 1)
                picks.append(gather_ref[at, half + (mate & (half - 1))][:, :RANK])
            shallow.append(join_parts(mul_nt(joint(*picks), tie_ref[half + i])))

    pushed = jnp.zeros((ALL, RANK), F32)
    for level in range(2, dev_levels):
        node = device >> (dev_levels - level)
        row = 2**level - 4 + node
        side = device >> (dev_levels - level - 1) & 1
        parts = sum(
            mul_nt(tree[2**level + top_partners_ref[row, f]], top_b[row, f]) for f in range(3)
        )
        here = split_parts(join_parts(parts) + pushed)
        pushed = join_parts(jnp.dot(here, top_e[row, side], preferred_element_type=F32))

    root = split_parts(shallow[0] + pushed)
    both = join_parts(jnp.dot(root, move_ref[leaves - 1], preferred_element_type=F32))
    down[0] = split_parts(shallow[1] + jnp.where(core == 0, both[:, :RANK], both[:, RANK:]))
    for depth in range(levels):
        first = 2**depth - 1

        def work(nodes, depth=depth, first=first):
            outs = [
                jnp.dot(down[first + i], move_ref[first + i], preferred_element_type=F32)
                for i in nodes
            ]
            for i, out in zip(nodes, outs):
                node = first + i
                if depth + 2 <= SPAN:
                    kid = 2 ** (depth + 1) + 2 * i
                    base = side_by_side(shallow[kid], shallow[kid + 1])
                else:
                    base = local_ref[node]
                pair = base + join_parts(out)
                if depth == levels - 1:
                    for c in range(2):
                        value = pair[:, c * RANK : (c + 1) * RANK]
                        one, two = value[:PART], value[PART:]
                        mine_ref[2 * i + c] = jnp.where(core == 0, one, two).astype(BF)
                        other_ref[2 * i + c] = jnp.where(core == 0, two, one).astype(BF)
                else:
                    down[2 * node + 1] = split_parts(pair[:, :RANK])
                    down[2 * node + 2] = split_parts(pair[:, RANK:])

        if depth < SPAN:
            work(list(range(2**depth)))
        else:
            over_nodes(2**depth, 8, work)


def final_kernel(
    scale_ref, mine_ref, got_ref, basis, noise, vec, near_hbm, swap_hbm, out_hbm,
    near, swap, out, sems,
):
    core = whole(scale_ref[4])
    leaves = mine_ref.shape[0]
    chunks = 4
    per = leaves // chunks
    wide = per * LEAF
    work = []
    for part, low_ref in enumerate((mine_ref, got_ref)):
        base = jnp.where(core == part, 0, leaves)
        for c in range(chunks):
            piece = pl.ds(pl.multiple_of((base + c * per) * LEAF, wide), wide)
            work.append((low_ref, base, c * per, piece))
    loads = fetch(
        [
            pair
            for _, _, _, piece in work
            for pair in (
                (near_hbm.at[:, piece], near.at[:, piece]),
                (swap_hbm.at[:, piece], swap.at[:, piece]),
            )
        ],
        sems,
    )
    sends = []
    for i, (low_ref, base, start, piece) in enumerate(work):
        loads[2 * i].wait()
        loads[2 * i + 1].wait()

        def last(nodes, low_ref=low_ref, base=base, start=start):
            rows = [start + n for n in nodes]
            fars = [
                jnp.dot(low_ref[n], basis[base + n], preferred_element_type=F32) for n in rows
            ]
            for n, far in zip(rows, fars):
                here = lanes(base + n)
                total = near[:, here] + swap[:, here]
                out[:, here] = total + noise[:, here] * vec[:, here].astype(F32) + far

        over_nodes(per, 8, last)
        send = pltpu.make_async_copy(
            out.at[:, piece], out_hbm.at[:, piece], sems.at[len(loads) + i]
        )
        send.start()
        sends.append(send)
    for send in sends:
        send.wait()


def swap_mask(value, mask):
    total = lax.axis_size("leaf") * lax.axis_size("sub")
    return lax.ppermute(value, ("leaf", "sub"), [(i, i ^ mask) for i in range(total)])


def after(value, anchor):
    return lax.optimization_barrier((value, anchor))[0]


def body(
    points, inv_scale, noise, vectors, leaf_basis, local_transfer, top_transfer,
    local_coupling, top_coupling, local_partners, top_partners, near_offsets, near_cols,
):
    subs = lax.axis_size("sub")
    count = lax.axis_size("leaf") * subs
    dev_levels = count.bit_length() - 1
    device = lax.axis_index("leaf") * subs + lax.axis_index("sub")
    core = lax.axis_index("vec")
    scale = jnp.concatenate([inv_scale, jnp.stack([device, core]).astype(F32)])
    size = vectors.shape[1]
    leaves = near_offsets.shape[0]
    slots = near_cols.shape[0]
    half = size // 2
    sds = jax.ShapeDtypeStruct
    scratch_blocks = [
        VMEM((PAIR, LEAF, LEAF), F32), VMEM((PAIR, LEAF, LEAF), F32),
        VMEM((PAIR, LEAF, LEAF), BF), VMEM((PAIR, LEAF, LEAF), BF),
    ]

    got = lax.ppermute(vectors, "vec", [(0, 1), (1, 0)])

    pack = pl.pallas_call(
        pack_kernel,
        name="pack",
        out_shape=sds((24, half), BF),
        in_specs=[sspec(), hspec(), hspec(), hspec()],
        out_specs=vspec(),
        scratch_shapes=[
            VMEM((3, half), F32), VMEM((PART, half), BF), VMEM((PART, half), BF),
            pltpu.SemaphoreType.DMA((3,)),
        ],
        compiler_params=params(60),
    )(scale, points, vectors, got)
    axes = ("leaf", "sub")
    left = lax.ppermute(pack, axes, [(i, i + 1) for i in range(count - 1)])
    right = lax.ppermute(pack, axes, [(i + 1, i) for i in range(count - 1)])

    moves_raw = jnp.transpose(local_transfer, (1, 2, 3, 0))
    part = leaves // 2
    coef, export, moves = pl.pallas_call(
        up_kernel,
        name="up",
        out_shape=(
            sds((2 * part - 1, 2 * ALL, 2 * RANK), BF), sds((EXPORT, 2 * ALL, 2 * RANK), BF),
            sds((part, RANK, 2 * RANK), BF),
        ),
        in_specs=[sspec(), vspec(), hspec(), hspec()],
        out_specs=(vspec(),) * 3,
        scratch_shapes=[
            VMEM((part, RANK, LEAF), BF), VMEM(moves_raw.shape, BF),
            VMEM((leaves // 8, RANK * 8, 2 * RANK), F32),
            VMEM((part - 1, 2 * ALL, 2 * RANK), BF), pltpu.SemaphoreType.DMA((8,)),
        ],
        compiler_params=params(60),
        cost_estimate=pl.CostEstimate(flops=8 * 10**9, bytes_accessed=8 << 20, transcendentals=0),
    )(scale, pack, leaf_basis, moves_raw)
    from_core = lax.ppermute(export, "vec", [(0, 1), (1, 0)])
    pack, _ = lax.optimization_barrier((pack, export))
    first, second, row_feat, far_list, far_count = pl.pallas_call(
        near_local_kernel,
        name="near_local",
        out_shape=(
            sds((PART, size), F32), sds((PART, size), F32), sds((leaves, 32, LEAF), BF),
            sds((slots + PAD,), jnp.int32), sds((1,), jnp.int32),
        ),
        in_specs=[sspec()] * 3 + [vspec()] * 2,
        out_specs=(vspec(), vspec(), vspec(), sspec(), sspec()),
        scratch_shapes=[
            VMEM((leaves // 2 + 1, LEAF, 32), BF), VMEM((leaves // 2 + 1, 16, LEAF), BF),
            *scratch_blocks, SMEM((slots + PAD,), jnp.int32),
        ],
        compiler_params=params(22),
        cost_estimate=pl.CostEstimate(
            flops=36 * 10**9, bytes_accessed=8 << 20, transcendentals=190 * 2**17
        ),
    )(scale, near_offsets, near_cols, points, pack)

    from_core = after(from_core, far_list)
    near_pair = jnp.stack([export[0:4], from_core[0:4]])
    coef_late, near_pair = lax.optimization_barrier((coef, near_pair))
    from_next = swap_mask(near_pair, 1)
    ties_raw = jnp.transpose(local_coupling, (1, 2, 3, 0))
    mates = jnp.transpose(local_partners)
    local, ties = pl.pallas_call(
        couple_kernel,
        name="couple",
        out_shape=(
            sds((part - 1, ALL, 2 * RANK), F32), sds((EXPORT, RANK, 3 * RANK), BF),
        ),
        in_specs=[sspec()] * 2 + [vspec(), hspec()],
        out_specs=(vspec(),) * 2,
        scratch_shapes=[
            VMEM(ties_raw.shape, BF),
            VMEM((leaves // 4, RANK * 8, 2 * RANK), F32),
            VMEM((leaves // 4, RANK * 8, RANK), F32), pltpu.SemaphoreType.DMA((4,)),
        ],
        compiler_params=params(36),
        cost_estimate=pl.CostEstimate(flops=16 * 10**9, bytes_accessed=8 << 20, transcendentals=0),
    )(scale, mates, coef_late, ties_raw)

    first, _, from_next = lax.optimization_barrier((first, local, from_next))
    quad = jnp.concatenate([near_pair[:, 0:2], from_next[:, 0:2]], axis=0)
    from_far = [swap_mask(quad, mask) for mask in (2, 4, 6)]
    mine, other = pl.pallas_call(
        near_halo_kernel,
        name="near_halo",
        out_shape=(sds((PART, size), F32), sds((PART, size), F32)),
        in_specs=[sspec()] * 3 + [vspec()] * 5,
        out_specs=(vspec(), vspec()),
        scratch_shapes=[
            VMEM((PART, size), F32), VMEM((PART, size), F32),
            VMEM((leaves + 1, LEAF, 32), BF), VMEM((leaves + 1, 16, LEAF), BF),
            *scratch_blocks,
        ],
        compiler_params=params(26),
        cost_estimate=pl.CostEstimate(
            flops=20 * 10**9, bytes_accessed=8 << 20, transcendentals=60 * 2**17
        ),
    )(scale, far_list, far_count, row_feat, left, right, first, second)
    swapped = lax.ppermute(other, "vec", [(0, 1), (1, 0)])

    tops = export[None, 0:1]
    if dev_levels > SPAN:
        tops = jnp.concatenate(
            [export[None, 0:1], from_core[None, 0:1], from_next[:, 0:1]]
            + [part[:, 0:1] for part in from_far],
            axis=0,
        )
        for bit in range(SPAN, dev_levels):
            tops = jnp.concatenate([tops, swap_mask(tops, 2**bit)], axis=0)
    low_mine, low_other = pl.pallas_call(
        lambda *refs: down_kernel(dev_levels, *refs[:11], refs[11:14], *refs[14:]),
        name="down",
        out_shape=(sds((part, PART, RANK), BF), sds((part, PART, RANK), BF)),
        in_specs=[sspec()] * 3 + [vspec()] * 12,
        out_specs=(vspec(), vspec()),
        scratch_shapes=[
            VMEM((2 * 2**SPAN, EXPORT, 2 * ALL, 2 * RANK), BF),
            VMEM((part - 1, 2 * ALL, RANK), BF), VMEM((2 * count, 2 * ALL, RANK), BF),
        ],
        compiler_params=params(14),
        cost_estimate=pl.CostEstimate(flops=40 * 10**9, bytes_accessed=4 << 20, transcendentals=0),
    )(
        scale, mates, top_partners, top_transfer, top_coupling, ties, local, moves,
        export, from_core, from_next, *from_far, tops,
    )
    low_got = lax.ppermute(low_other, "vec", [(0, 1), (1, 0)])

    return pl.pallas_call(
        final_kernel,
        name="final",
        out_shape=sds((PART, size), F32),
        in_specs=[sspec()] + [vspec()] * 5 + [hspec()] * 2,
        out_specs=hspec(),
        scratch_shapes=[VMEM((PART, size), F32)] * 3 + [pltpu.SemaphoreType.DMA((24,))],
        compiler_params=params(10),
        cost_estimate=pl.CostEstimate(flops=2 * 10**9, bytes_accessed=4 << 20, transcendentals=0),
    )(scale, low_mine, low_got, leaf_basis, noise.reshape(1, size), vectors, mine, swapped)


def solution(mesh):
    return jax.shard_map(
        body,
        mesh=mesh,
        in_specs=(
            P("groups", ("leaf", "sub")),
            P("groups"),
            P(("groups", "leaf", "sub")),
            P(("groups", "vec"), ("leaf", "sub")),
            P(("groups", "leaf", "sub"), None, None),
            P(("groups", "leaf", "sub"), None, None, None),
            P("groups", None, None, None),
            P(("groups", "leaf", "sub"), None, None, None),
            P("groups", None, None, None),
            P(("groups", "leaf", "sub"), None),
            P("groups", None),
            P(("groups", "leaf", "sub")),
            P(("groups", "leaf", "sub")),
        ),
        out_specs=P(("groups", "vec"), ("leaf", "sub")),
        check_vma=False,
    )
```

```python
import functools
import math

import jax
import jax.numpy as jnp
from jax import lax
from jax.experimental import pallas as pl
from jax.experimental.pallas import tpu as pltpu
from jax.sharding import PartitionSpec as P

BF = jnp.bfloat16
F32 = jnp.float32
LEAF = 256
RANK = 64
SPAN = 3
PART = 8
ALL = 2 * PART
EXPORT = 2**SPAN
NEG_LOG2E = -1.0 / math.log(2.0)
ROOT3 = math.sqrt(3.0)
TINY = 1e-12
PAIR = 2
PAD = 16
TURNS = 2
CODE_BITS = 10
CODE = 2**CODE_BITS
VMEM = pltpu.VMEM
SMEM = pltpu.SMEM
NT = (((1,), (1,)), ((), ()))


def vspec():
    return pl.BlockSpec(memory_space=pltpu.VMEM)


def sspec():
    return pl.BlockSpec(memory_space=pltpu.SMEM)


def hspec():
    return pl.BlockSpec(memory_space=pltpu.HBM)


def fetch(pairs, sems):
    copies = [
        pltpu.make_async_copy(source, target, sems.at[i])
        for i, (source, target) in enumerate(pairs)
    ]
    for copy in copies:
        copy.start()
    return copies


def params(mib):
    return pltpu.CompilerParams(vmem_limit_bytes=mib << 20)


def lanes(index):
    return pl.ds(pl.multiple_of(index * LEAF, LEAF), LEAF)


def whole(scalar):
    return scalar.astype(jnp.int32)


def coordinate_rows(raw, scale_ref):
    width = raw.shape[1]
    row = lax.broadcasted_iota(jnp.int32, (8, width), 0)
    scale = jnp.where(
        row == 0, scale_ref[0], jnp.where(row == 1, scale_ref[1], scale_ref[2])
    )
    full = jnp.concatenate([raw, jnp.zeros((5, width), F32)], axis=0)
    scaled = (full - 0.5) * (scale * ROOT3)
    scaled = jnp.where(row < 3, scaled, 0.0)
    high = scaled.astype(BF).astype(F32)
    rest = (scaled - high).astype(BF).astype(F32)
    return high + pltpu.roll(rest, 4, 0)


def norm_parts(rows):
    swapped = pltpu.roll(rows, 4, 0)
    norm = jnp.sum(rows * (rows + swapped), axis=0, keepdims=True)
    high = norm.astype(BF).astype(F32)
    rest = norm - high
    mid = rest.astype(BF).astype(F32)
    return swapped, high, mid, rest - mid


def row_features(rows):
    swapped, high, mid, low = norm_parts(rows)
    row = lax.broadcasted_iota(jnp.int32, rows.shape, 0)
    tail = jnp.where(
        row < 3,
        1.0,
        jnp.where(row == 3, high, jnp.where(row == 4, mid, jnp.where(row == 5, low, 0.0))),
    )
    return jnp.concatenate([rows, swapped, tail, jnp.zeros_like(rows)], axis=0).astype(BF)


def col_features(rows):
    _, high, mid, low = norm_parts(rows)
    row = lax.broadcasted_iota(jnp.int32, rows.shape, 0)
    tail = jnp.where(
        row == 0,
        high,
        jnp.where(row == 1, mid, jnp.where(row == 2, low, jnp.where(row < 6, 1.0, 0.0))),
    )
    both = -2.0 * rows
    return jnp.concatenate([both, both, tail, jnp.zeros_like(rows)], axis=0).T.astype(BF)


def matern(squared):
    squared = jnp.maximum(squared, TINY)
    dist = squared * lax.rsqrt(squared)
    return ((1.0 + dist) * jnp.exp2(dist * NEG_LOG2E)).astype(BF)


def pack_kernel(scale_ref, points_hbm, vec_hbm, got_hbm, out_ref, points, mine, got, sems):
    half = out_ref.shape[1]
    core = whole(scale_ref[4])
    there = pl.ds(pl.multiple_of(core * half, half), half)
    copies = fetch(
        [
            (points_hbm.at[:, there], points), (vec_hbm.at[:, there], mine),
            (got_hbm.at[:, there], got),
        ],
        sems,
    )
    for copy in copies:
        copy.wait()

    def step(i, _):
        here = pl.ds(pl.multiple_of(i * 2048, 2048), 2048)
        rows = coordinate_rows(points[:, here], scale_ref)
        one, two = mine[:, here].astype(F32), got[:, here].astype(F32)
        first, second = jnp.where(core == 0, one, two), jnp.where(core == 0, two, one)
        out_ref[:, here] = jnp.concatenate([first, second, rows], axis=0).astype(BF)
        return 0

    lax.fori_loop(0, half // 2048, step, 0)


def block_loop(count, place, list_ref, row_ref, col_ref, val_ref, sums, s0, s1, k0, k1):
    def accumulate(first, kern):
        for q in range(PAIR):
            code = list_ref[first + q]
            here = lanes(code >> CODE_BITS)
            part = jnp.dot(
                val_ref[place(code & (CODE - 1))], kern[q], preferred_element_type=F32
            )
            sums[0][:, here] += part[:PART]
            sums[1][:, here] += part[PART:]

    def distance(first, out):
        for q in range(PAIR):
            code = list_ref[first + q]
            out[q] = jnp.dot(
                col_ref[place(code & (CODE - 1))],
                row_ref[code >> CODE_BITS],
                preferred_element_type=F32,
            )

    def evaluate(squared, kern):
        for q in range(PAIR):
            kern[q] = matern(squared[q])

    k1[...] = jnp.zeros_like(k1)
    distance(0, s0)

    def step(it, _):
        for turn in range(TURNS):
            first = (it * TURNS + turn) * 2 * PAIR
            accumulate(jnp.maximum(first - PAIR, 0), k1)
            distance(first + PAIR, s1)
            evaluate(s0, k0)
            accumulate(first, k0)
            distance(first + 2 * PAIR, s0)
            evaluate(s1, k1)
        return 0

    turns = (count + TURNS * 2 * PAIR - 1) // (TURNS * 2 * PAIR)
    lax.fori_loop(0, turns, step, 0)
    accumulate(jnp.maximum(turns * TURNS * 2 * PAIR - PAIR, 0), k1)


def diagonal_loop(first_leaf, count, row_ref, col_ref, val_ref, sums, s0, s1, k0, k1):
    mid = LEAF // 2

    def distance(first, out):
        for q in range(PAIR):
            col = jnp.minimum(first + q, count - 1)
            rows = row_ref[first_leaf + col]
            out[q, :mid] = jnp.dot(col_ref[col, :mid], rows, preferred_element_type=F32)
            out[q, mid:, mid:] = jnp.dot(
                col_ref[col, mid:], rows[:, mid:], preferred_element_type=F32
            )

    def evaluate(squared, kern):
        for q in range(PAIR):
            kern[q, :mid] = matern(squared[q, :mid])
            kern[q, mid:, mid:] = matern(squared[q, mid:, mid:])

    def accumulate(first, kern):
        for q in range(PAIR):
            col = jnp.maximum(first + q, 0)
            values = val_ref[col]
            part = jnp.dot(values[:, :mid], kern[q, :mid], preferred_element_type=F32)
            left = mul_nt(values[:, mid:], kern[q, :mid, mid:])
            right = jnp.dot(values[:, mid:], kern[q, mid:, mid:], preferred_element_type=F32)
            part = part + jnp.concatenate([left, right], axis=1)
            here = lanes(first_leaf + col)
            sums[0][:, here] += part[:PART]
            sums[1][:, here] += part[PART:]

    k1[...] = jnp.zeros_like(k1)
    distance(0, s0)

    def step(it, _):
        for turn in range(TURNS):
            first = (it * TURNS + turn) * 2 * PAIR
            accumulate(first - PAIR, k1)
            distance(first + PAIR, s1)
            evaluate(s0, k0)
            accumulate(first, k0)
            distance(first + 2 * PAIR, s0)
            evaluate(s1, k1)
        return 0

    lax.fori_loop(0, count // (TURNS * 2 * PAIR), step, 0)
    accumulate(count - PAIR, k1)


def load_columns(pack_ref, base, count, col_ref, val_ref):
    def step(i, _):
        for q in range(4):
            leaf = i * 4 + q
            val_ref[base + leaf] = pack_ref[0:16, lanes(leaf)]
            col_ref[base + leaf] = col_features(pack_ref[16:24, lanes(leaf)].astype(F32))
        return 0

    lax.fori_loop(0, count // 4, step, 0)


def near_local_kernel(
    scale_ref, offs_ref, cols_ref, points_ref, pack_ref,
    mine_ref, other_ref, row_ref, far_list, far_count,
    col_ref, val_ref, s0, s1, k0, k1, own_list,
):
    device, half_id = whole(scale_ref[3]), whole(scale_ref[4])
    leaves = offs_ref.shape[0]
    half = leaves // 2
    slots = cols_ref.shape[0]
    each = slots // leaves

    far_base = device * leaves - leaves + half_id * half
    half_bits = half.bit_length() - 1

    def rows_step(i, carry):
        row, code, own, far = carry
        for q in range(2):
            leaf = i * 2 + q
            row_ref[leaf] = row_features(coordinate_rows(points_ref[:, lanes(leaf)], scale_ref))
            mine_ref[:, lanes(leaf)] = jnp.zeros((PART, LEAF), F32)
            other_ref[:, lanes(leaf)] = jnp.zeros((PART, LEAF), F32)
            for w in range(each):
                slot = leaf * each + w
                begins = offs_ref[jnp.minimum(row + 1, leaves - 1)] == slot
                row = jnp.where(begins, row + 1, row)
                code = jnp.where(begins, code + CODE, code)
                place = cols_ref[slot] - far_base
                own_list[own] = code + (place - leaves)
                far_list[far] = code + place
                block = place >> half_bits
                own = jnp.where(block + jnp.where(begins, 8, 0) == 2, own + 1, own)
                far = jnp.where((block & 3) == 0, far + 1, far)
        return row, code, own, far

    zero = jnp.int32(0)
    _, _, own, far = lax.fori_loop(0, leaves // 2, rows_step, (zero - 1, zero - CODE, zero, zero))
    for q in range(PAD):
        own_list[own + q] = half
        far_list[far + q] = 8 * half
    far_count[0] = far
    load_columns(pack_ref, 0, half, col_ref, val_ref)
    val_ref[half] = jnp.zeros((16, LEAF), BF)
    col_ref[half] = jnp.zeros(col_ref.shape[1:], BF)
    sums = (mine_ref, other_ref)
    diagonal_loop(half_id * half, half, row_ref, col_ref, val_ref, sums, s0, s1, k0, k1)
    block_loop(own, lambda c: c, own_list, row_ref, col_ref, val_ref, sums, s0, s1, k0, k1)


def near_halo_kernel(
    scale_ref, far_list, far_count, row_ref, left_ref, right_ref, first_in, second_in,
    mine_ref, other_ref,
    first, second, col_ref, val_ref, s0, s1, k0, k1,
):
    core = whole(scale_ref[4])
    half = left_ref.shape[1] // LEAF
    bits = half.bit_length() - 1
    count = far_count[0]

    def place(code):
        return (code & (half - 1)) | ((code >> (bits + 2)) << bits)

    def load(i, _):
        for q in range(4):
            code = far_list[i * 4 + q] & (CODE - 1)
            here = lanes(code & (half - 1))
            after = code >= 4 * half
            values = jnp.where(after, right_ref[0:16, here], left_ref[0:16, here])
            rows = jnp.where(after, right_ref[16:24, here], left_ref[16:24, here])
            val_ref[place(code)] = values
            col_ref[place(code)] = col_features(rows.astype(F32))
        return 0

    first[...] = first_in[...]
    second[...] = second_in[...]
    lax.fori_loop(0, (count + 3) // 4, load, 0)
    val_ref[2 * half] = jnp.zeros((16, LEAF), BF)
    col_ref[2 * half] = jnp.zeros(col_ref.shape[1:], BF)
    sums = (first, second)
    block_loop(count, place, far_list, row_ref, col_ref, val_ref, sums, s0, s1, k0, k1)

    @pl.when(core == 0)
    def _():
        mine_ref[...] = first[...]
        other_ref[...] = second[...]

    @pl.when(core == 1)
    def _():
        mine_ref[...] = second[...]
        other_ref[...] = first[...]


def split_parts(value):
    high = value.astype(BF).astype(F32)
    return jnp.concatenate([high, value - high], axis=0).astype(BF)


def join_parts(value):
    return value[0:ALL] + value[ALL : 2 * ALL]


def mul_nt(left, right):
    return lax.dot_general(left, right, NT, preferred_element_type=F32)


def over_nodes(count, unroll, work):
    group = min(unroll, count)
    if count == group:
        work([jnp.int32(i) for i in range(count)])
        return

    def step(i, _):
        work([i * group + q for q in range(group)])
        return 0

    lax.fori_loop(0, count // group, step, 0)


def store_turned(flat, r, block):
    turned = block.T
    count = turned.shape[0] // 8
    width = turned.shape[1]
    rows = pl.ds(pl.multiple_of(r * 8, 8), 8)
    flat[0:count, rows] = turned[: count * 8].reshape(count, 8, width)
    rest = turned.shape[0] - count * 8
    flat[count, pl.ds(pl.multiple_of(r * 8, 8), rest)] = turned[count * 8 :]


def load_node(flat, node):
    return flat[node >> 3, pl.ds(node & 7, RANK, stride=8)].astype(BF)


def side_by_side(first, second):
    return jnp.concatenate([first, second], axis=1)


def doubled(pair):
    low = lax.broadcasted_iota(jnp.int32, pair.shape, 1) < RANK
    turned = pltpu.roll(pair, RANK, 1)
    return jnp.where(low, pair, turned), jnp.where(low, turned, pair)


def up_kernel(
    scale_ref, pack_ref, basis_hbm, raw_hbm, coef_ref, export_ref, front_ref, move_ref,
    basis_ref, raw_ref, flat, pairs, sems,
):
    core = whole(scale_ref[4])
    leaves = basis_ref.shape[0]
    levels = leaves.bit_length() - 1
    chunks = 4
    per = leaves // chunks
    deep = RANK // chunks
    copies = fetch(
        [
            pair
            for c in range(chunks)
            for pair in (
                (
                    basis_hbm.at[pl.ds(core * leaves + c * per, per)],
                    basis_ref.at[c * per : (c + 1) * per],
                ),
                (
                    raw_hbm.at[:, c * deep : (c + 1) * deep],
                    raw_ref.at[:, c * deep : (c + 1) * deep],
                ),
            )
        ],
        sems,
    )

    def keep(parent, first, second):
        pair = side_by_side(first, second)
        pairs[parent] = split_parts(pair)
        one, two = doubled(pair)
        coef_ref[2 * parent + 1] = split_parts(one)
        coef_ref[2 * parent + 2] = split_parts(two)

    def leaf_step(it, _):
        outs = []
        for q in range(8):
            leaf = it * 8 + q
            outs.append(mul_nt(pack_ref[0:ALL, lanes(leaf)], basis_ref[leaf]))
        for q in range(8):
            r = it * 8 + q
            block = jnp.concatenate([raw_ref[0, r], raw_ref[1, r]], axis=0).astype(F32)
            store_turned(flat, r, block)
        for q in range(4):
            keep(leaves // 2 - 1 + it * 4 + q, outs[2 * q], outs[2 * q + 1])
        return 0

    for c in range(chunks):
        for copy in copies[2 * c : 2 * c + 2]:
            copy.wait()
        lax.fori_loop(c * per // 8, (c + 1) * per // 8, leaf_step, 0)
    root_move = load_node(flat, 0)
    move_ref[leaves - 1] = root_move
    for depth in range(levels - 1, 0, -1):
        first = 2**depth - 1
        above = 2 ** (depth - 1) - 1
        start = 2 ** (depth + 1) - 1 + core * 2**depth

        def work(nodes, first=first, above=above, start=start):
            outs = []
            for j in nodes:
                for c in range(2):
                    move = load_node(flat, start + 2 * j + c)
                    move_ref[first + 2 * j + c] = move
                    outs.append(mul_nt(pairs[first + 2 * j + c], move))
            for j, i in enumerate(nodes):
                keep(above + i, join_parts(outs[2 * j]), join_parts(outs[2 * j + 1]))

        over_nodes(2 ** (depth - 1), 8, work)
    move = load_node(flat, 1 + core)
    move_ref[0] = move
    crown = join_parts(mul_nt(pairs[0], move))
    crown = split_parts(side_by_side(crown, crown))
    coef_ref[0] = crown
    side = lax.broadcasted_iota(jnp.int32, crown.shape, 1) // RANK
    root = join_parts(mul_nt(jnp.where(side == core, crown.astype(F32), 0.0).astype(BF), root_move))
    export_ref[0] = split_parts(side_by_side(root, root))
    export_ref[1:EXPORT] = coef_ref[0 : EXPORT - 1]
    front_ref[0] = export_ref[0 : EXPORT // 2]


def joint(first, second, third):
    return jnp.concatenate([first, second, third], axis=1)


def couple_kernel(
    scale_ref, partners_ref, coef_ref, raw_hbm, local_ref, tie_ref, raw_ref, wide, thin, sems,
):
    device, core = whole(scale_ref[3]), whole(scale_ref[4])
    levels = (raw_ref.shape[3] + 1).bit_length() - 2
    chunks = 4
    deep = RANK // chunks
    copies = fetch(
        [
            (raw_hbm.at[:, c * deep : (c + 1) * deep], raw_ref.at[:, c * deep : (c + 1) * deep])
            for c in range(chunks)
        ],
        sems,
    )
    low = lax.broadcasted_iota(jnp.int32, (2 * ALL, 2 * RANK), 1) < RANK

    def turn(i, _):
        for q in range(8):
            r = i * 8 + q
            block = jnp.concatenate([raw_ref[0, r], raw_ref[1, r]], axis=0).astype(F32)
            store_turned(wide, r, block)
            store_turned(thin, r, raw_ref[2, r].astype(F32))
        return 0

    for c in range(chunks):
        copies[c].wait()
        lax.fori_loop(c * deep // 8, (c + 1) * deep // 8, turn, 0)

    def tie(node):
        return jnp.concatenate([load_node(wide, node), load_node(thin, node)], axis=1)

    tie_ref[0] = tie(0)
    for depth in range(1, SPAN + 1):
        for i in range(2 ** (depth - 1)):
            tie_ref[2 ** (depth - 1) + i] = tie(2**depth - 1 + core * 2 ** (depth - 1) + i)
    for depth in range(SPAN + 1, levels + 1):
        half = 2 ** (depth - 1)
        above = half // 2 - 1
        start = 2**depth - 1 + core * half
        shift = half - 1 - device * 2**depth - core * half

        def work(nodes, above=above, start=start, shift=shift):
            outs = []
            for j in nodes:
                for c in range(2):
                    node = start + 2 * j + c
                    mates = [coef_ref[partners_ref[f, node] + shift] for f in range(3)]
                    left = jnp.concatenate(
                        [jnp.where(low, mates[0], mates[1]), mates[2][:, :RANK]], axis=1
                    )
                    outs.append(mul_nt(left, tie(node)))
            for j, i in enumerate(nodes):
                local_ref[above + i] = side_by_side(
                    join_parts(outs[2 * j]), join_parts(outs[2 * j + 1])
                )

        over_nodes(half // 2, 8, work)


def down_kernel(
    dev_levels, scale_ref, partners_ref, top_partners_ref, top_e, top_b, tie_ref,
    local_ref, move_ref, own_ref, core_ref, next_ref, far_refs, tops_ref, mine_ref, other_ref,
    gather_ref, down, tree,
):
    device, core = whole(scale_ref[3]), whole(scale_ref[4])
    self_id = 2 * device + core
    gather_ref[0] = own_ref[...]
    gather_ref[1] = core_ref[...]
    gather_ref[2:4, 0:4] = next_ref[...]
    for i, far_ref in enumerate(far_refs):
        gather_ref[4 * i + 4 : 4 * i + 8, 0:2] = far_ref[...]
    root_ref = gather_ref if dev_levels == SPAN else tops_ref
    leaves = mine_ref.shape[0]
    levels = leaves.bit_length() - 1
    count = 2**dev_levels

    def roots(nodes):
        for i in nodes:
            parts = join_parts(root_ref[(2 * i) ^ self_id, 0].astype(F32)) + join_parts(
                root_ref[(2 * i + 1) ^ self_id, 0].astype(F32)
            )
            tree[count + i] = split_parts(parts[:, :RANK])

    over_nodes(count, 8, roots)
    for level in range(dev_levels - 1, 1, -1):

        def work(nodes, level=level):
            outs = []
            for i in nodes:
                row = 2**level - 4 + i
                kids = [tree[2 ** (level + 1) + 2 * i + c] for c in range(2)]
                outs.append(mul_nt(kids[0], top_e[row, 0]) + mul_nt(kids[1], top_e[row, 1]))
            for i, out in zip(nodes, outs):
                tree[2**level + i] = split_parts(join_parts(out))

        over_nodes(2**level, 4, work)

    mates = [tree[count + partners_ref[f, 0]] for f in range(3)]
    shallow = [join_parts(mul_nt(joint(*mates), tie_ref[0]))]
    for depth in range(1, SPAN + 1):
        half = 2 ** (depth - 1)
        for i in range(half):
            node = 2**depth - 1 + core * half + i
            picks = []
            for f in range(3):
                mate = partners_ref[f, node]
                at = ((mate >> (depth - 1)) ^ self_id) & (2 * 2**SPAN - 1)
                picks.append(gather_ref[at, half + (mate & (half - 1))][:, :RANK])
            shallow.append(join_parts(mul_nt(joint(*picks), tie_ref[half + i])))

    pushed = jnp.zeros((ALL, RANK), F32)
    for level in range(2, dev_levels):
        node = device >> (dev_levels - level)
        row = 2**level - 4 + node
        side = device >> (dev_levels - level - 1) & 1
        parts = sum(
            mul_nt(tree[2**level + top_partners_ref[row, f]], top_b[row, f]) for f in range(3)
        )
        here = split_parts(join_parts(parts) + pushed)
        pushed = join_parts(jnp.dot(here, top_e[row, side], preferred_element_type=F32))

    root = split_parts(shallow[0] + pushed)
    both = join_parts(jnp.dot(root, move_ref[leaves - 1], preferred_element_type=F32))
    down[0] = split_parts(shallow[1] + jnp.where(core == 0, both[:, :RANK], both[:, RANK:]))
    for depth in range(levels):
        first = 2**depth - 1

        def work(nodes, depth=depth, first=first):
            outs = [
                jnp.dot(down[first + i], move_ref[first + i], preferred_element_type=F32)
                for i in nodes
            ]
            for i, out in zip(nodes, outs):
                node = first + i
                if depth + 2 <= SPAN:
                    kid = 2 ** (depth + 1) + 2 * i
                    base = side_by_side(shallow[kid], shallow[kid + 1])
                else:
                    base = local_ref[node]
                pair = base + join_parts(out)
                if depth == levels - 1:
                    for c in range(2):
                        value = pair[:, c * RANK : (c + 1) * RANK]
                        one, two = value[:PART], value[PART:]
                        mine_ref[2 * i + c] = jnp.where(core == 0, one, two).astype(BF)
                        other_ref[2 * i + c] = jnp.where(core == 0, two, one).astype(BF)
                else:
                    down[2 * node + 1] = split_parts(pair[:, :RANK])
                    down[2 * node + 2] = split_parts(pair[:, RANK:])

        if depth < SPAN:
            work(list(range(2**depth)))
        else:
            over_nodes(2**depth, 8, work)


def final_kernel(
    scale_ref, mine_ref, got_ref, basis, noise, vec, near, swap, out_hbm, out, sems
):
    core = whole(scale_ref[4])
    leaves = mine_ref.shape[0]
    chunks = 2
    per = leaves // chunks
    wide = per * LEAF
    sends = []
    for part, low_ref in enumerate((mine_ref, got_ref)):
        base = jnp.where(core == part, 0, leaves)
        for c in range(chunks):

            def last(nodes, c=c, low_ref=low_ref, base=base):
                rows = [c * per + i for i in nodes]
                fars = [
                    jnp.dot(low_ref[n], basis[base + n], preferred_element_type=F32)
                    for n in rows
                ]
                for n, far in zip(rows, fars):
                    here = lanes(base + n)
                    total = near[:, here] + swap[:, here]
                    out[:, here] = total + noise[:, here] * vec[:, here].astype(F32) + far

            over_nodes(per, 8, last)
            piece = pl.ds(pl.multiple_of((base + c * per) * LEAF, wide), wide)
            send = pltpu.make_async_copy(
                out.at[:, piece], out_hbm.at[:, piece], sems.at[part * chunks + c]
            )
            send.start()
            sends.append(send)
    for send in sends:
        send.wait()


def swap_mask(value, mask):
    total = lax.axis_size("leaf") * lax.axis_size("sub")
    return lax.ppermute(value, ("leaf", "sub"), [(i, i ^ mask) for i in range(total)])


def after(value, anchor):
    return lax.optimization_barrier((value, anchor))[0]


def body(
    points, inv_scale, noise, vectors, leaf_basis, local_transfer, top_transfer,
    local_coupling, top_coupling, local_partners, top_partners, near_offsets, near_cols,
):
    subs = lax.axis_size("sub")
    count = lax.axis_size("leaf") * subs
    dev_levels = count.bit_length() - 1
    device = lax.axis_index("leaf") * subs + lax.axis_index("sub")
    core = lax.axis_index("vec")
    scale = jnp.concatenate([inv_scale, jnp.stack([device, core]).astype(F32)])
    size = vectors.shape[1]
    leaves = near_offsets.shape[0]
    slots = near_cols.shape[0]
    half = size // 2
    sds = jax.ShapeDtypeStruct
    scratch_blocks = [
        VMEM((PAIR, LEAF, LEAF), F32), VMEM((PAIR, LEAF, LEAF), F32),
        VMEM((PAIR, LEAF, LEAF), BF), VMEM((PAIR, LEAF, LEAF), BF),
    ]

    got = lax.ppermute(vectors, "vec", [(0, 1), (1, 0)])

    pack = pl.pallas_call(
        pack_kernel,
        name="pack",
        out_shape=sds((24, half), BF),
        in_specs=[sspec(), hspec(), hspec(), hspec()],
        out_specs=vspec(),
        scratch_shapes=[
            VMEM((3, half), F32), VMEM((PART, half), BF), VMEM((PART, half), BF),
            pltpu.SemaphoreType.DMA((3,)),
        ],
        compiler_params=params(8),
    )(scale, points, vectors, got)
    axes = ("leaf", "sub")
    left = lax.ppermute(pack, axes, [(i, i + 1) for i in range(count - 1)])
    right = lax.ppermute(pack, axes, [(i + 1, i) for i in range(count - 1)])

    moves_raw = jnp.transpose(local_transfer, (1, 2, 3, 0))
    part = leaves // 2
    coef, export, front, moves = pl.pallas_call(
        up_kernel,
        name="up",
        out_shape=(
            sds((2 * part - 1, 2 * ALL, 2 * RANK), BF), sds((EXPORT, 2 * ALL, 2 * RANK), BF),
            sds((1, EXPORT // 2, 2 * ALL, 2 * RANK), BF), sds((part, RANK, 2 * RANK), BF),
        ),
        in_specs=[sspec(), vspec(), hspec(), hspec()],
        out_specs=(vspec(),) * 4,
        scratch_shapes=[
            VMEM((part, RANK, LEAF), BF), VMEM(moves_raw.shape, BF),
            VMEM((leaves // 8, RANK * 8, 2 * RANK), F32),
            VMEM((part - 1, 2 * ALL, 2 * RANK), BF), pltpu.SemaphoreType.DMA((8,)),
        ],
        compiler_params=params(18),
        cost_estimate=pl.CostEstimate(flops=8 * 10**9, bytes_accessed=8 << 20, transcendentals=0),
    )(scale, pack, leaf_basis, moves_raw)
    from_core = lax.ppermute(export, "vec", [(0, 1), (1, 0)])
    pack, _ = lax.optimization_barrier((pack, export))
    first, second, row_feat, far_list, far_count = pl.pallas_call(
        near_local_kernel,
        name="near_local",
        out_shape=(
            sds((PART, size), F32), sds((PART, size), F32), sds((leaves, 32, LEAF), BF),
            sds((slots + PAD,), jnp.int32), sds((1,), jnp.int32),
        ),
        in_specs=[sspec()] * 3 + [vspec()] * 2,
        out_specs=(vspec(), vspec(), vspec(), sspec(), sspec()),
        scratch_shapes=[
            VMEM((leaves // 2 + 1, LEAF, 32), BF), VMEM((leaves // 2 + 1, 16, LEAF), BF),
            *scratch_blocks, SMEM((slots + PAD,), jnp.int32),
        ],
        compiler_params=params(22),
        cost_estimate=pl.CostEstimate(
            flops=36 * 10**9, bytes_accessed=8 << 20, transcendentals=190 * 2**17
        ),
    )(scale, near_offsets, near_cols, points, pack)

    from_core = after(from_core, far_list)
    near_pair = jnp.concatenate([front, from_core[None, 0 : EXPORT // 2]], axis=0)
    coef_late, near_pair = lax.optimization_barrier((coef, near_pair))
    from_next = swap_mask(near_pair, 1)
    ties_raw = jnp.transpose(local_coupling, (1, 2, 3, 0))
    mates = jnp.transpose(local_partners)
    local, ties = pl.pallas_call(
        couple_kernel,
        name="couple",
        out_shape=(
            sds((part - 1, ALL, 2 * RANK), F32), sds((EXPORT, RANK, 3 * RANK), BF),
        ),
        in_specs=[sspec()] * 2 + [vspec(), hspec()],
        out_specs=(vspec(),) * 2,
        scratch_shapes=[
            VMEM(ties_raw.shape, BF),
            VMEM((leaves // 4, RANK * 8, 2 * RANK), F32),
            VMEM((leaves // 4, RANK * 8, RANK), F32), pltpu.SemaphoreType.DMA((4,)),
        ],
        compiler_params=params(36),
        cost_estimate=pl.CostEstimate(flops=16 * 10**9, bytes_accessed=8 << 20, transcendentals=0),
    )(scale, mates, coef_late, ties_raw)

    first, _, from_next = lax.optimization_barrier((first, local, from_next))
    quad = jnp.concatenate([near_pair[:, 0:2], from_next[:, 0:2]], axis=0)
    from_far = [swap_mask(quad, mask) for mask in (2, 4, 6)]
    mine, other = pl.pallas_call(
        near_halo_kernel,
        name="near_halo",
        out_shape=(sds((PART, size), F32), sds((PART, size), F32)),
        in_specs=[sspec()] * 3 + [vspec()] * 5,
        out_specs=(vspec(), vspec()),
        scratch_shapes=[
            VMEM((PART, size), F32), VMEM((PART, size), F32),
            VMEM((leaves + 1, LEAF, 32), BF), VMEM((leaves + 1, 16, LEAF), BF),
            *scratch_blocks,
        ],
        compiler_params=params(26),
        cost_estimate=pl.CostEstimate(
            flops=20 * 10**9, bytes_accessed=8 << 20, transcendentals=60 * 2**17
        ),
    )(scale, far_list, far_count, row_feat, left, right, first, second)
    swapped = lax.ppermute(other, "vec", [(0, 1), (1, 0)])

    tops = export
    if dev_levels > SPAN:
        tops = jnp.concatenate(
            [export[None, 0:1], from_core[None, 0:1], from_next[:, 0:1]]
            + [part[:, 0:1] for part in from_far],
            axis=0,
        )
        for bit in range(SPAN, dev_levels):
            tops = jnp.concatenate([tops, swap_mask(tops, 2**bit)], axis=0)
    low_mine, low_other = pl.pallas_call(
        lambda *refs: down_kernel(dev_levels, *refs[:11], refs[11:14], *refs[14:]),
        name="down",
        out_shape=(sds((part, PART, RANK), BF), sds((part, PART, RANK), BF)),
        in_specs=[sspec()] * 3 + [vspec()] * 12,
        out_specs=(vspec(), vspec()),
        scratch_shapes=[
            VMEM((2 * 2**SPAN, EXPORT, 2 * ALL, 2 * RANK), BF),
            VMEM((part - 1, 2 * ALL, RANK), BF), VMEM((2 * count, 2 * ALL, RANK), BF),
        ],
        compiler_params=params(14),
        cost_estimate=pl.CostEstimate(flops=40 * 10**9, bytes_accessed=4 << 20, transcendentals=0),
    )(
        scale, mates, top_partners, top_transfer, top_coupling, ties, local, moves,
        export, from_core, from_next, *from_far, tops,
    )
    low_got = lax.ppermute(low_other, "vec", [(0, 1), (1, 0)])

    return pl.pallas_call(
        final_kernel,
        name="final",
        out_shape=sds((PART, size), F32),
        in_specs=[sspec()] + [vspec()] * 7,
        out_specs=hspec(),
        scratch_shapes=[VMEM((PART, size), F32), pltpu.SemaphoreType.DMA((4,))],
        compiler_params=params(10),
        cost_estimate=pl.CostEstimate(flops=2 * 10**9, bytes_accessed=4 << 20, transcendentals=0),
    )(scale, low_mine, low_got, leaf_basis, noise.reshape(1, size), vectors, mine, swapped)


def solution(mesh):
    return jax.shard_map(
        body,
        mesh=mesh,
        in_specs=(
            P("groups", ("leaf", "sub")),
            P("groups"),
            P(("groups", "leaf", "sub")),
            P(("groups", "vec"), ("leaf", "sub")),
            P(("groups", "leaf", "sub"), None, None),
            P(("groups", "leaf", "sub"), None, None, None),
            P("groups", None, None, None),
            P(("groups", "leaf", "sub"), None, None, None),
            P("groups", None, None, None),
            P(("groups", "leaf", "sub"), None),
            P("groups", None),
            P(("groups", "leaf", "sub")),
            P(("groups", "leaf", "sub")),
        ),
        out_specs=P(("groups", "vec"), ("leaf", "sub")),
        check_vma=False,
    )
```

```python
import functools
import math

import jax
import jax.numpy as jnp
from jax import lax
from jax.experimental import pallas as pl
from jax.experimental.pallas import tpu as pltpu
from jax.sharding import PartitionSpec as P

BF = jnp.bfloat16
F32 = jnp.float32
LEAF = 256
RANK = 64
SPAN = 3
PART = 8
ALL = 2 * PART
EXPORT = 2**SPAN
NEG_LOG2E = -1.0 / math.log(2.0)
ROOT3 = math.sqrt(3.0)
TINY = 1e-12
PAIR = 2
TURNS = 2
CODE_BITS = 10
CODE = 2**CODE_BITS
VMEM = pltpu.VMEM
SMEM = pltpu.SMEM
NT = (((1,), (1,)), ((), ()))


def vspec():
    return pl.BlockSpec(memory_space=pltpu.VMEM)


def sspec():
    return pl.BlockSpec(memory_space=pltpu.SMEM)


def hspec():
    return pl.BlockSpec(memory_space=pltpu.HBM)


def fetch(pairs, sems):
    copies = [
        pltpu.make_async_copy(source, target, sems.at[i])
        for i, (source, target) in enumerate(pairs)
    ]
    for copy in copies:
        copy.start()
    return copies


def params(mib):
    return pltpu.CompilerParams(vmem_limit_bytes=mib << 20)


def lanes(index):
    return pl.ds(pl.multiple_of(index * LEAF, LEAF), LEAF)


def whole(scalar):
    return scalar.astype(jnp.int32)


def coordinate_rows(raw, scale_ref):
    width = raw.shape[1]
    row = lax.broadcasted_iota(jnp.int32, (8, width), 0)
    scale = jnp.where(
        row == 0, scale_ref[0], jnp.where(row == 1, scale_ref[1], scale_ref[2])
    )
    full = jnp.concatenate([raw, jnp.zeros((5, width), F32)], axis=0)
    scaled = (full - 0.5) * (scale * ROOT3)
    scaled = jnp.where(row < 3, scaled, 0.0)
    high = scaled.astype(BF).astype(F32)
    rest = (scaled - high).astype(BF).astype(F32)
    return high + pltpu.roll(rest, 4, 0)


def norm_parts(rows):
    swapped = pltpu.roll(rows, 4, 0)
    norm = jnp.sum(rows * (rows + swapped), axis=0, keepdims=True)
    high = norm.astype(BF).astype(F32)
    rest = norm - high
    mid = rest.astype(BF).astype(F32)
    return swapped, high, mid, rest - mid


def row_features(rows):
    swapped, high, mid, low = norm_parts(rows)
    row = lax.broadcasted_iota(jnp.int32, rows.shape, 0)
    tail = jnp.where(
        row < 3,
        1.0,
        jnp.where(row == 3, high, jnp.where(row == 4, mid, jnp.where(row == 5, low, 0.0))),
    )
    return jnp.concatenate([rows, swapped, tail, jnp.zeros_like(rows)], axis=0).astype(BF)


def col_features(rows):
    _, high, mid, low = norm_parts(rows)
    row = lax.broadcasted_iota(jnp.int32, rows.shape, 0)
    tail = jnp.where(
        row == 0,
        high,
        jnp.where(row == 1, mid, jnp.where(row == 2, low, jnp.where(row < 6, 1.0, 0.0))),
    )
    both = -2.0 * rows
    return jnp.concatenate([both, both, tail, jnp.zeros_like(rows)], axis=0).T.astype(BF)


def matern(squared):
    squared = jnp.maximum(squared, TINY)
    dist = squared * lax.rsqrt(squared)
    return ((1.0 + dist) * jnp.exp2(dist * NEG_LOG2E)).astype(BF)


def pack_kernel(scale_ref, points_hbm, vec_hbm, got_hbm, out_ref, points, mine, got, sems):
    half = out_ref.shape[1]
    core = whole(scale_ref[4])
    there = pl.ds(pl.multiple_of(core * half, half), half)
    copies = fetch(
        [
            (points_hbm.at[:, there], points), (vec_hbm.at[:, there], mine),
            (got_hbm.at[:, there], got),
        ],
        sems,
    )
    for copy in copies:
        copy.wait()

    def step(i, _):
        here = pl.ds(pl.multiple_of(i * 2048, 2048), 2048)
        rows = coordinate_rows(points[:, here], scale_ref)
        one, two = mine[:, here].astype(F32), got[:, here].astype(F32)
        first, second = jnp.where(core == 0, one, two), jnp.where(core == 0, two, one)
        out_ref[:, here] = jnp.concatenate([first, second, rows], axis=0).astype(BF)
        return 0

    lax.fori_loop(0, half // 2048, step, 0)


def plan_kernel(scale_ref, offs_ref, cols_ref, out_ref):
    device, half_id = whole(scale_ref[3]), whole(scale_ref[4])
    leaves = offs_ref.shape[1]
    slots = cols_ref.shape[1]
    room = out_ref.shape[1]
    half = leaves // 2
    half_bits = half.bit_length() - 1
    begins = jnp.broadcast_to(offs_ref[...].astype(F32), (8, leaves)).T[:, 0:1]
    slot = lax.broadcasted_iota(jnp.int32, (leaves, slots), 1).astype(F32)
    row = jnp.sum(jnp.where(begins <= slot, 1.0, 0.0), axis=0, keepdims=True) - 1.0
    first = jnp.sum(jnp.where(begins == slot, 1.0, 0.0), axis=0, keepdims=True)
    place = cols_ref[...] - (device * leaves - leaves + half_id * half)
    block = place >> half_bits
    own = jnp.where(block == 2, 1.0 - first, 0.0)
    far = jnp.where((block & 3) == 0, 1.0, 0.0)
    kinds = jnp.concatenate([own, far, jnp.zeros((6, slots), F32)], axis=0)
    earlier = lax.broadcasted_iota(jnp.int32, (slots, slots), 0)
    later = lax.broadcasted_iota(jnp.int32, (slots, slots), 1)
    upto = jnp.where(earlier <= later, 1.0, 0.0).astype(BF)
    rank = jnp.dot(kinds.astype(BF), upto, preferred_element_type=F32)
    turned = rank.T
    target = lax.broadcasted_iota(jnp.int32, (slots, room), 1).astype(F32) + 1.0
    at = lax.broadcasted_iota(jnp.int32, (1, room), 1).astype(F32)
    upper, lower = (place >> 4).astype(F32), (place & 15).astype(F32)
    lists = []
    for kind, (mask, shift, spare) in enumerate(
        ((own, float(leaves), float(half)), (far, 0.0, 8.0 * half))
    ):
        parts = jnp.concatenate(
            [row * mask, upper * mask, lower * mask, jnp.zeros((5, slots), F32)], axis=0
        )
        hits = jnp.where(turned[:, kind : kind + 1] == target, 1.0, 0.0).astype(BF)
        got = jnp.dot(parts.astype(BF), hits, preferred_element_type=F32)
        code = got[0:1] * float(CODE) + got[1:2] * 16.0 + got[2:3] - shift
        total = rank[kind : kind + 1, slots - 1 : slots]
        lists.append((jnp.where(at < total, code, spare), total))
    out_ref[...] = jnp.concatenate(
        [
            lists[0][0], lists[1][0],
            jnp.broadcast_to(lists[0][1], (1, room)), jnp.broadcast_to(lists[1][1], (1, room)),
            jnp.zeros((4, room), F32),
        ],
        axis=0,
    ).astype(jnp.int32)


def block_loop(kind, place, plan_ref, row_ref, col_ref, val_ref, sums, s0, s1, k0, k1):
    def accumulate(first, kern):
        for q in range(PAIR):
            code = plan_ref[kind, first + q]
            here = lanes(code >> CODE_BITS)
            part = jnp.dot(
                val_ref[place(code & (CODE - 1))], kern[q], preferred_element_type=F32
            )
            sums[0][:, here] += part[:PART]
            sums[1][:, here] += part[PART:]

    def distance(first, out):
        for q in range(PAIR):
            code = plan_ref[kind, first + q]
            out[q] = jnp.dot(
                col_ref[place(code & (CODE - 1))],
                row_ref[code >> CODE_BITS],
                preferred_element_type=F32,
            )

    def evaluate(squared, kern):
        for q in range(PAIR):
            kern[q] = matern(squared[q])

    k1[...] = jnp.zeros_like(k1)
    distance(0, s0)

    def step(it, _):
        for turn in range(TURNS):
            first = (it * TURNS + turn) * 2 * PAIR
            accumulate(jnp.maximum(first - PAIR, 0), k1)
            distance(first + PAIR, s1)
            evaluate(s0, k0)
            accumulate(first, k0)
            distance(first + 2 * PAIR, s0)
            evaluate(s1, k1)
        return 0

    count = plan_ref[2 + kind, 0]
    turns = (count + TURNS * 2 * PAIR - 1) // (TURNS * 2 * PAIR)
    lax.fori_loop(0, turns, step, 0)
    accumulate(jnp.maximum(turns * TURNS * 2 * PAIR - PAIR, 0), k1)


def diagonal_loop(first_leaf, count, row_ref, col_ref, val_ref, sums, s0, s1, k0, k1):
    mid = LEAF // 2

    def distance(first, out):
        for q in range(PAIR):
            col = jnp.minimum(first + q, count - 1)
            rows = row_ref[first_leaf + col]
            out[q, :mid] = jnp.dot(col_ref[col, :mid], rows, preferred_element_type=F32)
            out[q, mid:, mid:] = jnp.dot(
                col_ref[col, mid:], rows[:, mid:], preferred_element_type=F32
            )

    def evaluate(squared, kern):
        for q in range(PAIR):
            kern[q, :mid] = matern(squared[q, :mid])
            kern[q, mid:, mid:] = matern(squared[q, mid:, mid:])

    def accumulate(first, kern):
        for q in range(PAIR):
            col = jnp.maximum(first + q, 0)
            values = val_ref[col]
            part = jnp.dot(values[:, :mid], kern[q, :mid], preferred_element_type=F32)
            left = mul_nt(values[:, mid:], kern[q, :mid, mid:])
            right = jnp.dot(values[:, mid:], kern[q, mid:, mid:], preferred_element_type=F32)
            part = part + jnp.concatenate([left, right], axis=1)
            here = lanes(first_leaf + col)
            sums[0][:, here] += part[:PART]
            sums[1][:, here] += part[PART:]

    k1[...] = jnp.zeros_like(k1)
    distance(0, s0)

    def step(it, _):
        for turn in range(TURNS):
            first = (it * TURNS + turn) * 2 * PAIR
            accumulate(first - PAIR, k1)
            distance(first + PAIR, s1)
            evaluate(s0, k0)
            accumulate(first, k0)
            distance(first + 2 * PAIR, s0)
            evaluate(s1, k1)
        return 0

    lax.fori_loop(0, count // (TURNS * 2 * PAIR), step, 0)
    accumulate(count - PAIR, k1)


def load_columns(pack_ref, base, count, col_ref, val_ref):
    def step(i, _):
        for q in range(4):
            leaf = i * 4 + q
            val_ref[base + leaf] = pack_ref[0:16, lanes(leaf)]
            col_ref[base + leaf] = col_features(pack_ref[16:24, lanes(leaf)].astype(F32))
        return 0

    lax.fori_loop(0, count // 4, step, 0)


def near_local_kernel(
    scale_ref, plan_ref, points_ref, pack_ref,
    mine_ref, other_ref, row_ref,
    col_ref, val_ref, s0, s1, k0, k1,
):
    half_id = whole(scale_ref[4])
    leaves = row_ref.shape[0]
    half = leaves // 2

    def rows_step(i, _):
        for q in range(4):
            leaf = i * 4 + q
            row_ref[leaf] = row_features(coordinate_rows(points_ref[:, lanes(leaf)], scale_ref))
            mine_ref[:, lanes(leaf)] = jnp.zeros((PART, LEAF), F32)
            other_ref[:, lanes(leaf)] = jnp.zeros((PART, LEAF), F32)
        return 0

    lax.fori_loop(0, leaves // 4, rows_step, 0)
    load_columns(pack_ref, 0, half, col_ref, val_ref)
    val_ref[half] = jnp.zeros((16, LEAF), BF)
    col_ref[half] = jnp.zeros(col_ref.shape[1:], BF)
    sums = (mine_ref, other_ref)
    diagonal_loop(half_id * half, half, row_ref, col_ref, val_ref, sums, s0, s1, k0, k1)
    block_loop(0, lambda c: c, plan_ref, row_ref, col_ref, val_ref, sums, s0, s1, k0, k1)


def near_halo_kernel(
    scale_ref, plan_ref, row_ref, left_ref, right_ref, first_in, second_in,
    mine_ref, other_ref,
    first, second, col_ref, val_ref, s0, s1, k0, k1,
):
    core = whole(scale_ref[4])
    half = left_ref.shape[1] // LEAF
    bits = half.bit_length() - 1
    count = plan_ref[3, 0]

    def place(code):
        return (code & (half - 1)) | ((code >> (bits + 2)) << bits)

    def load(i, _):
        for q in range(4):
            code = plan_ref[1, i * 4 + q] & (CODE - 1)
            here = lanes(code & (half - 1))
            after = code >= 4 * half
            values = jnp.where(after, right_ref[0:16, here], left_ref[0:16, here])
            rows = jnp.where(after, right_ref[16:24, here], left_ref[16:24, here])
            val_ref[place(code)] = values
            col_ref[place(code)] = col_features(rows.astype(F32))
        return 0

    first[...] = first_in[...]
    second[...] = second_in[...]
    lax.fori_loop(0, (count + 3) // 4, load, 0)
    val_ref[2 * half] = jnp.zeros((16, LEAF), BF)
    col_ref[2 * half] = jnp.zeros(col_ref.shape[1:], BF)
    sums = (first, second)
    block_loop(1, place, plan_ref, row_ref, col_ref, val_ref, sums, s0, s1, k0, k1)

    @pl.when(core == 0)
    def _():
        mine_ref[...] = first[...]
        other_ref[...] = second[...]

    @pl.when(core == 1)
    def _():
        mine_ref[...] = second[...]
        other_ref[...] = first[...]


def split_parts(value):
    high = value.astype(BF).astype(F32)
    return jnp.concatenate([high, value - high], axis=0).astype(BF)


def join_parts(value):
    return value[0:ALL] + value[ALL : 2 * ALL]


def mul_nt(left, right):
    return lax.dot_general(left, right, NT, preferred_element_type=F32)


def over_nodes(count, unroll, work):
    group = min(unroll, count)
    if count == group:
        work([jnp.int32(i) for i in range(count)])
        return

    def step(i, _):
        work([i * group + q for q in range(group)])
        return 0

    lax.fori_loop(0, count // group, step, 0)


def store_turned(flat, r, block):
    turned = block.T
    count = turned.shape[0] // 8
    width = turned.shape[1]
    rows = pl.ds(pl.multiple_of(r * 8, 8), 8)
    flat[0:count, rows] = turned[: count * 8].reshape(count, 8, width)
    rest = turned.shape[0] - count * 8
    flat[count, pl.ds(pl.multiple_of(r * 8, 8), rest)] = turned[count * 8 :]


def load_node(flat, node):
    return flat[node >> 3, pl.ds(node & 7, RANK, stride=8)].astype(BF)


def side_by_side(first, second):
    return jnp.concatenate([first, second], axis=1)


def doubled(pair):
    low = lax.broadcasted_iota(jnp.int32, pair.shape, 1) < RANK
    turned = pltpu.roll(pair, RANK, 1)
    return jnp.where(low, pair, turned), jnp.where(low, turned, pair)


def up_kernel(
    scale_ref, pack_ref, basis_hbm, raw_hbm, coef_ref, export_ref, front_ref, move_ref,
    basis_ref, raw_ref, flat, pairs, sems,
):
    core = whole(scale_ref[4])
    leaves = basis_ref.shape[0]
    levels = leaves.bit_length() - 1
    chunks = 4
    per = leaves // chunks
    deep = RANK // chunks
    copies = fetch(
        [
            pair
            for c in range(chunks)
            for pair in (
                (
                    basis_hbm.at[pl.ds(core * leaves + c * per, per)],
                    basis_ref.at[c * per : (c + 1) * per],
                ),
                (
                    raw_hbm.at[:, c * deep : (c + 1) * deep],
                    raw_ref.at[:, c * deep : (c + 1) * deep],
                ),
            )
        ],
        sems,
    )

    def keep(parent, first, second):
        pair = side_by_side(first, second)
        pairs[parent] = split_parts(pair)
        one, two = doubled(pair)
        coef_ref[2 * parent + 1] = split_parts(one)
        coef_ref[2 * parent + 2] = split_parts(two)

    def leaf_step(it, _):
        outs = []
        for q in range(8):
            leaf = it * 8 + q
            outs.append(mul_nt(pack_ref[0:ALL, lanes(leaf)], basis_ref[leaf]))
        for q in range(8):
            r = it * 8 + q
            block = jnp.concatenate([raw_ref[0, r], raw_ref[1, r]], axis=0).astype(F32)
            store_turned(flat, r, block)
        for q in range(4):
            keep(leaves // 2 - 1 + it * 4 + q, outs[2 * q], outs[2 * q + 1])
        return 0

    for c in range(chunks):
        for copy in copies[2 * c : 2 * c + 2]:
            copy.wait()
        lax.fori_loop(c * per // 8, (c + 1) * per // 8, leaf_step, 0)
    root_move = load_node(flat, 0)
    move_ref[leaves - 1] = root_move
    for depth in range(levels - 1, 0, -1):
        first = 2**depth - 1
        above = 2 ** (depth - 1) - 1
        start = 2 ** (depth + 1) - 1 + core * 2**depth

        def work(nodes, first=first, above=above, start=start):
            outs = []
            for j in nodes:
                for c in range(2):
                    move = load_node(flat, start + 2 * j + c)
                    move_ref[first + 2 * j + c] = move
                    outs.append(mul_nt(pairs[first + 2 * j + c], move))
            for j, i in enumerate(nodes):
                keep(above + i, join_parts(outs[2 * j]), join_parts(outs[2 * j + 1]))

        over_nodes(2 ** (depth - 1), 8, work)
    move = load_node(flat, 1 + core)
    move_ref[0] = move
    crown = join_parts(mul_nt(pairs[0], move))
    crown = split_parts(side_by_side(crown, crown))
    coef_ref[0] = crown
    side = lax.broadcasted_iota(jnp.int32, crown.shape, 1) // RANK
    root = join_parts(mul_nt(jnp.where(side == core, crown.astype(F32), 0.0).astype(BF), root_move))
    export_ref[0] = split_parts(side_by_side(root, root))
    export_ref[1:EXPORT] = coef_ref[0 : EXPORT - 1]
    front_ref[0] = export_ref[0 : EXPORT // 2]


def joint(first, second, third):
    return jnp.concatenate([first, second, third], axis=1)


def couple_kernel(
    scale_ref, partners_ref, coef_ref, raw_hbm, local_ref, tie_ref, raw_ref, wide, thin, sems,
):
    device, core = whole(scale_ref[3]), whole(scale_ref[4])
    levels = (raw_ref.shape[3] + 1).bit_length() - 2
    chunks = 4
    deep = RANK // chunks
    copies = fetch(
        [
            (raw_hbm.at[:, c * deep : (c + 1) * deep], raw_ref.at[:, c * deep : (c + 1) * deep])
            for c in range(chunks)
        ],
        sems,
    )
    low = lax.broadcasted_iota(jnp.int32, (2 * ALL, 2 * RANK), 1) < RANK

    def turn(i, _):
        for q in range(8):
            r = i * 8 + q
            block = jnp.concatenate([raw_ref[0, r], raw_ref[1, r]], axis=0).astype(F32)
            store_turned(wide, r, block)
            store_turned(thin, r, raw_ref[2, r].astype(F32))
        return 0

    for c in range(chunks):
        copies[c].wait()
        lax.fori_loop(c * deep // 8, (c + 1) * deep // 8, turn, 0)

    def tie(node):
        return jnp.concatenate([load_node(wide, node), load_node(thin, node)], axis=1)

    tie_ref[0] = tie(0)
    for depth in range(1, SPAN + 1):
        for i in range(2 ** (depth - 1)):
            tie_ref[2 ** (depth - 1) + i] = tie(2**depth - 1 + core * 2 ** (depth - 1) + i)
    for depth in range(SPAN + 1, levels + 1):
        half = 2 ** (depth - 1)
        above = half // 2 - 1
        start = 2**depth - 1 + core * half
        shift = half - 1 - device * 2**depth - core * half

        def work(nodes, above=above, start=start, shift=shift):
            outs = []
            for j in nodes:
                for c in range(2):
                    node = start + 2 * j + c
                    mates = [coef_ref[partners_ref[f, node] + shift] for f in range(3)]
                    left = jnp.concatenate(
                        [jnp.where(low, mates[0], mates[1]), mates[2][:, :RANK]], axis=1
                    )
                    outs.append(mul_nt(left, tie(node)))
            for j, i in enumerate(nodes):
                local_ref[above + i] = side_by_side(
                    join_parts(outs[2 * j]), join_parts(outs[2 * j + 1])
                )

        over_nodes(half // 2, 8, work)


def down_kernel(
    dev_levels, scale_ref, partners_ref, top_partners_ref, top_e, top_b, tie_ref,
    local_ref, move_ref, own_ref, core_ref, next_ref, far_refs, tops_ref, mine_ref, other_ref,
    gather_ref, down, tree,
):
    device, core = whole(scale_ref[3]), whole(scale_ref[4])
    self_id = 2 * device + core
    gather_ref[0] = own_ref[...]
    gather_ref[1] = core_ref[...]
    gather_ref[2:4, 0:4] = next_ref[...]
    for i, far_ref in enumerate(far_refs):
        gather_ref[4 * i + 4 : 4 * i + 8, 0:2] = far_ref[...]
    root_ref = gather_ref if dev_levels == SPAN else tops_ref
    leaves = mine_ref.shape[0]
    levels = leaves.bit_length() - 1
    count = 2**dev_levels

    def roots(nodes):
        for i in nodes:
            parts = join_parts(root_ref[(2 * i) ^ self_id, 0].astype(F32)) + join_parts(
                root_ref[(2 * i + 1) ^ self_id, 0].astype(F32)
            )
            tree[count + i] = split_parts(parts[:, :RANK])

    over_nodes(count, 8, roots)
    for level in range(dev_levels - 1, 1, -1):

        def work(nodes, level=level):
            outs = []
            for i in nodes:
                row = 2**level - 4 + i
                kids = [tree[2 ** (level + 1) + 2 * i + c] for c in range(2)]
                outs.append(mul_nt(kids[0], top_e[row, 0]) + mul_nt(kids[1], top_e[row, 1]))
            for i, out in zip(nodes, outs):
                tree[2**level + i] = split_parts(join_parts(out))

        over_nodes(2**level, 4, work)

    mates = [tree[count + partners_ref[f, 0]] for f in range(3)]
    shallow = [join_parts(mul_nt(joint(*mates), tie_ref[0]))]
    for depth in range(1, SPAN + 1):
        half = 2 ** (depth - 1)
        for i in range(half):
            node = 2**depth - 1 + core * half + i
            picks = []
            for f in range(3):
                mate = partners_ref[f, node]
                at = ((mate >> (depth - 1)) ^ self_id) & (2 * 2**SPAN - 1)
                picks.append(gather_ref[at, half + (mate & (half - 1))][:, :RANK])
            shallow.append(join_parts(mul_nt(joint(*picks), tie_ref[half + i])))

    pushed = jnp.zeros((ALL, RANK), F32)
    for level in range(2, dev_levels):
        node = device >> (dev_levels - level)
        row = 2**level - 4 + node
        side = device >> (dev_levels - level - 1) & 1
        parts = sum(
            mul_nt(tree[2**level + top_partners_ref[row, f]], top_b[row, f]) for f in range(3)
        )
        here = split_parts(join_parts(parts) + pushed)
        pushed = join_parts(jnp.dot(here, top_e[row, side], preferred_element_type=F32))

    root = split_parts(shallow[0] + pushed)
    both = join_parts(jnp.dot(root, move_ref[leaves - 1], preferred_element_type=F32))
    down[0] = split_parts(shallow[1] + jnp.where(core == 0, both[:, :RANK], both[:, RANK:]))
    for depth in range(levels):
        first = 2**depth - 1

        def work(nodes, depth=depth, first=first):
            outs = [
                jnp.dot(down[first + i], move_ref[first + i], preferred_element_type=F32)
                for i in nodes
            ]
            for i, out in zip(nodes, outs):
                node = first + i
                if depth + 2 <= SPAN:
                    kid = 2 ** (depth + 1) + 2 * i
                    base = side_by_side(shallow[kid], shallow[kid + 1])
                else:
                    base = local_ref[node]
                pair = base + join_parts(out)
                if depth == levels - 1:
                    for c in range(2):
                        value = pair[:, c * RANK : (c + 1) * RANK]
                        one, two = value[:PART], value[PART:]
                        mine_ref[2 * i + c] = jnp.where(core == 0, one, two).astype(BF)
                        other_ref[2 * i + c] = jnp.where(core == 0, two, one).astype(BF)
                else:
                    down[2 * node + 1] = split_parts(pair[:, :RANK])
                    down[2 * node + 2] = split_parts(pair[:, RANK:])

        if depth < SPAN:
            work(list(range(2**depth)))
        else:
            over_nodes(2**depth, 8, work)


def final_kernel(
    scale_ref, mine_ref, got_ref, basis, noise, vec, near, swap, out_hbm, out, sems
):
    core = whole(scale_ref[4])
    leaves = mine_ref.shape[0]
    chunks = 2
    per = leaves // chunks
    wide = per * LEAF
    sends = []
    for part, low_ref in enumerate((mine_ref, got_ref)):
        base = jnp.where(core == part, 0, leaves)
        for c in range(chunks):

            def last(nodes, c=c, low_ref=low_ref, base=base):
                rows = [c * per + i for i in nodes]
                fars = [
                    jnp.dot(low_ref[n], basis[base + n], preferred_element_type=F32)
                    for n in rows
                ]
                for n, far in zip(rows, fars):
                    here = lanes(base + n)
                    total = near[:, here] + swap[:, here]
                    out[:, here] = total + noise[:, here] * vec[:, here].astype(F32) + far

            over_nodes(per, 8, last)
            piece = pl.ds(pl.multiple_of((base + c * per) * LEAF, wide), wide)
            send = pltpu.make_async_copy(
                out.at[:, piece], out_hbm.at[:, piece], sems.at[part * chunks + c]
            )
            send.start()
            sends.append(send)
    for send in sends:
        send.wait()


def swap_mask(value, mask):
    total = lax.axis_size("leaf") * lax.axis_size("sub")
    return lax.ppermute(value, ("leaf", "sub"), [(i, i ^ mask) for i in range(total)])


def after(value, anchor):
    return lax.optimization_barrier((value, anchor))[0]


def body(
    points, inv_scale, noise, vectors, leaf_basis, local_transfer, top_transfer,
    local_coupling, top_coupling, local_partners, top_partners, near_offsets, near_cols,
):
    subs = lax.axis_size("sub")
    count = lax.axis_size("leaf") * subs
    dev_levels = count.bit_length() - 1
    device = lax.axis_index("leaf") * subs + lax.axis_index("sub")
    core = lax.axis_index("vec")
    scale = jnp.concatenate([inv_scale, jnp.stack([device, core]).astype(F32)])
    size = vectors.shape[1]
    leaves = near_offsets.shape[0]
    slots = near_cols.shape[0]
    half = size // 2
    sds = jax.ShapeDtypeStruct
    scratch_blocks = [
        VMEM((PAIR, LEAF, LEAF), F32), VMEM((PAIR, LEAF, LEAF), F32),
        VMEM((PAIR, LEAF, LEAF), BF), VMEM((PAIR, LEAF, LEAF), BF),
    ]

    got = lax.ppermute(vectors, "vec", [(0, 1), (1, 0)])

    plan = pl.pallas_call(
        plan_kernel,
        name="plan",
        out_shape=sds((8, slots + 128), jnp.int32),
        in_specs=[sspec(), vspec(), vspec()],
        out_specs=vspec(),
        compiler_params=params(16),
    )(scale, near_offsets.reshape(1, leaves), near_cols.reshape(1, slots))

    pack = pl.pallas_call(
        pack_kernel,
        name="pack",
        out_shape=sds((24, half), BF),
        in_specs=[sspec(), hspec(), hspec(), hspec()],
        out_specs=vspec(),
        scratch_shapes=[
            VMEM((3, half), F32), VMEM((PART, half), BF), VMEM((PART, half), BF),
            pltpu.SemaphoreType.DMA((3,)),
        ],
        compiler_params=params(8),
    )(scale, points, vectors, got)
    axes = ("leaf", "sub")
    left = lax.ppermute(pack, axes, [(i, i + 1) for i in range(count - 1)])
    right = lax.ppermute(pack, axes, [(i + 1, i) for i in range(count - 1)])

    moves_raw = jnp.transpose(local_transfer, (1, 2, 3, 0))
    part = leaves // 2
    coef, export, front, moves = pl.pallas_call(
        up_kernel,
        name="up",
        out_shape=(
            sds((2 * part - 1, 2 * ALL, 2 * RANK), BF), sds((EXPORT, 2 * ALL, 2 * RANK), BF),
            sds((1, EXPORT // 2, 2 * ALL, 2 * RANK), BF), sds((part, RANK, 2 * RANK), BF),
        ),
        in_specs=[sspec(), vspec(), hspec(), hspec()],
        out_specs=(vspec(),) * 4,
        scratch_shapes=[
            VMEM((part, RANK, LEAF), BF), VMEM(moves_raw.shape, BF),
            VMEM((leaves // 8, RANK * 8, 2 * RANK), F32),
            VMEM((part - 1, 2 * ALL, 2 * RANK), BF), pltpu.SemaphoreType.DMA((8,)),
        ],
        compiler_params=params(18),
        cost_estimate=pl.CostEstimate(flops=8 * 10**9, bytes_accessed=8 << 20, transcendentals=0),
    )(scale, pack, leaf_basis, moves_raw)
    from_core = lax.ppermute(export, "vec", [(0, 1), (1, 0)])
    pack, _ = lax.optimization_barrier((pack, export))
    first, second, row_feat = pl.pallas_call(
        near_local_kernel,
        name="near_local",
        out_shape=(
            sds((PART, size), F32), sds((PART, size), F32), sds((leaves, 32, LEAF), BF),
        ),
        in_specs=[sspec()] * 2 + [vspec()] * 2,
        out_specs=(vspec(), vspec(), vspec()),
        scratch_shapes=[
            VMEM((leaves // 2 + 1, LEAF, 32), BF), VMEM((leaves // 2 + 1, 16, LEAF), BF),
            *scratch_blocks,
        ],
        compiler_params=params(22),
        cost_estimate=pl.CostEstimate(
            flops=36 * 10**9, bytes_accessed=8 << 20, transcendentals=190 * 2**17
        ),
    )(scale, plan, points, pack)

    from_core = after(from_core, first)
    near_pair = jnp.concatenate([front, from_core[None, 0 : EXPORT // 2]], axis=0)
    coef_late, near_pair = lax.optimization_barrier((coef, near_pair))
    from_next = swap_mask(near_pair, 1)
    ties_raw = jnp.transpose(local_coupling, (1, 2, 3, 0))
    mates = jnp.transpose(local_partners)
    local, ties = pl.pallas_call(
        couple_kernel,
        name="couple",
        out_shape=(
            sds((part - 1, ALL, 2 * RANK), F32), sds((EXPORT, RANK, 3 * RANK), BF),
        ),
        in_specs=[sspec()] * 2 + [vspec(), hspec()],
        out_specs=(vspec(),) * 2,
        scratch_shapes=[
            VMEM(ties_raw.shape, BF),
            VMEM((leaves // 4, RANK * 8, 2 * RANK), F32),
            VMEM((leaves // 4, RANK * 8, RANK), F32), pltpu.SemaphoreType.DMA((4,)),
        ],
        compiler_params=params(36),
        cost_estimate=pl.CostEstimate(flops=16 * 10**9, bytes_accessed=8 << 20, transcendentals=0),
    )(scale, mates, coef_late, ties_raw)

    first, _, from_next = lax.optimization_barrier((first, local, from_next))
    quad = jnp.concatenate([near_pair[:, 0:2], from_next[:, 0:2]], axis=0)
    from_far = [swap_mask(quad, mask) for mask in (2, 4, 6)]
    mine, other = pl.pallas_call(
        near_halo_kernel,
        name="near_halo",
        out_shape=(sds((PART, size), F32), sds((PART, size), F32)),
        in_specs=[sspec()] * 2 + [vspec()] * 5,
        out_specs=(vspec(), vspec()),
        scratch_shapes=[
            VMEM((PART, size), F32), VMEM((PART, size), F32),
            VMEM((leaves + 1, LEAF, 32), BF), VMEM((leaves + 1, 16, LEAF), BF),
            *scratch_blocks,
        ],
        compiler_params=params(26),
        cost_estimate=pl.CostEstimate(
            flops=20 * 10**9, bytes_accessed=8 << 20, transcendentals=60 * 2**17
        ),
    )(scale, plan, row_feat, left, right, first, second)
    swapped = lax.ppermute(other, "vec", [(0, 1), (1, 0)])

    tops = export
    if dev_levels > SPAN:
        tops = jnp.concatenate(
            [export[None, 0:1], from_core[None, 0:1], from_next[:, 0:1]]
            + [part[:, 0:1] for part in from_far],
            axis=0,
        )
        for bit in range(SPAN, dev_levels):
            tops = jnp.concatenate([tops, swap_mask(tops, 2**bit)], axis=0)
    low_mine, low_other = pl.pallas_call(
        lambda *refs: down_kernel(dev_levels, *refs[:11], refs[11:14], *refs[14:]),
        name="down",
        out_shape=(sds((part, PART, RANK), BF), sds((part, PART, RANK), BF)),
        in_specs=[sspec()] * 3 + [vspec()] * 12,
        out_specs=(vspec(), vspec()),
        scratch_shapes=[
            VMEM((2 * 2**SPAN, EXPORT, 2 * ALL, 2 * RANK), BF),
            VMEM((part - 1, 2 * ALL, RANK), BF), VMEM((2 * count, 2 * ALL, RANK), BF),
        ],
        compiler_params=params(14),
        cost_estimate=pl.CostEstimate(flops=40 * 10**9, bytes_accessed=4 << 20, transcendentals=0),
    )(
        scale, mates, top_partners, top_transfer, top_coupling, ties, local, moves,
        export, from_core, from_next, *from_far, tops,
    )
    low_got = lax.ppermute(low_other, "vec", [(0, 1), (1, 0)])

    return pl.pallas_call(
        final_kernel,
        name="final",
        out_shape=sds((PART, size), F32),
        in_specs=[sspec()] + [vspec()] * 7,
        out_specs=hspec(),
        scratch_shapes=[VMEM((PART, size), F32), pltpu.SemaphoreType.DMA((4,))],
        compiler_params=params(10),
        cost_estimate=pl.CostEstimate(flops=2 * 10**9, bytes_accessed=4 << 20, transcendentals=0),
    )(scale, low_mine, low_got, leaf_basis, noise.reshape(1, size), vectors, mine, swapped)


def solution(mesh):
    return jax.shard_map(
        body,
        mesh=mesh,
        in_specs=(
            P("groups", ("leaf", "sub")),
            P("groups"),
            P(("groups", "leaf", "sub")),
            P(("groups", "vec"), ("leaf", "sub")),
            P(("groups", "leaf", "sub"), None, None),
            P(("groups", "leaf", "sub"), None, None, None),
            P("groups", None, None, None),
            P(("groups", "leaf", "sub"), None, None, None),
            P("groups", None, None, None),
            P(("groups", "leaf", "sub"), None),
            P("groups", None),
            P(("groups", "leaf", "sub")),
            P(("groups", "leaf", "sub")),
        ),
        out_specs=P(("groups", "vec"), ("leaf", "sub")),
        check_vma=False,
    )
```

```python
import functools
import math

import jax
import jax.numpy as jnp
from jax import lax
from jax.experimental import pallas as pl
from jax.experimental.pallas import tpu as pltpu
from jax.sharding import PartitionSpec as P

BF = jnp.bfloat16
F32 = jnp.float32
LEAF = 256
RANK = 64
SPAN = 3
PART = 8
ALL = 2 * PART
EXPORT = 2**SPAN
NEG_LOG2E = -1.0 / math.log(2.0)
ROOT3 = math.sqrt(3.0)
TINY = 1e-12
PAIR = 2
TURNS = 2
CODE_BITS = 10
CODE = 2**CODE_BITS
VMEM = pltpu.VMEM
SMEM = pltpu.SMEM
NT = (((1,), (1,)), ((), ()))


def vspec():
    return pl.BlockSpec(memory_space=pltpu.VMEM)


def sspec():
    return pl.BlockSpec(memory_space=pltpu.SMEM)


def hspec():
    return pl.BlockSpec(memory_space=pltpu.HBM)


def params(mib):
    return pltpu.CompilerParams(vmem_limit_bytes=mib << 20)


def lanes(index):
    return pl.ds(pl.multiple_of(index * LEAF, LEAF), LEAF)


def whole(scalar):
    return scalar.astype(jnp.int32)


def coordinate_rows(raw, scale_ref):
    width = raw.shape[1]
    row = lax.broadcasted_iota(jnp.int32, (8, width), 0)
    scale = jnp.where(
        row == 0, scale_ref[0], jnp.where(row == 1, scale_ref[1], scale_ref[2])
    )
    full = jnp.concatenate([raw, jnp.zeros((5, width), F32)], axis=0)
    scaled = (full - 0.5) * (scale * ROOT3)
    scaled = jnp.where(row < 3, scaled, 0.0)
    high = scaled.astype(BF).astype(F32)
    rest = (scaled - high).astype(BF).astype(F32)
    return high + pltpu.roll(rest, 4, 0)


def norm_parts(rows):
    swapped = pltpu.roll(rows, 4, 0)
    norm = jnp.sum(rows * (rows + swapped), axis=0, keepdims=True)
    high = norm.astype(BF).astype(F32)
    rest = norm - high
    mid = rest.astype(BF).astype(F32)
    return swapped, high, mid, rest - mid


def row_features(rows):
    swapped, high, mid, low = norm_parts(rows)
    row = lax.broadcasted_iota(jnp.int32, rows.shape, 0)
    tail = jnp.where(
        row < 3,
        1.0,
        jnp.where(row == 3, high, jnp.where(row == 4, mid, jnp.where(row == 5, low, 0.0))),
    )
    return jnp.concatenate([rows, swapped, tail, jnp.zeros_like(rows)], axis=0).astype(BF)


def col_features(rows):
    _, high, mid, low = norm_parts(rows)
    row = lax.broadcasted_iota(jnp.int32, rows.shape, 0)
    tail = jnp.where(
        row == 0,
        high,
        jnp.where(row == 1, mid, jnp.where(row == 2, low, jnp.where(row < 6, 1.0, 0.0))),
    )
    both = -2.0 * rows
    return jnp.concatenate([both, both, tail, jnp.zeros_like(rows)], axis=0).T.astype(BF)


def matern(squared):
    squared = jnp.maximum(squared, TINY)
    dist = squared * lax.rsqrt(squared)
    return ((1.0 + dist) * jnp.exp2(dist * NEG_LOG2E)).astype(BF)


def pack_kernel(scale_ref, points, mine, got, out_ref):
    half = out_ref.shape[1]
    core = whole(scale_ref[4])

    def step(i, _):
        here = pl.ds(pl.multiple_of(i * 2048, 2048), 2048)
        there = pl.ds(pl.multiple_of(core * half + i * 2048, 2048), 2048)
        rows = coordinate_rows(points[:, there], scale_ref)
        one, two = mine[:, there].astype(F32), got[:, there].astype(F32)
        first, second = jnp.where(core == 0, one, two), jnp.where(core == 0, two, one)
        out_ref[:, here] = jnp.concatenate([first, second, rows], axis=0).astype(BF)
        return 0

    lax.fori_loop(0, half // 2048, step, 0)


def plan_kernel(scale_ref, offs_ref, cols_ref, out_ref):
    device, half_id = whole(scale_ref[3]), whole(scale_ref[4])
    leaves = offs_ref.shape[1]
    slots = cols_ref.shape[1]
    room = out_ref.shape[1]
    half = leaves // 2
    half_bits = half.bit_length() - 1
    begins = jnp.broadcast_to(offs_ref[...].astype(F32), (8, leaves)).T[:, 0:1]
    slot = lax.broadcasted_iota(jnp.int32, (leaves, slots), 1).astype(F32)
    row = jnp.sum(jnp.where(begins <= slot, 1.0, 0.0), axis=0, keepdims=True) - 1.0
    first = jnp.sum(jnp.where(begins == slot, 1.0, 0.0), axis=0, keepdims=True)
    place = cols_ref[...] - (device * leaves - leaves + half_id * half)
    block = place >> half_bits
    own = jnp.where(block == 2, 1.0 - first, 0.0)
    far = jnp.where((block & 3) == 0, 1.0, 0.0)
    kinds = jnp.concatenate([own, far, jnp.zeros((6, slots), F32)], axis=0)
    earlier = lax.broadcasted_iota(jnp.int32, (slots, slots), 0)
    later = lax.broadcasted_iota(jnp.int32, (slots, slots), 1)
    upto = jnp.where(earlier <= later, 1.0, 0.0).astype(BF)
    rank = jnp.dot(kinds.astype(BF), upto, preferred_element_type=F32)
    turned = rank.T
    target = lax.broadcasted_iota(jnp.int32, (slots, room), 1).astype(F32) + 1.0
    at = lax.broadcasted_iota(jnp.int32, (1, room), 1).astype(F32)
    upper, lower = (place >> 4).astype(F32), (place & 15).astype(F32)
    lists = []
    for kind, (mask, shift, spare) in enumerate(
        ((own, float(leaves), float(half)), (far, 0.0, 8.0 * half))
    ):
        parts = jnp.concatenate(
            [row * mask, upper * mask, lower * mask, jnp.zeros((5, slots), F32)], axis=0
        )
        hits = jnp.where(turned[:, kind : kind + 1] == target, 1.0, 0.0).astype(BF)
        got = jnp.dot(parts.astype(BF), hits, preferred_element_type=F32)
        code = got[0:1] * float(CODE) + got[1:2] * 16.0 + got[2:3] - shift
        total = rank[kind : kind + 1, slots - 1 : slots]
        lists.append((jnp.where(at < total, code, spare), total))
    out_ref[...] = jnp.concatenate(
        [
            lists[0][0], lists[1][0],
            jnp.broadcast_to(lists[0][1], (1, room)), jnp.broadcast_to(lists[1][1], (1, room)),
            jnp.zeros((4, room), F32),
        ],
        axis=0,
    ).astype(jnp.int32)


def block_loop(kind, place, plan_ref, row_ref, col_ref, val_ref, sums, s0, s1, k0, k1):
    def accumulate(first, kern):
        for q in range(PAIR):
            code = plan_ref[kind, first + q]
            here = lanes(code >> CODE_BITS)
            part = jnp.dot(
                val_ref[place(code & (CODE - 1))], kern[q], preferred_element_type=F32
            )
            sums[0][:, here] += part[:PART]
            sums[1][:, here] += part[PART:]

    def distance(first, out):
        for q in range(PAIR):
            code = plan_ref[kind, first + q]
            out[q] = jnp.dot(
                col_ref[place(code & (CODE - 1))],
                row_ref[code >> CODE_BITS],
                preferred_element_type=F32,
            )

    def evaluate(squared, kern):
        for q in range(PAIR):
            kern[q] = matern(squared[q])

    k1[...] = jnp.zeros_like(k1)
    distance(0, s0)

    def step(it, _):
        for turn in range(TURNS):
            first = (it * TURNS + turn) * 2 * PAIR
            accumulate(jnp.maximum(first - PAIR, 0), k1)
            distance(first + PAIR, s1)
            evaluate(s0, k0)
            accumulate(first, k0)
            distance(first + 2 * PAIR, s0)
            evaluate(s1, k1)
        return 0

    count = plan_ref[2 + kind, 0]
    turns = (count + TURNS * 2 * PAIR - 1) // (TURNS * 2 * PAIR)
    lax.fori_loop(0, turns, step, 0)
    accumulate(jnp.maximum(turns * TURNS * 2 * PAIR - PAIR, 0), k1)


def diagonal_loop(first_leaf, count, row_ref, col_ref, val_ref, sums, s0, s1, k0, k1):
    mid = LEAF // 2

    def distance(first, out):
        for q in range(PAIR):
            col = jnp.minimum(first + q, count - 1)
            rows = row_ref[first_leaf + col]
            out[q, :mid] = jnp.dot(col_ref[col, :mid], rows, preferred_element_type=F32)
            out[q, mid:, mid:] = jnp.dot(
                col_ref[col, mid:], rows[:, mid:], preferred_element_type=F32
            )

    def evaluate(squared, kern):
        for q in range(PAIR):
            kern[q, :mid] = matern(squared[q, :mid])
            kern[q, mid:, mid:] = matern(squared[q, mid:, mid:])

    def accumulate(first, kern):
        for q in range(PAIR):
            col = jnp.maximum(first + q, 0)
            values = val_ref[col]
            part = jnp.dot(values[:, :mid], kern[q, :mid], preferred_element_type=F32)
            left = mul_nt(values[:, mid:], kern[q, :mid, mid:])
            right = jnp.dot(values[:, mid:], kern[q, mid:, mid:], preferred_element_type=F32)
            part = part + jnp.concatenate([left, right], axis=1)
            here = lanes(first_leaf + col)
            sums[0][:, here] += part[:PART]
            sums[1][:, here] += part[PART:]

    k1[...] = jnp.zeros_like(k1)
    distance(0, s0)

    def step(it, _):
        for turn in range(TURNS):
            first = (it * TURNS + turn) * 2 * PAIR
            accumulate(first - PAIR, k1)
            distance(first + PAIR, s1)
            evaluate(s0, k0)
            accumulate(first, k0)
            distance(first + 2 * PAIR, s0)
            evaluate(s1, k1)
        return 0

    lax.fori_loop(0, count // (TURNS * 2 * PAIR), step, 0)
    accumulate(count - PAIR, k1)


def load_columns(pack_ref, base, count, col_ref, val_ref):
    def step(i, _):
        for q in range(4):
            leaf = i * 4 + q
            val_ref[base + leaf] = pack_ref[0:16, lanes(leaf)]
            col_ref[base + leaf] = col_features(pack_ref[16:24, lanes(leaf)].astype(F32))
        return 0

    lax.fori_loop(0, count // 4, step, 0)


def near_local_kernel(
    scale_ref, plan_ref, points_ref, pack_ref,
    mine_ref, other_ref, row_ref,
    col_ref, val_ref, s0, s1, k0, k1,
):
    half_id = whole(scale_ref[4])
    leaves = row_ref.shape[0]
    half = leaves // 2

    def rows_step(i, _):
        for q in range(4):
            leaf = i * 4 + q
            row_ref[leaf] = row_features(coordinate_rows(points_ref[:, lanes(leaf)], scale_ref))
            mine_ref[:, lanes(leaf)] = jnp.zeros((PART, LEAF), F32)
            other_ref[:, lanes(leaf)] = jnp.zeros((PART, LEAF), F32)
        return 0

    lax.fori_loop(0, leaves // 4, rows_step, 0)
    load_columns(pack_ref, 0, half, col_ref, val_ref)
    val_ref[half] = jnp.zeros((16, LEAF), BF)
    col_ref[half] = jnp.zeros(col_ref.shape[1:], BF)
    sums = (mine_ref, other_ref)
    diagonal_loop(half_id * half, half, row_ref, col_ref, val_ref, sums, s0, s1, k0, k1)
    block_loop(0, lambda c: c, plan_ref, row_ref, col_ref, val_ref, sums, s0, s1, k0, k1)


def near_halo_kernel(
    scale_ref, plan_ref, row_ref, inner_ref, outer_ref, first_in, second_in,
    mine_ref, other_ref,
    first, second, col_ref, val_ref, s0, s1, k0, k1,
):
    core = whole(scale_ref[4])
    half = inner_ref.shape[1] // LEAF
    odd = whole(scale_ref[3]) & 1
    bits = half.bit_length() - 1
    count = plan_ref[3, 0]

    def place(code):
        return (code & (half - 1)) | ((code >> (bits + 2)) << bits)

    def load(i, _):
        for q in range(4):
            code = plan_ref[1, i * 4 + q] & (CODE - 1)
            here = lanes(code & (half - 1))
            paired = (code >> (bits + 2)) + odd == 1
            values = jnp.where(paired, inner_ref[0:16, here], outer_ref[0:16, here])
            rows = jnp.where(paired, inner_ref[16:24, here], outer_ref[16:24, here])
            val_ref[place(code)] = values
            col_ref[place(code)] = col_features(rows.astype(F32))
        return 0

    first[...] = first_in[...]
    second[...] = second_in[...]
    lax.fori_loop(0, (count + 3) // 4, load, 0)
    val_ref[2 * half] = jnp.zeros((16, LEAF), BF)
    col_ref[2 * half] = jnp.zeros(col_ref.shape[1:], BF)
    sums = (first, second)
    block_loop(1, place, plan_ref, row_ref, col_ref, val_ref, sums, s0, s1, k0, k1)

    @pl.when(core == 0)
    def _():
        mine_ref[...] = first[...]
        other_ref[...] = second[...]

    @pl.when(core == 1)
    def _():
        mine_ref[...] = second[...]
        other_ref[...] = first[...]


def split_parts(value):
    high = value.astype(BF).astype(F32)
    return jnp.concatenate([high, value - high], axis=0).astype(BF)


def join_parts(value):
    return value[0:ALL] + value[ALL : 2 * ALL]


def mul_nt(left, right):
    return lax.dot_general(left, right, NT, preferred_element_type=F32)


def over_nodes(count, unroll, work):
    group = min(unroll, count)
    if count == group:
        work([jnp.int32(i) for i in range(count)])
        return

    def step(i, _):
        work([i * group + q for q in range(group)])
        return 0

    lax.fori_loop(0, count // group, step, 0)


def store_turned(flat, r, block):
    turned = block.T
    count = turned.shape[0] // 8
    width = turned.shape[1]
    rows = pl.ds(pl.multiple_of(r * 8, 8), 8)
    flat[0:count, rows] = turned[: count * 8].reshape(count, 8, width)
    rest = turned.shape[0] - count * 8
    flat[count, pl.ds(pl.multiple_of(r * 8, 8), rest)] = turned[count * 8 :]


def load_node(flat, node):
    return flat[node >> 3, pl.ds(node & 7, RANK, stride=8)].astype(BF)


def side_by_side(first, second):
    return jnp.concatenate([first, second], axis=1)


def doubled(pair):
    low = lax.broadcasted_iota(jnp.int32, pair.shape, 1) < RANK
    turned = pltpu.roll(pair, RANK, 1)
    return jnp.where(low, pair, turned), jnp.where(low, turned, pair)


def up_kernel(
    scale_ref, pack_ref, basis_ref, raw_ref, coef_ref, export_ref, front_ref, move_ref,
    flat, pairs,
):
    core = whole(scale_ref[4])
    leaves = move_ref.shape[0]
    levels = leaves.bit_length() - 1
    base = core * leaves

    def keep(parent, first, second):
        pair = side_by_side(first, second)
        pairs[parent] = split_parts(pair)
        one, two = doubled(pair)
        coef_ref[2 * parent + 1] = split_parts(one)
        coef_ref[2 * parent + 2] = split_parts(two)

    def leaf_step(it, _):
        outs = []
        for q in range(8):
            leaf = it * 8 + q
            outs.append(mul_nt(pack_ref[0:ALL, lanes(leaf)], basis_ref[base + leaf]))
        for q in range(8):
            r = it * 8 + q
            block = jnp.concatenate([raw_ref[0, r], raw_ref[1, r]], axis=0).astype(F32)
            store_turned(flat, r, block)
        for q in range(4):
            keep(leaves // 2 - 1 + it * 4 + q, outs[2 * q], outs[2 * q + 1])
        return 0

    lax.fori_loop(0, leaves // 8, leaf_step, 0)
    root_move = load_node(flat, 0)
    move_ref[leaves - 1] = root_move
    for depth in range(levels - 1, 0, -1):
        first = 2**depth - 1
        above = 2 ** (depth - 1) - 1
        start = 2 ** (depth + 1) - 1 + core * 2**depth

        def work(nodes, first=first, above=above, start=start):
            outs = []
            for j in nodes:
                for c in range(2):
                    move = load_node(flat, start + 2 * j + c)
                    move_ref[first + 2 * j + c] = move
                    outs.append(mul_nt(pairs[first + 2 * j + c], move))
            for j, i in enumerate(nodes):
                keep(above + i, join_parts(outs[2 * j]), join_parts(outs[2 * j + 1]))

        over_nodes(2 ** (depth - 1), 8, work)
    move = load_node(flat, 1 + core)
    move_ref[0] = move
    crown = join_parts(mul_nt(pairs[0], move))
    crown = split_parts(side_by_side(crown, crown))
    coef_ref[0] = crown
    side = lax.broadcasted_iota(jnp.int32, crown.shape, 1) // RANK
    root = join_parts(mul_nt(jnp.where(side == core, crown.astype(F32), 0.0).astype(BF), root_move))
    export_ref[0] = split_parts(side_by_side(root, root))
    export_ref[1:EXPORT] = coef_ref[0 : EXPORT - 1]
    front_ref[0] = export_ref[0 : EXPORT // 2]


def joint(first, second, third):
    return jnp.concatenate([first, second, third], axis=1)


def couple_kernel(
    scale_ref, partners_ref, coef_ref, raw_ref, local_ref, tie_ref, wide, thin,
):
    device, core = whole(scale_ref[3]), whole(scale_ref[4])
    levels = (raw_ref.shape[3] + 1).bit_length() - 2
    low = lax.broadcasted_iota(jnp.int32, (2 * ALL, 2 * RANK), 1) < RANK

    def turn(i, _):
        for q in range(8):
            r = i * 8 + q
            block = jnp.concatenate([raw_ref[0, r], raw_ref[1, r]], axis=0).astype(F32)
            store_turned(wide, r, block)
            store_turned(thin, r, raw_ref[2, r].astype(F32))
        return 0

    lax.fori_loop(0, RANK // 8, turn, 0)

    def tie(node):
        return jnp.concatenate([load_node(wide, node), load_node(thin, node)], axis=1)

    tie_ref[0] = tie(0)
    for depth in range(1, SPAN + 1):
        for i in range(2 ** (depth - 1)):
            tie_ref[2 ** (depth - 1) + i] = tie(2**depth - 1 + core * 2 ** (depth - 1) + i)
    for depth in range(SPAN + 1, levels + 1):
        half = 2 ** (depth - 1)
        above = half // 2 - 1
        start = 2**depth - 1 + core * half
        shift = half - 1 - device * 2**depth - core * half

        def work(nodes, above=above, start=start, shift=shift):
            outs = []
            for j in nodes:
                for c in range(2):
                    node = start + 2 * j + c
                    mates = [coef_ref[partners_ref[f, node] + shift] for f in range(3)]
                    left = jnp.concatenate(
                        [jnp.where(low, mates[0], mates[1]), mates[2][:, :RANK]], axis=1
                    )
                    outs.append(mul_nt(left, tie(node)))
            for j, i in enumerate(nodes):
                local_ref[above + i] = side_by_side(
                    join_parts(outs[2 * j]), join_parts(outs[2 * j + 1])
                )

        over_nodes(half // 2, 8, work)


def down_kernel(
    dev_levels, scale_ref, partners_ref, top_partners_ref, top_e, top_b, tie_ref,
    local_ref, move_ref, own_ref, core_ref, next_ref, far_refs, tops_ref, mine_ref, other_ref,
    gather_ref, down, tree,
):
    device, core = whole(scale_ref[3]), whole(scale_ref[4])
    self_id = 2 * device + core
    gather_ref[0] = own_ref[...]
    gather_ref[1] = core_ref[...]
    gather_ref[2:4, 0:4] = next_ref[...]
    for i, far_ref in enumerate(far_refs):
        gather_ref[4 * i + 4 : 4 * i + 8, 0:2] = far_ref[...]
    root_ref = gather_ref if dev_levels == SPAN else tops_ref
    leaves = mine_ref.shape[0]
    levels = leaves.bit_length() - 1
    count = 2**dev_levels

    def roots(nodes):
        for i in nodes:
            parts = join_parts(root_ref[(2 * i) ^ self_id, 0].astype(F32)) + join_parts(
                root_ref[(2 * i + 1) ^ self_id, 0].astype(F32)
            )
            tree[count + i] = split_parts(parts[:, :RANK])

    over_nodes(count, 8, roots)
    for level in range(dev_levels - 1, 1, -1):

        def work(nodes, level=level):
            outs = []
            for i in nodes:
                row = 2**level - 4 + i
                kids = [tree[2 ** (level + 1) + 2 * i + c] for c in range(2)]
                outs.append(mul_nt(kids[0], top_e[row, 0]) + mul_nt(kids[1], top_e[row, 1]))
            for i, out in zip(nodes, outs):
                tree[2**level + i] = split_parts(join_parts(out))

        over_nodes(2**level, 4, work)

    mates = [tree[count + partners_ref[f, 0]] for f in range(3)]
    shallow = [join_parts(mul_nt(joint(*mates), tie_ref[0]))]
    for depth in range(1, SPAN + 1):
        half = 2 ** (depth - 1)
        for i in range(half):
            node = 2**depth - 1 + core * half + i
            picks = []
            for f in range(3):
                mate = partners_ref[f, node]
                at = ((mate >> (depth - 1)) ^ self_id) & (2 * 2**SPAN - 1)
                picks.append(gather_ref[at, half + (mate & (half - 1))][:, :RANK])
            shallow.append(join_parts(mul_nt(joint(*picks), tie_ref[half + i])))

    pushed = jnp.zeros((ALL, RANK), F32)
    for level in range(2, dev_levels):
        node = device >> (dev_levels - level)
        row = 2**level - 4 + node
        side = device >> (dev_levels - level - 1) & 1
        parts = sum(
            mul_nt(tree[2**level + top_partners_ref[row, f]], top_b[row, f]) for f in range(3)
        )
        here = split_parts(join_parts(parts) + pushed)
        pushed = join_parts(jnp.dot(here, top_e[row, side], preferred_element_type=F32))

    root = split_parts(shallow[0] + pushed)
    both = join_parts(jnp.dot(root, move_ref[leaves - 1], preferred_element_type=F32))
    down[0] = split_parts(shallow[1] + jnp.where(core == 0, both[:, :RANK], both[:, RANK:]))
    for depth in range(levels):
        first = 2**depth - 1

        def work(nodes, depth=depth, first=first):
            outs = [
                jnp.dot(down[first + i], move_ref[first + i], preferred_element_type=F32)
                for i in nodes
            ]
            for i, out in zip(nodes, outs):
                node = first + i
                if depth + 2 <= SPAN:
                    kid = 2 ** (depth + 1) + 2 * i
                    base = side_by_side(shallow[kid], shallow[kid + 1])
                else:
                    base = local_ref[node]
                pair = base + join_parts(out)
                if depth == levels - 1:
                    for c in range(2):
                        value = pair[:, c * RANK : (c + 1) * RANK]
                        one, two = value[:PART], value[PART:]
                        mine_ref[2 * i + c] = jnp.where(core == 0, one, two).astype(BF)
                        other_ref[2 * i + c] = jnp.where(core == 0, two, one).astype(BF)
                else:
                    down[2 * node + 1] = split_parts(pair[:, :RANK])
                    down[2 * node + 2] = split_parts(pair[:, RANK:])

        if depth < SPAN:
            work(list(range(2**depth)))
        else:
            over_nodes(2**depth, 8, work)


def final_kernel(
    scale_ref, mine_ref, got_ref, basis, noise, vec, near, swap, out_hbm, out, sems
):
    core = whole(scale_ref[4])
    leaves = mine_ref.shape[0]
    chunks = 2
    per = leaves // chunks
    wide = per * LEAF
    sends = []
    for part, low_ref in enumerate((mine_ref, got_ref)):
        base = jnp.where(core == part, 0, leaves)
        for c in range(chunks):

            def last(nodes, c=c, low_ref=low_ref, base=base):
                rows = [c * per + i for i in nodes]
                fars = [
                    jnp.dot(low_ref[n], basis[base + n], preferred_element_type=F32)
                    for n in rows
                ]
                for n, far in zip(rows, fars):
                    here = lanes(base + n)
                    total = near[:, here] + swap[:, here]
                    out[:, here] = total + noise[:, here] * vec[:, here].astype(F32) + far

            over_nodes(per, 8, last)
            piece = pl.ds(pl.multiple_of((base + c * per) * LEAF, wide), wide)
            send = pltpu.make_async_copy(
                out.at[:, piece], out_hbm.at[:, piece], sems.at[part * chunks + c]
            )
            send.start()
            sends.append(send)
    for send in sends:
        send.wait()


def swap_mask(value, mask):
    total = lax.axis_size("leaf") * lax.axis_size("sub")
    return lax.ppermute(value, ("leaf", "sub"), [(i, i ^ mask) for i in range(total)])


def after(value, anchor):
    return lax.optimization_barrier((value, anchor))[0]


def body(
    points, inv_scale, noise, vectors, leaf_basis, local_transfer, top_transfer,
    local_coupling, top_coupling, local_partners, top_partners, near_offsets, near_cols,
):
    subs = lax.axis_size("sub")
    count = lax.axis_size("leaf") * subs
    dev_levels = count.bit_length() - 1
    device = lax.axis_index("leaf") * subs + lax.axis_index("sub")
    core = lax.axis_index("vec")
    scale = jnp.concatenate([inv_scale, jnp.stack([device, core]).astype(F32)])
    size = vectors.shape[1]
    leaves = near_offsets.shape[0]
    slots = near_cols.shape[0]
    half = size // 2
    sds = jax.ShapeDtypeStruct
    scratch_blocks = [
        VMEM((PAIR, LEAF, LEAF), F32), VMEM((PAIR, LEAF, LEAF), F32),
        VMEM((PAIR, LEAF, LEAF), BF), VMEM((PAIR, LEAF, LEAF), BF),
    ]

    got = lax.ppermute(vectors, "vec", [(0, 1), (1, 0)])

    plan = pl.pallas_call(
        plan_kernel,
        name="plan",
        out_shape=sds((8, slots + 128), jnp.int32),
        in_specs=[sspec(), vspec(), vspec()],
        out_specs=vspec(),
        compiler_params=params(8),
        cost_estimate=pl.CostEstimate(flops=3 * 10**9, bytes_accessed=1 << 16, transcendentals=0),
    )(scale, near_offsets.reshape(1, leaves), near_cols.reshape(1, slots))

    pack = pl.pallas_call(
        pack_kernel,
        name="pack",
        out_shape=sds((24, half), BF),
        in_specs=[sspec(), vspec(), vspec(), vspec()],
        out_specs=vspec(),
        compiler_params=params(8),
        cost_estimate=pl.CostEstimate(flops=2 * 10**9, bytes_accessed=2 << 20, transcendentals=0),
    )(scale, points, vectors, got)
    axes = ("leaf", "sub")
    inner = lax.ppermute(pack, axes, [(i, i ^ 1) for i in range(count)])
    outer = lax.ppermute(
        pack, axes, [(i, ((i + 1) ^ 1) - 1) for i in range(1, count - 1)]
    )

    moves_raw = jnp.transpose(local_transfer, (1, 2, 3, 0))
    part = leaves // 2
    coef, export, front, moves = pl.pallas_call(
        up_kernel,
        name="up",
        out_shape=(
            sds((2 * part - 1, 2 * ALL, 2 * RANK), BF), sds((EXPORT, 2 * ALL, 2 * RANK), BF),
            sds((1, EXPORT // 2, 2 * ALL, 2 * RANK), BF), sds((part, RANK, 2 * RANK), BF),
        ),
        in_specs=[sspec(), vspec(), vspec(), vspec()],
        out_specs=(vspec(),) * 4,
        scratch_shapes=[
            VMEM((leaves // 8, RANK * 8, 2 * RANK), F32),
            VMEM((part - 1, 2 * ALL, 2 * RANK), BF),
        ],
        compiler_params=params(18),
        cost_estimate=pl.CostEstimate(flops=8 * 10**9, bytes_accessed=8 << 20, transcendentals=0),
    )(scale, pack, leaf_basis, moves_raw)
    from_core = lax.ppermute(export, "vec", [(0, 1), (1, 0)])
    pack, _ = lax.optimization_barrier((pack, export))
    first, second, row_feat = pl.pallas_call(
        near_local_kernel,
        name="near_local",
        out_shape=(
            sds((PART, size), F32), sds((PART, size), F32), sds((leaves, 32, LEAF), BF),
        ),
        in_specs=[sspec()] * 2 + [vspec()] * 2,
        out_specs=(vspec(), vspec(), vspec()),
        scratch_shapes=[
            VMEM((leaves // 2 + 1, LEAF, 32), BF), VMEM((leaves // 2 + 1, 16, LEAF), BF),
            *scratch_blocks,
        ],
        compiler_params=params(22),
        cost_estimate=pl.CostEstimate(
            flops=36 * 10**9, bytes_accessed=8 << 20, transcendentals=190 * 2**17
        ),
    )(scale, plan, points, pack)

    from_core = after(from_core, first)
    near_pair = jnp.concatenate([front, from_core[None, 0 : EXPORT // 2]], axis=0)
    coef_late, near_pair = lax.optimization_barrier((coef, near_pair))
    from_next = swap_mask(near_pair, 1)
    ties_raw = jnp.transpose(local_coupling, (1, 2, 3, 0))
    mates = jnp.transpose(local_partners)
    local, ties = pl.pallas_call(
        couple_kernel,
        name="couple",
        out_shape=(
            sds((part - 1, ALL, 2 * RANK), F32), sds((EXPORT, RANK, 3 * RANK), BF),
        ),
        in_specs=[sspec()] * 2 + [vspec(), vspec()],
        out_specs=(vspec(),) * 2,
        scratch_shapes=[
            VMEM((leaves // 4, RANK * 8, 2 * RANK), F32),
            VMEM((leaves // 4, RANK * 8, RANK), F32),
        ],
        compiler_params=params(30),
        cost_estimate=pl.CostEstimate(flops=16 * 10**9, bytes_accessed=8 << 20, transcendentals=0),
    )(scale, mates, coef_late, ties_raw)

    first, _, from_next = lax.optimization_barrier((first, local, from_next))
    quad = jnp.concatenate([near_pair[:, 0:2], from_next[:, 0:2]], axis=0)
    from_far = [swap_mask(quad, mask) for mask in (2, 4, 6)]
    mine, other = pl.pallas_call(
        near_halo_kernel,
        name="near_halo",
        out_shape=(sds((PART, size), F32), sds((PART, size), F32)),
        in_specs=[sspec()] * 2 + [vspec()] * 5,
        out_specs=(vspec(), vspec()),
        scratch_shapes=[
            VMEM((PART, size), F32), VMEM((PART, size), F32),
            VMEM((leaves + 1, LEAF, 32), BF), VMEM((leaves + 1, 16, LEAF), BF),
            *scratch_blocks,
        ],
        compiler_params=params(26),
        cost_estimate=pl.CostEstimate(
            flops=20 * 10**9, bytes_accessed=8 << 20, transcendentals=60 * 2**17
        ),
    )(scale, plan, row_feat, inner, outer, first, second)
    swapped = lax.ppermute(other, "vec", [(0, 1), (1, 0)])

    tops = export
    if dev_levels > SPAN:
        tops = jnp.concatenate(
            [export[None, 0:1], from_core[None, 0:1], from_next[:, 0:1]]
            + [part[:, 0:1] for part in from_far],
            axis=0,
        )
        for bit in range(SPAN, dev_levels):
            tops = jnp.concatenate([tops, swap_mask(tops, 2**bit)], axis=0)
    low_mine, low_other = pl.pallas_call(
        lambda *refs: down_kernel(dev_levels, *refs[:11], refs[11:14], *refs[14:]),
        name="down",
        out_shape=(sds((part, PART, RANK), BF), sds((part, PART, RANK), BF)),
        in_specs=[sspec()] * 3 + [vspec()] * 12,
        out_specs=(vspec(), vspec()),
        scratch_shapes=[
            VMEM((2 * 2**SPAN, EXPORT, 2 * ALL, 2 * RANK), BF),
            VMEM((part - 1, 2 * ALL, RANK), BF), VMEM((2 * count, 2 * ALL, RANK), BF),
        ],
        compiler_params=params(14),
        cost_estimate=pl.CostEstimate(flops=40 * 10**9, bytes_accessed=4 << 20, transcendentals=0),
    )(
        scale, mates, top_partners, top_transfer, top_coupling, ties, local, moves,
        export, from_core, from_next, *from_far, tops,
    )
    low_got = lax.ppermute(low_other, "vec", [(0, 1), (1, 0)])

    return pl.pallas_call(
        final_kernel,
        name="final",
        out_shape=sds((PART, size), F32),
        in_specs=[sspec()] + [vspec()] * 7,
        out_specs=hspec(),
        scratch_shapes=[VMEM((PART, size), F32), pltpu.SemaphoreType.DMA((4,))],
        compiler_params=params(10),
        cost_estimate=pl.CostEstimate(flops=2 * 10**9, bytes_accessed=4 << 20, transcendentals=0),
    )(scale, low_mine, low_got, leaf_basis, noise.reshape(1, size), vectors, mine, swapped)


def solution(mesh):
    return jax.shard_map(
        body,
        mesh=mesh,
        in_specs=(
            P("groups", ("leaf", "sub")),
            P("groups"),
            P(("groups", "leaf", "sub")),
            P(("groups", "vec"), ("leaf", "sub")),
            P(("groups", "leaf", "sub"), None, None),
            P(("groups", "leaf", "sub"), None, None, None),
            P("groups", None, None, None),
            P(("groups", "leaf", "sub"), None, None, None),
            P("groups", None, None, None),
            P(("groups", "leaf", "sub"), None),
            P("groups", None),
            P(("groups", "leaf", "sub")),
            P(("groups", "leaf", "sub")),
        ),
        out_specs=P(("groups", "vec"), ("leaf", "sub")),
        check_vma=False,
    )
```

```python
import functools
import math

import jax
import jax.numpy as jnp
from jax import lax
from jax.experimental import pallas as pl
from jax.experimental.pallas import tpu as pltpu
from jax.sharding import PartitionSpec as P

BF = jnp.bfloat16
F32 = jnp.float32
LEAF = 256
RANK = 64
SPAN = 3
PART = 8
ALL = 2 * PART
EXPORT = 2**SPAN
NEG_LOG2E = -1.0 / math.log(2.0)
ROOT3 = math.sqrt(3.0)
TINY = 1e-12
PAIR = 2
TURNS = 2
CODE_BITS = 10
CODE = 2**CODE_BITS
VMEM = pltpu.VMEM
SMEM = pltpu.SMEM
NT = (((1,), (1,)), ((), ()))


def vspec():
    return pl.BlockSpec(memory_space=pltpu.VMEM)


def sspec():
    return pl.BlockSpec(memory_space=pltpu.SMEM)


def hspec():
    return pl.BlockSpec(memory_space=pltpu.HBM)


def params(mib):
    return pltpu.CompilerParams(vmem_limit_bytes=mib << 20)


def lanes(index):
    return pl.ds(pl.multiple_of(index * LEAF, LEAF), LEAF)


def whole(scalar):
    return scalar.astype(jnp.int32)


def coordinate_rows(raw, scale_ref):
    width = raw.shape[1]
    row = lax.broadcasted_iota(jnp.int32, (8, width), 0)
    scale = jnp.where(
        row == 0, scale_ref[0], jnp.where(row == 1, scale_ref[1], scale_ref[2])
    )
    full = jnp.concatenate([raw, jnp.zeros((5, width), F32)], axis=0)
    scaled = (full - 0.5) * (scale * ROOT3)
    scaled = jnp.where(row < 3, scaled, 0.0)
    high = scaled.astype(BF).astype(F32)
    rest = (scaled - high).astype(BF).astype(F32)
    return high + pltpu.roll(rest, 4, 0)


def norm_parts(rows):
    swapped = pltpu.roll(rows, 4, 0)
    norm = jnp.sum(rows * (rows + swapped), axis=0, keepdims=True)
    high = norm.astype(BF).astype(F32)
    rest = norm - high
    mid = rest.astype(BF).astype(F32)
    return swapped, high, mid, rest - mid


def row_features(rows):
    swapped, high, mid, low = norm_parts(rows)
    row = lax.broadcasted_iota(jnp.int32, rows.shape, 0)
    tail = jnp.where(
        row < 3,
        1.0,
        jnp.where(row == 3, high, jnp.where(row == 4, mid, jnp.where(row == 5, low, 0.0))),
    )
    return jnp.concatenate([rows, swapped, tail, jnp.zeros_like(rows)], axis=0).astype(BF)


def col_features(rows):
    _, high, mid, low = norm_parts(rows)
    row = lax.broadcasted_iota(jnp.int32, rows.shape, 0)
    tail = jnp.where(
        row == 0,
        high,
        jnp.where(row == 1, mid, jnp.where(row == 2, low, jnp.where(row < 6, 1.0, 0.0))),
    )
    both = -2.0 * rows
    return jnp.concatenate([both, both, tail, jnp.zeros_like(rows)], axis=0).T.astype(BF)


def matern(squared):
    squared = jnp.maximum(squared, TINY)
    dist = squared * lax.rsqrt(squared)
    return ((1.0 + dist) * jnp.exp2(dist * NEG_LOG2E)).astype(BF)


def pack_kernel(scale_ref, points, mine, got, out_ref):
    half = out_ref.shape[1]
    core = whole(scale_ref[4])

    def step(i, _):
        here = pl.ds(pl.multiple_of(i * 2048, 2048), 2048)
        there = pl.ds(pl.multiple_of(core * half + i * 2048, 2048), 2048)
        rows = coordinate_rows(points[:, there], scale_ref)
        one, two = mine[:, there].astype(F32), got[:, there].astype(F32)
        first, second = jnp.where(core == 0, one, two), jnp.where(core == 0, two, one)
        out_ref[:, here] = jnp.concatenate([first, second, rows], axis=0).astype(BF)
        return 0

    lax.fori_loop(0, half // 2048, step, 0)


def plan_kernel(scale_ref, offs_ref, cols_ref, out_ref):
    device, half_id = whole(scale_ref[3]), whole(scale_ref[4])
    leaves = offs_ref.shape[1]
    slots = cols_ref.shape[1]
    room = out_ref.shape[1]
    half = leaves // 2
    half_bits = half.bit_length() - 1
    begins = jnp.broadcast_to(offs_ref[...].astype(F32), (8, leaves)).T[:, 0:1]
    slot = lax.broadcasted_iota(jnp.int32, (leaves, slots), 1).astype(F32)
    row = jnp.sum(jnp.where(begins <= slot, 1.0, 0.0), axis=0, keepdims=True) - 1.0
    first = jnp.sum(jnp.where(begins == slot, 1.0, 0.0), axis=0, keepdims=True)
    place = cols_ref[...] - (device * leaves - leaves + half_id * half)
    block = place >> half_bits
    own = jnp.where(block == 2, 1.0 - first, 0.0)
    far = jnp.where((block & 3) == 0, 1.0, 0.0)
    kinds = jnp.concatenate([own, far, jnp.zeros((6, slots), F32)], axis=0)
    earlier = lax.broadcasted_iota(jnp.int32, (slots, slots), 0)
    later = lax.broadcasted_iota(jnp.int32, (slots, slots), 1)
    upto = jnp.where(earlier <= later, 1.0, 0.0).astype(BF)
    rank = jnp.dot(kinds.astype(BF), upto, preferred_element_type=F32)
    turned = rank.T
    target = lax.broadcasted_iota(jnp.int32, (slots, room), 1).astype(F32) + 1.0
    at = lax.broadcasted_iota(jnp.int32, (1, room), 1).astype(F32)
    upper, lower = (place >> 4).astype(F32), (place & 15).astype(F32)
    lists = []
    for kind, (mask, shift, spare) in enumerate(
        ((own, float(leaves), float(half)), (far, 0.0, 8.0 * half))
    ):
        parts = jnp.concatenate(
            [row * mask, upper * mask, lower * mask, jnp.zeros((5, slots), F32)], axis=0
        )
        hits = jnp.where(turned[:, kind : kind + 1] == target, 1.0, 0.0).astype(BF)
        got = jnp.dot(parts.astype(BF), hits, preferred_element_type=F32)
        code = got[0:1] * float(CODE) + got[1:2] * 16.0 + got[2:3] - shift
        total = rank[kind : kind + 1, slots - 1 : slots]
        lists.append((jnp.where(at < total, code, spare), total))
    out_ref[...] = jnp.concatenate(
        [
            lists[0][0], lists[1][0],
            jnp.broadcast_to(lists[0][1], (1, room)), jnp.broadcast_to(lists[1][1], (1, room)),
            jnp.zeros((4, room), F32),
        ],
        axis=0,
    ).astype(jnp.int32)


def pipeline(turns, unroll, ahead_first, accumulate, distance, evaluate, s0, s1, k0, k1):
    def half_turn(first, near, ahead, ready, filled):
        for q in range(PAIR):
            if ahead_first:
                distance(first + PAIR + q, ahead.at[q])
            accumulate(first - PAIR + q, ready.at[q])
            if not ahead_first:
                distance(first + PAIR + q, ahead.at[q])
            evaluate(near.at[q], filled.at[q])

    k1[...] = jnp.zeros_like(k1)
    for q in range(PAIR):
        distance(q, s0.at[q])

    def step(it, _):
        for turn in range(unroll):
            first = (it * unroll + turn) * 2 * PAIR
            half_turn(first, s0, s1, k1, k0)
            half_turn(first + PAIR, s1, s0, k0, k1)
        return 0

    lax.fori_loop(0, turns, step, 0)
    for q in range(PAIR):
        accumulate(turns * unroll * 2 * PAIR - PAIR + q, k1.at[q])


def block_loop(kind, unroll, place, plan_ref, row_ref, col_ref, val_ref, sums, s0, s1, k0, k1):
    def accumulate(slot, kern):
        code = plan_ref[kind, jnp.maximum(slot, 0)]
        here = lanes(code >> CODE_BITS)
        part = jnp.dot(val_ref[place(code & (CODE - 1))], kern[...], preferred_element_type=F32)
        sums[0][:, here] += part[:PART]
        sums[1][:, here] += part[PART:]

    def distance(slot, out):
        code = plan_ref[kind, slot]
        out[...] = jnp.dot(
            col_ref[place(code & (CODE - 1))],
            row_ref[code >> CODE_BITS],
            preferred_element_type=F32,
        )

    def evaluate(squared, kern):
        kern[...] = matern(squared[...])


    count = plan_ref[2 + kind, 0]
    turns = (count + unroll * 2 * PAIR - 1) // (unroll * 2 * PAIR)
    pipeline(turns, unroll, True, accumulate, distance, evaluate, s0, s1, k0, k1)


def diagonal_loop(first_leaf, count, row_ref, col_ref, val_ref, sums, s0, s1, k0, k1):
    mid = LEAF // 2

    def distance(slot, out):
        col = jnp.minimum(slot, count - 1)
        rows = row_ref[first_leaf + col]
        out[:mid] = jnp.dot(col_ref[col, :mid], rows, preferred_element_type=F32)
        out[mid:, mid:] = jnp.dot(col_ref[col, mid:], rows[:, mid:], preferred_element_type=F32)

    def evaluate(squared, kern):
        kern[:mid] = matern(squared[:mid])
        kern[mid:, mid:] = matern(squared[mid:, mid:])

    def accumulate(slot, kern):
        col = jnp.maximum(slot, 0)
        values = val_ref[col]
        part = jnp.dot(values[:, :mid], kern[:mid], preferred_element_type=F32)
        left = mul_nt(values[:, mid:], kern[:mid, mid:])
        right = jnp.dot(values[:, mid:], kern[mid:, mid:], preferred_element_type=F32)
        part = part + jnp.concatenate([left, right], axis=1)
        here = lanes(first_leaf + col)
        sums[0][:, here] += part[:PART]
        sums[1][:, here] += part[PART:]

    turns = count // (TURNS * 2 * PAIR)
    pipeline(turns, TURNS, False, accumulate, distance, evaluate, s0, s1, k0, k1)


def load_columns(pack_ref, base, count, col_ref, val_ref):
    def step(i, _):
        for q in range(8):
            leaf = i * 8 + q
            val_ref[base + leaf] = pack_ref[0:16, lanes(leaf)]
            col_ref[base + leaf] = col_features(pack_ref[16:24, lanes(leaf)].astype(F32))
        return 0

    lax.fori_loop(0, count // 8, step, 0)


def near_local_kernel(
    scale_ref, plan_ref, points_ref, pack_ref,
    mine_ref, other_ref, row_ref,
    col_ref, val_ref, s0, s1, k0, k1,
):
    half_id = whole(scale_ref[4])
    leaves = row_ref.shape[0]
    half = leaves // 2

    def rows_step(i, _):
        for q in range(4):
            leaf = i * 4 + q
            row_ref[leaf] = row_features(coordinate_rows(points_ref[:, lanes(leaf)], scale_ref))
            mine_ref[:, lanes(leaf)] = jnp.zeros((PART, LEAF), F32)
            other_ref[:, lanes(leaf)] = jnp.zeros((PART, LEAF), F32)
        return 0

    lax.fori_loop(0, leaves // 4, rows_step, 0)
    load_columns(pack_ref, 0, half, col_ref, val_ref)
    val_ref[half] = jnp.zeros((16, LEAF), BF)
    col_ref[half] = jnp.zeros(col_ref.shape[1:], BF)
    sums = (mine_ref, other_ref)
    diagonal_loop(half_id * half, half, row_ref, col_ref, val_ref, sums, s0, s1, k0, k1)
    block_loop(0, TURNS, lambda c: c, plan_ref, row_ref, col_ref, val_ref, sums, s0, s1, k0, k1)


def near_halo_kernel(
    scale_ref, plan_ref, row_ref, inner_ref, outer_ref, first_in, second_in,
    mine_ref, other_ref,
    first, second, col_ref, val_ref, s0, s1, k0, k1,
):
    core = whole(scale_ref[4])
    half = inner_ref.shape[1] // LEAF
    odd = whole(scale_ref[3]) & 1
    bits = half.bit_length() - 1
    count = plan_ref[3, 0]

    def place(code):
        return (code & (half - 1)) | ((code >> (bits + 2)) << bits)

    def load(i, _):
        for q in range(4):
            code = plan_ref[1, i * 4 + q] & (CODE - 1)
            here = lanes(code & (half - 1))
            paired = (code >> (bits + 2)) + odd == 1
            values = jnp.where(paired, inner_ref[0:16, here], outer_ref[0:16, here])
            rows = jnp.where(paired, inner_ref[16:24, here], outer_ref[16:24, here])
            val_ref[place(code)] = values
            col_ref[place(code)] = col_features(rows.astype(F32))
        return 0

    first[...] = first_in[...]
    second[...] = second_in[...]
    lax.fori_loop(0, (count + 3) // 4, load, 0)
    val_ref[2 * half] = jnp.zeros((16, LEAF), BF)
    col_ref[2 * half] = jnp.zeros(col_ref.shape[1:], BF)
    sums = (first, second)
    block_loop(1, 1, place, plan_ref, row_ref, col_ref, val_ref, sums, s0, s1, k0, k1)

    @pl.when(core == 0)
    def _():
        mine_ref[...] = first[...]
        other_ref[...] = second[...]

    @pl.when(core == 1)
    def _():
        mine_ref[...] = second[...]
        other_ref[...] = first[...]


def split_parts(value):
    high = value.astype(BF).astype(F32)
    return jnp.concatenate([high, value - high], axis=0).astype(BF)


def join_parts(value):
    return value[0:ALL] + value[ALL : 2 * ALL]


def mul_nt(left, right):
    return lax.dot_general(left, right, NT, preferred_element_type=F32)


def over_nodes(count, unroll, work):
    group = min(unroll, count)
    if count == group:
        work([jnp.int32(i) for i in range(count)])
        return

    def step(i, _):
        work([i * group + q for q in range(group)])
        return 0

    lax.fori_loop(0, count // group, step, 0)


def store_turned(flat, r, block):
    turned = block.T
    count = turned.shape[0] // 8
    width = turned.shape[1]
    rows = pl.ds(pl.multiple_of(r * 8, 8), 8)
    flat[0:count, rows] = turned[: count * 8].reshape(count, 8, width)
    rest = turned.shape[0] - count * 8
    flat[count, pl.ds(pl.multiple_of(r * 8, 8), rest)] = turned[count * 8 :]


def load_node(flat, node):
    return flat[node >> 3, pl.ds(node & 7, RANK, stride=8)].astype(BF)


def side_by_side(first, second):
    return jnp.concatenate([first, second], axis=1)


def doubled(pair):
    low = lax.broadcasted_iota(jnp.int32, pair.shape, 1) < RANK
    turned = pltpu.roll(pair, RANK, 1)
    return jnp.where(low, pair, turned), jnp.where(low, turned, pair)


def up_kernel(
    scale_ref, pack_ref, basis_ref, raw_ref, coef_ref, export_ref, front_ref, move_ref,
    flat, pairs,
):
    core = whole(scale_ref[4])
    leaves = move_ref.shape[0]
    levels = leaves.bit_length() - 1
    base = core * leaves

    def keep(parent, first, second):
        pair = side_by_side(first, second)
        pairs[parent] = split_parts(pair)
        one, two = doubled(pair)
        coef_ref[2 * parent + 1] = split_parts(one)
        coef_ref[2 * parent + 2] = split_parts(two)

    def leaf_step(it, _):
        outs = []
        for q in range(8):
            leaf = it * 8 + q
            outs.append(mul_nt(pack_ref[0:ALL, lanes(leaf)], basis_ref[base + leaf]))
        for q in range(8):
            r = it * 8 + q
            block = jnp.concatenate([raw_ref[0, r], raw_ref[1, r]], axis=0).astype(F32)
            store_turned(flat, r, block)
        for q in range(4):
            keep(leaves // 2 - 1 + it * 4 + q, outs[2 * q], outs[2 * q + 1])
        return 0

    lax.fori_loop(0, leaves // 8, leaf_step, 0)
    root_move = load_node(flat, 0)
    move_ref[leaves - 1] = root_move
    for depth in range(levels - 1, 0, -1):
        first = 2**depth - 1
        above = 2 ** (depth - 1) - 1
        start = 2 ** (depth + 1) - 1 + core * 2**depth

        def work(nodes, first=first, above=above, start=start):
            outs = []
            for j in nodes:
                for c in range(2):
                    move = load_node(flat, start + 2 * j + c)
                    move_ref[first + 2 * j + c] = move
                    outs.append(mul_nt(pairs[first + 2 * j + c], move))
            for j, i in enumerate(nodes):
                keep(above + i, join_parts(outs[2 * j]), join_parts(outs[2 * j + 1]))

        over_nodes(2 ** (depth - 1), 8, work)
    move = load_node(flat, 1 + core)
    move_ref[0] = move
    crown = join_parts(mul_nt(pairs[0], move))
    crown = split_parts(side_by_side(crown, crown))
    coef_ref[0] = crown
    side = lax.broadcasted_iota(jnp.int32, crown.shape, 1) // RANK
    root = join_parts(mul_nt(jnp.where(side == core, crown.astype(F32), 0.0).astype(BF), root_move))
    export_ref[0] = split_parts(side_by_side(root, root))
    export_ref[1:EXPORT] = coef_ref[0 : EXPORT - 1]
    front_ref[0] = export_ref[0 : EXPORT // 2]


def joint(first, second, third):
    return jnp.concatenate([first, second, third], axis=1)


def couple_kernel(
    scale_ref, partners_ref, coef_ref, raw_ref, local_ref, tie_ref, wide, thin,
):
    device, core = whole(scale_ref[3]), whole(scale_ref[4])
    levels = (raw_ref.shape[3] + 1).bit_length() - 2
    low = lax.broadcasted_iota(jnp.int32, (2 * ALL, 2 * RANK), 1) < RANK

    def turn(i, _):
        for q in range(8):
            r = i * 8 + q
            block = jnp.concatenate([raw_ref[0, r], raw_ref[1, r]], axis=0).astype(F32)
            store_turned(wide, r, block)
            store_turned(thin, r, raw_ref[2, r].astype(F32))
        return 0

    lax.fori_loop(0, RANK // 8, turn, 0)

    def tie(node):
        return jnp.concatenate([load_node(wide, node), load_node(thin, node)], axis=1)

    tie_ref[0] = tie(0)
    for depth in range(1, SPAN + 1):
        for i in range(2 ** (depth - 1)):
            tie_ref[2 ** (depth - 1) + i] = tie(2**depth - 1 + core * 2 ** (depth - 1) + i)
    for depth in range(SPAN + 1, levels + 1):
        half = 2 ** (depth - 1)
        above = half // 2 - 1
        start = 2**depth - 1 + core * half
        shift = half - 1 - device * 2**depth - core * half

        def work(nodes, above=above, start=start, shift=shift):
            outs = []
            for j in nodes:
                for c in range(2):
                    node = start + 2 * j + c
                    mates = [coef_ref[partners_ref[f, node] + shift] for f in range(3)]
                    left = jnp.concatenate(
                        [jnp.where(low, mates[0], mates[1]), mates[2][:, :RANK]], axis=1
                    )
                    outs.append(mul_nt(left, tie(node)))
            for j, i in enumerate(nodes):
                local_ref[above + i] = side_by_side(
                    join_parts(outs[2 * j]), join_parts(outs[2 * j + 1])
                )

        over_nodes(half // 2, 8, work)


def down_kernel(
    dev_levels, scale_ref, partners_ref, top_partners_ref, top_e, top_b, tie_ref,
    local_ref, move_ref, own_ref, core_ref, next_ref, far_refs, tops_ref, mine_ref, other_ref,
    gather_ref, down, tree,
):
    device, core = whole(scale_ref[3]), whole(scale_ref[4])
    self_id = 2 * device + core
    gather_ref[0] = own_ref[...]
    gather_ref[1] = core_ref[...]
    gather_ref[2:4, 0:4] = next_ref[...]
    for i, far_ref in enumerate(far_refs):
        gather_ref[4 * i + 4 : 4 * i + 8, 0:2] = far_ref[...]
    root_ref = gather_ref if dev_levels == SPAN else tops_ref
    leaves = mine_ref.shape[0]
    levels = leaves.bit_length() - 1
    count = 2**dev_levels

    def roots(nodes):
        for i in nodes:
            parts = join_parts(root_ref[(2 * i) ^ self_id, 0].astype(F32)) + join_parts(
                root_ref[(2 * i + 1) ^ self_id, 0].astype(F32)
            )
            tree[count + i] = split_parts(parts[:, :RANK])

    over_nodes(count, 8, roots)
    for level in range(dev_levels - 1, 1, -1):

        def work(nodes, level=level):
            outs = []
            for i in nodes:
                row = 2**level - 4 + i
                kids = [tree[2 ** (level + 1) + 2 * i + c] for c in range(2)]
                outs.append(mul_nt(kids[0], top_e[row, 0]) + mul_nt(kids[1], top_e[row, 1]))
            for i, out in zip(nodes, outs):
                tree[2**level + i] = split_parts(join_parts(out))

        over_nodes(2**level, 4, work)

    mates = [tree[count + partners_ref[f, 0]] for f in range(3)]
    shallow = [join_parts(mul_nt(joint(*mates), tie_ref[0]))]
    for depth in range(1, SPAN + 1):
        half = 2 ** (depth - 1)
        for i in range(half):
            node = 2**depth - 1 + core * half + i
            picks = []
            for f in range(3):
                mate = partners_ref[f, node]
                at = ((mate >> (depth - 1)) ^ self_id) & (2 * 2**SPAN - 1)
                picks.append(gather_ref[at, half + (mate & (half - 1))][:, :RANK])
            shallow.append(join_parts(mul_nt(joint(*picks), tie_ref[half + i])))

    pushed = jnp.zeros((ALL, RANK), F32)
    for level in range(2, dev_levels):
        node = device >> (dev_levels - level)
        row = 2**level - 4 + node
        side = device >> (dev_levels - level - 1) & 1
        parts = sum(
            mul_nt(tree[2**level + top_partners_ref[row, f]], top_b[row, f]) for f in range(3)
        )
        here = split_parts(join_parts(parts) + pushed)
        pushed = join_parts(jnp.dot(here, top_e[row, side], preferred_element_type=F32))

    root = split_parts(shallow[0] + pushed)
    both = join_parts(jnp.dot(root, move_ref[leaves - 1], preferred_element_type=F32))
    down[0] = split_parts(shallow[1] + jnp.where(core == 0, both[:, :RANK], both[:, RANK:]))
    for depth in range(levels):
        first = 2**depth - 1

        def work(nodes, depth=depth, first=first):
            outs = [
                jnp.dot(down[first + i], move_ref[first + i], preferred_element_type=F32)
                for i in nodes
            ]
            for i, out in zip(nodes, outs):
                node = first + i
                if depth + 2 <= SPAN:
                    kid = 2 ** (depth + 1) + 2 * i
                    base = side_by_side(shallow[kid], shallow[kid + 1])
                else:
                    base = local_ref[node]
                pair = base + join_parts(out)
                if depth == levels - 1:
                    for c in range(2):
                        value = pair[:, c * RANK : (c + 1) * RANK]
                        one, two = value[:PART], value[PART:]
                        mine_ref[2 * i + c] = jnp.where(core == 0, one, two).astype(BF)
                        other_ref[2 * i + c] = jnp.where(core == 0, two, one).astype(BF)
                else:
                    down[2 * node + 1] = split_parts(pair[:, :RANK])
                    down[2 * node + 2] = split_parts(pair[:, RANK:])

        if depth < SPAN:
            work(list(range(2**depth)))
        else:
            over_nodes(2**depth, 8, work)


def final_kernel(
    scale_ref, mine_ref, got_ref, basis, noise, vec, near, swap, out_hbm, out, sems
):
    core = whole(scale_ref[4])
    leaves = mine_ref.shape[0]
    chunks = 2
    per = leaves // chunks
    wide = per * LEAF
    sends = []
    for part, low_ref in enumerate((mine_ref, got_ref)):
        base = jnp.where(core == part, 0, leaves)
        for c in range(chunks):

            def last(nodes, c=c, low_ref=low_ref, base=base):
                rows = [c * per + i for i in nodes]
                fars = [
                    jnp.dot(low_ref[n], basis[base + n], preferred_element_type=F32)
                    for n in rows
                ]
                for n, far in zip(rows, fars):
                    here = lanes(base + n)
                    total = near[:, here] + swap[:, here]
                    out[:, here] = total + noise[:, here] * vec[:, here].astype(F32) + far

            over_nodes(per, 8, last)
            piece = pl.ds(pl.multiple_of((base + c * per) * LEAF, wide), wide)
            send = pltpu.make_async_copy(
                out.at[:, piece], out_hbm.at[:, piece], sems.at[part * chunks + c]
            )
            send.start()
            sends.append(send)
    for send in sends:
        send.wait()


def swap_mask(value, mask):
    total = lax.axis_size("leaf") * lax.axis_size("sub")
    return lax.ppermute(value, ("leaf", "sub"), [(i, i ^ mask) for i in range(total)])


def after(value, anchor):
    return lax.optimization_barrier((value, anchor))[0]


def body(
    points, inv_scale, noise, vectors, leaf_basis, local_transfer, top_transfer,
    local_coupling, top_coupling, local_partners, top_partners, near_offsets, near_cols,
):
    subs = lax.axis_size("sub")
    count = lax.axis_size("leaf") * subs
    dev_levels = count.bit_length() - 1
    device = lax.axis_index("leaf") * subs + lax.axis_index("sub")
    core = lax.axis_index("vec")
    scale = jnp.concatenate([inv_scale, jnp.stack([device, core]).astype(F32)])
    size = vectors.shape[1]
    leaves = near_offsets.shape[0]
    slots = near_cols.shape[0]
    half = size // 2
    sds = jax.ShapeDtypeStruct
    scratch_blocks = [
        VMEM((PAIR, LEAF, LEAF), F32), VMEM((PAIR, LEAF, LEAF), F32),
        VMEM((PAIR, LEAF, LEAF), BF), VMEM((PAIR, LEAF, LEAF), BF),
    ]

    got = lax.ppermute(vectors, "vec", [(0, 1), (1, 0)])

    plan = pl.pallas_call(
        plan_kernel,
        name="plan",
        out_shape=sds((8, slots + 128), jnp.int32),
        in_specs=[sspec(), vspec(), vspec()],
        out_specs=vspec(),
        compiler_params=params(8),
        cost_estimate=pl.CostEstimate(flops=3 * 10**9, bytes_accessed=1 << 16, transcendentals=0),
    )(scale, near_offsets.reshape(1, leaves), near_cols.reshape(1, slots))

    pack = pl.pallas_call(
        pack_kernel,
        name="pack",
        out_shape=sds((24, half), BF),
        in_specs=[sspec(), vspec(), vspec(), vspec()],
        out_specs=vspec(),
        compiler_params=params(8),
        cost_estimate=pl.CostEstimate(flops=2 * 10**9, bytes_accessed=2 << 20, transcendentals=0),
    )(scale, points, vectors, got)
    axes = ("leaf", "sub")
    inner = lax.ppermute(pack, axes, [(i, i ^ 1) for i in range(count)])
    outer = lax.ppermute(
        pack, axes, [(i, ((i + 1) ^ 1) - 1) for i in range(1, count - 1)]
    )

    moves_raw = jnp.transpose(local_transfer, (1, 2, 3, 0))
    part = leaves // 2
    coef, export, front, moves = pl.pallas_call(
        up_kernel,
        name="up",
        out_shape=(
            sds((2 * part - 1, 2 * ALL, 2 * RANK), BF), sds((EXPORT, 2 * ALL, 2 * RANK), BF),
            sds((1, EXPORT // 2, 2 * ALL, 2 * RANK), BF), sds((part, RANK, 2 * RANK), BF),
        ),
        in_specs=[sspec(), vspec(), vspec(), vspec()],
        out_specs=(vspec(),) * 4,
        scratch_shapes=[
            VMEM((leaves // 8, RANK * 8, 2 * RANK), F32),
            VMEM((part - 1, 2 * ALL, 2 * RANK), BF),
        ],
        compiler_params=params(18),
        cost_estimate=pl.CostEstimate(flops=8 * 10**9, bytes_accessed=8 << 20, transcendentals=0),
    )(scale, pack, leaf_basis, moves_raw)
    from_core = lax.ppermute(export, "vec", [(0, 1), (1, 0)])
    pack, _ = lax.optimization_barrier((pack, export))
    first, second, row_feat = pl.pallas_call(
        near_local_kernel,
        name="near_local",
        out_shape=(
            sds((PART, size), F32), sds((PART, size), F32), sds((leaves, 32, LEAF), BF),
        ),
        in_specs=[sspec()] * 2 + [vspec()] * 2,
        out_specs=(vspec(), vspec(), vspec()),
        scratch_shapes=[
            VMEM((leaves // 2 + 1, LEAF, 32), BF), VMEM((leaves // 2 + 1, 16, LEAF), BF),
            *scratch_blocks,
        ],
        compiler_params=params(22),
        cost_estimate=pl.CostEstimate(
            flops=36 * 10**9, bytes_accessed=8 << 20, transcendentals=190 * 2**17
        ),
    )(scale, plan, points, pack)

    from_core = after(from_core, first)
    near_pair = jnp.concatenate([front, from_core[None, 0 : EXPORT // 2]], axis=0)
    coef_late, near_pair = lax.optimization_barrier((coef, near_pair))
    from_next = swap_mask(near_pair, 1)
    ties_raw = jnp.transpose(local_coupling, (1, 2, 3, 0))
    mates = jnp.transpose(local_partners)
    local, ties = pl.pallas_call(
        couple_kernel,
        name="couple",
        out_shape=(
            sds((part - 1, ALL, 2 * RANK), F32), sds((EXPORT, RANK, 3 * RANK), BF),
        ),
        in_specs=[sspec()] * 2 + [vspec(), vspec()],
        out_specs=(vspec(),) * 2,
        scratch_shapes=[
            VMEM((leaves // 4, RANK * 8, 2 * RANK), F32),
            VMEM((leaves // 4, RANK * 8, RANK), F32),
        ],
        compiler_params=params(30),
        cost_estimate=pl.CostEstimate(flops=16 * 10**9, bytes_accessed=8 << 20, transcendentals=0),
    )(scale, mates, coef_late, ties_raw)

    first, _, from_next = lax.optimization_barrier((first, local, from_next))
    quad = jnp.concatenate([near_pair[:, 0:2], from_next[:, 0:2]], axis=0)
    from_far = [swap_mask(quad, mask) for mask in (2, 4, 6)]
    mine, other = pl.pallas_call(
        near_halo_kernel,
        name="near_halo",
        out_shape=(sds((PART, size), F32), sds((PART, size), F32)),
        in_specs=[sspec()] * 2 + [vspec()] * 5,
        out_specs=(vspec(), vspec()),
        scratch_shapes=[
            VMEM((PART, size), F32), VMEM((PART, size), F32),
            VMEM((leaves + 1, LEAF, 32), BF), VMEM((leaves + 1, 16, LEAF), BF),
            *scratch_blocks,
        ],
        compiler_params=params(26),
        cost_estimate=pl.CostEstimate(
            flops=20 * 10**9, bytes_accessed=8 << 20, transcendentals=60 * 2**17
        ),
    )(scale, plan, row_feat, inner, outer, first, second)
    swapped = lax.ppermute(other, "vec", [(0, 1), (1, 0)])

    tops = export
    if dev_levels > SPAN:
        tops = jnp.concatenate(
            [export[None, 0:1], from_core[None, 0:1], from_next[:, 0:1]]
            + [part[:, 0:1] for part in from_far],
            axis=0,
        )
        for bit in range(SPAN, dev_levels):
            tops = jnp.concatenate([tops, swap_mask(tops, 2**bit)], axis=0)
    low_mine, low_other = pl.pallas_call(
        lambda *refs: down_kernel(dev_levels, *refs[:11], refs[11:14], *refs[14:]),
        name="down",
        out_shape=(sds((part, PART, RANK), BF), sds((part, PART, RANK), BF)),
        in_specs=[sspec()] * 3 + [vspec()] * 12,
        out_specs=(vspec(), vspec()),
        scratch_shapes=[
            VMEM((2 * 2**SPAN, EXPORT, 2 * ALL, 2 * RANK), BF),
            VMEM((part - 1, 2 * ALL, RANK), BF), VMEM((2 * count, 2 * ALL, RANK), BF),
        ],
        compiler_params=params(14),
        cost_estimate=pl.CostEstimate(flops=40 * 10**9, bytes_accessed=4 << 20, transcendentals=0),
    )(
        scale, mates, top_partners, top_transfer, top_coupling, ties, local, moves,
        export, from_core, from_next, *from_far, tops,
    )
    low_got = lax.ppermute(low_other, "vec", [(0, 1), (1, 0)])

    return pl.pallas_call(
        final_kernel,
        name="final",
        out_shape=sds((PART, size), F32),
        in_specs=[sspec()] + [vspec()] * 7,
        out_specs=hspec(),
        scratch_shapes=[VMEM((PART, size), F32), pltpu.SemaphoreType.DMA((4,))],
        compiler_params=params(10),
        cost_estimate=pl.CostEstimate(flops=2 * 10**9, bytes_accessed=4 << 20, transcendentals=0),
    )(scale, low_mine, low_got, leaf_basis, noise.reshape(1, size), vectors, mine, swapped)


def solution(mesh):
    return jax.shard_map(
        body,
        mesh=mesh,
        in_specs=(
            P("groups", ("leaf", "sub")),
            P("groups"),
            P(("groups", "leaf", "sub")),
            P(("groups", "vec"), ("leaf", "sub")),
            P(("groups", "leaf", "sub"), None, None),
            P(("groups", "leaf", "sub"), None, None, None),
            P("groups", None, None, None),
            P(("groups", "leaf", "sub"), None, None, None),
            P("groups", None, None, None),
            P(("groups", "leaf", "sub"), None),
            P("groups", None),
            P(("groups", "leaf", "sub")),
            P(("groups", "leaf", "sub")),
        ),
        out_specs=P(("groups", "vec"), ("leaf", "sub")),
        check_vma=False,
    )
```

```python
import functools
import math

import jax
import jax.numpy as jnp
from jax import lax
from jax.experimental import pallas as pl
from jax.experimental.pallas import tpu as pltpu
from jax.sharding import PartitionSpec as P

BF = jnp.bfloat16
F32 = jnp.float32
LEAF = 256
RANK = 64
SPAN = 3
PART = 8
ALL = 2 * PART
EXPORT = 2**SPAN
NEG_LOG2E = -1.0 / math.log(2.0)
ROOT3 = math.sqrt(3.0)
TINY = 1e-12
PAIR = 2
TURNS = 2
CODE_BITS = 10
CODE = 2**CODE_BITS
VMEM = pltpu.VMEM
SMEM = pltpu.SMEM
NT = (((1,), (1,)), ((), ()))


def vspec():
    return pl.BlockSpec(memory_space=pltpu.VMEM)


def sspec():
    return pl.BlockSpec(memory_space=pltpu.SMEM)


def hspec():
    return pl.BlockSpec(memory_space=pltpu.HBM)


def params(mib):
    return pltpu.CompilerParams(vmem_limit_bytes=mib << 20)


def lanes(index):
    return pl.ds(pl.multiple_of(index * LEAF, LEAF), LEAF)


def whole(scalar):
    return scalar.astype(jnp.int32)


def coordinate_rows(raw, scale_ref):
    width = raw.shape[1]
    row = lax.broadcasted_iota(jnp.int32, (8, width), 0)
    scale = jnp.where(
        row == 0, scale_ref[0], jnp.where(row == 1, scale_ref[1], scale_ref[2])
    )
    full = jnp.concatenate([raw, jnp.zeros((5, width), F32)], axis=0)
    scaled = (full - 0.5) * (scale * ROOT3)
    scaled = jnp.where(row < 3, scaled, 0.0)
    high = scaled.astype(BF).astype(F32)
    rest = (scaled - high).astype(BF).astype(F32)
    return high + pltpu.roll(rest, 4, 0)


def norm_parts(rows):
    swapped = pltpu.roll(rows, 4, 0)
    norm = jnp.sum(rows * (rows + swapped), axis=0, keepdims=True)
    high = norm.astype(BF).astype(F32)
    rest = norm - high
    mid = rest.astype(BF).astype(F32)
    return swapped, high, mid, rest - mid


def row_features(rows):
    swapped, high, mid, low = norm_parts(rows)
    row = lax.broadcasted_iota(jnp.int32, rows.shape, 0)
    tail = jnp.where(
        row < 3,
        1.0,
        jnp.where(row == 3, high, jnp.where(row == 4, mid, jnp.where(row == 5, low, 0.0))),
    )
    return jnp.concatenate([rows, swapped, tail, jnp.zeros_like(rows)], axis=0).astype(BF)


def col_features(rows):
    _, high, mid, low = norm_parts(rows)
    row = lax.broadcasted_iota(jnp.int32, rows.shape, 0)
    tail = jnp.where(
        row == 0,
        high,
        jnp.where(row == 1, mid, jnp.where(row == 2, low, jnp.where(row < 6, 1.0, 0.0))),
    )
    both = -2.0 * rows
    return jnp.concatenate([both, both, tail, jnp.zeros_like(rows)], axis=0).T.astype(BF)


def matern(squared):
    squared = jnp.maximum(squared, TINY)
    dist = squared * lax.rsqrt(squared)
    return ((1.0 + dist) * jnp.exp2(dist * NEG_LOG2E)).astype(BF)


def pack_kernel(scale_ref, points, mine, got, out_ref):
    half = out_ref.shape[1]
    core = whole(scale_ref[4])

    def step(i, _):
        here = pl.ds(pl.multiple_of(i * 2048, 2048), 2048)
        there = pl.ds(pl.multiple_of(core * half + i * 2048, 2048), 2048)
        rows = coordinate_rows(points[:, there], scale_ref)
        one, two = mine[:, there].astype(F32), got[:, there].astype(F32)
        first, second = jnp.where(core == 0, one, two), jnp.where(core == 0, two, one)
        out_ref[:, here] = jnp.concatenate([first, second, rows], axis=0).astype(BF)
        return 0

    lax.fori_loop(0, half // 2048, step, 0)


def plan_kernel(scale_ref, offs_ref, cols_ref, out_ref):
    device, half_id = whole(scale_ref[3]), whole(scale_ref[4])
    leaves = offs_ref.shape[1]
    slots = cols_ref.shape[1]
    room = out_ref.shape[1]
    half = leaves // 2
    half_bits = half.bit_length() - 1
    begins = jnp.broadcast_to(offs_ref[...].astype(F32), (8, leaves)).T[:, 0:1]
    slot = lax.broadcasted_iota(jnp.int32, (leaves, slots), 1).astype(F32)
    row = jnp.sum(jnp.where(begins <= slot, 1.0, 0.0), axis=0, keepdims=True) - 1.0
    first = jnp.sum(jnp.where(begins == slot, 1.0, 0.0), axis=0, keepdims=True)
    place = cols_ref[...] - (device * leaves - leaves + half_id * half)
    block = place >> half_bits
    own = jnp.where(block == 2, 1.0 - first, 0.0)
    far = jnp.where((block & 3) == 0, 1.0, 0.0)
    kinds = jnp.concatenate([own, far, jnp.zeros((6, slots), F32)], axis=0)
    earlier = lax.broadcasted_iota(jnp.int32, (slots, slots), 0)
    later = lax.broadcasted_iota(jnp.int32, (slots, slots), 1)
    upto = jnp.where(earlier <= later, 1.0, 0.0).astype(BF)
    rank = jnp.dot(kinds.astype(BF), upto, preferred_element_type=F32)
    turned = rank.T
    target = lax.broadcasted_iota(jnp.int32, (slots, room), 1).astype(F32) + 1.0
    at = lax.broadcasted_iota(jnp.int32, (1, room), 1).astype(F32)
    upper, lower = (place >> 4).astype(F32), (place & 15).astype(F32)
    lists = []
    for kind, (mask, shift, spare) in enumerate(
        ((own, float(leaves), float(half)), (far, 0.0, 8.0 * half))
    ):
        parts = jnp.concatenate(
            [row * mask, upper * mask, lower * mask, jnp.zeros((5, slots), F32)], axis=0
        )
        hits = jnp.where(turned[:, kind : kind + 1] == target, 1.0, 0.0).astype(BF)
        got = jnp.dot(parts.astype(BF), hits, preferred_element_type=F32)
        code = got[0:1] * float(CODE) + got[1:2] * 16.0 + got[2:3] - shift
        total = rank[kind : kind + 1, slots - 1 : slots]
        lists.append((jnp.where(at < total, code, spare), total))
    out_ref[...] = jnp.concatenate(
        [
            lists[0][0], lists[1][0],
            jnp.broadcast_to(lists[0][1], (1, room)), jnp.broadcast_to(lists[1][1], (1, room)),
            jnp.zeros((4, room), F32),
        ],
        axis=0,
    ).astype(jnp.int32)


def pipeline(turns, unroll, ahead_first, accumulate, distance, evaluate, s0, s1, k0, k1):
    def half_turn(first, near, ahead, ready, filled):
        for q in range(PAIR):
            if ahead_first:
                distance(first + PAIR + q, ahead.at[q])
            accumulate(first - PAIR + q, ready.at[q])
            if not ahead_first:
                distance(first + PAIR + q, ahead.at[q])
            evaluate(near.at[q], filled.at[q])

    k1[...] = jnp.zeros_like(k1)
    for q in range(PAIR):
        distance(q, s0.at[q])

    def step(it, _):
        for turn in range(unroll):
            first = (it * unroll + turn) * 2 * PAIR
            half_turn(first, s0, s1, k1, k0)
            half_turn(first + PAIR, s1, s0, k0, k1)
        return 0

    lax.fori_loop(0, turns, step, 0)
    for q in range(PAIR):
        accumulate(turns * unroll * 2 * PAIR - PAIR + q, k1.at[q])


def block_loop(kind, unroll, place, plan_ref, row_ref, col_ref, val_ref, sums, s0, s1, k0, k1):
    def accumulate(slot, kern):
        code = plan_ref[kind, jnp.maximum(slot, 0)]
        here = lanes(code >> CODE_BITS)
        part = jnp.dot(val_ref[place(code & (CODE - 1))], kern[...], preferred_element_type=F32)
        sums[0][:, here] += part[:PART]
        sums[1][:, here] += part[PART:]

    def distance(slot, out):
        code = plan_ref[kind, slot]
        out[...] = jnp.dot(
            col_ref[place(code & (CODE - 1))],
            row_ref[code >> CODE_BITS],
            preferred_element_type=F32,
        )

    def evaluate(squared, kern):
        kern[...] = matern(squared[...])


    count = plan_ref[2 + kind, 0]
    turns = (count + unroll * 2 * PAIR - 1) // (unroll * 2 * PAIR)
    pipeline(turns, unroll, True, accumulate, distance, evaluate, s0, s1, k0, k1)


def diagonal_loop(first_leaf, count, row_ref, col_ref, val_ref, sums, s0, s1, k0, k1):
    mid = LEAF // 2

    def distance(slot, out):
        col = jnp.minimum(slot, count - 1)
        rows = row_ref[first_leaf + col]
        out[:mid] = jnp.dot(col_ref[col, :mid], rows, preferred_element_type=F32)
        out[mid:, mid:] = jnp.dot(col_ref[col, mid:], rows[:, mid:], preferred_element_type=F32)

    def evaluate(squared, kern):
        kern[:mid] = matern(squared[:mid])
        kern[mid:, mid:] = matern(squared[mid:, mid:])

    def accumulate(slot, kern):
        col = jnp.maximum(slot, 0)
        values = val_ref[col]
        part = jnp.dot(values[:, :mid], kern[:mid], preferred_element_type=F32)
        left = mul_nt(values[:, mid:], kern[:mid, mid:])
        right = jnp.dot(values[:, mid:], kern[mid:, mid:], preferred_element_type=F32)
        part = part + jnp.concatenate([left, right], axis=1)
        here = lanes(first_leaf + col)
        sums[0][:, here] += part[:PART]
        sums[1][:, here] += part[PART:]

    turns = count // (TURNS * 2 * PAIR)
    pipeline(turns, TURNS, False, accumulate, distance, evaluate, s0, s1, k0, k1)


def load_columns(pack_ref, base, count, col_ref, val_ref):
    def step(i, _):
        for q in range(8):
            leaf = i * 8 + q
            val_ref[base + leaf] = pack_ref[0:16, lanes(leaf)]
            col_ref[base + leaf] = col_features(pack_ref[16:24, lanes(leaf)].astype(F32))
        return 0

    lax.fori_loop(0, count // 8, step, 0)


def near_local_kernel(
    scale_ref, plan_ref, points_ref, pack_ref,
    mine_ref, other_ref, row_ref,
    col_ref, val_ref, s0, s1, k0, k1,
):
    half_id = whole(scale_ref[4])
    leaves = row_ref.shape[0]
    half = leaves // 2

    def rows_step(i, _):
        for q in range(4):
            leaf = i * 4 + q
            row_ref[leaf] = row_features(coordinate_rows(points_ref[:, lanes(leaf)], scale_ref))
            mine_ref[:, lanes(leaf)] = jnp.zeros((PART, LEAF), F32)
            other_ref[:, lanes(leaf)] = jnp.zeros((PART, LEAF), F32)
        return 0

    lax.fori_loop(0, leaves // 4, rows_step, 0)
    load_columns(pack_ref, 0, half, col_ref, val_ref)
    val_ref[half] = jnp.zeros((16, LEAF), BF)
    col_ref[half] = jnp.zeros(col_ref.shape[1:], BF)
    sums = (mine_ref, other_ref)
    diagonal_loop(half_id * half, half, row_ref, col_ref, val_ref, sums, s0, s1, k0, k1)
    block_loop(0, TURNS, lambda c: c, plan_ref, row_ref, col_ref, val_ref, sums, s0, s1, k0, k1)


def near_halo_kernel(
    scale_ref, plan_ref, row_ref, inner_ref, outer_ref, first_in, second_in,
    mine_ref, other_ref,
    first, second, col_ref, val_ref, s0, s1, k0, k1,
):
    core = whole(scale_ref[4])
    half = inner_ref.shape[1] // LEAF
    odd = whole(scale_ref[3]) & 1
    bits = half.bit_length() - 1
    count = plan_ref[3, 0]

    def place(code):
        return (code & (half - 1)) | ((code >> (bits + 2)) << bits)

    def load(i, _):
        for q in range(4):
            code = plan_ref[1, i * 4 + q] & (CODE - 1)
            here = lanes(code & (half - 1))
            paired = (code >> (bits + 2)) + odd == 1
            values = jnp.where(paired, inner_ref[0:16, here], outer_ref[0:16, here])
            rows = jnp.where(paired, inner_ref[16:24, here], outer_ref[16:24, here])
            val_ref[place(code)] = values
            col_ref[place(code)] = col_features(rows.astype(F32))
        return 0

    first[...] = first_in[...]
    second[...] = second_in[...]
    lax.fori_loop(0, (count + 3) // 4, load, 0)
    val_ref[2 * half] = jnp.zeros((16, LEAF), BF)
    col_ref[2 * half] = jnp.zeros(col_ref.shape[1:], BF)
    sums = (first, second)
    block_loop(1, 1, place, plan_ref, row_ref, col_ref, val_ref, sums, s0, s1, k0, k1)

    @pl.when(core == 0)
    def _():
        mine_ref[...] = first[...]
        other_ref[...] = second[...]

    @pl.when(core == 1)
    def _():
        mine_ref[...] = second[...]
        other_ref[...] = first[...]


def split_parts(value):
    high = value.astype(BF).astype(F32)
    return jnp.concatenate([high, value - high], axis=0).astype(BF)


def join_parts(value):
    return value[0:ALL] + value[ALL : 2 * ALL]


def mul_nt(left, right):
    return lax.dot_general(left, right, NT, preferred_element_type=F32)


def over_nodes(count, unroll, work):
    group = min(unroll, count)
    if count == group:
        work([jnp.int32(i) for i in range(count)])
        return

    def step(i, _):
        work([i * group + q for q in range(group)])
        return 0

    lax.fori_loop(0, count // group, step, 0)


def store_turned(flat, r, block):
    turned = block.T
    count = turned.shape[0] // 8
    width = turned.shape[1]
    rows = pl.ds(pl.multiple_of(r * 8, 8), 8)
    flat[0:count, rows] = turned[: count * 8].reshape(count, 8, width)
    rest = turned.shape[0] - count * 8
    flat[count, pl.ds(pl.multiple_of(r * 8, 8), rest)] = turned[count * 8 :]


def load_node(flat, node):
    return flat[node >> 3, pl.ds(node & 7, RANK, stride=8)].astype(BF)


def side_by_side(first, second):
    return jnp.concatenate([first, second], axis=1)


def doubled(pair):
    low = lax.broadcasted_iota(jnp.int32, pair.shape, 1) < RANK
    turned = pltpu.roll(pair, RANK, 1)
    return jnp.where(low, pair, turned), jnp.where(low, turned, pair)


def up_kernel(
    scale_ref, pack_ref, basis_ref, raw_ref, coef_ref, export_ref, front_ref, move_ref,
    flat, pairs,
):
    core = whole(scale_ref[4])
    leaves = move_ref.shape[0]
    levels = leaves.bit_length() - 1
    base = core * leaves

    def keep(parent, first, second):
        pair = side_by_side(first, second)
        pairs[parent] = split_parts(pair)
        one, two = doubled(pair)
        coef_ref[2 * parent + 1] = split_parts(one)
        coef_ref[2 * parent + 2] = split_parts(two)

    def leaf_step(it, _):
        outs = []
        for q in range(8):
            leaf = it * 8 + q
            outs.append(mul_nt(pack_ref[0:ALL, lanes(leaf)], basis_ref[base + leaf]))
        for q in range(8):
            r = it * 8 + q
            block = jnp.concatenate([raw_ref[0, r], raw_ref[1, r]], axis=0).astype(F32)
            store_turned(flat, r, block)
        for q in range(4):
            keep(leaves // 2 - 1 + it * 4 + q, outs[2 * q], outs[2 * q + 1])
        return 0

    lax.fori_loop(0, leaves // 8, leaf_step, 0)
    root_move = load_node(flat, 0)
    move_ref[leaves - 1] = root_move
    for depth in range(levels - 1, 0, -1):
        first = 2**depth - 1
        above = 2 ** (depth - 1) - 1
        start = 2 ** (depth + 1) - 1 + core * 2**depth

        def work(nodes, first=first, above=above, start=start):
            outs = []
            for j in nodes:
                for c in range(2):
                    move = load_node(flat, start + 2 * j + c)
                    move_ref[first + 2 * j + c] = move
                    outs.append(mul_nt(pairs[first + 2 * j + c], move))
            for j, i in enumerate(nodes):
                keep(above + i, join_parts(outs[2 * j]), join_parts(outs[2 * j + 1]))

        over_nodes(2 ** (depth - 1), 8, work)
    move = load_node(flat, 1 + core)
    move_ref[0] = move
    crown = join_parts(mul_nt(pairs[0], move))
    crown = split_parts(side_by_side(crown, crown))
    coef_ref[0] = crown
    side = lax.broadcasted_iota(jnp.int32, crown.shape, 1) // RANK
    root = join_parts(mul_nt(jnp.where(side == core, crown.astype(F32), 0.0).astype(BF), root_move))
    export_ref[0] = split_parts(side_by_side(root, root))
    export_ref[1:EXPORT] = coef_ref[0 : EXPORT - 1]
    front_ref[0] = export_ref[0 : EXPORT // 2]


def joint(first, second, third):
    return jnp.concatenate([first, second, third], axis=1)


def couple_kernel(
    scale_ref, partners_ref, coef_ref, raw_ref, local_ref, tie_ref, wide, thin,
):
    device, core = whole(scale_ref[3]), whole(scale_ref[4])
    levels = (raw_ref.shape[3] + 1).bit_length() - 2
    low = lax.broadcasted_iota(jnp.int32, (2 * ALL, 2 * RANK), 1) < RANK

    def turn(i, _):
        for q in range(8):
            r = i * 8 + q
            block = jnp.concatenate([raw_ref[0, r], raw_ref[1, r]], axis=0).astype(F32)
            store_turned(wide, r, block)
            store_turned(thin, r, raw_ref[2, r].astype(F32))
        return 0

    lax.fori_loop(0, RANK // 8, turn, 0)

    def tie(node):
        return jnp.concatenate([load_node(wide, node), load_node(thin, node)], axis=1)

    tie_ref[0] = tie(0)
    for depth in range(1, SPAN + 1):
        for i in range(2 ** (depth - 1)):
            tie_ref[2 ** (depth - 1) + i] = tie(2**depth - 1 + core * 2 ** (depth - 1) + i)
    for depth in range(SPAN + 1, levels + 1):
        half = 2 ** (depth - 1)
        above = half // 2 - 1
        start = 2**depth - 1 + core * half
        shift = half - 1 - device * 2**depth - core * half

        def work(nodes, above=above, start=start, shift=shift):
            outs = []
            for j in nodes:
                for c in range(2):
                    node = start + 2 * j + c
                    mates = [coef_ref[partners_ref[f, node] + shift] for f in range(3)]
                    left = jnp.concatenate(
                        [jnp.where(low, mates[0], mates[1]), mates[2][:, :RANK]], axis=1
                    )
                    outs.append(mul_nt(left, tie(node)))
            for j, i in enumerate(nodes):
                local_ref[above + i] = side_by_side(
                    join_parts(outs[2 * j]), join_parts(outs[2 * j + 1])
                )

        over_nodes(half // 2, 8, work)


def down_kernel(
    dev_levels, scale_ref, partners_ref, top_partners_ref, top_e, top_b, tie_ref,
    local_ref, move_ref, own_ref, core_ref, next_ref, far_refs, tops_ref, mine_ref, other_ref,
    gather_ref, down, tree,
):
    device, core = whole(scale_ref[3]), whole(scale_ref[4])
    self_id = 2 * device + core
    gather_ref[0] = own_ref[...]
    gather_ref[1] = core_ref[...]
    gather_ref[2:4, 0:4] = next_ref[...]
    for i, far_ref in enumerate(far_refs):
        gather_ref[4 * i + 4 : 4 * i + 8, 0:2] = far_ref[...]
    root_ref = gather_ref if dev_levels == SPAN else tops_ref
    leaves = mine_ref.shape[0]
    levels = leaves.bit_length() - 1
    count = 2**dev_levels

    def roots(nodes):
        for i in nodes:
            parts = join_parts(root_ref[(2 * i) ^ self_id, 0].astype(F32)) + join_parts(
                root_ref[(2 * i + 1) ^ self_id, 0].astype(F32)
            )
            tree[count + i] = split_parts(parts[:, :RANK])

    over_nodes(count, 8, roots)
    for level in range(dev_levels - 1, 1, -1):

        def work(nodes, level=level):
            outs = []
            for i in nodes:
                row = 2**level - 4 + i
                kids = [tree[2 ** (level + 1) + 2 * i + c] for c in range(2)]
                outs.append(mul_nt(kids[0], top_e[row, 0]) + mul_nt(kids[1], top_e[row, 1]))
            for i, out in zip(nodes, outs):
                tree[2**level + i] = split_parts(join_parts(out))

        over_nodes(2**level, 4, work)

    mates = [tree[count + partners_ref[f, 0]] for f in range(3)]
    shallow = [join_parts(mul_nt(joint(*mates), tie_ref[0]))]
    for depth in range(1, SPAN + 1):
        half = 2 ** (depth - 1)
        for i in range(half):
            node = 2**depth - 1 + core * half + i
            picks = []
            for f in range(3):
                mate = partners_ref[f, node]
                at = ((mate >> (depth - 1)) ^ self_id) & (2 * 2**SPAN - 1)
                picks.append(gather_ref[at, half + (mate & (half - 1))][:, :RANK])
            shallow.append(join_parts(mul_nt(joint(*picks), tie_ref[half + i])))

    pushed = jnp.zeros((ALL, RANK), F32)
    for level in range(2, dev_levels):
        node = device >> (dev_levels - level)
        row = 2**level - 4 + node
        side = device >> (dev_levels - level - 1) & 1
        parts = sum(
            mul_nt(tree[2**level + top_partners_ref[row, f]], top_b[row, f]) for f in range(3)
        )
        here = split_parts(join_parts(parts) + pushed)
        pushed = join_parts(jnp.dot(here, top_e[row, side], preferred_element_type=F32))

    root = split_parts(shallow[0] + pushed)
    both = join_parts(jnp.dot(root, move_ref[leaves - 1], preferred_element_type=F32))
    down[0] = split_parts(shallow[1] + jnp.where(core == 0, both[:, :RANK], both[:, RANK:]))
    for depth in range(levels):
        first = 2**depth - 1

        def work(nodes, depth=depth, first=first):
            outs = [
                jnp.dot(down[first + i], move_ref[first + i], preferred_element_type=F32)
                for i in nodes
            ]
            for i, out in zip(nodes, outs):
                node = first + i
                if depth + 2 <= SPAN:
                    kid = 2 ** (depth + 1) + 2 * i
                    base = side_by_side(shallow[kid], shallow[kid + 1])
                else:
                    base = local_ref[node]
                pair = base + join_parts(out)
                if depth == levels - 1:
                    for c in range(2):
                        value = pair[:, c * RANK : (c + 1) * RANK]
                        one, two = value[:PART], value[PART:]
                        mine_ref[2 * i + c] = jnp.where(core == 0, one, two).astype(BF)
                        other_ref[2 * i + c] = jnp.where(core == 0, two, one).astype(BF)
                else:
                    down[2 * node + 1] = split_parts(pair[:, :RANK])
                    down[2 * node + 2] = split_parts(pair[:, RANK:])

        if depth < SPAN:
            work(list(range(2**depth)))
        else:
            over_nodes(2**depth, 8, work)


def final_kernel(
    scale_ref, mine_ref, got_ref, basis, noise, vec, near, swap, out_hbm, out, sems
):
    core = whole(scale_ref[4])
    leaves = mine_ref.shape[0]
    chunks = 2
    per = leaves // chunks
    wide = per * LEAF
    sends = []
    for part, low_ref in enumerate((mine_ref, got_ref)):
        base = jnp.where(core == part, 0, leaves)
        for c in range(chunks):

            def last(nodes, c=c, low_ref=low_ref, base=base):
                rows = [c * per + i for i in nodes]
                fars = [
                    jnp.dot(low_ref[n], basis[base + n], preferred_element_type=F32)
                    for n in rows
                ]
                for n, far in zip(rows, fars):
                    here = lanes(base + n)
                    total = near[:, here] + swap[:, here]
                    out[:, here] = total + noise[:, here] * vec[:, here].astype(F32) + far

            over_nodes(per, 8, last)
            piece = pl.ds(pl.multiple_of((base + c * per) * LEAF, wide), wide)
            send = pltpu.make_async_copy(
                out.at[:, piece], out_hbm.at[:, piece], sems.at[part * chunks + c]
            )
            send.start()
            sends.append(send)
    for send in sends:
        send.wait()


def swap_mask(value, mask):
    total = lax.axis_size("leaf") * lax.axis_size("sub")
    return lax.ppermute(value, ("leaf", "sub"), [(i, i ^ mask) for i in range(total)])


def after(value, anchor):
    return lax.optimization_barrier((value, anchor))[0]


def body(
    points, inv_scale, noise, vectors, leaf_basis, local_transfer, top_transfer,
    local_coupling, top_coupling, local_partners, top_partners, near_offsets, near_cols,
):
    subs = lax.axis_size("sub")
    count = lax.axis_size("leaf") * subs
    dev_levels = count.bit_length() - 1
    device = lax.axis_index("leaf") * subs + lax.axis_index("sub")
    core = lax.axis_index("vec")
    scale = jnp.concatenate([inv_scale, jnp.stack([device, core]).astype(F32)])
    size = vectors.shape[1]
    leaves = near_offsets.shape[0]
    slots = near_cols.shape[0]
    half = size // 2
    sds = jax.ShapeDtypeStruct
    scratch_blocks = [
        VMEM((PAIR, LEAF, LEAF), F32), VMEM((PAIR, LEAF, LEAF), F32),
        VMEM((PAIR, LEAF, LEAF), BF), VMEM((PAIR, LEAF, LEAF), BF),
    ]

    got = lax.ppermute(vectors, "vec", [(0, 1), (1, 0)])

    plan = pl.pallas_call(
        plan_kernel,
        name="plan",
        out_shape=sds((8, slots + 128), jnp.int32),
        in_specs=[sspec(), vspec(), vspec()],
        out_specs=vspec(),
        compiler_params=params(8),
        cost_estimate=pl.CostEstimate(flops=3 * 10**9, bytes_accessed=1 << 16, transcendentals=0),
    )(scale, near_offsets.reshape(1, leaves), near_cols.reshape(1, slots))

    pack = pl.pallas_call(
        pack_kernel,
        name="pack",
        out_shape=sds((24, half), BF),
        in_specs=[sspec(), vspec(), vspec(), vspec()],
        out_specs=vspec(),
        compiler_params=params(8),
        cost_estimate=pl.CostEstimate(flops=2 * 10**9, bytes_accessed=2 << 20, transcendentals=0),
    )(scale, points, vectors, got)
    axes = ("leaf", "sub")
    inner = lax.ppermute(pack, axes, [(i, i ^ 1) for i in range(count)])
    outer = lax.ppermute(
        pack, axes, [(i, ((i + 1) ^ 1) - 1) for i in range(1, count - 1)]
    )

    moves_raw = jnp.transpose(local_transfer, (1, 2, 3, 0))
    part = leaves // 2
    coef, export, front, moves = pl.pallas_call(
        up_kernel,
        name="up",
        out_shape=(
            sds((2 * part - 1, 2 * ALL, 2 * RANK), BF), sds((EXPORT, 2 * ALL, 2 * RANK), BF),
            sds((1, EXPORT // 2, 2 * ALL, 2 * RANK), BF), sds((part, RANK, 2 * RANK), BF),
        ),
        in_specs=[sspec(), vspec(), vspec(), vspec()],
        out_specs=(vspec(),) * 4,
        scratch_shapes=[
            VMEM((leaves // 8, RANK * 8, 2 * RANK), F32),
            VMEM((part - 1, 2 * ALL, 2 * RANK), BF),
        ],
        compiler_params=params(18),
        cost_estimate=pl.CostEstimate(flops=1 * 10**9, bytes_accessed=8 << 20, transcendentals=0),
    )(scale, pack, leaf_basis, moves_raw)
    from_core = lax.ppermute(export, "vec", [(0, 1), (1, 0)])
    pack, _ = lax.optimization_barrier((pack, export))
    first, second, row_feat = pl.pallas_call(
        near_local_kernel,
        name="near_local",
        out_shape=(
            sds((PART, size), F32), sds((PART, size), F32), sds((leaves, 32, LEAF), BF),
        ),
        in_specs=[sspec()] * 2 + [vspec()] * 2,
        out_specs=(vspec(), vspec(), vspec()),
        scratch_shapes=[
            VMEM((leaves // 2 + 1, LEAF, 32), BF), VMEM((leaves // 2 + 1, 16, LEAF), BF),
            *scratch_blocks,
        ],
        compiler_params=params(22),
        cost_estimate=pl.CostEstimate(
            flops=1 * 10**9, bytes_accessed=8 << 20, transcendentals=190 * 2**17
        ),
    )(scale, plan, points, pack)

    from_core = after(from_core, first)
    near_pair = jnp.concatenate([front, from_core[None, 0 : EXPORT // 2]], axis=0)
    coef_late, near_pair = lax.optimization_barrier((coef, near_pair))
    from_next = swap_mask(near_pair, 1)
    ties_raw = jnp.transpose(local_coupling, (1, 2, 3, 0))
    mates = jnp.transpose(local_partners)
    local, ties = pl.pallas_call(
        couple_kernel,
        name="couple",
        out_shape=(
            sds((part - 1, ALL, 2 * RANK), F32), sds((EXPORT, RANK, 3 * RANK), BF),
        ),
        in_specs=[sspec()] * 2 + [vspec(), vspec()],
        out_specs=(vspec(),) * 2,
        scratch_shapes=[
            VMEM((leaves // 4, RANK * 8, 2 * RANK), F32),
            VMEM((leaves // 4, RANK * 8, RANK), F32),
        ],
        compiler_params=params(30),
        cost_estimate=pl.CostEstimate(flops=1 * 10**9, bytes_accessed=8 << 20, transcendentals=0),
    )(scale, mates, coef_late, ties_raw)

    first, _, from_next = lax.optimization_barrier((first, local, from_next))
    quad = jnp.concatenate([near_pair[:, 0:2], from_next[:, 0:2]], axis=0)
    from_far = [swap_mask(quad, mask) for mask in (2, 4, 6)]
    mine, other = pl.pallas_call(
        near_halo_kernel,
        name="near_halo",
        out_shape=(sds((PART, size), F32), sds((PART, size), F32)),
        in_specs=[sspec()] * 2 + [vspec()] * 5,
        out_specs=(vspec(), vspec()),
        scratch_shapes=[
            VMEM((PART, size), F32), VMEM((PART, size), F32),
            VMEM((leaves + 1, LEAF, 32), BF), VMEM((leaves + 1, 16, LEAF), BF),
            *scratch_blocks,
        ],
        compiler_params=params(26),
        cost_estimate=pl.CostEstimate(
            flops=20 * 10**9, bytes_accessed=8 << 20, transcendentals=60 * 2**17
        ),
    )(scale, plan, row_feat, inner, outer, first, second)
    swapped = lax.ppermute(other, "vec", [(0, 1), (1, 0)])

    tops = export
    if dev_levels > SPAN:
        tops = jnp.concatenate(
            [export[None, 0:1], from_core[None, 0:1], from_next[:, 0:1]]
            + [part[:, 0:1] for part in from_far],
            axis=0,
        )
        for bit in range(SPAN, dev_levels):
            tops = jnp.concatenate([tops, swap_mask(tops, 2**bit)], axis=0)
    low_mine, low_other = pl.pallas_call(
        lambda *refs: down_kernel(dev_levels, *refs[:11], refs[11:14], *refs[14:]),
        name="down",
        out_shape=(sds((part, PART, RANK), BF), sds((part, PART, RANK), BF)),
        in_specs=[sspec()] * 3 + [vspec()] * 12,
        out_specs=(vspec(), vspec()),
        scratch_shapes=[
            VMEM((2 * 2**SPAN, EXPORT, 2 * ALL, 2 * RANK), BF),
            VMEM((part - 1, 2 * ALL, RANK), BF), VMEM((2 * count, 2 * ALL, RANK), BF),
        ],
        compiler_params=params(14),
        cost_estimate=pl.CostEstimate(flops=40 * 10**9, bytes_accessed=4 << 20, transcendentals=0),
    )(
        scale, mates, top_partners, top_transfer, top_coupling, ties, local, moves,
        export, from_core, from_next, *from_far, tops,
    )
    low_got = lax.ppermute(low_other, "vec", [(0, 1), (1, 0)])

    return pl.pallas_call(
        final_kernel,
        name="final",
        out_shape=sds((PART, size), F32),
        in_specs=[sspec()] + [vspec()] * 7,
        out_specs=hspec(),
        scratch_shapes=[VMEM((PART, size), F32), pltpu.SemaphoreType.DMA((4,))],
        compiler_params=params(10),
        cost_estimate=pl.CostEstimate(flops=2 * 10**9, bytes_accessed=4 << 20, transcendentals=0),
    )(scale, low_mine, low_got, leaf_basis, noise.reshape(1, size), vectors, mine, swapped)


def solution(mesh):
    return jax.shard_map(
        body,
        mesh=mesh,
        in_specs=(
            P("groups", ("leaf", "sub")),
            P("groups"),
            P(("groups", "leaf", "sub")),
            P(("groups", "vec"), ("leaf", "sub")),
            P(("groups", "leaf", "sub"), None, None),
            P(("groups", "leaf", "sub"), None, None, None),
            P("groups", None, None, None),
            P(("groups", "leaf", "sub"), None, None, None),
            P("groups", None, None, None),
            P(("groups", "leaf", "sub"), None),
            P("groups", None),
            P(("groups", "leaf", "sub")),
            P(("groups", "leaf", "sub")),
        ),
        out_specs=P(("groups", "vec"), ("leaf", "sub")),
        check_vma=False,
    )
```

```python
import functools
import math

import jax
import jax.numpy as jnp
from jax import lax
from jax.experimental import pallas as pl
from jax.experimental.pallas import tpu as pltpu
from jax.sharding import PartitionSpec as P

BF = jnp.bfloat16
F32 = jnp.float32
LEAF = 256
RANK = 64
SPAN = 3
PART = 8
ALL = 2 * PART
EXPORT = 2**SPAN
NEG_LOG2E = -1.0 / math.log(2.0)
ROOT3 = math.sqrt(3.0)
TINY = 1e-12
PAIR = 2
TURNS = 2
CODE_BITS = 10
CODE = 2**CODE_BITS
VMEM = pltpu.VMEM
SMEM = pltpu.SMEM
NT = (((1,), (1,)), ((), ()))


def vspec():
    return pl.BlockSpec(memory_space=pltpu.VMEM)


def sspec():
    return pl.BlockSpec(memory_space=pltpu.SMEM)


def hspec():
    return pl.BlockSpec(memory_space=pltpu.HBM)


def params(mib):
    return pltpu.CompilerParams(vmem_limit_bytes=mib << 20)


def lanes(index):
    return pl.ds(pl.multiple_of(index * LEAF, LEAF), LEAF)


def whole(scalar):
    return scalar.astype(jnp.int32)


def coordinate_rows(raw, scale_ref):
    width = raw.shape[1]
    row = lax.broadcasted_iota(jnp.int32, (8, width), 0)
    scale = jnp.where(
        row == 0, scale_ref[0], jnp.where(row == 1, scale_ref[1], scale_ref[2])
    )
    full = jnp.concatenate([raw, jnp.zeros((5, width), F32)], axis=0)
    scaled = (full - 0.5) * (scale * ROOT3)
    scaled = jnp.where(row < 3, scaled, 0.0)
    high = scaled.astype(BF).astype(F32)
    rest = (scaled - high).astype(BF).astype(F32)
    return high + pltpu.roll(rest, 4, 0)


def norm_parts(rows):
    swapped = pltpu.roll(rows, 4, 0)
    norm = jnp.sum(rows * (rows + swapped), axis=0, keepdims=True)
    high = norm.astype(BF).astype(F32)
    rest = norm - high
    mid = rest.astype(BF).astype(F32)
    return swapped, high, mid, rest - mid


def row_features(rows):
    swapped, high, mid, low = norm_parts(rows)
    row = lax.broadcasted_iota(jnp.int32, rows.shape, 0)
    tail = jnp.where(
        row < 3,
        1.0,
        jnp.where(row == 3, high, jnp.where(row == 4, mid, jnp.where(row == 5, low, 0.0))),
    )
    return jnp.concatenate([rows, swapped, tail, jnp.zeros_like(rows)], axis=0).astype(BF)


def col_features(rows):
    _, high, mid, low = norm_parts(rows)
    row = lax.broadcasted_iota(jnp.int32, rows.shape, 0)
    tail = jnp.where(
        row == 0,
        high,
        jnp.where(row == 1, mid, jnp.where(row == 2, low, jnp.where(row < 6, 1.0, 0.0))),
    )
    both = -2.0 * rows
    return jnp.concatenate([both, both, tail, jnp.zeros_like(rows)], axis=0).T.astype(BF)


def matern(squared):
    squared = jnp.maximum(squared, TINY)
    dist = squared * lax.rsqrt(squared)
    return ((1.0 + dist) * jnp.exp2(dist * NEG_LOG2E)).astype(BF)


def pack_kernel(scale_ref, points, mine, got, out_ref):
    half = out_ref.shape[1]
    core = whole(scale_ref[4])

    def step(i, _):
        here = pl.ds(pl.multiple_of(i * 2048, 2048), 2048)
        there = pl.ds(pl.multiple_of(core * half + i * 2048, 2048), 2048)
        rows = coordinate_rows(points[:, there], scale_ref)
        one, two = mine[:, there].astype(F32), got[:, there].astype(F32)
        first, second = jnp.where(core == 0, one, two), jnp.where(core == 0, two, one)
        out_ref[:, here] = jnp.concatenate([first, second, rows], axis=0).astype(BF)
        return 0

    lax.fori_loop(0, half // 2048, step, 0)


def plan_kernel(leaves, scale_ref, ids_ref, out_ref):
    device, half_id = whole(scale_ref[3]), whole(scale_ref[4])
    slots = ids_ref.shape[1] - leaves
    offs, cols = ids_ref[:, :leaves], ids_ref[:, leaves:]
    room = out_ref.shape[1]
    half = leaves // 2
    half_bits = half.bit_length() - 1
    begins = jnp.broadcast_to(offs.astype(F32), (8, leaves)).T[:, 0:1]
    slot = lax.broadcasted_iota(jnp.int32, (leaves, slots), 1).astype(F32)
    row = jnp.sum(jnp.where(begins <= slot, 1.0, 0.0), axis=0, keepdims=True) - 1.0
    first = jnp.sum(jnp.where(begins == slot, 1.0, 0.0), axis=0, keepdims=True)
    place = cols - (device * leaves - leaves + half_id * half)
    block = place >> half_bits
    own = jnp.where(block == 2, 1.0 - first, 0.0)
    far = jnp.where((block & 3) == 0, 1.0, 0.0)
    kinds = jnp.concatenate([own, far, jnp.zeros((6, slots), F32)], axis=0)
    earlier = lax.broadcasted_iota(jnp.int32, (slots, slots), 0)
    later = lax.broadcasted_iota(jnp.int32, (slots, slots), 1)
    upto = jnp.where(earlier <= later, 1.0, 0.0).astype(BF)
    rank = jnp.dot(kinds.astype(BF), upto, preferred_element_type=F32)
    turned = rank.T
    target = lax.broadcasted_iota(jnp.int32, (slots, room), 1).astype(F32) + 1.0
    at = lax.broadcasted_iota(jnp.int32, (1, room), 1).astype(F32)
    upper, lower = (place >> 4).astype(F32), (place & 15).astype(F32)
    lists = []
    for kind, (mask, shift, spare) in enumerate(
        ((own, float(leaves), float(half)), (far, 0.0, 8.0 * half))
    ):
        parts = jnp.concatenate(
            [row * mask, upper * mask, lower * mask, jnp.zeros((5, slots), F32)], axis=0
        )
        hits = jnp.where(turned[:, kind : kind + 1] == target, 1.0, 0.0).astype(BF)
        got = jnp.dot(parts.astype(BF), hits, preferred_element_type=F32)
        code = got[0:1] * float(CODE) + got[1:2] * 16.0 + got[2:3] - shift
        total = rank[kind : kind + 1, slots - 1 : slots]
        lists.append((jnp.where(at < total, code, spare), total))
    out_ref[...] = jnp.concatenate(
        [
            lists[0][0], lists[1][0],
            jnp.broadcast_to(lists[0][1], (1, room)), jnp.broadcast_to(lists[1][1], (1, room)),
            jnp.zeros((4, room), F32),
        ],
        axis=0,
    ).astype(jnp.int32)


def pipeline(turns, unroll, ahead_first, accumulate, distance, evaluate, s0, s1, k0, k1):
    def half_turn(first, near, ahead, ready, filled):
        for q in range(PAIR):
            if ahead_first:
                distance(first + PAIR + q, ahead.at[q])
            accumulate(first - PAIR + q, ready.at[q])
            if not ahead_first:
                distance(first + PAIR + q, ahead.at[q])
            evaluate(near.at[q], filled.at[q])

    k1[...] = jnp.zeros_like(k1)
    for q in range(PAIR):
        distance(q, s0.at[q])

    def step(it, _):
        for turn in range(unroll):
            first = (it * unroll + turn) * 2 * PAIR
            half_turn(first, s0, s1, k1, k0)
            half_turn(first + PAIR, s1, s0, k0, k1)
        return 0

    lax.fori_loop(0, turns, step, 0)
    for q in range(PAIR):
        accumulate(turns * unroll * 2 * PAIR - PAIR + q, k1.at[q])


def block_loop(kind, unroll, place, plan_ref, row_ref, col_ref, val_ref, sums, s0, s1, k0, k1):
    def accumulate(slot, kern):
        code = plan_ref[kind, jnp.maximum(slot, 0)]
        here = lanes(code >> CODE_BITS)
        part = jnp.dot(val_ref[place(code & (CODE - 1))], kern[...], preferred_element_type=F32)
        sums[0][:, here] += part[:PART]
        sums[1][:, here] += part[PART:]

    def distance(slot, out):
        code = plan_ref[kind, slot]
        out[...] = jnp.dot(
            col_ref[place(code & (CODE - 1))],
            row_ref[code >> CODE_BITS],
            preferred_element_type=F32,
        )

    def evaluate(squared, kern):
        kern[...] = matern(squared[...])


    count = plan_ref[2 + kind, 0]
    turns = (count + unroll * 2 * PAIR - 1) // (unroll * 2 * PAIR)
    pipeline(turns, unroll, True, accumulate, distance, evaluate, s0, s1, k0, k1)


def diagonal_loop(first_leaf, count, row_ref, col_ref, val_ref, sums, s0, s1, k0, k1):
    mid = LEAF // 2

    def distance(slot, out):
        col = jnp.minimum(slot, count - 1)
        rows = row_ref[first_leaf + col]
        out[:mid] = jnp.dot(col_ref[col, :mid], rows, preferred_element_type=F32)
        out[mid:, mid:] = jnp.dot(col_ref[col, mid:], rows[:, mid:], preferred_element_type=F32)

    def evaluate(squared, kern):
        kern[:mid] = matern(squared[:mid])
        kern[mid:, mid:] = matern(squared[mid:, mid:])

    def accumulate(slot, kern):
        col = jnp.maximum(slot, 0)
        values = val_ref[col]
        part = jnp.dot(values[:, :mid], kern[:mid], preferred_element_type=F32)
        left = mul_nt(values[:, mid:], kern[:mid, mid:])
        right = jnp.dot(values[:, mid:], kern[mid:, mid:], preferred_element_type=F32)
        part = part + jnp.concatenate([left, right], axis=1)
        here = lanes(first_leaf + col)
        sums[0][:, here] += part[:PART]
        sums[1][:, here] += part[PART:]

    turns = count // (TURNS * 2 * PAIR)
    pipeline(turns, TURNS, False, accumulate, distance, evaluate, s0, s1, k0, k1)


def load_columns(pack_ref, base, count, col_ref, val_ref):
    def step(i, _):
        for q in range(8):
            leaf = i * 8 + q
            val_ref[base + leaf] = pack_ref[0:16, lanes(leaf)]
            col_ref[base + leaf] = col_features(pack_ref[16:24, lanes(leaf)].astype(F32))
        return 0

    lax.fori_loop(0, count // 8, step, 0)


def near_local_kernel(
    scale_ref, plan_ref, points_ref, pack_ref,
    mine_ref, other_ref, row_ref,
    col_ref, val_ref, s0, s1, k0, k1,
):
    half_id = whole(scale_ref[4])
    leaves = row_ref.shape[0]
    half = leaves // 2

    def rows_step(i, _):
        for q in range(4):
            leaf = i * 4 + q
            row_ref[leaf] = row_features(coordinate_rows(points_ref[:, lanes(leaf)], scale_ref))
            mine_ref[:, lanes(leaf)] = jnp.zeros((PART, LEAF), F32)
            other_ref[:, lanes(leaf)] = jnp.zeros((PART, LEAF), F32)
        return 0

    lax.fori_loop(0, leaves // 4, rows_step, 0)
    load_columns(pack_ref, 0, half, col_ref, val_ref)
    val_ref[half] = jnp.zeros((16, LEAF), BF)
    col_ref[half] = jnp.zeros(col_ref.shape[1:], BF)
    sums = (mine_ref, other_ref)
    diagonal_loop(half_id * half, half, row_ref, col_ref, val_ref, sums, s0, s1, k0, k1)
    block_loop(0, TURNS, lambda c: c, plan_ref, row_ref, col_ref, val_ref, sums, s0, s1, k0, k1)


def near_halo_kernel(
    scale_ref, plan_ref, row_ref, inner_ref, outer_ref, first_in, second_in,
    mine_ref, other_ref,
    first, second, col_ref, val_ref, s0, s1, k0, k1,
):
    core = whole(scale_ref[4])
    half = inner_ref.shape[1] // LEAF
    odd = whole(scale_ref[3]) & 1
    bits = half.bit_length() - 1
    count = plan_ref[3, 0]

    def place(code):
        return (code & (half - 1)) | ((code >> (bits + 2)) << bits)

    def load(i, _):
        for q in range(4):
            code = plan_ref[1, i * 4 + q] & (CODE - 1)
            here = lanes(code & (half - 1))
            paired = (code >> (bits + 2)) + odd == 1
            values = jnp.where(paired, inner_ref[0:16, here], outer_ref[0:16, here])
            rows = jnp.where(paired, inner_ref[16:24, here], outer_ref[16:24, here])
            val_ref[place(code)] = values
            col_ref[place(code)] = col_features(rows.astype(F32))
        return 0

    first[...] = first_in[...]
    second[...] = second_in[...]
    lax.fori_loop(0, (count + 3) // 4, load, 0)
    val_ref[2 * half] = jnp.zeros((16, LEAF), BF)
    col_ref[2 * half] = jnp.zeros(col_ref.shape[1:], BF)
    sums = (first, second)
    block_loop(1, 1, place, plan_ref, row_ref, col_ref, val_ref, sums, s0, s1, k0, k1)

    @pl.when(core == 0)
    def _():
        mine_ref[...] = first[...]
        other_ref[...] = second[...]

    @pl.when(core == 1)
    def _():
        mine_ref[...] = second[...]
        other_ref[...] = first[...]


def split_parts(value):
    high = value.astype(BF).astype(F32)
    return jnp.concatenate([high, value - high], axis=0).astype(BF)


def join_parts(value):
    return value[0:ALL] + value[ALL : 2 * ALL]


def mul_nt(left, right):
    return lax.dot_general(left, right, NT, preferred_element_type=F32)


def over_nodes(count, unroll, work):
    group = min(unroll, count)
    if count == group:
        work([jnp.int32(i) for i in range(count)])
        return

    def step(i, _):
        work([i * group + q for q in range(group)])
        return 0

    lax.fori_loop(0, count // group, step, 0)


def store_turned(flat, r, block):
    turned = block.T
    count = turned.shape[0] // 8
    width = turned.shape[1]
    rows = pl.ds(pl.multiple_of(r * 8, 8), 8)
    flat[0:count, rows] = turned[: count * 8].reshape(count, 8, width)
    rest = turned.shape[0] - count * 8
    flat[count, pl.ds(pl.multiple_of(r * 8, 8), rest)] = turned[count * 8 :]


def load_node(flat, node):
    return flat[node >> 3, pl.ds(node & 7, RANK, stride=8)].astype(BF)


def side_by_side(first, second):
    return jnp.concatenate([first, second], axis=1)


def doubled(pair):
    low = lax.broadcasted_iota(jnp.int32, pair.shape, 1) < RANK
    turned = pltpu.roll(pair, RANK, 1)
    return jnp.where(low, pair, turned), jnp.where(low, turned, pair)


def up_kernel(
    scale_ref, pack_ref, basis_ref, raw_ref, coef_ref, export_ref, front_ref, move_ref,
    flat, pairs,
):
    core = whole(scale_ref[4])
    leaves = move_ref.shape[0]
    levels = leaves.bit_length() - 1
    base = core * leaves

    def keep(parent, first, second):
        pair = side_by_side(first, second)
        pairs[parent] = split_parts(pair)
        one, two = doubled(pair)
        coef_ref[2 * parent + 1] = split_parts(one)
        coef_ref[2 * parent + 2] = split_parts(two)

    def leaf_step(it, _):
        outs = []
        for q in range(8):
            leaf = it * 8 + q
            outs.append(mul_nt(pack_ref[0:ALL, lanes(leaf)], basis_ref[base + leaf]))
        for q in range(8):
            r = it * 8 + q
            block = jnp.concatenate([raw_ref[0, r], raw_ref[1, r]], axis=0).astype(F32)
            store_turned(flat, r, block)
        for q in range(4):
            keep(leaves // 2 - 1 + it * 4 + q, outs[2 * q], outs[2 * q + 1])
        return 0

    lax.fori_loop(0, leaves // 8, leaf_step, 0)
    root_move = load_node(flat, 0)
    move_ref[leaves - 1] = root_move
    for depth in range(levels - 1, 0, -1):
        first = 2**depth - 1
        above = 2 ** (depth - 1) - 1
        start = 2 ** (depth + 1) - 1 + core * 2**depth

        def work(nodes, first=first, above=above, start=start):
            outs = []
            for j in nodes:
                for c in range(2):
                    move = load_node(flat, start + 2 * j + c)
                    move_ref[first + 2 * j + c] = move
                    outs.append(mul_nt(pairs[first + 2 * j + c], move))
            for j, i in enumerate(nodes):
                keep(above + i, join_parts(outs[2 * j]), join_parts(outs[2 * j + 1]))

        over_nodes(2 ** (depth - 1), 8, work)
    move = load_node(flat, 1 + core)
    move_ref[0] = move
    crown = join_parts(mul_nt(pairs[0], move))
    crown = split_parts(side_by_side(crown, crown))
    coef_ref[0] = crown
    side = lax.broadcasted_iota(jnp.int32, crown.shape, 1) // RANK
    root = join_parts(mul_nt(jnp.where(side == core, crown.astype(F32), 0.0).astype(BF), root_move))
    export_ref[0] = split_parts(side_by_side(root, root))
    export_ref[1:EXPORT] = coef_ref[0 : EXPORT - 1]
    front_ref[0] = export_ref[0 : EXPORT // 2]


def joint(first, second, third):
    return jnp.concatenate([first, second, third], axis=1)


def couple_kernel(
    scale_ref, partners_ref, coef_ref, raw_ref, local_ref, tie_ref, wide, thin,
):
    device, core = whole(scale_ref[3]), whole(scale_ref[4])
    levels = (raw_ref.shape[3] + 1).bit_length() - 2
    low = lax.broadcasted_iota(jnp.int32, (2 * ALL, 2 * RANK), 1) < RANK

    def turn(i, _):
        for q in range(8):
            r = i * 8 + q
            block = jnp.concatenate([raw_ref[0, r], raw_ref[1, r]], axis=0).astype(F32)
            store_turned(wide, r, block)
            store_turned(thin, r, raw_ref[2, r].astype(F32))
        return 0

    lax.fori_loop(0, RANK // 8, turn, 0)

    def tie(node):
        return jnp.concatenate([load_node(wide, node), load_node(thin, node)], axis=1)

    tie_ref[0] = tie(0)
    for depth in range(1, SPAN + 1):
        for i in range(2 ** (depth - 1)):
            tie_ref[2 ** (depth - 1) + i] = tie(2**depth - 1 + core * 2 ** (depth - 1) + i)
    for depth in range(SPAN + 1, levels + 1):
        half = 2 ** (depth - 1)
        above = half // 2 - 1
        start = 2**depth - 1 + core * half
        shift = half - 1 - device * 2**depth - core * half

        def work(nodes, above=above, start=start, shift=shift):
            outs = []
            for j in nodes:
                for c in range(2):
                    node = start + 2 * j + c
                    mates = [coef_ref[partners_ref[f, node] + shift] for f in range(3)]
                    left = jnp.concatenate(
                        [jnp.where(low, mates[0], mates[1]), mates[2][:, :RANK]], axis=1
                    )
                    outs.append(mul_nt(left, tie(node)))
            for j, i in enumerate(nodes):
                local_ref[above + i] = side_by_side(
                    join_parts(outs[2 * j]), join_parts(outs[2 * j + 1])
                )

        over_nodes(half // 2, 8, work)


def down_kernel(
    dev_levels, scale_ref, partners_ref, top_partners_ref, top_e, top_b, tie_ref,
    local_ref, move_ref, own_ref, core_ref, next_ref, far_refs, tops_ref, mine_ref, other_ref,
    gather_ref, down, tree,
):
    device, core = whole(scale_ref[3]), whole(scale_ref[4])
    self_id = 2 * device + core
    gather_ref[0] = own_ref[...]
    gather_ref[1] = core_ref[...]
    gather_ref[2:4, 0:4] = next_ref[...]
    for i, far_ref in enumerate(far_refs):
        gather_ref[4 * i + 4 : 4 * i + 8, 0:2] = far_ref[...]
    root_ref = gather_ref if dev_levels == SPAN else tops_ref
    leaves = mine_ref.shape[0]
    levels = leaves.bit_length() - 1
    count = 2**dev_levels

    def roots(nodes):
        for i in nodes:
            parts = join_parts(root_ref[(2 * i) ^ self_id, 0].astype(F32)) + join_parts(
                root_ref[(2 * i + 1) ^ self_id, 0].astype(F32)
            )
            tree[count + i] = split_parts(parts[:, :RANK])

    over_nodes(count, 8, roots)
    for level in range(dev_levels - 1, 1, -1):

        def work(nodes, level=level):
            outs = []
            for i in nodes:
                row = 2**level - 4 + i
                kids = [tree[2 ** (level + 1) + 2 * i + c] for c in range(2)]
                outs.append(mul_nt(kids[0], top_e[row, 0]) + mul_nt(kids[1], top_e[row, 1]))
            for i, out in zip(nodes, outs):
                tree[2**level + i] = split_parts(join_parts(out))

        over_nodes(2**level, 4, work)

    mates = [tree[count + partners_ref[f, 0]] for f in range(3)]
    shallow = [join_parts(mul_nt(joint(*mates), tie_ref[0]))]
    for depth in range(1, SPAN + 1):
        half = 2 ** (depth - 1)
        for i in range(half):
            node = 2**depth - 1 + core * half + i
            picks = []
            for f in range(3):
                mate = partners_ref[f, node]
                at = ((mate >> (depth - 1)) ^ self_id) & (2 * 2**SPAN - 1)
                picks.append(gather_ref[at, half + (mate & (half - 1))][:, :RANK])
            shallow.append(join_parts(mul_nt(joint(*picks), tie_ref[half + i])))

    pushed = jnp.zeros((ALL, RANK), F32)
    for level in range(2, dev_levels):
        node = device >> (dev_levels - level)
        row = 2**level - 4 + node
        side = device >> (dev_levels - level - 1) & 1
        parts = sum(
            mul_nt(tree[2**level + top_partners_ref[row, f]], top_b[row, f]) for f in range(3)
        )
        here = split_parts(join_parts(parts) + pushed)
        pushed = join_parts(jnp.dot(here, top_e[row, side], preferred_element_type=F32))

    root = split_parts(shallow[0] + pushed)
    both = join_parts(jnp.dot(root, move_ref[leaves - 1], preferred_element_type=F32))
    down[0] = split_parts(shallow[1] + jnp.where(core == 0, both[:, :RANK], both[:, RANK:]))
    for depth in range(levels):
        first = 2**depth - 1

        def work(nodes, depth=depth, first=first):
            outs = [
                jnp.dot(down[first + i], move_ref[first + i], preferred_element_type=F32)
                for i in nodes
            ]
            for i, out in zip(nodes, outs):
                node = first + i
                if depth + 2 <= SPAN:
                    kid = 2 ** (depth + 1) + 2 * i
                    base = side_by_side(shallow[kid], shallow[kid + 1])
                else:
                    base = local_ref[node]
                pair = base + join_parts(out)
                if depth == levels - 1:
                    for c in range(2):
                        value = pair[:, c * RANK : (c + 1) * RANK]
                        one, two = value[:PART], value[PART:]
                        mine_ref[2 * i + c] = jnp.where(core == 0, one, two).astype(BF)
                        other_ref[2 * i + c] = jnp.where(core == 0, two, one).astype(BF)
                else:
                    down[2 * node + 1] = split_parts(pair[:, :RANK])
                    down[2 * node + 2] = split_parts(pair[:, RANK:])

        if depth < SPAN:
            work(list(range(2**depth)))
        else:
            over_nodes(2**depth, 8, work)


def final_kernel(
    scale_ref, mine_ref, got_ref, basis, noise, vec, near_hbm, swap_hbm, out_hbm,
    near, swap, out, sems,
):
    core = whole(scale_ref[4])
    leaves = mine_ref.shape[0]
    loads = [
        pltpu.make_async_copy(near_hbm, near, sems.at[0]),
        pltpu.make_async_copy(swap_hbm, swap, sems.at[1]),
    ]
    for load in loads:
        load.start()
    for part, low_ref in enumerate((mine_ref, got_ref)):
        base = jnp.where(core == part, 0, leaves)

        def last(nodes, low_ref=low_ref, base=base):
            fars = [
                jnp.dot(low_ref[n], basis[base + n], preferred_element_type=F32) for n in nodes
            ]
            for n, far in zip(nodes, fars):
                here = lanes(base + n)
                out[:, here] = noise[:, here] * vec[:, here].astype(F32) + far

        over_nodes(leaves, 8, last)
    for load in loads:
        load.wait()
    chunks = 4
    wide = out.shape[1] // chunks
    sends = []
    for c in range(chunks):
        piece = slice(c * wide, (c + 1) * wide)
        out[:, piece] += near[:, piece] + swap[:, piece]
        send = pltpu.make_async_copy(out.at[:, piece], out_hbm.at[:, piece], sems.at[2 + c])
        send.start()
        sends.append(send)
    for send in sends:
        send.wait()


def swap_mask(value, mask):
    total = lax.axis_size("leaf") * lax.axis_size("sub")
    return lax.ppermute(value, ("leaf", "sub"), [(i, i ^ mask) for i in range(total)])


def after(value, anchor):
    return lax.optimization_barrier((value, anchor))[0]


def body(
    points, inv_scale, noise, vectors, leaf_basis, local_transfer, top_transfer,
    local_coupling, top_coupling, local_partners, top_partners, near_offsets, near_cols,
):
    subs = lax.axis_size("sub")
    count = lax.axis_size("leaf") * subs
    dev_levels = count.bit_length() - 1
    device = lax.axis_index("leaf") * subs + lax.axis_index("sub")
    core = lax.axis_index("vec")
    scale = jnp.concatenate([inv_scale, jnp.stack([device, core]).astype(F32)])
    size = vectors.shape[1]
    leaves = near_offsets.shape[0]
    slots = near_cols.shape[0]
    half = size // 2
    sds = jax.ShapeDtypeStruct
    scratch_blocks = [
        VMEM((PAIR, LEAF, LEAF), F32), VMEM((PAIR, LEAF, LEAF), F32),
        VMEM((PAIR, LEAF, LEAF), BF), VMEM((PAIR, LEAF, LEAF), BF),
    ]

    got = lax.ppermute(vectors, "vec", [(0, 1), (1, 0)])

    plan = pl.pallas_call(
        functools.partial(plan_kernel, leaves),
        name="plan",
        out_shape=sds((8, slots + 128), jnp.int32),
        in_specs=[sspec(), vspec()],
        out_specs=vspec(),
        compiler_params=params(8),
        cost_estimate=pl.CostEstimate(flops=3 * 10**9, bytes_accessed=1 << 16, transcendentals=0),
    )(scale, jnp.concatenate([near_offsets, near_cols]).reshape(1, leaves + slots))

    pack = pl.pallas_call(
        pack_kernel,
        name="pack",
        out_shape=sds((24, half), BF),
        in_specs=[sspec(), vspec(), vspec(), vspec()],
        out_specs=vspec(),
        compiler_params=params(8),
        cost_estimate=pl.CostEstimate(flops=2 * 10**9, bytes_accessed=2 << 20, transcendentals=0),
    )(scale, points, vectors, got)
    axes = ("leaf", "sub")
    inner = lax.ppermute(pack, axes, [(i, i ^ 1) for i in range(count)])
    outer = lax.ppermute(
        pack, axes, [(i, ((i + 1) ^ 1) - 1) for i in range(1, count - 1)]
    )

    moves_raw = jnp.transpose(local_transfer, (1, 2, 3, 0))
    part = leaves // 2
    coef, export, front, moves = pl.pallas_call(
        up_kernel,
        name="up",
        out_shape=(
            sds((2 * part - 1, 2 * ALL, 2 * RANK), BF), sds((EXPORT, 2 * ALL, 2 * RANK), BF),
            sds((1, EXPORT // 2, 2 * ALL, 2 * RANK), BF), sds((part, RANK, 2 * RANK), BF),
        ),
        in_specs=[sspec(), vspec(), vspec(), vspec()],
        out_specs=(vspec(),) * 4,
        scratch_shapes=[
            VMEM((leaves // 8, RANK * 8, 2 * RANK), F32),
            VMEM((part - 1, 2 * ALL, 2 * RANK), BF),
        ],
        compiler_params=params(18),
        cost_estimate=pl.CostEstimate(flops=8 * 10**9, bytes_accessed=8 << 20, transcendentals=0),
    )(scale, pack, leaf_basis, moves_raw)
    from_core = lax.ppermute(export, "vec", [(0, 1), (1, 0)])
    pack, _ = lax.optimization_barrier((pack, export))
    first, second, row_feat = pl.pallas_call(
        near_local_kernel,
        name="near_local",
        out_shape=(
            sds((PART, size), F32), sds((PART, size), F32), sds((leaves, 32, LEAF), BF),
        ),
        in_specs=[sspec()] * 2 + [vspec()] * 2,
        out_specs=(vspec(), vspec(), vspec()),
        scratch_shapes=[
            VMEM((leaves // 2 + 1, LEAF, 32), BF), VMEM((leaves // 2 + 1, 16, LEAF), BF),
            *scratch_blocks,
        ],
        compiler_params=params(22),
        cost_estimate=pl.CostEstimate(
            flops=36 * 10**9, bytes_accessed=8 << 20, transcendentals=190 * 2**17
        ),
    )(scale, plan, points, pack)

    from_core = after(from_core, first)
    near_pair = jnp.concatenate([front, from_core[None, 0 : EXPORT // 2]], axis=0)
    coef_late, near_pair = lax.optimization_barrier((coef, near_pair))
    from_next = swap_mask(near_pair, 1)
    ties_raw = jnp.transpose(local_coupling, (1, 2, 3, 0))
    mates = jnp.transpose(local_partners)
    local, ties = pl.pallas_call(
        couple_kernel,
        name="couple",
        out_shape=(
            sds((part - 1, ALL, 2 * RANK), F32), sds((EXPORT, RANK, 3 * RANK), BF),
        ),
        in_specs=[sspec()] * 2 + [vspec(), vspec()],
        out_specs=(vspec(),) * 2,
        scratch_shapes=[
            VMEM((leaves // 4, RANK * 8, 2 * RANK), F32),
            VMEM((leaves // 4, RANK * 8, RANK), F32),
        ],
        compiler_params=params(30),
        cost_estimate=pl.CostEstimate(flops=16 * 10**9, bytes_accessed=8 << 20, transcendentals=0),
    )(scale, mates, coef_late, ties_raw)

    first, _, from_next = lax.optimization_barrier((first, local, from_next))
    quad = jnp.concatenate([near_pair[:, 0:2], from_next[:, 0:2]], axis=0)
    from_far = [swap_mask(quad, mask) for mask in (2, 4, 6)]
    mine, other = pl.pallas_call(
        near_halo_kernel,
        name="near_halo",
        out_shape=(sds((PART, size), F32), sds((PART, size), F32)),
        in_specs=[sspec()] * 2 + [vspec()] * 5,
        out_specs=(vspec(), vspec()),
        scratch_shapes=[
            VMEM((PART, size), F32), VMEM((PART, size), F32),
            VMEM((leaves + 1, LEAF, 32), BF), VMEM((leaves + 1, 16, LEAF), BF),
            *scratch_blocks,
        ],
        compiler_params=params(26),
        cost_estimate=pl.CostEstimate(
            flops=20 * 10**9, bytes_accessed=8 << 20, transcendentals=60 * 2**17
        ),
    )(scale, plan, row_feat, inner, outer, first, second)
    swapped = lax.ppermute(other, "vec", [(0, 1), (1, 0)])

    tops = export
    if dev_levels > SPAN:
        tops = jnp.concatenate(
            [export[None, 0:1], from_core[None, 0:1], from_next[:, 0:1]]
            + [part[:, 0:1] for part in from_far],
            axis=0,
        )
        for bit in range(SPAN, dev_levels):
            tops = jnp.concatenate([tops, swap_mask(tops, 2**bit)], axis=0)
    low_mine, low_other = pl.pallas_call(
        lambda *refs: down_kernel(dev_levels, *refs[:11], refs[11:14], *refs[14:]),
        name="down",
        out_shape=(sds((part, PART, RANK), BF), sds((part, PART, RANK), BF)),
        in_specs=[sspec()] * 3 + [vspec()] * 12,
        out_specs=(vspec(), vspec()),
        scratch_shapes=[
            VMEM((2 * 2**SPAN, EXPORT, 2 * ALL, 2 * RANK), BF),
            VMEM((part - 1, 2 * ALL, RANK), BF), VMEM((2 * count, 2 * ALL, RANK), BF),
        ],
        compiler_params=params(14),
        cost_estimate=pl.CostEstimate(flops=40 * 10**9, bytes_accessed=4 << 20, transcendentals=0),
    )(
        scale, mates, top_partners, top_transfer, top_coupling, ties, local, moves,
        export, from_core, from_next, *from_far, tops,
    )
    low_got = lax.ppermute(low_other, "vec", [(0, 1), (1, 0)])

    return pl.pallas_call(
        final_kernel,
        name="final",
        out_shape=sds((PART, size), F32),
        in_specs=[sspec()] + [vspec()] * 5 + [hspec()] * 2,
        out_specs=hspec(),
        scratch_shapes=[VMEM((PART, size), F32)] * 3 + [pltpu.SemaphoreType.DMA((6,))],
        compiler_params=params(10),
        cost_estimate=pl.CostEstimate(flops=2 * 10**9, bytes_accessed=4 << 20, transcendentals=0),
    )(scale, low_mine, low_got, leaf_basis, noise.reshape(1, size), vectors, mine, swapped)


def solution(mesh):
    return jax.shard_map(
        body,
        mesh=mesh,
        in_specs=(
            P("groups", ("leaf", "sub")),
            P("groups"),
            P(("groups", "leaf", "sub")),
            P(("groups", "vec"), ("leaf", "sub")),
            P(("groups", "leaf", "sub"), None, None),
            P(("groups", "leaf", "sub"), None, None, None),
            P("groups", None, None, None),
            P(("groups", "leaf", "sub"), None, None, None),
            P("groups", None, None, None),
            P(("groups", "leaf", "sub"), None),
            P("groups", None),
            P(("groups", "leaf", "sub")),
            P(("groups", "leaf", "sub")),
        ),
        out_specs=P(("groups", "vec"), ("leaf", "sub")),
        check_vma=False,
    )
```

```python
import functools
import math

import jax
import jax.numpy as jnp
from jax import lax
from jax.experimental import pallas as pl
from jax.experimental.pallas import tpu as pltpu
from jax.sharding import PartitionSpec as P

BF = jnp.bfloat16
F32 = jnp.float32
LEAF = 256
RANK = 64
SPAN = 3
PART = 8
ALL = 2 * PART
EXPORT = 2**SPAN
NEG_LOG2E = -1.0 / math.log(2.0)
ROOT3 = math.sqrt(3.0)
TINY = 1e-12
PAIR = 2
TURNS = 2
CODE_BITS = 10
CODE = 2**CODE_BITS
VMEM = pltpu.VMEM
SMEM = pltpu.SMEM
NT = (((1,), (1,)), ((), ()))


def vspec():
    return pl.BlockSpec(memory_space=pltpu.VMEM)


def sspec():
    return pl.BlockSpec(memory_space=pltpu.SMEM)


def hspec():
    return pl.BlockSpec(memory_space=pltpu.HBM)


def params(mib):
    return pltpu.CompilerParams(vmem_limit_bytes=mib << 20)


def lanes(index):
    return pl.ds(pl.multiple_of(index * LEAF, LEAF), LEAF)


def whole(scalar):
    return scalar.astype(jnp.int32)


def coordinate_rows(raw, scale_ref):
    width = raw.shape[1]
    row = lax.broadcasted_iota(jnp.int32, (8, width), 0)
    scale = jnp.where(
        row == 0, scale_ref[0], jnp.where(row == 1, scale_ref[1], scale_ref[2])
    )
    full = jnp.concatenate([raw, jnp.zeros((5, width), F32)], axis=0)
    scaled = (full - 0.5) * (scale * ROOT3)
    scaled = jnp.where(row < 3, scaled, 0.0)
    high = scaled.astype(BF).astype(F32)
    rest = (scaled - high).astype(BF).astype(F32)
    return high + pltpu.roll(rest, 4, 0)


def norm_parts(rows):
    swapped = pltpu.roll(rows, 4, 0)
    norm = jnp.sum(rows * (rows + swapped), axis=0, keepdims=True)
    high = norm.astype(BF).astype(F32)
    rest = norm - high
    mid = rest.astype(BF).astype(F32)
    return swapped, high, mid, rest - mid


def row_features(rows):
    swapped, high, mid, low = norm_parts(rows)
    row = lax.broadcasted_iota(jnp.int32, rows.shape, 0)
    tail = jnp.where(
        row < 3,
        1.0,
        jnp.where(row == 3, high, jnp.where(row == 4, mid, jnp.where(row == 5, low, 0.0))),
    )
    return jnp.concatenate([rows, swapped, tail, jnp.zeros_like(rows)], axis=0).astype(BF)


def col_features(rows):
    _, high, mid, low = norm_parts(rows)
    row = lax.broadcasted_iota(jnp.int32, rows.shape, 0)
    tail = jnp.where(
        row == 0,
        high,
        jnp.where(row == 1, mid, jnp.where(row == 2, low, jnp.where(row < 6, 1.0, 0.0))),
    )
    both = -2.0 * rows
    return jnp.concatenate([both, both, tail, jnp.zeros_like(rows)], axis=0).T.astype(BF)


def matern(squared):
    squared = jnp.maximum(squared, TINY)
    dist = squared * lax.rsqrt(squared)
    return ((1.0 + dist) * jnp.exp2(dist * NEG_LOG2E)).astype(BF)


def pack_kernel(scale_ref, points, mine, got, out_ref):
    half = out_ref.shape[1]
    core = whole(scale_ref[4])

    def step(i, _):
        here = pl.ds(pl.multiple_of(i * 2048, 2048), 2048)
        there = pl.ds(pl.multiple_of(core * half + i * 2048, 2048), 2048)
        rows = coordinate_rows(points[:, there], scale_ref)
        one, two = mine[:, there].astype(F32), got[:, there].astype(F32)
        first, second = jnp.where(core == 0, one, two), jnp.where(core == 0, two, one)
        out_ref[:, here] = jnp.concatenate([first, second, rows], axis=0).astype(BF)
        return 0

    lax.fori_loop(0, half // 2048, step, 0)


def plan_kernel(leaves, scale_ref, ids_ref, out_ref):
    device, half_id = whole(scale_ref[3]), whole(scale_ref[4])
    slots = ids_ref.shape[1] - leaves
    offs, cols = ids_ref[:, :leaves], ids_ref[:, leaves:]
    room = out_ref.shape[1]
    half = leaves // 2
    half_bits = half.bit_length() - 1
    begins = jnp.broadcast_to(offs.astype(F32), (8, leaves)).T[:, 0:1]
    slot = lax.broadcasted_iota(jnp.int32, (leaves, slots), 1).astype(F32)
    row = jnp.sum(jnp.where(begins <= slot, 1.0, 0.0), axis=0, keepdims=True) - 1.0
    first = jnp.sum(jnp.where(begins == slot, 1.0, 0.0), axis=0, keepdims=True)
    place = cols - (device * leaves - leaves + half_id * half)
    block = place >> half_bits
    own = jnp.where(block == 2, 1.0 - first, 0.0)
    far = jnp.where((block & 3) == 0, 1.0, 0.0)
    kinds = jnp.concatenate([own, far, jnp.zeros((6, slots), F32)], axis=0)
    earlier = lax.broadcasted_iota(jnp.int32, (slots, slots), 0)
    later = lax.broadcasted_iota(jnp.int32, (slots, slots), 1)
    upto = jnp.where(earlier <= later, 1.0, 0.0).astype(BF)
    rank = jnp.dot(kinds.astype(BF), upto, preferred_element_type=F32)
    turned = rank.T
    target = lax.broadcasted_iota(jnp.int32, (slots, room), 1).astype(F32) + 1.0
    at = lax.broadcasted_iota(jnp.int32, (1, room), 1).astype(F32)
    upper, lower = (place >> 4).astype(F32), (place & 15).astype(F32)
    lists = []
    for kind, (mask, shift, spare) in enumerate(
        ((own, float(leaves), float(half)), (far, 0.0, 8.0 * half))
    ):
        parts = jnp.concatenate(
            [row * mask, upper * mask, lower * mask, jnp.zeros((5, slots), F32)], axis=0
        )
        hits = jnp.where(turned[:, kind : kind + 1] == target, 1.0, 0.0).astype(BF)
        got = jnp.dot(parts.astype(BF), hits, preferred_element_type=F32)
        code = got[0:1] * float(CODE) + got[1:2] * 16.0 + got[2:3] - shift
        total = rank[kind : kind + 1, slots - 1 : slots]
        lists.append((jnp.where(at < total, code, spare), total))
    out_ref[...] = jnp.concatenate(
        [
            lists[0][0], lists[1][0],
            jnp.broadcast_to(lists[0][1], (1, room)), jnp.broadcast_to(lists[1][1], (1, room)),
            jnp.zeros((4, room), F32),
        ],
        axis=0,
    ).astype(jnp.int32)


def pipeline(turns, unroll, ahead_first, accumulate, distance, evaluate, s0, s1, k0, k1):
    def half_turn(first, near, ahead, ready, filled):
        for q in range(PAIR):
            if ahead_first:
                distance(first + PAIR + q, ahead.at[q])
            accumulate(first - PAIR + q, ready.at[q])
            if not ahead_first:
                distance(first + PAIR + q, ahead.at[q])
            evaluate(near.at[q], filled.at[q])

    k1[...] = jnp.zeros_like(k1)
    for q in range(PAIR):
        distance(q, s0.at[q])

    def step(it, _):
        for turn in range(unroll):
            first = (it * unroll + turn) * 2 * PAIR
            half_turn(first, s0, s1, k1, k0)
            half_turn(first + PAIR, s1, s0, k0, k1)
        return 0

    lax.fori_loop(0, turns, step, 0)
    for q in range(PAIR):
        accumulate(turns * unroll * 2 * PAIR - PAIR + q, k1.at[q])


def block_loop(kind, unroll, place, plan_ref, row_ref, col_ref, val_ref, sums, s0, s1, k0, k1):
    def accumulate(slot, kern):
        code = plan_ref[kind, jnp.maximum(slot, 0)]
        here = lanes(code >> CODE_BITS)
        part = jnp.dot(val_ref[place(code & (CODE - 1))], kern[...], preferred_element_type=F32)
        sums[0][:, here] += part[:PART]
        sums[1][:, here] += part[PART:]

    def distance(slot, out):
        code = plan_ref[kind, slot]
        out[...] = jnp.dot(
            col_ref[place(code & (CODE - 1))],
            row_ref[code >> CODE_BITS],
            preferred_element_type=F32,
        )

    def evaluate(squared, kern):
        kern[...] = matern(squared[...])


    count = plan_ref[2 + kind, 0]
    turns = (count + unroll * 2 * PAIR - 1) // (unroll * 2 * PAIR)
    pipeline(turns, unroll, True, accumulate, distance, evaluate, s0, s1, k0, k1)


def diagonal_loop(first_leaf, count, row_ref, col_ref, val_ref, sums, s0, s1, k0, k1):
    mid = LEAF // 2

    def distance(slot, out):
        col = jnp.minimum(slot, count - 1)
        rows = row_ref[first_leaf + col]
        out[:mid] = jnp.dot(col_ref[col, :mid], rows, preferred_element_type=F32)
        out[mid:, mid:] = jnp.dot(col_ref[col, mid:], rows[:, mid:], preferred_element_type=F32)

    def evaluate(squared, kern):
        kern[:mid] = matern(squared[:mid])
        kern[mid:, mid:] = matern(squared[mid:, mid:])

    def accumulate(slot, kern):
        col = jnp.maximum(slot, 0)
        values = val_ref[col]
        part = jnp.dot(values[:, :mid], kern[:mid], preferred_element_type=F32)
        left = mul_nt(values[:, mid:], kern[:mid, mid:])
        right = jnp.dot(values[:, mid:], kern[mid:, mid:], preferred_element_type=F32)
        part = part + jnp.concatenate([left, right], axis=1)
        here = lanes(first_leaf + col)
        sums[0][:, here] += part[:PART]
        sums[1][:, here] += part[PART:]

    turns = count // (TURNS * 2 * PAIR)
    pipeline(turns, TURNS, False, accumulate, distance, evaluate, s0, s1, k0, k1)


def load_columns(pack_ref, base, count, col_ref, val_ref):
    def step(i, _):
        for q in range(8):
            leaf = i * 8 + q
            val_ref[base + leaf] = pack_ref[0:16, lanes(leaf)]
            col_ref[base + leaf] = col_features(pack_ref[16:24, lanes(leaf)].astype(F32))
        return 0

    lax.fori_loop(0, count // 8, step, 0)


def near_local_kernel(
    scale_ref, plan_ref, points_ref, pack_ref,
    mine_ref, other_ref, row_ref,
    col_ref, val_ref, s0, s1, k0, k1,
):
    half_id = whole(scale_ref[4])
    leaves = row_ref.shape[0]
    half = leaves // 2

    def rows_step(i, _):
        for q in range(4):
            leaf = i * 4 + q
            row_ref[leaf] = row_features(coordinate_rows(points_ref[:, lanes(leaf)], scale_ref))
            mine_ref[:, lanes(leaf)] = jnp.zeros((PART, LEAF), F32)
            other_ref[:, lanes(leaf)] = jnp.zeros((PART, LEAF), F32)
        return 0

    lax.fori_loop(0, leaves // 4, rows_step, 0)
    load_columns(pack_ref, 0, half, col_ref, val_ref)
    val_ref[half] = jnp.zeros((16, LEAF), BF)
    col_ref[half] = jnp.zeros(col_ref.shape[1:], BF)
    sums = (mine_ref, other_ref)
    diagonal_loop(half_id * half, half, row_ref, col_ref, val_ref, sums, s0, s1, k0, k1)
    block_loop(0, TURNS, lambda c: c, plan_ref, row_ref, col_ref, val_ref, sums, s0, s1, k0, k1)


def near_halo_kernel(
    scale_ref, plan_ref, row_ref, inner_ref, outer_ref, first_in, second_in,
    mine_ref, other_ref,
    first, second, col_ref, val_ref, s0, s1, k0, k1,
):
    core = whole(scale_ref[4])
    half = inner_ref.shape[1] // LEAF
    odd = whole(scale_ref[3]) & 1
    bits = half.bit_length() - 1
    count = plan_ref[3, 0]

    def place(code):
        return (code & (half - 1)) | ((code >> (bits + 2)) << bits)

    def load(i, _):
        for q in range(4):
            code = plan_ref[1, i * 4 + q] & (CODE - 1)
            here = lanes(code & (half - 1))
            paired = (code >> (bits + 2)) + odd == 1
            values = jnp.where(paired, inner_ref[0:16, here], outer_ref[0:16, here])
            rows = jnp.where(paired, inner_ref[16:24, here], outer_ref[16:24, here])
            val_ref[place(code)] = values
            col_ref[place(code)] = col_features(rows.astype(F32))
        return 0

    first[...] = first_in[...]
    second[...] = second_in[...]
    lax.fori_loop(0, (count + 3) // 4, load, 0)
    val_ref[2 * half] = jnp.zeros((16, LEAF), BF)
    col_ref[2 * half] = jnp.zeros(col_ref.shape[1:], BF)
    sums = (first, second)
    block_loop(1, 1, place, plan_ref, row_ref, col_ref, val_ref, sums, s0, s1, k0, k1)

    @pl.when(core == 0)
    def _():
        mine_ref[...] = first[...]
        other_ref[...] = second[...]

    @pl.when(core == 1)
    def _():
        mine_ref[...] = second[...]
        other_ref[...] = first[...]


def split_parts(value):
    high = value.astype(BF).astype(F32)
    return jnp.concatenate([high, value - high], axis=0).astype(BF)


def join_parts(value):
    return value[0:ALL] + value[ALL : 2 * ALL]


def mul_nt(left, right):
    return lax.dot_general(left, right, NT, preferred_element_type=F32)


def over_nodes(count, unroll, work):
    group = min(unroll, count)
    if count == group:
        work([jnp.int32(i) for i in range(count)])
        return

    def step(i, _):
        work([i * group + q for q in range(group)])
        return 0

    lax.fori_loop(0, count // group, step, 0)


def store_turned(flat, r, block):
    turned = block.T
    count = turned.shape[0] // 8
    width = turned.shape[1]
    rows = pl.ds(pl.multiple_of(r * 8, 8), 8)
    flat[0:count, rows] = turned[: count * 8].reshape(count, 8, width)
    rest = turned.shape[0] - count * 8
    flat[count, pl.ds(pl.multiple_of(r * 8, 8), rest)] = turned[count * 8 :]


def load_node(flat, node):
    return flat[node >> 3, pl.ds(node & 7, RANK, stride=8)].astype(BF)


def side_by_side(first, second):
    return jnp.concatenate([first, second], axis=1)


def doubled(pair):
    low = lax.broadcasted_iota(jnp.int32, pair.shape, 1) < RANK
    turned = pltpu.roll(pair, RANK, 1)
    return jnp.where(low, pair, turned), jnp.where(low, turned, pair)


def up_kernel(
    scale_ref, pack_ref, basis_ref, raw_ref, coef_ref, export_ref, front_ref, move_ref,
    flat, pairs,
):
    core = whole(scale_ref[4])
    leaves = move_ref.shape[0]
    levels = leaves.bit_length() - 1
    base = core * leaves

    def keep(parent, first, second):
        pair = side_by_side(first, second)
        pairs[parent] = split_parts(pair)
        one, two = doubled(pair)
        coef_ref[2 * parent + 1] = split_parts(one)
        coef_ref[2 * parent + 2] = split_parts(two)

    def leaf_step(it, _):
        outs = []
        for q in range(8):
            leaf = it * 8 + q
            outs.append(mul_nt(pack_ref[0:ALL, lanes(leaf)], basis_ref[base + leaf]))
        for q in range(8):
            r = it * 8 + q
            block = jnp.concatenate([raw_ref[0, r], raw_ref[1, r]], axis=0).astype(F32)
            store_turned(flat, r, block)
        for q in range(4):
            keep(leaves // 2 - 1 + it * 4 + q, outs[2 * q], outs[2 * q + 1])
        return 0

    lax.fori_loop(0, leaves // 8, leaf_step, 0)
    root_move = load_node(flat, 0)
    move_ref[leaves - 1] = root_move
    for depth in range(levels - 1, 0, -1):
        first = 2**depth - 1
        above = 2 ** (depth - 1) - 1
        start = 2 ** (depth + 1) - 1 + core * 2**depth

        def work(nodes, first=first, above=above, start=start):
            outs = []
            for j in nodes:
                for c in range(2):
                    move = load_node(flat, start + 2 * j + c)
                    move_ref[first + 2 * j + c] = move
                    outs.append(mul_nt(pairs[first + 2 * j + c], move))
            for j, i in enumerate(nodes):
                keep(above + i, join_parts(outs[2 * j]), join_parts(outs[2 * j + 1]))

        over_nodes(2 ** (depth - 1), 8, work)
    move = load_node(flat, 1 + core)
    move_ref[0] = move
    crown = join_parts(mul_nt(pairs[0], move))
    crown = split_parts(side_by_side(crown, crown))
    coef_ref[0] = crown
    side = lax.broadcasted_iota(jnp.int32, crown.shape, 1) // RANK
    root = join_parts(mul_nt(jnp.where(side == core, crown.astype(F32), 0.0).astype(BF), root_move))
    export_ref[0] = split_parts(side_by_side(root, root))
    export_ref[1:EXPORT] = coef_ref[0 : EXPORT - 1]
    front_ref[0] = export_ref[0 : EXPORT // 2]


def joint(first, second, third):
    return jnp.concatenate([first, second, third], axis=1)


def couple_kernel(
    scale_ref, partners_ref, coef_ref, raw_ref, local_ref, tie_ref, wide, thin,
):
    device, core = whole(scale_ref[3]), whole(scale_ref[4])
    levels = (raw_ref.shape[3] + 1).bit_length() - 2
    low = lax.broadcasted_iota(jnp.int32, (2 * ALL, 2 * RANK), 1) < RANK

    def turn(i, _):
        for q in range(8):
            r = i * 8 + q
            block = jnp.concatenate([raw_ref[0, r], raw_ref[1, r]], axis=0).astype(F32)
            store_turned(wide, r, block)
            store_turned(thin, r, raw_ref[2, r].astype(F32))
        return 0

    lax.fori_loop(0, RANK // 8, turn, 0)

    def tie(node):
        return jnp.concatenate([load_node(wide, node), load_node(thin, node)], axis=1)

    tie_ref[0] = tie(0)
    for depth in range(1, SPAN + 1):
        for i in range(2 ** (depth - 1)):
            tie_ref[2 ** (depth - 1) + i] = tie(2**depth - 1 + core * 2 ** (depth - 1) + i)
    for depth in range(SPAN + 1, levels + 1):
        half = 2 ** (depth - 1)
        above = half // 2 - 1
        start = 2**depth - 1 + core * half
        shift = half - 1 - device * 2**depth - core * half

        def work(nodes, above=above, start=start, shift=shift):
            outs = []
            for j in nodes:
                for c in range(2):
                    node = start + 2 * j + c
                    mates = [coef_ref[partners_ref[f, node] + shift] for f in range(3)]
                    left = jnp.concatenate(
                        [jnp.where(low, mates[0], mates[1]), mates[2][:, :RANK]], axis=1
                    )
                    outs.append(mul_nt(left, tie(node)))
            for j, i in enumerate(nodes):
                local_ref[above + i] = side_by_side(
                    join_parts(outs[2 * j]), join_parts(outs[2 * j + 1])
                )

        over_nodes(half // 2, 8, work)


def down_kernel(
    dev_levels, scale_ref, partners_ref, top_partners_ref, top_e, top_b, tie_ref,
    local_ref, move_ref, own_ref, core_ref, next_ref, far_refs, tops_ref, mine_ref, other_ref,
    gather_ref, down, tree,
):
    device, core = whole(scale_ref[3]), whole(scale_ref[4])
    self_id = 2 * device + core
    gather_ref[0] = own_ref[...]
    gather_ref[1] = core_ref[...]
    gather_ref[2:4, 0:4] = next_ref[...]
    for i, far_ref in enumerate(far_refs):
        gather_ref[4 * i + 4 : 4 * i + 8, 0:2] = far_ref[...]
    root_ref = gather_ref if dev_levels == SPAN else tops_ref
    leaves = mine_ref.shape[0]
    levels = leaves.bit_length() - 1
    count = 2**dev_levels

    def roots(nodes):
        for i in nodes:
            parts = join_parts(root_ref[(2 * i) ^ self_id, 0].astype(F32)) + join_parts(
                root_ref[(2 * i + 1) ^ self_id, 0].astype(F32)
            )
            tree[count + i] = split_parts(parts[:, :RANK])

    over_nodes(count, 8, roots)
    for level in range(dev_levels - 1, 1, -1):

        def work(nodes, level=level):
            outs = []
            for i in nodes:
                row = 2**level - 4 + i
                kids = [tree[2 ** (level + 1) + 2 * i + c] for c in range(2)]
                outs.append(mul_nt(kids[0], top_e[row, 0]) + mul_nt(kids[1], top_e[row, 1]))
            for i, out in zip(nodes, outs):
                tree[2**level + i] = split_parts(join_parts(out))

        over_nodes(2**level, 4, work)

    mates = [tree[count + partners_ref[f, 0]] for f in range(3)]
    shallow = [join_parts(mul_nt(joint(*mates), tie_ref[0]))]
    for depth in range(1, SPAN + 1):
        half = 2 ** (depth - 1)
        for i in range(half):
            node = 2**depth - 1 + core * half + i
            picks = []
            for f in range(3):
                mate = partners_ref[f, node]
                at = ((mate >> (depth - 1)) ^ self_id) & (2 * 2**SPAN - 1)
                picks.append(gather_ref[at, half + (mate & (half - 1))][:, :RANK])
            shallow.append(join_parts(mul_nt(joint(*picks), tie_ref[half + i])))

    pushed = jnp.zeros((ALL, RANK), F32)
    for level in range(2, dev_levels):
        node = device >> (dev_levels - level)
        row = 2**level - 4 + node
        side = device >> (dev_levels - level - 1) & 1
        parts = sum(
            mul_nt(tree[2**level + top_partners_ref[row, f]], top_b[row, f]) for f in range(3)
        )
        here = split_parts(join_parts(parts) + pushed)
        pushed = join_parts(jnp.dot(here, top_e[row, side], preferred_element_type=F32))

    root = split_parts(shallow[0] + pushed)
    both = join_parts(jnp.dot(root, move_ref[leaves - 1], preferred_element_type=F32))
    down[0] = split_parts(shallow[1] + jnp.where(core == 0, both[:, :RANK], both[:, RANK:]))
    for depth in range(levels):
        first = 2**depth - 1

        def work(nodes, depth=depth, first=first):
            outs = [
                jnp.dot(down[first + i], move_ref[first + i], preferred_element_type=F32)
                for i in nodes
            ]
            for i, out in zip(nodes, outs):
                node = first + i
                if depth + 2 <= SPAN:
                    kid = 2 ** (depth + 1) + 2 * i
                    base = side_by_side(shallow[kid], shallow[kid + 1])
                else:
                    base = local_ref[node]
                pair = base + join_parts(out)
                if depth == levels - 1:
                    for c in range(2):
                        value = pair[:, c * RANK : (c + 1) * RANK]
                        one, two = value[:PART], value[PART:]
                        mine_ref[2 * i + c] = jnp.where(core == 0, one, two).astype(BF)
                        other_ref[2 * i + c] = jnp.where(core == 0, two, one).astype(BF)
                else:
                    down[2 * node + 1] = split_parts(pair[:, :RANK])
                    down[2 * node + 2] = split_parts(pair[:, RANK:])

        if depth < SPAN:
            work(list(range(2**depth)))
        else:
            over_nodes(2**depth, 8, work)


def final_kernel(
    scale_ref, mine_ref, got_ref, basis, noise, vec, near, swap, out_hbm, out, sems
):
    core = whole(scale_ref[4])
    leaves = mine_ref.shape[0]
    chunks = 2
    per = leaves // chunks
    wide = per * LEAF
    sends = []
    for part, low_ref in enumerate((mine_ref, got_ref)):
        base = jnp.where(core == part, 0, leaves)
        for c in range(chunks):

            def last(nodes, c=c, low_ref=low_ref, base=base):
                rows = [c * per + i for i in nodes]
                fars = [
                    jnp.dot(low_ref[n], basis[base + n], preferred_element_type=F32)
                    for n in rows
                ]
                for n, far in zip(rows, fars):
                    here = lanes(base + n)
                    total = near[:, here] + swap[:, here]
                    out[:, here] = total + noise[:, here] * vec[:, here].astype(F32) + far

            over_nodes(per, 8, last)
            piece = pl.ds(pl.multiple_of((base + c * per) * LEAF, wide), wide)
            send = pltpu.make_async_copy(
                out.at[:, piece], out_hbm.at[:, piece], sems.at[part * chunks + c]
            )
            send.start()
            sends.append(send)
    for send in sends:
        send.wait()


def swap_mask(value, mask):
    total = lax.axis_size("leaf") * lax.axis_size("sub")
    return lax.ppermute(value, ("leaf", "sub"), [(i, i ^ mask) for i in range(total)])


def after(value, anchor):
    return lax.optimization_barrier((value, anchor))[0]


def body(
    points, inv_scale, noise, vectors, leaf_basis, local_transfer, top_transfer,
    local_coupling, top_coupling, local_partners, top_partners, near_offsets, near_cols,
):
    subs = lax.axis_size("sub")
    count = lax.axis_size("leaf") * subs
    dev_levels = count.bit_length() - 1
    device = lax.axis_index("leaf") * subs + lax.axis_index("sub")
    core = lax.axis_index("vec")
    scale = jnp.concatenate([inv_scale, jnp.stack([device, core]).astype(F32)])
    size = vectors.shape[1]
    leaves = near_offsets.shape[0]
    slots = near_cols.shape[0]
    half = size // 2
    sds = jax.ShapeDtypeStruct
    scratch_blocks = [
        VMEM((PAIR, LEAF, LEAF), F32), VMEM((PAIR, LEAF, LEAF), F32),
        VMEM((PAIR, LEAF, LEAF), BF), VMEM((PAIR, LEAF, LEAF), BF),
    ]

    got = lax.ppermute(vectors, "vec", [(0, 1), (1, 0)])

    plan = pl.pallas_call(
        functools.partial(plan_kernel, leaves),
        name="plan",
        out_shape=sds((8, slots + 128), jnp.int32),
        in_specs=[sspec(), vspec()],
        out_specs=vspec(),
        compiler_params=params(8),
        cost_estimate=pl.CostEstimate(flops=3 * 10**9, bytes_accessed=1 << 16, transcendentals=0),
    )(scale, jnp.concatenate([near_offsets, near_cols]).reshape(1, leaves + slots))

    pack = pl.pallas_call(
        pack_kernel,
        name="pack",
        out_shape=sds((24, half), BF),
        in_specs=[sspec(), vspec(), vspec(), vspec()],
        out_specs=vspec(),
        compiler_params=params(8),
        cost_estimate=pl.CostEstimate(flops=2 * 10**9, bytes_accessed=2 << 20, transcendentals=0),
    )(scale, points, vectors, got)
    axes = ("leaf", "sub")
    inner = lax.ppermute(pack, axes, [(i, i ^ 1) for i in range(count)])
    outer = lax.ppermute(
        pack, axes, [(i, ((i + 1) ^ 1) - 1) for i in range(1, count - 1)]
    )

    moves_raw = jnp.transpose(local_transfer, (1, 2, 3, 0))
    part = leaves // 2
    coef, export, front, moves = pl.pallas_call(
        up_kernel,
        name="up",
        out_shape=(
            sds((2 * part - 1, 2 * ALL, 2 * RANK), BF), sds((EXPORT, 2 * ALL, 2 * RANK), BF),
            sds((1, EXPORT // 2, 2 * ALL, 2 * RANK), BF), sds((part, RANK, 2 * RANK), BF),
        ),
        in_specs=[sspec(), vspec(), vspec(), vspec()],
        out_specs=(vspec(),) * 4,
        scratch_shapes=[
            VMEM((leaves // 8, RANK * 8, 2 * RANK), F32),
            VMEM((part - 1, 2 * ALL, 2 * RANK), BF),
        ],
        compiler_params=params(18),
        cost_estimate=pl.CostEstimate(flops=8 * 10**9, bytes_accessed=8 << 20, transcendentals=0),
    )(scale, pack, leaf_basis, moves_raw)
    from_core = lax.ppermute(export, "vec", [(0, 1), (1, 0)])
    pack, _ = lax.optimization_barrier((pack, export))
    first, second, row_feat = pl.pallas_call(
        near_local_kernel,
        name="near_local",
        out_shape=(
            sds((PART, size), F32), sds((PART, size), F32), sds((leaves, 32, LEAF), BF),
        ),
        in_specs=[sspec()] * 2 + [vspec()] * 2,
        out_specs=(vspec(), vspec(), vspec()),
        scratch_shapes=[
            VMEM((leaves // 2 + 1, LEAF, 32), BF), VMEM((leaves // 2 + 1, 16, LEAF), BF),
            *scratch_blocks,
        ],
        compiler_params=params(22),
        cost_estimate=pl.CostEstimate(
            flops=36 * 10**9, bytes_accessed=8 << 20, transcendentals=190 * 2**17
        ),
    )(scale, plan, points, pack)

    from_core = after(from_core, first)
    near_pair = jnp.concatenate([front, from_core[None, 0 : EXPORT // 2]], axis=0)
    coef_late, near_pair = lax.optimization_barrier((coef, near_pair))
    from_next = swap_mask(near_pair, 1)
    ties_raw = jnp.transpose(local_coupling, (1, 2, 3, 0))
    mates = jnp.transpose(local_partners)
    local, ties = pl.pallas_call(
        couple_kernel,
        name="couple",
        out_shape=(
            sds((part - 1, ALL, 2 * RANK), F32), sds((EXPORT, RANK, 3 * RANK), BF),
        ),
        in_specs=[sspec()] * 2 + [vspec(), vspec()],
        out_specs=(vspec(),) * 2,
        scratch_shapes=[
            VMEM((leaves // 4, RANK * 8, 2 * RANK), F32),
            VMEM((leaves // 4, RANK * 8, RANK), F32),
        ],
        compiler_params=params(30),
        cost_estimate=pl.CostEstimate(flops=16 * 10**9, bytes_accessed=8 << 20, transcendentals=0),
    )(scale, mates, coef_late, ties_raw)

    first, _, from_next = lax.optimization_barrier((first, local, from_next))
    quad = jnp.concatenate([near_pair[:, 0:2], from_next[:, 0:2]], axis=0)
    from_far = [swap_mask(quad, mask) for mask in (2, 4, 6)]
    mine, other = pl.pallas_call(
        near_halo_kernel,
        name="near_halo",
        out_shape=(sds((PART, size), F32), sds((PART, size), F32)),
        in_specs=[sspec()] * 2 + [vspec()] * 5,
        out_specs=(vspec(), vspec()),
        scratch_shapes=[
            VMEM((PART, size), F32), VMEM((PART, size), F32),
            VMEM((leaves + 1, LEAF, 32), BF), VMEM((leaves + 1, 16, LEAF), BF),
            *scratch_blocks,
        ],
        compiler_params=params(26),
        cost_estimate=pl.CostEstimate(
            flops=20 * 10**9, bytes_accessed=8 << 20, transcendentals=60 * 2**17
        ),
    )(scale, plan, row_feat, inner, outer, first, second)
    swapped = lax.ppermute(other, "vec", [(0, 1), (1, 0)])

    tops = export
    if dev_levels > SPAN:
        tops = jnp.concatenate(
            [export[None, 0:1], from_core[None, 0:1], from_next[:, 0:1]]
            + [part[:, 0:1] for part in from_far],
            axis=0,
        )
        for bit in range(SPAN, dev_levels):
            tops = jnp.concatenate([tops, swap_mask(tops, 2**bit)], axis=0)
    low_mine, low_other = pl.pallas_call(
        lambda *refs: down_kernel(dev_levels, *refs[:11], refs[11:14], *refs[14:]),
        name="down",
        out_shape=(sds((part, PART, RANK), BF), sds((part, PART, RANK), BF)),
        in_specs=[sspec()] * 3 + [vspec()] * 12,
        out_specs=(vspec(), vspec()),
        scratch_shapes=[
            VMEM((2 * 2**SPAN, EXPORT, 2 * ALL, 2 * RANK), BF),
            VMEM((part - 1, 2 * ALL, RANK), BF), VMEM((2 * count, 2 * ALL, RANK), BF),
        ],
        compiler_params=params(14),
        cost_estimate=pl.CostEstimate(flops=40 * 10**9, bytes_accessed=4 << 20, transcendentals=0),
    )(
        scale, mates, top_partners, top_transfer, top_coupling, ties, local, moves,
        export, from_core, from_next, *from_far, tops,
    )
    low_got = lax.ppermute(low_other, "vec", [(0, 1), (1, 0)])

    return pl.pallas_call(
        final_kernel,
        name="final",
        out_shape=sds((PART, size), F32),
        in_specs=[sspec()] + [vspec()] * 7,
        out_specs=hspec(),
        scratch_shapes=[VMEM((PART, size), F32), pltpu.SemaphoreType.DMA((4,))],
        compiler_params=params(10),
        cost_estimate=pl.CostEstimate(flops=2 * 10**9, bytes_accessed=4 << 20, transcendentals=0),
    )(scale, low_mine, low_got, leaf_basis, noise.reshape(1, size), vectors, mine, swapped)


def solution(mesh):
    return jax.shard_map(
        body,
        mesh=mesh,
        in_specs=(
            P("groups", ("leaf", "sub")),
            P("groups"),
            P(("groups", "leaf", "sub")),
            P(("groups", "vec"), ("leaf", "sub")),
            P(("groups", "leaf", "sub"), None, None),
            P(("groups", "leaf", "sub"), None, None, None),
            P("groups", None, None, None),
            P(("groups", "leaf", "sub"), None, None, None),
            P("groups", None, None, None),
            P(("groups", "leaf", "sub"), None),
            P("groups", None),
            P(("groups", "leaf", "sub")),
            P(("groups", "leaf", "sub")),
        ),
        out_specs=P(("groups", "vec"), ("leaf", "sub")),
        check_vma=False,
    )
```
